32 devices in a mesh: dp: 16 (over z, y, x), mp: 2 (over core).
Axes of the slice: x: 2, y: 2, z: 4, core: 2. Of those that a mesh axis runs over, the one named last changes fastest.
Arguments:
- images: float32 [512, 16, 16, 3], P(('dp', 'mp')), may hold values from -4 to 4
- noise: float32 [512, 16, 16, 3], P(('dp', 'mp')), may hold values from -5 to 5
- timestep: int32 [512], P(('dp', 'mp')), may hold values from 8 to 64, as said below
- stride: int32 [512], P(('dp', 'mp')), may hold values from 4 to 8
- bucket: int32 [512], P(('dp', 'mp')), may hold values from 0 to 15, as said below
- steps_table: int32 [16], replicated, may hold values from 2 to 4
- master: float32 [2076672], P(('dp', 'mp'))
- first_moment: float32 [2076672], P(('dp', 'mp'))
- second_moment: float32 [2076672], P(('dp', 'mp')), as said below
- teacher: bfloat16 [2076672], P(('dp', 'mp'))
- step_count: int32 [1], replicated, may hold values from 2 to 20
Outputs:
- loss: float32 [], replicated
- new_master: float32 [2076672], P(('dp', 'mp'))
- new_first: float32 [2076672], P(('dp', 'mp'))
- new_second: float32 [2076672], P(('dp', 'mp'))
The draws below stay inside these ranges and needn't reach their ends.
Inputs may be any that keep to these rules, and one draw needn't show every extreme that they name: All images of one index of dp share one bucket; some index of dp holds a bucket of 4 steps. Each image's timestep is at least its bucket's step count times its stride. `second_moment`: Positive.
All inputs are finite; a program needn't handle non-finite values.
Results may differ from the reference program's by a relative error of at most 0.0012.
The reference program's roundings to bfloat16 on the way count: a program that leaves them out, or rounds other values in their place, can miss the bound.
Values may be sent and summed in bfloat16 or wider, within the bound.
A program may use at most 128 MiB of HBM per device.

```python
import math
import jax
import jax.numpy as jnp
from jax import lax

C1 = 128
C2 = 256
GROUPS = 32
SIDE = 16
IMG_DEV = 16
KMAX = 4
TGRID = 64
NBUCK = 16
IMAGES = 512
SHARDS = 32
PARAMS = 2076672
N_DP = 16


def segments_drawn():
    matrices = [('w_in', 27, C1), ('w_down', 9 * C1, C2), ('w_res1', 9 * C2, C2), ('w_res2', 9 * C2, C2), ('w_time', C1, C2), ('w_qkv', C2, 3 * C2), ('w_proj', C2, C2), ('w_up', 9 * C2, C1), ('w_final', 9 * C1, 3)]
    vectors = [('g1', C2), ('s1', C2), ('g2', C2), ('s2', C2), ('g3', C2), ('s3', C2), ('g4', C1), ('s4', C1), ('b_in', C1), ('b_down', C2), ('b_res1', C2), ('b_res2', C2), ('b_time', C2), ('b_query', C2), ('b_value', C2), ('b_proj', C2), ('b_up', C1), ('b_final', 3)]
    listing = []
    cursor = 0
    for entry_name, height, breadth in matrices:
        listing.append((entry_name, cursor, (height, breadth), 'matrix'))
        cursor += height * breadth
    for entry_name, length in vectors:
        listing.append((entry_name, cursor, (length,), 'gain' if entry_name[0] != 'b' else 'bias'))
        cursor += length
    return listing


def spread_of_drawn(entry_name, entry_shape):
    value_spread = entry_shape[0] ** (-0.5)
    if entry_name == 'w_proj':
        value_spread = value_spread * (SIDE * SIDE / 4.0) ** 0.5
    return value_spread


def layout_vectors():
    stored = jnp.arange(PARAMS)
    shard_len = PARAMS // SHARDS
    position = stored % shard_len * SHARDS + stored // shard_len
    center = jnp.zeros((PARAMS,), jnp.float32)
    spread = jnp.full((PARAMS,), 0.1, jnp.float32)
    grad_size = jnp.full((PARAMS,), 0.04 * IMAGES ** (-0.5), jnp.float32)
    for entry_name, offset, entry_shape, entry_kind in segments_drawn():
        inside = (position >= offset) & (position < offset + math.prod(entry_shape))
        if entry_kind == 'matrix':
            spread = jnp.where(inside, spread_of_drawn(entry_name, entry_shape), spread)
        else:
            grad_size = jnp.where(inside, 0.4 * IMAGES ** (-0.5), grad_size)
        if entry_kind == 'gain':
            center = jnp.where(inside, 1.0, center)
    return (center, spread, grad_size)


def weight_values(key):
    center, spread, grad_size = layout_vectors()
    base_draw = jax.random.truncated_normal(key, -4.0, 4.0, (PARAMS,), jnp.float32)
    return center + spread * base_draw


def draw_master(key, part):
    return weight_values(jax.random.fold_in(key, 1))


def draw_teacher(key, part):
    return weight_values(jax.random.fold_in(key, 2)).astype(jnp.bfloat16)


def draw_first_moment(key, part):
    center, spread, grad_size = layout_vectors()
    return grad_size * jax.random.uniform(jax.random.fold_in(key, 3), (PARAMS,), jnp.float32, -1.5, 1.5)


def draw_second_moment(key, part):
    center, spread, grad_size = layout_vectors()
    factor = jnp.exp(jax.random.uniform(jax.random.fold_in(key, 4), (PARAMS,), jnp.float32, math.log(0.5), math.log(8.0)))
    return jnp.square(grad_size) * factor


def integer_plan(key):
    base_key = jax.random.fold_in(key, 5)
    key_table, key_force, key_bucket, key_stride, key_time = jax.random.split(base_key, 5)
    counts_table = 2 + jax.random.randint(key_table, (NBUCK,), 0, KMAX - 1)
    forced = jax.random.randint(key_force, (), 0, NBUCK)
    counts_table = counts_table.at[forced].set(KMAX)
    device_bucket = jax.random.randint(key_bucket, (N_DP,), 0, NBUCK).at[0].set(forced)
    bucket_ids = jnp.repeat(device_bucket, IMAGES // N_DP)
    counts = counts_table[bucket_ids]
    stride_ids = jax.random.randint(key_stride, (IMAGES,), 4, 9)
    lowest = counts * stride_ids
    timestep_ids = jax.random.randint(key_time, (IMAGES,), lowest, TGRID + 1).at[0].set(TGRID)
    return (counts_table, bucket_ids, stride_ids, timestep_ids)


def draw_steps_table(key, part):
    return integer_plan(key)[0]


def draw_bucket(key, part):
    return integer_plan(key)[1]


def draw_stride(key, part):
    return integer_plan(key)[2]


def draw_timestep(key, part):
    return integer_plan(key)[3]


def steps_of(stream_key, extent, cuts, least, largest):
    def one(dim, parts):
        draws = jax.random.uniform(jax.random.fold_in(jax.random.fold_in(stream_key, 6), dim), (parts,), jnp.float32, least / len(cuts), largest / len(cuts))
        return jnp.repeat(jnp.exp(draws), extent[dim] // parts).reshape((-1,) + (1,) * (len(extent) - dim - 1))

    level = one(*cuts[0])
    for cut in cuts[1:]:
        level = level * one(*cut)
    return level


def scatter_about(rng, extent, width, reach, cuts=(), kind=jnp.bfloat16):
    entries = jax.random.normal(rng, extent, jnp.float32) * width
    if len(cuts) > 0:
        entries = steps_of(rng, extent, cuts, -0.22, 0.18) * entries
    return jnp.clip(entries, min=-reach, max=reach).astype(kind)


def setup_inputs(seed: int = 0) -> dict:
    keys = jax.random.split(jax.random.key(seed), 12)
    images = scatter_about(keys[0], (IMAGES, SIDE, SIDE, 3), 1.0, 4.0, ((0, 32),), jnp.float32)
    noise = scatter_about(keys[1], (IMAGES, SIDE, SIDE, 3), 1.0, 5.0, ((0, 32),), jnp.float32)
    timestep = draw_timestep(jax.random.fold_in(keys[11], 71), 0)
    stride = draw_stride(jax.random.fold_in(keys[11], 71), 0)
    bucket = draw_bucket(jax.random.fold_in(keys[11], 71), 0)
    steps_table = draw_steps_table(jax.random.fold_in(keys[11], 71), 0)
    master = draw_master(jax.random.fold_in(keys[11], 71), 0)
    first_moment = draw_first_moment(jax.random.fold_in(keys[11], 71), 0)
    second_moment = draw_second_moment(jax.random.fold_in(keys[11], 71), 0)
    teacher = draw_teacher(jax.random.fold_in(keys[11], 71), 0)
    step_count = jax.random.randint(keys[10], (1,), 2, 21).astype(jnp.int32)
    return dict(images=images, noise=noise, timestep=timestep, stride=stride, bucket=bucket, steps_table=steps_table, master=master, first_moment=first_moment, second_moment=second_moment, teacher=teacher, step_count=step_count)


@jax.custom_vjp
def low(v):
    return lax.optimization_barrier(v.astype(jnp.bfloat16)).astype(jnp.float32)

@jax.custom_vjp
def low_back(v):
    return v

def low_keep(v):
    return (low(v), None)

def low_pass(kept, grad):
    return (grad,)

def back_keep(v):
    return (v, None)

def back_low(kept, grad):
    return (low(grad),)
low.defvjp(low_keep, low_pass)
low_back.defvjp(back_keep, back_low)
HIGHEST = lax.Precision.HIGHEST

def segments():
    matrices = [('w_in', 27, C1), ('w_down', 9 * C1, C2), ('w_res1', 9 * C2, C2), ('w_res2', 9 * C2, C2), ('w_time', C1, C2), ('w_qkv', C2, 3 * C2), ('w_proj', C2, C2), ('w_up', 9 * C2, C1), ('w_final', 9 * C1, 3)]
    vectors = [('g1', C2), ('s1', C2), ('g2', C2), ('s2', C2), ('g3', C2), ('s3', C2), ('g4', C1), ('s4', C1), ('b_in', C1), ('b_down', C2), ('b_res1', C2), ('b_res2', C2), ('b_time', C2), ('b_query', C2), ('b_value', C2), ('b_proj', C2), ('b_up', C1), ('b_final', 3)]
    listing = []
    cursor = 0
    for entry_name, height, breadth in matrices:
        listing.append((entry_name, cursor, (height, breadth), 'matrix'))
        cursor += height * breadth
    for entry_name, length in vectors:
        listing.append((entry_name, cursor, (length,), 'gain' if entry_name[0] != 'b' else 'bias'))
        cursor += length
    return listing

def stored_order(flat_vector):
    return flat_vector.reshape(SHARDS, -1).T.reshape(-1)

def logical_of(position):
    shard_len = PARAMS // SHARDS
    return position % shard_len * SHARDS + position // shard_len

def unpack(flat_vector):
    weights = {}
    for entry_name, offset, entry_shape, entry_kind in segments():
        amount = math.prod(entry_shape)
        weights[entry_name] = flat_vector[offset:offset + amount].reshape(entry_shape)
    return weights

def spread_of(entry_name, entry_shape):
    value_spread = entry_shape[0] ** (-0.5)
    if entry_name == 'w_proj':
        value_spread = value_spread * (SIDE * SIDE / 4.0) ** 0.5
    return value_spread

def rates(position):
    learn = jnp.zeros(position.shape, jnp.float32)
    decay = jnp.zeros(position.shape, jnp.float32)
    for entry_name, offset, entry_shape, entry_kind in segments():
        inside = (position >= offset) & (position < offset + math.prod(entry_shape))
        if entry_kind == 'matrix':
            learn = jnp.where(inside, 0.5 * spread_of(entry_name, entry_shape), learn)
            decay = jnp.where(inside, 0.01, decay)
        elif entry_kind == 'gain':
            learn = jnp.where(inside, 0.2, learn)
        else:
            learn = jnp.where(inside, 0.05, learn)
    return (learn, decay)

def patches(source, step_size):
    padded = jnp.pad(source, ((0, 0), (1, 1), (1, 1), (0, 0)))
    height, breadth = (source.shape[1], source.shape[2])
    pieces = [padded[:, row_at:row_at + height:step_size, col_at:col_at + breadth:step_size, :] for row_at in range(3) for col_at in range(3)]
    return jnp.concatenate(pieces, axis=3)

def group_norm(source, gain_vec, shift_vec):
    grouped = source.reshape(source.shape[0], -1, GROUPS, source.shape[-1] // GROUPS)
    center = lax.optimization_barrier(jnp.mean(grouped, axis=(1, 3), keepdims=True))
    spread = lax.optimization_barrier(jnp.mean(jnp.square(grouped - center), axis=(1, 3), keepdims=True))
    normed = ((grouped - center) * lax.rsqrt(spread + 1e-05)).reshape(source.shape)
    return normed * gain_vec + shift_vec

def norm_act(source, gain_vec, shift_vec):
    return jax.nn.silu(group_norm(source, gain_vec, shift_vec))

def angle_of(step_int):
    return 0.1 + 1.35 * step_int.astype(jnp.float32) / TGRID

def coef_cos(step_int):
    return jnp.cos(angle_of(step_int))[:, None, None, None]

def coef_sin(step_int):
    return jnp.sin(angle_of(step_int))[:, None, None, None]

def time_features(time_step):
    halfway = C1 // 2
    freqs = jnp.exp(-math.log(1000.0) * jnp.arange(halfway).astype(jnp.float32) / halfway)
    phases = time_step.astype(jnp.float32)[:, None] * freqs
    return jnp.concatenate([jnp.sin(phases), jnp.cos(phases)], axis=1)

def conv(source, weight, shift_vec, step_size):
    columns = patches(low(source), step_size)
    product = jnp.einsum('nhwk,ko->nhwo', columns, weight, precision=HIGHEST)
    return low_back(product) + shift_vec

def both_ways(value):
    return low(low_back(value))

def attention(tokens, weights):
    normed = group_norm(tokens, weights['g3'], weights['s3'])
    bias_qkv = jnp.concatenate([weights['b_query'], jnp.zeros((C2,), jnp.float32), weights['b_value']])
    joined = both_ways(jnp.einsum('npc,ck->npk', low(normed), weights['w_qkv'], precision=HIGHEST) + bias_qkv)
    queries, key_part, values = (joined[..., :C2], joined[..., C2:2 * C2], joined[..., 2 * C2:])
    scores = low_back(jnp.einsum('npc,nqc->npq', queries, key_part, precision=HIGHEST) * C2 ** (-0.5))
    attend = jax.nn.softmax(scores, axis=-1)
    mixture = both_ways(jnp.einsum('npq,nqc->npc', low(attend), values, precision=HIGHEST))
    product = jnp.einsum('npc,co->npo', mixture, weights['w_proj'], precision=HIGHEST)
    return low_back(product) + weights['b_proj']

def net(weights, noisy, time_step):
    batch_size = noisy.shape[0]
    top_feat = conv(noisy, weights['w_in'], weights['b_in'], 1)
    low_feat = conv(top_feat, weights['w_down'], weights['b_down'], 2)
    res_mid = conv(norm_act(low_feat, weights['g1'], weights['s1']), weights['w_res1'], weights['b_res1'], 1)
    features = jax.nn.silu(time_features(time_step))
    embedded = low_back(jnp.dot(low(features), weights['w_time'], precision=HIGHEST)) + weights['b_time']
    res_mid = res_mid + embedded[:, None, None, :]
    res_out = low_feat + conv(norm_act(res_mid, weights['g2'], weights['s2']), weights['w_res2'], weights['b_res2'], 1)
    tokens = res_out.reshape(batch_size, -1, C2)
    att_out = res_out + attention(tokens, weights).reshape(res_out.shape)
    widened = jnp.repeat(jnp.repeat(att_out, 2, axis=1), 2, axis=2)
    up_feat = conv(widened, weights['w_up'], weights['b_up'], 1) + top_feat
    return conv(norm_act(up_feat, weights['g4'], weights['s4']), weights['w_final'], weights['b_final'], 1)

def teacher_run(weights, noisy, time_now, step_len, count_img):
    latent = noisy
    for turn_at in range(KMAX):
        active = turn_at < count_img
        current = jnp.where(active, time_now - turn_at * step_len, time_now)
        later = current - step_len
        estimate = net(weights, latent, current)
        stepped = coef_cos(later) * estimate + coef_sin(later) * (latent - coef_cos(current) * estimate) / coef_sin(current)
        latent = jnp.where(active[:, None, None, None], stepped, latent)
    return latent

def reference(images, noise, timestep, stride, bucket, steps_table, master, first_moment, second_moment, teacher, step_count):
    count_img = jnp.take(steps_table, bucket)
    noisy = coef_cos(timestep) * images + coef_sin(timestep) * noise
    blocks = IMAGES // IMG_DEV

    def split_blocks(array):
        return array.reshape((blocks, IMG_DEV) + array.shape[1:])
    teacher_w = unpack(stored_order(teacher.astype(jnp.float32)))
    latent = lax.map(lambda group: teacher_run(teacher_w, group[0], group[1], group[2], group[3]), (split_blocks(noisy), split_blocks(timestep), split_blocks(stride), split_blocks(count_img)))
    latent = latent.reshape(noisy.shape)
    final_t = timestep - count_img * stride
    target = (coef_sin(timestep) * latent - coef_sin(final_t) * noisy) / jnp.sin(angle_of(timestep) - angle_of(final_t))[:, None, None, None]
    snr_weight = jnp.maximum(jnp.square(coef_cos(timestep) / coef_sin(timestep)), 1.0)[:, 0, 0, 0]
    mean_tgt = lax.optimization_barrier(jnp.mean(target, axis=(0, 1, 2)))
    var_tgt = lax.optimization_barrier(jnp.mean(jnp.square(target), axis=(0, 1, 2))) - jnp.square(mean_tgt)
    checked = jax.checkpoint(net)

    def objective(flat_master):
        weights = unpack(stored_order(low(flat_master)))
        preds = lax.map(lambda group: checked(weights, group[0], group[1]), (split_blocks(noisy), split_blocks(timestep)))
        preds = preds.reshape(noisy.shape)
        errors = lax.optimization_barrier(jnp.mean(jnp.square(preds - target), axis=(1, 2, 3)))
        mse_part = jnp.sum(snr_weight * errors) / IMAGES
        mean_pred = lax.optimization_barrier(jnp.mean(preds, axis=(0, 1, 2)))
        var_pred = lax.optimization_barrier(jnp.mean(jnp.square(preds), axis=(0, 1, 2))) - jnp.square(mean_pred)
        return mse_part + jnp.sum(jnp.square(mean_pred - mean_tgt) + jnp.square(var_pred - var_tgt))
    loss, pullback = jax.vjp(objective, master)
    gradient = pullback(jnp.ones_like(loss))[0]
    learn, decay = rates(logical_of(jnp.arange(PARAMS)))
    steps_done = step_count[0].astype(jnp.float32)
    new_first = 0.5 * first_moment + 0.5 * gradient
    new_second = 0.5 * second_moment + 0.5 * jnp.square(gradient)
    fix_rate = 1.0 - jnp.power(0.5, steps_done)
    new_master = master - learn * (new_first / fix_rate / (jnp.sqrt(new_second / fix_rate) + 1e-08) + decay * master)
    return (loss, new_master, new_first, new_second)
```

```python
import math
import jax
import jax.numpy as jnp
from jax import lax
from jax.experimental import pallas as pl
from jax.experimental.pallas import tpu as pltpu
from jax.sharding import PartitionSpec as P

C1, C2, N = 128, 256, 16
SIDE, TGRID, KMAX = 16, 64, 4
F32, BF = jnp.float32, jnp.bfloat16
O_DOWN, O_R1, O_R2, O_TIME, O_QKV, O_PROJ, O_UP, MID = 0, 1152, 3456, 5760, 5888, 6656, 6912, 8064
HEAD = 3456
BLOCK = {}
_at = 54
for _name, _wide in (("g1",2),("s1",2),("g2",2),("s2",2),("g3",2),("s3",2),("g4",1),("s4",1),("b_in",1),("b_down",2),("b_res1",2),
                     ("b_res2",2),("b_time",2),("b_query",2),("b_value",2),("b_proj",2),("b_up",1),("b_final",1)):
    BLOCK[_name] = (_at, _wide)
    _at += _wide

def iota(shape, d): return lax.broadcasted_iota(jnp.int32, shape, d)

def nt(a, b): return lax.dot_general(a, b, (((1,),(1,)),((),())), preferred_element_type=F32)
def nn(a, b): return lax.dot_general(a, b, (((1,),(0,)),((),())), preferred_element_type=F32)

def one_hot(cond): return jnp.where(cond, 1.0, 0.0).astype(BF)

def split3(v):
    hi = v.astype(BF); r = v - hi.astype(F32)
    mid = r.astype(BF); lo = (r - mid.astype(F32)).astype(BF)
    return jnp.concatenate([hi, mid, lo], axis=0)

def group_sum(v, per):
    C = v.shape[1]
    G = one_hot(iota((C,C),0)//per == iota((C,C),1)//per)
    r = nn(split3(v), G)
    return r[0:N] + r[N:2*N] + r[2*N:3*N]

def prep(tg_ref, wt_ref, wup_ref, win_ref, wfin_ref, wfb_ref, sm_ref, D):
    R = 256 // D
    row, o = iota((256,256),1), iota((256,256),0)
    dev, m = row // R, row % R
    perm = one_hot(o == (dev + ((-HEAD) % D)) % D + D * m)
    CH = 1152
    for c in range(7):
        wt_ref[:, c*CH:(c+1)*CH] = nn(perm, tg_ref[:, c*CH:(c+1)*CH]).astype(BF)
    kk, ci = iota((256,256),0), iota((256,256),1)
    peo = one_hot(ci == 2*(kk % 128) + kk // 128)
    for t in range(9):
        cs = O_UP + t*128
        both = jnp.concatenate([wt_ref[0:128, cs:cs+128], wt_ref[128:256, cs:cs+128]], axis=1)
        wup_ref[t] = nn(both, peo).astype(BF)
    kq, lq = iota((768,768),0), iota((768,768),1)
    pq = one_hot(kq == 3*(lq % 256) + lq // 256)
    wt_ref[:, O_QKV:O_QKV+768] = nn(wt_ref[:, O_QKV:O_QKV+768], pq).astype(BF)
    perm0 = one_hot(o == dev + D * m)
    sm_ref[...] = nn(perm0, tg_ref[:, MID:MID+128]).T
    halves = jnp.concatenate([sm_ref[0:32, 0:128], sm_ref[0:32, 128:256]], axis=0).astype(BF)
    l, r = iota((128,64),0), iota((128,64),1)
    k = 3*(l % 9) + l // 9
    win_ref[...] = nn(one_hot((l < 27) & (r == 32*(k % 2) + k // 2)), halves).astype(BF)
    t16, r16 = iota((16,64),0), iota((16,64),1)
    pieces = []
    for h in range(3):
        blk = 27 + 3*t16 + h
        pieces.append(nn(one_hot((t16 < 9) & (r16 == 32*(blk % 2) + blk // 2)), halves))
    flat = jnp.concatenate(pieces, axis=1).astype(BF)
    acc = jnp.zeros((128,128), F32)
    for c in range(3):
        wc = nn(flat, one_hot(iota((384,128),0) == 3*iota((384,128),1) + c)).astype(BF)
        acc += nn(one_hot((iota((128,16),1) < 9) & (iota((128,16),0) == 9*c + iota((128,16),1))), wc)
    wfb = acc.astype(BF)
    wfb_ref[...] = wfb
    a, z = iota((128,128),0), iota((128,128),1)
    for t in range(9):
        wfin_ref[:, 128*t:128*t+128] = nn(one_hot((a < 27) & (z == 9*(a // 9) + t)), wfb).astype(BF)

def final_bias(sm_ref):
    b = sm_ref[42:43, 0:128].astype(BF)
    return nn(b, one_hot((iota((128,128),1) < 27) & (iota((128,128),0) == iota((128,128),1) // 9)))

def gn_stats(load, rows, per, C, count):
    def s1(i, acc): return acc + jnp.sum(load(i), axis=0)
    m = group_sum(lax.fori_loop(0, rows, s1, jnp.zeros((N,C),F32)), per) * (1.0/count)
    def s2(i, acc): return acc + jnp.sum(jnp.square(load(i) - m), axis=0)
    v = group_sum(lax.fori_loop(0, rows, s2, jnp.zeros((N,C),F32)), per) * (1.0/count)
    return m, lax.rsqrt(v + 1e-5)

def sigmoid(x): return 1.0 / (1.0 + jnp.exp(-x))

def vec(v_ref, name, C=C2):
    at, wide = BLOCK[name]
    return jnp.concatenate([v_ref[b//2:b//2+1, 128*(b%2):128*(b%2)+128] for b in range(at, at+wide)], axis=1)

def net(x_ref, feat, wt, wup, win, wfin, v_ref, sc):
    xp, tp, top, low, ap, mid, res, qkv, ob, yp, up, ep = (sc[k] for k in ("xp","tp","top","low","ap","mid","res","qkv","ob","yp","up","ep"))
    lane = iota((1,1,128),2)
    def save(si, m, inv):
        if "st" in sc:
            C = m.shape[1]
            sc["st"][2*si,:,0:C] = m
            sc["st"][2*si+1,:,0:C] = inv
    bfin = final_bias(v_ref)
    def a0(y, _):
        xp[y+1, 1:17] = x_ref[pl.ds(y*16,16)].astype(BF)
        return 0
    lax.fori_loop(0,16,a0,0)
    def a1(y2, _):
        pieces=[]
        for k in range(4):
            y = y2*4+k
            cols = jnp.zeros((16,16,128),BF)
            for t in range(9):
                w = xp[y+t//3, t%3:t%3+16]
                cols = jnp.where((lane%9==t)&(lane<27), w, cols) if t else jnp.where((lane%9==0)&(lane<27), w, jnp.zeros_like(w))
            if "cols" in sc: sc["cols"][pl.ds(y*16,16)] = cols
            pieces.append(cols.reshape(256,128))
        r = nn(jnp.concatenate(pieces,axis=0), win[...]) + vec(v_ref,"b_in",C1)
        top[pl.ds(y2*64,64)] = r.reshape(64,16,128)
        rb = r.astype(BF).reshape(4,8,2,16,128)
        for k in range(4):
            p = y2*4+k+1
            tp[p//2, p%2, 0:8, 1] = rb[k,:,0]
            tp[p//2, p%2, 1:9, 0] = rb[k,:,1]
        return 0
    lax.fori_loop(0,4,a1,0)
    taps=[]
    for t in range(9):
        ty,tx=t//3,t%3
        taps.append(tp[ty//2:ty//2+8, ty%2, tx//2:tx//2+8, tx%2].reshape(1024,128))
    low[...] = (nt(jnp.concatenate(taps,axis=1), wt[:,O_DOWN:O_DOWN+1152]) + vec(v_ref,"b_down")).reshape(64,16,256)
    def norm_act(src, g, s, si):
        m, inv = gn_stats(lambda i: src[pl.ds(i*8,8)], 8, 8, 256, 512.0)
        save(si, m, inv)
        def b(y,_):
            z = (src[pl.ds(y*8,8)] - m)*inv*vec(v_ref,g) + vec(v_ref,s)
            ap[y+1,1:9] = (z*sigmoid(z)).astype(BF)
            return 0
        lax.fori_loop(0,8,b,0)
    def conv3(off):
        return nt(jnp.concatenate([ap[t//3:t//3+8, t%3:t%3+8].reshape(1024,256) for t in range(9)],axis=1), wt[:,off:off+2304])
    norm_act(low,"g1","s1",0)
    emb = nt(feat, wt[:,O_TIME:O_TIME+128]) + vec(v_ref,"b_time")
    mid[...] = (conv3(O_R1) + vec(v_ref,"b_res1")).reshape(64,16,256) + emb
    norm_act(mid,"g2","s2",1)
    res[...] = low[...] + (conv3(O_R2) + vec(v_ref,"b_res2")).reshape(64,16,256)
    m, inv = gn_stats(lambda i: res[pl.ds(i*8,8)], 8, 8, 256, 512.0)
    save(2, m, inv)
    nb = ((res[...]-m)*inv*vec(v_ref,"g3") + vec(v_ref,"s3")).astype(BF).reshape(1024,256)
    q = nt(nb, wt[:,O_QKV:O_QKV+256]) + vec(v_ref,"b_query")
    k_ = nt(nb, wt[:,O_QKV+256:O_QKV+512])
    v_ = nt(nb, wt[:,O_QKV+512:O_QKV+768])+vec(v_ref,"b_value")
    for i, z in enumerate((q, k_, v_)):
        z = z.astype(BF).astype(F32)
        qkv[2*i] = z[:,0:128]
        qkv[2*i+1] = z[:,128:256]
    def att(n,_):
        x = [jnp.concatenate([qkv[h,pl.ds(n,64,stride=16),:] for h in (2*k,2*k+1)],axis=1).astype(BF) for k in range(3)]
        s = nt(x[0],x[1])*(C2**-0.5)
        e = jnp.exp(s - jnp.max(s,axis=1,keepdims=True))
        p = e/jnp.sum(e,axis=1,keepdims=True)
        o = nn(p.astype(BF), x[2]).astype(BF).astype(F32)
        ob[0,pl.ds(n,64,stride=16),:] = o[:,0:128]
        ob[1,pl.ds(n,64,stride=16),:] = o[:,128:256]
        return 0
    lax.fori_loop(0,16,att,0,unroll=4)
    obb = jnp.concatenate([ob[0],ob[1]],axis=1).astype(BF)
    if "obb" in sc: sc["obb"][...] = obb
    att_out = res[...].reshape(1024,256) + (nt(obb, wt[:,O_PROJ:O_PROJ+256]) + vec(v_ref,"b_proj"))
    attb = att_out.astype(BF)
    if "attb" in sc: sc["attb"][...] = attb
    for t in range(9):
        yp[t,1:9,1:9] = nt(attb, wup[t]).reshape(8,8,16,128)
    def u(i,_):
        for a in range(2):
            for b in range(2):
                acc=None
                for t in range(9):
                    r,c=t//3-1,t%3-1
                    dr=(a+r)//2; dc=(b+c)//2
                    v=yp[t, i+dr+1, 1+dc:9+dc]
                    acc = v if acc is None else acc+v
                up[i,a,:,b] = acc + vec(v_ref,"b_up",C1) + sc["top6"][i,a,:,b]
        return 0
    lax.fori_loop(0,8,u,0)
    upf = sc["up3"]
    m, inv = gn_stats(lambda i: upf[pl.ds(i*16,16)], 16, 4, 128, 1024.0)
    save(3, m, inv)
    def b4(y,_):
        z = (upf[pl.ds(y*16,16)]-m)*inv*vec(v_ref,"g4",C1)+vec(v_ref,"s4",C1)
        ep[y+1,1:17] = (z*sigmoid(z)).astype(BF)
        return 0
    lax.fori_loop(0,16,b4,0)
    def fin(put):
        def f(y4,_):
            cols=jnp.concatenate([ep[pl.ds(y4*8+t//3,8), t%3:t%3+16].reshape(2048,128) for t in range(9)],axis=1)
            put(y4, (nt(cols, wfin[...])+bfin).reshape(128,16,128))
            return 0
        lax.fori_loop(0,2,f,0)
    return fin

def scratch():
    V=pltpu.VMEM
    return dict(wt=V((256,MID),BF), wup=V((9,128,256),BF), win=V((128,128),BF), wfin=V((128,1152),BF), wfb=V((128,128),BF), sm=V((128,256),F32), xp=V((18,18,16,128),BF), tp=V((9,2,9,2,16,128),BF),
      top=V((256,16,128),F32), low=V((64,16,256),F32), ap=V((10,10,16,256),BF), mid=V((64,16,256),F32), res=V((64,16,256),F32),
      qkv=V((6,1024,128),F32), ob=V((2,1024,128),F32), yp=V((9,10,10,16,128),F32), up=V((8,2,8,2,16,128),F32), ep=V((18,18,16,128),BF))
KEYS=list(scratch().keys())

def zero_borders(sc):
    for k in ("xp","ep","tp","ap","yp"):
        sc[k][...] = jnp.zeros(sc[k].shape, sc[k].dtype)

def views(sc):
    sc=dict(sc)
    sc["top6"]=sc["top"].reshape(8,2,8,2,16,128)
    sc["up3"]=sc["up"].reshape(256,16,128)
    return sc

def teacher_call(D, cnt, x, feat, ce, cl, tc, nc, tg):
    def kern(cnt_ref, x_ref, feat_ref, ce_ref, cl_ref, tc_ref, nc_ref, tg_ref, out_ref, *scr):
        sc = views(dict(zip(KEYS, scr)))
        zero_borders(sc)
        prep(tg_ref, *(sc[k] for k in WKEYS), D)
        out_ref[...] = x_ref[...]
        def step(j, _):
            fin = net(out_ref, feat_ref[j], sc["wt"], sc["wup"], sc["win"], sc["wfin"], sc["sm"], sc)
            ce_, cl_ = ce_ref[j], cl_ref[j]
            def put(y4, e):
                out_ref[pl.ds(y4*128,128)] = ce_*e + cl_*out_ref[pl.ds(y4*128,128)]
            fin(put)
            return 0
        lax.fori_loop(0, cnt_ref[0], step, 0)
        def tgt(i, _):
            out_ref[pl.ds(i*16,16)] = tc_ref[...]*out_ref[pl.ds(i*16,16)] + nc_ref[...]*x_ref[pl.ds(i*16,16)]
            return 0
        lax.fori_loop(0, 16, tgt, 0)
    vm = pl.BlockSpec(memory_space=pltpu.VMEM)
    return pl.pallas_call(kern, out_shape=jax.ShapeDtypeStruct((256,16,128),F32),
        in_specs=[pl.BlockSpec(memory_space=pltpu.SMEM)]+[vm]*7, out_specs=vm, scratch_shapes=list(scratch().values()), name="teacher_steps",
        compiler_params=pltpu.CompilerParams(vmem_limit_bytes=60<<20))(cnt, x, feat, ce, cl, tc, nc, tg)

WKEYS = ["wt","wup","win","wfin","wfb","sm"]
RES = ["wt","wup","wfb","sm","tp","low","mid","res","qkv","up"]
def student_call(D, x, tgt, snr, feat, tg):
    vm=pl.BlockSpec(memory_space=pltpu.VMEM)
    sh=scratch()
    extra=dict(st=pltpu.VMEM((8,16,256),F32),cols=pltpu.VMEM((256,16,128),BF),attb=pltpu.VMEM((1024,256),BF),obb=pltpu.VMEM((1024,256),BF))
    outs={k:sh[k] for k in RES}; outs.update(extra)
    scr={k:v for k,v in sh.items() if k not in outs}
    ok,sk=list(outs),list(scr)
    def kern(x_ref,t_ref,snr_ref,feat_ref,tg_ref,out_ref,sum_ref,*refs):
        sc=views(dict(zip(ok+sk,refs)))
        zero_borders(sc)
        prep(tg_ref,*(sc[k] for k in WKEYS),D)
        fin=net(x_ref,feat_ref[...],sc["wt"],sc["wup"],sc["win"],sc["wfin"],sc["sm"],sc)
        def put(y4,e): out_ref[pl.ds(y4*128,128)]=e
        fin(put)
        def s(i,c):
            t,o=t_ref[pl.ds(i*16,16)],out_ref[pl.ds(i*16,16)]
            d=o-t
            return tuple(a+jnp.sum(b,axis=0) for a,b in zip(c,(t,t*t,o,o*o,d*d)))
        z=jnp.zeros((N,128),F32)
        r=lax.fori_loop(0,16,s,(z,)*5)
        r=r[:4]+(r[4]*snr_ref[...],)
        sum_ref[...]=jnp.concatenate([jnp.sum(a,axis=0,keepdims=True) for a in r]+[jnp.zeros((3,128),F32)],axis=0)
    res=pl.pallas_call(kern,
        out_shape=(jax.ShapeDtypeStruct((256,16,128),F32),jax.ShapeDtypeStruct((8,128),F32))+tuple(jax.ShapeDtypeStruct(outs[k].shape,outs[k].dtype) for k in ok),
        in_specs=[vm]*5,out_specs=(vm,)*(2+len(ok)),scratch_shapes=[scr[k] for k in sk], name="student_forward",
        compiler_params=pltpu.CompilerParams(vmem_limit_bytes=62<<20))(x,tgt,snr,feat,tg)
    return res[0],res[1],dict(zip(ok,res[2:]))

def tn(a, b): return lax.dot_general(a, b, (((0,),(0,)),((),())), preferred_element_type=F32)

def bwd_kernel(x_refs, o_refs, sc):
    X, S = x_refs, sc
    (G,) = o_refs
    sg, sn_total = S["sg"], X["total"]
    v_ref, wt, wup, st = X["v"], X["wt"], X["wup"], X["st"]
    gp18, gcols, big, ep, dp, s_hi, s_lo, gp, ap, da, gres, gqkv, gmx, yd = (S[k] for k in ("gp18","gcols","big","ep","dp","s_hi","s_lo","gp","ap","da","gres","gqkv","gmx","yd"))
    lane = iota((1,1,128),2)
    for k in ("gp18","dp","gp","ap","yd"):
        S[k][...] = jnp.zeros(S[k].shape, S[k].dtype)
    sg[...] = jnp.zeros((128,256),F32)
    def put_block(b, val):
        sg[b//2:b//2+1, 128*(b%2):128*(b%2)+128] = val
    def put_vec(name, val, C=C2):
        at, wide = BLOCK[name]
        for k in range(wide):
            put_block(at+k, val[:, 128*k:128*k+128])
    def rowsum(a): return jnp.sum(a, axis=0, keepdims=True)
    def put_g(val, col, row0=0):
        rows, width = val.shape
        for c in range(width//128):
            for r in range(0, rows, 8):
                G[pl.ds((row0+r)*64+col//128+c, 8, stride=64),:] = val[r:r+8, c*128:c*128+128]
    pixels = 256.0*sn_total
    so = X["stat"][...]
    mt, mo = so[0:1]/pixels, so[2:3]/pixels
    vt_, vo = so[1:2]/pixels-mt*mt, so[3:4]/pixels-mo*mo
    cb = 4.0*(vo-vt_)/pixels
    ca = 2.0*(mo-mt)/pixels-cb*mo
    sn = X["snr"][...]*(2.0/(768.0*sn_total))
    acc=jnp.zeros((N,128),F32)
    def g0(y,acc):
        o=X["out"][pl.ds(y*16,16)]
        go = sn*(o-X["tgt"][pl.ds(y*16,16)]) + ca + cb*o
        gp18[y+1,1:17]=go.astype(BF)
        return acc+jnp.sum(go,axis=0)
    acc=lax.fori_loop(0,16,g0,acc)
    acc=rowsum(acc)
    lane2=iota((1,128),1)
    put_block(84, sum(jnp.where(lane2==c, jnp.sum(jnp.where(lane2==9*c,acc,0.0),axis=1,keepdims=True),0.0) for c in range(3)))
    def g1(y,_):
        for t in range(9):
            w = gp18[y+2-t//3, 2-t%3:18-t%3]
            cols = jnp.where((lane%9==t)&(lane<27), w, cols) if t else jnp.where((lane%9==0)&(lane<27), w, jnp.zeros_like(w))
        gcols[pl.ds(y*16,16)] = cols
        return 0
    lax.fori_loop(0,16,g1,0)
    big[...] = nn(gcols[...].reshape(4096,128), X["wfb"][...]).reshape(256,16,128)
    def gn_bwd(src, dref, si, gname, sname, C, per, rows, k, act_put, dx_put, silu=True):
        m, inv = st[2*si,:,0:C], st[2*si+1,:,0:C]
        g, s = vec(v_ref,gname,C), vec(v_ref,sname,C)
        def p1(y,c):
            A,B=c
            xh=(src[pl.ds(y*k,k)]-m)*inv
            d=dref[pl.ds(y*k,k)]
            z=xh*g+s
            if silu:
                sg=sigmoid(z); act=z*sg
                act_put(y,act.astype(BF))
                d=d*(sg+act*(1.0-sg))
                dref[pl.ds(y*k,k)]=d
            else:
                act_put(y,z.astype(BF))
            return A+jnp.sum(d,axis=0), B+jnp.sum(d*xh,axis=0)
        A,B=lax.fori_loop(0,rows,p1,(jnp.zeros((N,C),F32),jnp.zeros((N,C),F32)))
        put_vec(gname,rowsum(B),C); put_vec(sname,rowsum(A),C)
        cnt=1.0/(per*rows*k)
        ga=group_sum(g*A,per)*cnt; gb=group_sum(g*B,per)*cnt
        def p2(y,acc):
            xh=(src[pl.ds(y*k,k)]-m)*inv
            dx=inv*(g*dref[pl.ds(y*k,k)]-ga-xh*gb)
            return acc+jnp.sum(dx_put(y,dx),axis=0)
        return lambda: lax.fori_loop(0,rows,p2,jnp.zeros((N,C),F32))
    def act4(y,a): ep[pl.ds(y*16,16)]=a
    def dx4(y,dx):
        big[pl.ds(y*16,16)]=dx
        b=dx.astype(BF).reshape(8,2,16,128)
        p=y+1
        dp[p//2,p%2,0:8,1]=b[:,0]
        dp[p//2,p%2,1:9,0]=b[:,1]
        return dx
    fin=gn_bwd(X["up"].reshape(256,16,128),big,3,"g4","s4",128,4,16,16,act4,dx4)
    dwf = tn(gcols[...].reshape(4096,128), ep[...].reshape(4096,128))
    flat = jnp.zeros((9,384),F32)
    for c in range(3):
        p3 = one_hot(iota((128,384),1) == 3*iota((128,384),0) + c)
        piece = dwf[9*c:9*c+9]
        hi = piece.astype(BF); rest = piece-hi.astype(F32)
        mi = rest.astype(BF); lo = (rest-mi.astype(F32)).astype(BF)
        flat += nn(hi,p3)+nn(mi,p3)+nn(lo,p3)
    for t in range(9):
        for h in range(3):
            put_block(27+3*t+h, flat[t:t+1,128*h:128*h+128])
    put_vec("b_up",rowsum(fin()),128)
    PAIR={-1:((1,0),(1,1)),0:((0,1),(1,0)),1:((0,0),(0,1))}
    def su(i,_):
        for r in (-1,0,1):
            (ra,pa),(rb,pb)=PAIR[r]
            V={}
            for cp in range(2):
                V[cp]=dp[i+ra,pa,:,cp].astype(F32)+dp[i+rb,pb,:,cp].astype(F32)
            for c in (-1,0,1):
                (ca_,qa),(cb_,qb)=PAIR[c]
                s=V[qa][ca_:ca_+8]+V[qb][cb_:cb_+8]
                t=(r+1)*3+c+1
                hi=s.astype(BF)
                s_hi[t,pl.ds(i*8,8)]=hi
                s_lo[t,pl.ds(i*8,8)]=(s-hi.astype(F32)).astype(BF)
        return 0
    lax.fori_loop(0,8,su,0)
    cat=lambda ref: jnp.concatenate([ref[t].reshape(1024,128) for t in range(9)],axis=1)
    wu=wup[...].reshape(1152,256)
    gatt=nn(cat(s_hi),wu)+nn(cat(s_lo),wu)
    gres[...]=gatt.reshape(64,16,256)
    put_vec("b_proj",rowsum(gatt))
    gab=gatt.astype(BF)
    attb=X["attb"][...]
    kk, ci = iota((256,256),1), iota((256,256),0)
    peo=one_hot(ci == 2*(kk % 128) + kk // 128)
    aeo=nn(attb,peo).astype(BF)
    for t in range(9):
        r=tn(s_hi[t].reshape(1024,128),aeo)+tn(s_lo[t].reshape(1024,128),aeo)
        put_g(r[:,0:128],O_UP+t*128,0); put_g(r[:,128:256],O_UP+t*128,128)
    obb=X["ob"][...]
    put_g(tn(gab,obb),O_PROJ)
    gm=nn(gab,wt[:,O_PROJ:O_PROJ+256]).astype(BF).astype(F32)
    gmx[0]=gm[:,0:128]; gmx[1]=gm[:,128:256]
    qkv=X["qkv"]
    sc_=C2**-0.5
    def att(n,_):
        q,k,v=[jnp.concatenate([qkv[h,pl.ds(n,64,stride=16),:] for h in (2*j,2*j+1)],axis=1).astype(BF) for j in range(3)]
        gmn=jnp.concatenate([gmx[h,pl.ds(n,64,stride=16),:] for h in (0,1)],axis=1).astype(BF)
        s=nt(q,k)*sc_
        e=jnp.exp(s-jnp.max(s,axis=1,keepdims=True))
        p=e/jnp.sum(e,axis=1,keepdims=True)
        ga=nt(gmn,v)
        gs=(p*(ga-jnp.sum(ga*p,axis=1,keepdims=True))).astype(BF)
        outs=(nn(gs,k)*sc_, tn(gs,q)*sc_, tn(p.astype(BF),gmn))
        for j,o in enumerate(outs):
            o=o.astype(BF).astype(F32)
            gqkv[2*j,pl.ds(n,64,stride=16),:]=o[:,0:128]
            gqkv[2*j+1,pl.ds(n,64,stride=16),:]=o[:,128:256]
        return 0
    lax.fori_loop(0,16,att,0,unroll=4)
    gq=[jnp.concatenate([gqkv[2*j],gqkv[2*j+1]],axis=1) for j in range(3)]
    put_vec("b_query",rowsum(gq[0])); put_vec("b_value",rowsum(gq[2]))
    gqb=[g.astype(BF) for g in gq]
    da[...]=nn(jnp.concatenate(gqb,axis=1),jnp.concatenate([wt[:,O_QKV+256*j:O_QKV+256*j+256] for j in range(3)],axis=0)).reshape(64,16,256)
    nbs=S["nb"]
    def act3(y,a): nbs[pl.ds(y*8,8)]=a
    def dx3(y,dx):
        z=gres[pl.ds(y*8,8)]+dx
        gres[pl.ds(y*8,8)]=z
        gp[y+1,1:9]=z.astype(BF)
        return z
    fin=gn_bwd(X["res"],da,2,"g3","s3",256,8,8,8,act3,dx3,silu=False)
    nb=nbs[...].reshape(1024,256)
    for j in range(3): put_g(tn(gqb[j],nb),O_QKV+256*j)
    put_vec("b_res2",rowsum(fin()))
    def conv_dgrad(off):
        return nn(jnp.concatenate([gp[2-t//3:10-t//3,2-t%3:10-t%3].reshape(1024,256) for t in range(9)],axis=1),
                  jnp.concatenate([wt[:,off+256*t:off+256*t+256] for t in range(9)],axis=0))
    def conv_wgrad(g,off):
        gt=g.T
        for t in range(9):
            put_g(nn(gt,ap[t//3:t//3+8,t%3:t%3+8].reshape(1024,256)),off+256*t)
    def act_(y,a): ap[y+1,1:9]=a
    da[...]=conv_dgrad(O_R2).reshape(64,16,256)
    def dxm(y,dx):
        gp[y+1,1:9]=dx.astype(BF)
        return dx
    fin=gn_bwd(X["mid"],da,1,"g2","s2",256,8,8,8,act_,dxm)
    conv_wgrad(gp[1:9,1:9].reshape(1024,256),O_R2)
    gemb=fin()
    put_vec("b_time",rowsum(gemb)); put_vec("b_res1",rowsum(gemb))
    put_g(tn(gemb.astype(BF),X["feat"][...]),O_TIME)
    da[...]=conv_dgrad(O_R1).reshape(64,16,256)
    def dxl(y,dx):
        z=gres[pl.ds(y*8,8)]+dx
        gp[y+1,1:9]=z.astype(BF)
        return z
    fin=gn_bwd(X["low"],da,0,"g1","s1",256,8,8,8,act_,dxl)
    conv_wgrad(gp[1:9,1:9].reshape(1024,256),O_R1)
    put_vec("b_down",rowsum(fin()))
    glb=gp[1:9,1:9].reshape(1024,256)
    glt=glb.T
    tp=X["tp"]
    for t in range(9):
        ty,tx=t//3,t%3
        yd[t,0:8,0:8]=nn(glb,wt[:,O_DOWN+128*t:O_DOWN+128*t+128]).reshape(8,8,16,128)
        put_g(nn(glt,tp[ty//2:ty//2+8,ty%2,tx//2:tx//2+8,tx%2].reshape(1024,128)),O_DOWN+128*t)
    big6=big.reshape(8,2,8,2,16,128)
    SRC={0:((1,0),),1:((0,1),(2,0))}
    def dt(i,acc):
        for a in range(2):
            for b in range(2):
                z=big6[i,a,:,b]
                for ty,oy in SRC[a]:
                    for tx,ox in SRC[b]:
                        z=z+yd[ty*3+tx,i+oy,ox:ox+8]
                S["dt"].reshape(8,2,8,2,16,128)[i,a,:,b]=z.astype(BF)
                acc=acc+jnp.sum(z,axis=0)
        return acc
    put_vec("b_in",rowsum(lax.fori_loop(0,8,dt,jnp.zeros((N,128),F32))),128)
    dwi=tn(X["cols"][...].reshape(4096,128),S["dt"][...].reshape(4096,128))
    for k in range(27):
        put_block(k, dwi[9*(k%3)+k//3:9*(k%3)+k//3+1])
    put_g(sg[...].T, MID)

def bwd_scratch():
    V=pltpu.VMEM
    return dict(gp18=V((18,18,16,128),BF),gcols=V((256,16,128),BF),big=V((256,16,128),F32),ep=V((256,16,128),BF),dp=V((9,2,9,2,16,128),BF),
      s_hi=V((9,64,16,128),BF),s_lo=V((9,64,16,128),BF),gp=V((10,10,16,256),BF),ap=V((10,10,16,256),BF),da=V((64,16,256),F32),gres=V((64,16,256),F32),
      gqkv=V((6,1024,128),F32),gmx=V((2,1024,128),F32),yd=V((9,9,9,16,128),F32),nb=V((64,16,256),BF),dt=V((256,16,128),BF),sg=V((128,256),F32))
BIN=["out","tgt","snr","stat","cols","tp","low","mid","res","qkv","obb","attb","up","st","feat","wt","wup","wfb","sm"]
def bwd_call(ins, total):
    vm=pl.BlockSpec(memory_space=pltpu.VMEM)
    sc=bwd_scratch(); keys=list(sc)
    def k(*refs):
        a=dict(zip(BIN,refs[:len(BIN)])); a["v"]=a["sm"]; a["ob"]=a["obb"]; a["total"]=float(total)
        bwd_kernel(a,refs[len(BIN):len(BIN)+1],dict(zip(keys,refs[len(BIN)+1:])))
    return pl.pallas_call(k,out_shape=jax.ShapeDtypeStruct((256*64,128),F32),
        in_specs=[vm]*len(BIN),out_specs=vm,scratch_shapes=list(sc.values()), name="student_backward",
        compiler_params=pltpu.CompilerParams(vmem_limit_bytes=62<<20))(*[ins[k] for k in BIN])


def segments():
    matrices = [("w_in", 27, C1), ("w_down", 9 * C1, C2), ("w_res1", 9 * C2, C2), ("w_res2", 9 * C2, C2), ("w_time", C1, C2),
                ("w_qkv", C2, 3 * C2), ("w_proj", C2, C2), ("w_up", 9 * C2, C1), ("w_final", 9 * C1, 3)]
    vectors = [("g1", C2), ("s1", C2), ("g2", C2), ("s2", C2), ("g3", C2), ("s3", C2), ("g4", C1), ("s4", C1), ("b_in", C1),
               ("b_down", C2), ("b_res1", C2), ("b_res2", C2), ("b_time", C2), ("b_query", C2), ("b_value", C2), ("b_proj", C2),
               ("b_up", C1), ("b_final", 3)]
    listing, cursor = [], 0
    for name, height, breadth in matrices:
        listing.append((name, cursor, (height, breadth), "matrix"))
        cursor += height * breadth
    for name, length in vectors:
        listing.append((name, cursor, (length,), "gain" if name[0] != "b" else "bias"))
        cursor += length
    return listing

def rates(position):
    learn = jnp.zeros(position.shape, F32)
    decay = jnp.zeros(position.shape, F32)
    for name, offset, shape, kind in segments():
        inside = (position >= offset) & (position < offset + math.prod(shape))
        if kind == "matrix":
            spread = shape[0] ** (-0.5) * ((SIDE * SIDE / 4.0) ** 0.5 if name == "w_proj" else 1.0)
            learn = jnp.where(inside, 0.5 * spread, learn)
            decay = jnp.where(inside, 0.01, decay)
        elif kind == "gain":
            learn = jnp.where(inside, 0.2, learn)
        else:
            learn = jnp.where(inside, 0.05, learn)
    return learn, decay

def angle_of(step):
    return 0.1 + 1.35 * step.astype(F32) / TGRID

def time_features(step):
    half = C1 // 2
    freqs = jnp.exp(-math.log(1000.0) * jnp.arange(half).astype(F32) / half)
    phases = step.astype(F32)[..., None] * freqs
    return jnp.concatenate([jnp.sin(phases), jnp.cos(phases)], axis=-1)

def to_columns(shard, start, D):
    R, L = 256 // D, shard.shape[0]
    body = R * MID
    if HEAD % D == 0:
        parts = [shard[start:start+body], shard[:start], shard[start+body:]]
    else:
        at = jnp.arange(L - body)
        parts = [lax.dynamic_slice(shard, (start,), (body,)), jnp.where(at < start, shard[:L-body], shard[body:])]
    cols = jnp.concatenate(parts).reshape(-1, R).T
    return jnp.pad(cols, ((0,0),(0,MID+128-cols.shape[1])))

def from_columns(cols, start, D, L):
    R = 256 // D
    body = R * MID
    q = cols[:, O_QKV:O_QKV+768].reshape(R,3,256).transpose(0,2,1).reshape(R,768)
    cols = jnp.concatenate([cols[:, :O_QKV], q, cols[:, O_PROJ:L//R]], axis=1)
    flat = cols.T.reshape(-1)
    if HEAD % D == 0:
        return jnp.concatenate([flat[body:body+start], flat[:body], flat[body+start:]])
    rest = flat[body:]
    at = jnp.arange(L)
    mid = lax.dynamic_update_slice(jnp.zeros((L,), F32), flat[:body], (start,))
    low = jnp.pad(rest, (0, body)); high = jnp.pad(rest, (body, 0))
    return jnp.where(at < start, low, jnp.where(at < start + body, mid, high))

def lanes(images):
    v = jnp.repeat(images.transpose(1,2,0,3).reshape(256,N,3), 9, axis=2)
    return jnp.pad(v, ((0,0),(0,0),(0,101)))

def local(images, noise, timestep, stride, bucket, steps_table, master, first_moment, second_moment, teacher, step_count):
    axes = ("dp", "mp")
    D = lax.axis_size("dp") * lax.axis_size("mp")
    me = lax.axis_index(axes)
    R, L = 256 // D, master.shape[0]
    start = HEAD // D if HEAD % D == 0 else (HEAD - me + D - 1) // D
    teacher_all = lax.all_gather(to_columns(teacher, start, D), axes, axis=0, tiled=True)
    student_all = lax.all_gather(to_columns(master.astype(BF), start, D), axes, axis=0, tiled=True)
    wide = lambda v: jnp.broadcast_to(v[..., None], v.shape + (128,))
    angle = angle_of(timestep)
    noisy = lanes(jnp.cos(angle)[:,None,None,None] * images + jnp.sin(angle)[:,None,None,None] * noise)
    picked = jnp.sum(jnp.where(jnp.arange(steps_table.shape[0]) == bucket[0], steps_table, 0))
    turn = jnp.arange(KMAX)[:, None]
    current = timestep[None] - turn * stride[None]
    later = current - stride[None]
    keep = jnp.sin(angle_of(later)) / jnp.sin(angle_of(current))
    take = jnp.cos(angle_of(later)) - keep * jnp.cos(angle_of(current))
    features = jax.nn.silu(time_features(current)).astype(BF)
    final_t = timestep - picked * stride
    below = jnp.sin(angle - angle_of(final_t))
    target = teacher_call(D, picked.reshape(1), noisy, features, wide(take), wide(keep), wide(jnp.sin(angle)/below),
                          wide(-jnp.sin(angle_of(final_t))/below), teacher_all)
    snr = wide(jnp.maximum(jnp.square(jnp.cos(angle)/jnp.sin(angle)), 1.0))
    out, sums, kept = student_call(D, noisy, target, snr, features[0], student_all)
    sums = lax.psum(sums, axes)
    total = images.shape[0] * D
    pick = sums[:5, 0:27:9]
    mean_t, mean_o = pick[0]/(256*total), pick[2]/(256*total)
    var_t, var_o = pick[1]/(256*total) - jnp.square(mean_t), pick[3]/(256*total) - jnp.square(mean_o)
    loss = jnp.sum(pick[4])/(768*total) + jnp.sum(jnp.square(mean_o-mean_t) + jnp.square(var_o-var_t))
    grads = bwd_call(dict(kept, out=out, tgt=target, snr=snr, stat=sums, feat=features[0]), total)
    order = grads.reshape(R, D, MID+128)
    if HEAD % D:
        order = jnp.concatenate([jnp.roll(order[:, :, :MID], HEAD % D, axis=1), order[:, :, MID:]], axis=2)
    part = lax.psum_scatter(order, axes, scatter_dimension=1, tiled=True).reshape(R, MID+128)
    grad = from_columns(part, start, D, L)
    learn, decay = rates(jnp.arange(L, dtype=jnp.int32) * D + me)
    steps_done = step_count[0].astype(F32)
    new_first = 0.5 * first_moment + 0.5 * grad
    new_second = 0.5 * second_moment + 0.5 * jnp.square(grad)
    fix_rate = 1.0 - jnp.power(0.5, steps_done)
    new_master = master - learn * (new_first / fix_rate / (jnp.sqrt(new_second / fix_rate) + 1e-08) + decay * master)
    return loss, new_master, new_first, new_second

def solution(mesh):
    s = P(("dp", "mp"))
    i = P(("dp", "mp"), None, None, None)
    return jax.shard_map(local, mesh=mesh, in_specs=(i, i, s, s, s, P(), s, s, s, s, P()), out_specs=(P(), s, s, s), check_vma=False)
```

```python
import math
import jax
import jax.numpy as jnp
from jax import lax
from jax.experimental import pallas as pl
from jax.experimental.pallas import tpu as pltpu
from jax.sharding import PartitionSpec as P

C1, C2, N = 128, 256, 16
SIDE, TGRID, KMAX = 16, 64, 4
F32, BF = jnp.float32, jnp.bfloat16
O_DOWN, O_R1, O_R2, O_TIME, O_QKV, O_PROJ, O_UP, MID = 0, 1152, 3456, 5760, 5888, 6656, 6912, 8064
HEAD = 3456
BLOCK = {}
_at = 54
for _name, _wide in (("g1",2),("s1",2),("g2",2),("s2",2),("g3",2),("s3",2),("g4",1),("s4",1),("b_in",1),("b_down",2),("b_res1",2),
                     ("b_res2",2),("b_time",2),("b_query",2),("b_value",2),("b_proj",2),("b_up",1),("b_final",1)):
    BLOCK[_name] = (_at, _wide)
    _at += _wide

def iota(shape, d): return lax.broadcasted_iota(jnp.int32, shape, d)

def nt(a, b): return lax.dot_general(a, b, (((1,),(1,)),((),())), preferred_element_type=F32)
def nn(a, b): return lax.dot_general(a, b, (((1,),(0,)),((),())), preferred_element_type=F32)

def one_hot(cond): return jnp.where(cond, 1.0, 0.0).astype(BF)

def split3(v):
    hi = v.astype(BF); r = v - hi.astype(F32)
    mid = r.astype(BF); lo = (r - mid.astype(F32)).astype(BF)
    return jnp.concatenate([hi, mid, lo], axis=0)

def group_sum(v, per):
    C = v.shape[1]
    G = one_hot(iota((C,C),0)//per == iota((C,C),1)//per)
    r = nn(split3(v), G)
    return r[0:N] + r[N:2*N] + r[2*N:3*N]

def prep(tg_ref, wt_ref, wup_ref, win_ref, wfin_ref, wfb_ref, sm_ref, D):
    R = 256 // D
    row, o = iota((256,256),1), iota((256,256),0)
    dev, m = row // R, row % R
    perm = one_hot(o == (dev + ((-HEAD) % D)) % D + D * m)
    CH = 1152
    for c in range(7):
        wt_ref[:, c*CH:(c+1)*CH] = nn(perm, tg_ref[:, c*CH:(c+1)*CH]).astype(BF)
    kk, ci = iota((256,256),0), iota((256,256),1)
    peo = one_hot(ci == 2*(kk % 128) + kk // 128)
    for t in range(9):
        cs = O_UP + t*128
        both = jnp.concatenate([wt_ref[0:128, cs:cs+128], wt_ref[128:256, cs:cs+128]], axis=1)
        wup_ref[t] = nn(both, peo).astype(BF)
    kq, lq = iota((768,768),0), iota((768,768),1)
    pq = one_hot(kq == 3*(lq % 256) + lq // 256)
    wt_ref[:, O_QKV:O_QKV+768] = nn(wt_ref[:, O_QKV:O_QKV+768], pq).astype(BF)
    perm0 = one_hot(o == dev + D * m)
    sm_ref[...] = nn(perm0, tg_ref[:, MID:MID+128]).T
    halves = jnp.concatenate([sm_ref[0:32, 0:128], sm_ref[0:32, 128:256]], axis=0).astype(BF)
    l, r = iota((128,64),0), iota((128,64),1)
    k = 3*(l % 9) + l // 9
    win_ref[...] = nn(one_hot((l < 27) & (r == 32*(k % 2) + k // 2)), halves).astype(BF)
    t16, r16 = iota((16,64),0), iota((16,64),1)
    pieces = []
    for h in range(3):
        blk = 27 + 3*t16 + h
        pieces.append(nn(one_hot((t16 < 9) & (r16 == 32*(blk % 2) + blk // 2)), halves))
    flat = jnp.concatenate(pieces, axis=1).astype(BF)
    acc = jnp.zeros((128,128), F32)
    for c in range(3):
        wc = nn(flat, one_hot(iota((384,128),0) == 3*iota((384,128),1) + c)).astype(BF)
        acc += nn(one_hot((iota((128,16),1) < 9) & (iota((128,16),0) == 9*c + iota((128,16),1))), wc)
    wfb = acc.astype(BF)
    wfb_ref[...] = wfb
    a, z = iota((128,128),0), iota((128,128),1)
    for t in range(9):
        wfin_ref[:, 128*t:128*t+128] = nn(one_hot((a < 27) & (z == 9*(a // 9) + t)), wfb).astype(BF)

def final_bias(sm_ref):
    b = sm_ref[42:43, 0:128].astype(BF)
    return nn(b, one_hot((iota((128,128),1) < 27) & (iota((128,128),0) == iota((128,128),1) // 9)))

def gn_stats(load, rows, per, C, count):
    def s1(i, acc): return acc + jnp.sum(load(i), axis=0)
    m = group_sum(lax.fori_loop(0, rows, s1, jnp.zeros((N,C),F32)), per) * (1.0/count)
    def s2(i, acc): return acc + jnp.sum(jnp.square(load(i) - m), axis=0)
    v = group_sum(lax.fori_loop(0, rows, s2, jnp.zeros((N,C),F32)), per) * (1.0/count)
    return m, lax.rsqrt(v + 1e-5)

def sigmoid(x): return 1.0 / (1.0 + jnp.exp(-x))

def vec(v_ref, name, C=C2):
    at, wide = BLOCK[name]
    return jnp.concatenate([v_ref[b//2:b//2+1, 128*(b%2):128*(b%2)+128] for b in range(at, at+wide)], axis=1)

def net(x_ref, feat, wt, wup, win, wfin, v_ref, sc):
    xp, tp, top, low, ap, mid, res, qkv, ob, yp, up, ep = (sc[k] for k in ("xp","tp","top","low","ap","mid","res","qkv","ob","yp","up","ep"))
    lane = iota((1,1,128),2)
    def save(si, m, inv):
        if "st" in sc:
            C = m.shape[1]
            sc["st"][2*si,:,0:C] = m
            sc["st"][2*si+1,:,0:C] = inv
    bfin = final_bias(v_ref)
    def a0(y, _):
        xp[y+1, 1:17] = x_ref[pl.ds(y*16,16)].astype(BF)
        return 0
    lax.fori_loop(0,16,a0,0)
    def a1(y2, _):
        pieces=[]
        for k in range(4):
            y = y2*4+k
            cols = jnp.zeros((16,16,128),BF)
            for t in range(9):
                w = xp[y+t//3, t%3:t%3+16]
                cols = jnp.where((lane%9==t)&(lane<27), w, cols) if t else jnp.where((lane%9==0)&(lane<27), w, jnp.zeros_like(w))
            if "cols" in sc: sc["cols"][pl.ds(y*16,16)] = cols
            pieces.append(cols.reshape(256,128))
        r = nn(jnp.concatenate(pieces,axis=0), win[...]) + vec(v_ref,"b_in",C1)
        top[pl.ds(y2*64,64)] = r.reshape(64,16,128)
        rb = r.astype(BF).reshape(4,8,2,16,128)
        for k in range(4):
            p = y2*4+k+1
            tp[p//2, p%2, 0:8, 1] = rb[k,:,0]
            tp[p//2, p%2, 1:9, 0] = rb[k,:,1]
        return 0
    lax.fori_loop(0,4,a1,0)
    taps=[]
    for t in range(9):
        ty,tx=t//3,t%3
        taps.append(tp[ty//2:ty//2+8, ty%2, tx//2:tx//2+8, tx%2].reshape(1024,128))
    low[...] = (nt(jnp.concatenate(taps,axis=1), wt[:,O_DOWN:O_DOWN+1152]) + vec(v_ref,"b_down")).reshape(64,16,256)
    def norm_act(src, g, s, si):
        m, inv = gn_stats(lambda i: src[pl.ds(i*8,8)], 8, 8, 256, 512.0)
        save(si, m, inv)
        def b(y,_):
            z = (src[pl.ds(y*8,8)] - m)*inv*vec(v_ref,g) + vec(v_ref,s)
            ap[y+1,1:9] = (z*sigmoid(z)).astype(BF)
            return 0
        lax.fori_loop(0,8,b,0)
    def conv3(off):
        return nt(jnp.concatenate([ap[t//3:t//3+8, t%3:t%3+8].reshape(1024,256) for t in range(9)],axis=1), wt[:,off:off+2304])
    norm_act(low,"g1","s1",0)
    emb = nt(feat, wt[:,O_TIME:O_TIME+128]) + vec(v_ref,"b_time")
    mid[...] = (conv3(O_R1) + vec(v_ref,"b_res1")).reshape(64,16,256) + emb
    norm_act(mid,"g2","s2",1)
    res[...] = low[...] + (conv3(O_R2) + vec(v_ref,"b_res2")).reshape(64,16,256)
    m, inv = gn_stats(lambda i: res[pl.ds(i*8,8)], 8, 8, 256, 512.0)
    save(2, m, inv)
    nb = ((res[...]-m)*inv*vec(v_ref,"g3") + vec(v_ref,"s3")).astype(BF).reshape(1024,256)
    q = nt(nb, wt[:,O_QKV:O_QKV+256]) + vec(v_ref,"b_query")
    k_ = nt(nb, wt[:,O_QKV+256:O_QKV+512])
    v_ = nt(nb, wt[:,O_QKV+512:O_QKV+768])+vec(v_ref,"b_value")
    for i, z in enumerate((q, k_, v_)):
        z = z.astype(BF).astype(F32)
        qkv[2*i] = z[:,0:128]
        qkv[2*i+1] = z[:,128:256]
    def att(n,_):
        x = [jnp.concatenate([qkv[h,pl.ds(n,64,stride=16),:] for h in (2*k,2*k+1)],axis=1).astype(BF) for k in range(3)]
        s = nt(x[0],x[1])*(C2**-0.5)
        e = jnp.exp(s - jnp.max(s,axis=1,keepdims=True))
        p = e/jnp.sum(e,axis=1,keepdims=True)
        o = nn(p.astype(BF), x[2]).astype(BF).astype(F32)
        ob[0,pl.ds(n,64,stride=16),:] = o[:,0:128]
        ob[1,pl.ds(n,64,stride=16),:] = o[:,128:256]
        return 0
    lax.fori_loop(0,16,att,0,unroll=4)
    obb = jnp.concatenate([ob[0],ob[1]],axis=1).astype(BF)
    if "obb" in sc: sc["obb"][...] = obb
    att_out = res[...].reshape(1024,256) + (nt(obb, wt[:,O_PROJ:O_PROJ+256]) + vec(v_ref,"b_proj"))
    attb = att_out.astype(BF)
    if "attb" in sc: sc["attb"][...] = attb
    for t in range(9):
        yp[t,1:9,1:9] = nt(attb, wup[t]).reshape(8,8,16,128)
    def u(i,_):
        for a in range(2):
            for b in range(2):
                acc=None
                for t in range(9):
                    r,c=t//3-1,t%3-1
                    dr=(a+r)//2; dc=(b+c)//2
                    v=yp[t, i+dr+1, 1+dc:9+dc]
                    acc = v if acc is None else acc+v
                up[i,a,:,b] = acc + vec(v_ref,"b_up",C1) + sc["top6"][i,a,:,b]
        return 0
    lax.fori_loop(0,8,u,0)
    upf = sc["up3"]
    m, inv = gn_stats(lambda i: upf[pl.ds(i*16,16)], 16, 4, 128, 1024.0)
    save(3, m, inv)
    def b4(y,_):
        z = (upf[pl.ds(y*16,16)]-m)*inv*vec(v_ref,"g4",C1)+vec(v_ref,"s4",C1)
        ep[y+1,1:17] = (z*sigmoid(z)).astype(BF)
        return 0
    lax.fori_loop(0,16,b4,0)
    def fin(put):
        def f(y4,_):
            cols=jnp.concatenate([ep[pl.ds(y4*8+t//3,8), t%3:t%3+16].reshape(2048,128) for t in range(9)],axis=1)
            put(y4, (nt(cols, wfin[...])+bfin).reshape(128,16,128))
            return 0
        lax.fori_loop(0,2,f,0)
    return fin

def scratch():
    V=pltpu.VMEM
    return dict(wt=V((256,MID),BF), wup=V((9,128,256),BF), win=V((128,128),BF), wfin=V((128,1152),BF), wfb=V((128,128),BF), sm=V((128,256),F32), xp=V((18,18,16,128),BF), tp=V((9,2,9,2,16,128),BF),
      top=V((256,16,128),F32), low=V((64,16,256),F32), ap=V((10,10,16,256),BF), mid=V((64,16,256),F32), res=V((64,16,256),F32),
      qkv=V((6,1024,128),F32), ob=V((2,1024,128),F32), yp=V((9,10,10,16,128),F32), up=V((8,2,8,2,16,128),F32), ep=V((18,18,16,128),BF))
KEYS=list(scratch().keys())

def zero_borders(sc):
    for k in ("xp","ep","tp","ap","yp"):
        sc[k][...] = jnp.zeros(sc[k].shape, sc[k].dtype)

def views(sc):
    sc=dict(sc)
    sc["top6"]=sc["top"].reshape(8,2,8,2,16,128)
    sc["up3"]=sc["up"].reshape(256,16,128)
    return sc

def teacher_call(D, cnt, x, feat, ce, cl, tc, nc, tg):
    def kern(cnt_ref, x_ref, feat_ref, ce_ref, cl_ref, tc_ref, nc_ref, tg_ref, out_ref, *scr):
        sc = views(dict(zip(KEYS, scr)))
        zero_borders(sc)
        prep(tg_ref, *(sc[k] for k in WKEYS), D)
        out_ref[...] = x_ref[...]
        def step(j, _):
            fin = net(out_ref, feat_ref[j], sc["wt"], sc["wup"], sc["win"], sc["wfin"], sc["sm"], sc)
            ce_, cl_ = ce_ref[j], cl_ref[j]
            def put(y4, e):
                out_ref[pl.ds(y4*128,128)] = ce_*e + cl_*out_ref[pl.ds(y4*128,128)]
            fin(put)
            return 0
        lax.fori_loop(0, cnt_ref[0], step, 0)
        def tgt(i, _):
            out_ref[pl.ds(i*16,16)] = tc_ref[...]*out_ref[pl.ds(i*16,16)] + nc_ref[...]*x_ref[pl.ds(i*16,16)]
            return 0
        lax.fori_loop(0, 16, tgt, 0)
    vm = pl.BlockSpec(memory_space=pltpu.VMEM)
    return pl.pallas_call(kern, out_shape=jax.ShapeDtypeStruct((256,16,128),F32),
        in_specs=[pl.BlockSpec(memory_space=pltpu.SMEM)]+[vm]*7, out_specs=vm, scratch_shapes=list(scratch().values()), name="teacher_steps",
        compiler_params=pltpu.CompilerParams(vmem_limit_bytes=60<<20))(cnt, x, feat, ce, cl, tc, nc, tg)

WKEYS = ["wt","wup","win","wfin","wfb","sm"]
RES = ["wt","wup","wfb","sm","tp","low","mid","res","qkv","up"]
def student_call(D, x, tgt, snr, feat, tg):
    vm=pl.BlockSpec(memory_space=pltpu.VMEM)
    sh=scratch()
    extra=dict(st=pltpu.VMEM((8,16,256),F32),cols=pltpu.VMEM((256,16,128),BF),attb=pltpu.VMEM((1024,256),BF),obb=pltpu.VMEM((1024,256),BF))
    outs={k:sh[k] for k in RES}; outs.update(extra)
    scr={k:v for k,v in sh.items() if k not in outs}
    ok,sk=list(outs),list(scr)
    def kern(x_ref,t_ref,snr_ref,feat_ref,tg_ref,out_ref,sum_ref,*refs):
        sc=views(dict(zip(ok+sk,refs)))
        zero_borders(sc)
        prep(tg_ref,*(sc[k] for k in WKEYS),D)
        fin=net(x_ref,feat_ref[...],sc["wt"],sc["wup"],sc["win"],sc["wfin"],sc["sm"],sc)
        def put(y4,e): out_ref[pl.ds(y4*128,128)]=e
        fin(put)
        def s(i,c):
            t,o=t_ref[pl.ds(i*16,16)],out_ref[pl.ds(i*16,16)]
            d=o-t
            return tuple(a+jnp.sum(b,axis=0) for a,b in zip(c,(t,t*t,o,o*o,d*d)))
        z=jnp.zeros((N,128),F32)
        r=lax.fori_loop(0,16,s,(z,)*5)
        r=r[:4]+(r[4]*snr_ref[...],)
        sum_ref[...]=jnp.concatenate([jnp.sum(a,axis=0,keepdims=True) for a in r]+[jnp.zeros((3,128),F32)],axis=0)
    res=pl.pallas_call(kern,
        out_shape=(jax.ShapeDtypeStruct((256,16,128),F32),jax.ShapeDtypeStruct((8,128),F32))+tuple(jax.ShapeDtypeStruct(outs[k].shape,outs[k].dtype) for k in ok),
        in_specs=[vm]*5,out_specs=(vm,)*(2+len(ok)),scratch_shapes=[scr[k] for k in sk], name="student_forward",
        compiler_params=pltpu.CompilerParams(vmem_limit_bytes=62<<20))(x,tgt,snr,feat,tg)
    return res[0],res[1],dict(zip(ok,res[2:]))

def tn(a, b): return lax.dot_general(a, b, (((0,),(0,)),((),())), preferred_element_type=F32)

def bwd_kernel(x_refs, o_refs, sc):
    X, S = x_refs, sc
    (G,) = o_refs
    sg, sn_total = S["sg"], X["total"]
    v_ref, wt, wup, st = X["v"], X["wt"], X["wup"], X["st"]
    gp18, gcols, big, ep, dp, s_hi, s_lo, gp, ap, da, gres, gqkv, gmx, yd = (S[k] for k in ("gp18","gcols","big","ep","dp","s_hi","s_lo","gp","ap","da","gres","gqkv","gmx","yd"))
    lane = iota((1,1,128),2)
    for k in ("gp18","dp","gp","ap","yd"):
        S[k][...] = jnp.zeros(S[k].shape, S[k].dtype)
    sg[...] = jnp.zeros((128,256),F32)
    def put_block(b, val):
        sg[b//2:b//2+1, 128*(b%2):128*(b%2)+128] = val
    def put_vec(name, val, C=C2):
        at, wide = BLOCK[name]
        for k in range(wide):
            put_block(at+k, val[:, 128*k:128*k+128])
    def rowsum(a): return jnp.sum(a, axis=0, keepdims=True)
    def put_g(val, col, row0=0):
        rows, width = val.shape
        for c in range(width//128):
            for r in range(0, rows, 8):
                G[pl.ds((row0+r)*64+col//128+c, 8, stride=64),:] = val[r:r+8, c*128:c*128+128]
    pixels = 256.0*sn_total
    so = X["stat"][...]
    mt, mo = so[0:1]/pixels, so[2:3]/pixels
    vt_, vo = so[1:2]/pixels-mt*mt, so[3:4]/pixels-mo*mo
    cb = 4.0*(vo-vt_)/pixels
    ca = 2.0*(mo-mt)/pixels-cb*mo
    sn = X["snr"][...]*(2.0/(768.0*sn_total))
    acc=jnp.zeros((N,128),F32)
    def g0(y,acc):
        o=X["out"][pl.ds(y*16,16)]
        go = sn*(o-X["tgt"][pl.ds(y*16,16)]) + ca + cb*o
        gp18[y+1,1:17]=go.astype(BF)
        return acc+jnp.sum(go,axis=0)
    acc=lax.fori_loop(0,16,g0,acc)
    acc=rowsum(acc)
    lane2=iota((1,128),1)
    put_block(84, sum(jnp.where(lane2==c, jnp.sum(jnp.where(lane2==9*c,acc,0.0),axis=1,keepdims=True),0.0) for c in range(3)))
    def g1(y,_):
        for t in range(9):
            w = gp18[y+2-t//3, 2-t%3:18-t%3]
            cols = jnp.where((lane%9==t)&(lane<27), w, cols) if t else jnp.where((lane%9==0)&(lane<27), w, jnp.zeros_like(w))
        gcols[pl.ds(y*16,16)] = cols
        return 0
    lax.fori_loop(0,16,g1,0)
    big[...] = nn(gcols[...].reshape(4096,128), X["wfb"][...]).reshape(256,16,128)
    def gn_bwd(src, dref, si, gname, sname, C, per, rows, k, act_put, dx_put, silu=True):
        m, inv = st[2*si,:,0:C], st[2*si+1,:,0:C]
        g, s = vec(v_ref,gname,C), vec(v_ref,sname,C)
        def p1(y,c):
            A,B=c
            xh=(src[pl.ds(y*k,k)]-m)*inv
            d=dref[pl.ds(y*k,k)]
            z=xh*g+s
            if silu:
                sg=sigmoid(z); act=z*sg
                act_put(y,act.astype(BF))
                d=d*(sg+act*(1.0-sg))
                dref[pl.ds(y*k,k)]=d
            else:
                act_put(y,z.astype(BF))
            return A+jnp.sum(d,axis=0), B+jnp.sum(d*xh,axis=0)
        A,B=lax.fori_loop(0,rows,p1,(jnp.zeros((N,C),F32),jnp.zeros((N,C),F32)))
        put_vec(gname,rowsum(B),C); put_vec(sname,rowsum(A),C)
        cnt=1.0/(per*rows*k)
        ga=group_sum(g*A,per)*cnt; gb=group_sum(g*B,per)*cnt
        def p2(y,acc):
            xh=(src[pl.ds(y*k,k)]-m)*inv
            dx=inv*(g*dref[pl.ds(y*k,k)]-ga-xh*gb)
            return acc+jnp.sum(dx_put(y,dx),axis=0)
        return lambda: lax.fori_loop(0,rows,p2,jnp.zeros((N,C),F32))
    def act4(y,a): ep[pl.ds(y*16,16)]=a
    def dx4(y,dx):
        big[pl.ds(y*16,16)]=dx
        b=dx.astype(BF).reshape(8,2,16,128)
        p=y+1
        dp[p//2,p%2,0:8,1]=b[:,0]
        dp[p//2,p%2,1:9,0]=b[:,1]
        return dx
    fin=gn_bwd(X["up"].reshape(256,16,128),big,3,"g4","s4",128,4,16,16,act4,dx4)
    dwf = tn(gcols[...].reshape(4096,128), ep[...].reshape(4096,128))
    flat = jnp.zeros((9,384),F32)
    for c in range(3):
        p3 = one_hot(iota((128,384),1) == 3*iota((128,384),0) + c)
        piece = dwf[9*c:9*c+9]
        hi = piece.astype(BF); rest = piece-hi.astype(F32)
        mi = rest.astype(BF); lo = (rest-mi.astype(F32)).astype(BF)
        flat += nn(hi,p3)+nn(mi,p3)+nn(lo,p3)
    for t in range(9):
        for h in range(3):
            put_block(27+3*t+h, flat[t:t+1,128*h:128*h+128])
    put_vec("b_up",rowsum(fin()),128)
    PAIR={-1:((1,0),(1,1)),0:((0,1),(1,0)),1:((0,0),(0,1))}
    def su(i,_):
        for r in (-1,0,1):
            (ra,pa),(rb,pb)=PAIR[r]
            V={}
            for cp in range(2):
                V[cp]=dp[i+ra,pa,:,cp].astype(F32)+dp[i+rb,pb,:,cp].astype(F32)
            for c in (-1,0,1):
                (ca_,qa),(cb_,qb)=PAIR[c]
                s=V[qa][ca_:ca_+8]+V[qb][cb_:cb_+8]
                t=(r+1)*3+c+1
                hi=s.astype(BF)
                s_hi[t,pl.ds(i*8,8)]=hi
                s_lo[t,pl.ds(i*8,8)]=(s-hi.astype(F32)).astype(BF)
        return 0
    lax.fori_loop(0,8,su,0)
    cat=lambda ref: jnp.concatenate([ref[t].reshape(1024,128) for t in range(9)],axis=1)
    wu=wup[...].reshape(1152,256)
    gatt=nn(cat(s_hi),wu)+nn(cat(s_lo),wu)
    gres[...]=gatt.reshape(64,16,256)
    put_vec("b_proj",rowsum(gatt))
    gab=gatt.astype(BF)
    attb=X["attb"][...]
    kk, ci = iota((256,256),1), iota((256,256),0)
    peo=one_hot(ci == 2*(kk % 128) + kk // 128)
    aeo=nn(attb,peo).astype(BF)
    for t in range(9):
        r=tn(s_hi[t].reshape(1024,128),aeo)+tn(s_lo[t].reshape(1024,128),aeo)
        put_g(r[:,0:128],O_UP+t*128,0); put_g(r[:,128:256],O_UP+t*128,128)
    obb=X["ob"][...]
    put_g(tn(gab,obb),O_PROJ)
    gm=nn(gab,wt[:,O_PROJ:O_PROJ+256]).astype(BF).astype(F32)
    gmx[0]=gm[:,0:128]; gmx[1]=gm[:,128:256]
    qkv=X["qkv"]
    sc_=C2**-0.5
    def att(n,_):
        q,k,v=[jnp.concatenate([qkv[h,pl.ds(n,64,stride=16),:] for h in (2*j,2*j+1)],axis=1).astype(BF) for j in range(3)]
        gmn=jnp.concatenate([gmx[h,pl.ds(n,64,stride=16),:] for h in (0,1)],axis=1).astype(BF)
        s=nt(q,k)*sc_
        e=jnp.exp(s-jnp.max(s,axis=1,keepdims=True))
        p=e/jnp.sum(e,axis=1,keepdims=True)
        ga=nt(gmn,v)
        gs=(p*(ga-jnp.sum(ga*p,axis=1,keepdims=True))).astype(BF)
        outs=(nn(gs,k)*sc_, tn(gs,q)*sc_, tn(p.astype(BF),gmn))
        for j,o in enumerate(outs):
            o=o.astype(BF).astype(F32)
            gqkv[2*j,pl.ds(n,64,stride=16),:]=o[:,0:128]
            gqkv[2*j+1,pl.ds(n,64,stride=16),:]=o[:,128:256]
        return 0
    lax.fori_loop(0,16,att,0,unroll=4)
    gq=[jnp.concatenate([gqkv[2*j],gqkv[2*j+1]],axis=1) for j in range(3)]
    put_vec("b_query",rowsum(gq[0])); put_vec("b_value",rowsum(gq[2]))
    gqb=[g.astype(BF) for g in gq]
    da[...]=nn(jnp.concatenate(gqb,axis=1),jnp.concatenate([wt[:,O_QKV+256*j:O_QKV+256*j+256] for j in range(3)],axis=0)).reshape(64,16,256)
    nbs=S["nb"]
    def act3(y,a): nbs[pl.ds(y*8,8)]=a
    def dx3(y,dx):
        z=gres[pl.ds(y*8,8)]+dx
        gres[pl.ds(y*8,8)]=z
        gp[y+1,1:9]=z.astype(BF)
        return z
    fin=gn_bwd(X["res"],da,2,"g3","s3",256,8,8,8,act3,dx3,silu=False)
    nb=nbs[...].reshape(1024,256)
    for j in range(3): put_g(tn(gqb[j],nb),O_QKV+256*j)
    put_vec("b_res2",rowsum(fin()))
    def conv_dgrad(off):
        return nn(jnp.concatenate([gp[2-t//3:10-t//3,2-t%3:10-t%3].reshape(1024,256) for t in range(9)],axis=1),
                  jnp.concatenate([wt[:,off+256*t:off+256*t+256] for t in range(9)],axis=0))
    def conv_wgrad(g,off):
        gt=g.T
        for t in range(9):
            put_g(nn(gt,ap[t//3:t//3+8,t%3:t%3+8].reshape(1024,256)),off+256*t)
    def act_(y,a): ap[y+1,1:9]=a
    da[...]=conv_dgrad(O_R2).reshape(64,16,256)
    def dxm(y,dx):
        gp[y+1,1:9]=dx.astype(BF)
        return dx
    fin=gn_bwd(X["mid"],da,1,"g2","s2",256,8,8,8,act_,dxm)
    conv_wgrad(gp[1:9,1:9].reshape(1024,256),O_R2)
    gemb=fin()
    put_vec("b_time",rowsum(gemb)); put_vec("b_res1",rowsum(gemb))
    put_g(tn(gemb.astype(BF),X["feat"][...]),O_TIME)
    da[...]=conv_dgrad(O_R1).reshape(64,16,256)
    def dxl(y,dx):
        z=gres[pl.ds(y*8,8)]+dx
        gp[y+1,1:9]=z.astype(BF)
        return z
    fin=gn_bwd(X["low"],da,0,"g1","s1",256,8,8,8,act_,dxl)
    conv_wgrad(gp[1:9,1:9].reshape(1024,256),O_R1)
    put_vec("b_down",rowsum(fin()))
    glb=gp[1:9,1:9].reshape(1024,256)
    glt=glb.T
    tp=X["tp"]
    for t in range(9):
        ty,tx=t//3,t%3
        yd[t,0:8,0:8]=nn(glb,wt[:,O_DOWN+128*t:O_DOWN+128*t+128]).reshape(8,8,16,128)
        put_g(nn(glt,tp[ty//2:ty//2+8,ty%2,tx//2:tx//2+8,tx%2].reshape(1024,128)),O_DOWN+128*t)
    big6=big.reshape(8,2,8,2,16,128)
    SRC={0:((1,0),),1:((0,1),(2,0))}
    def dt(i,acc):
        for a in range(2):
            for b in range(2):
                z=big6[i,a,:,b]
                for ty,oy in SRC[a]:
                    for tx,ox in SRC[b]:
                        z=z+yd[ty*3+tx,i+oy,ox:ox+8]
                S["dt"].reshape(8,2,8,2,16,128)[i,a,:,b]=z.astype(BF)
                acc=acc+jnp.sum(z,axis=0)
        return acc
    put_vec("b_in",rowsum(lax.fori_loop(0,8,dt,jnp.zeros((N,128),F32))),128)
    dwi=tn(X["cols"][...].reshape(4096,128),S["dt"][...].reshape(4096,128))
    for k in range(27):
        put_block(k, dwi[9*(k%3)+k//3:9*(k%3)+k//3+1])
    put_g(sg[...].T, MID)

def bwd_scratch():
    V=pltpu.VMEM
    return dict(gp18=V((18,18,16,128),BF),gcols=V((256,16,128),BF),big=V((256,16,128),F32),ep=V((256,16,128),BF),dp=V((9,2,9,2,16,128),BF),
      s_hi=V((9,64,16,128),BF),s_lo=V((9,64,16,128),BF),gp=V((10,10,16,256),BF),ap=V((10,10,16,256),BF),da=V((64,16,256),F32),gres=V((64,16,256),F32),
      gqkv=V((6,1024,128),F32),gmx=V((2,1024,128),F32),yd=V((9,9,9,16,128),F32),nb=V((64,16,256),BF),dt=V((256,16,128),BF),sg=V((128,256),F32))
BIN=["out","tgt","snr","stat","cols","tp","low","mid","res","qkv","obb","attb","up","st","feat","wt","wup","wfb","sm"]
def bwd_call(ins, total):
    vm=pl.BlockSpec(memory_space=pltpu.VMEM)
    sc=bwd_scratch(); keys=list(sc)
    def k(*refs):
        a=dict(zip(BIN,refs[:len(BIN)])); a["v"]=a["sm"]; a["ob"]=a["obb"]; a["total"]=float(total)
        bwd_kernel(a,refs[len(BIN):len(BIN)+1],dict(zip(keys,refs[len(BIN)+1:])))
    return pl.pallas_call(k,out_shape=jax.ShapeDtypeStruct((256*64,128),F32),
        in_specs=[vm]*len(BIN),out_specs=vm,scratch_shapes=list(sc.values()), name="student_backward",
        compiler_params=pltpu.CompilerParams(vmem_limit_bytes=62<<20))(*[ins[k] for k in BIN])

MESH = pl.DeviceIdType.MESH

def place():
    dp = lax.axis_index("dp")
    return dp // 4, dp // 2 % 2, dp % 2, lax.axis_index("mp")

def peer(z, y, x, c):
    return {"dp": z*4 + y*2 + x, "mp": c}

def greet(peers):
    barrier = pltpu.get_barrier_semaphore()
    for p in peers:
        pl.semaphore_signal(barrier, inc=1, device_id=p, device_id_type=MESH)
    pl.semaphore_wait(barrier, len(peers))

def partners():
    z, y, x, c = place()
    return [peer(z,y,x,1-c), peer(z,y,1-x,c), peer(z,1-y,x,c)] + [peer((z+o)%4,y,x,c) for o in (1,2,3)]

def gather_kernel(streams, in_ref, out_ref, send, recv, keep):
    z, y, x, c = place()
    wide = in_ref.shape[1] // streams
    greet(partners())
    own = pltpu.make_async_copy(in_ref, out_ref.at[z,y,x,c], keep)
    own.start()
    def cols(s): return pl.ds(s*wide, wide)
    def copies(s, p):
        if p == 0:
            return [pltpu.make_async_remote_copy(in_ref.at[:,cols(s)], out_ref.at[z,y,x,c,:,cols(s)], send.at[s,o-1], recv.at[s,3-o],
                    device_id=peer((z+o)%4,y,x,c), device_id_type=MESH) for o in (1,2,3)]
        first_x = s % 2 == 0
        if p == 1:
            part = out_ref.at[:,y,x,c,:,cols(s)]
            to = peer(z,y,1-x,c) if first_x else peer(z,1-y,x,c)
        elif p == 2:
            part = out_ref.at[:,y,:,c,:,cols(s)] if first_x else out_ref.at[:,:,x,c,:,cols(s)]
            to = peer(z,1-y,x,c) if first_x else peer(z,y,1-x,c)
        else:
            part = out_ref.at[:,:,:,c,:,cols(s)]
            to = peer(z,y,x,1-c)
        return [pltpu.make_async_remote_copy(part, part, send.at[s,p+2], recv.at[s,p+2], device_id=to, device_id_type=MESH)]
    own.wait()
    live = {}
    for step in range(streams + 4):
        for s in range(streams):
            p = step - s
            if 1 <= p <= 4:
                for d in live[s,p-1]: d.wait_recv()
            if 0 <= p <= 3:
                live[s,p] = copies(s,p)
                for d in live[s,p]: d.start()
    for s in range(streams):
        for p in range(4):
            for d in live[s,p]: d.wait_send()

def gather_call(block, cid, streams=4):
    rows, wide = block.shape
    any_ = pl.BlockSpec(memory_space=pl.ANY)
    out = pl.pallas_call(lambda *r: gather_kernel(streams, *r), out_shape=jax.ShapeDtypeStruct((4,2,2,2,rows,wide), block.dtype),
        in_specs=[any_], out_specs=any_, name="gather_columns",
        scratch_shapes=[pltpu.SemaphoreType.DMA((streams,6)), pltpu.SemaphoreType.DMA((streams,6)), pltpu.SemaphoreType.DMA],
        compiler_params=pltpu.CompilerParams(collective_id=cid, has_side_effects=True))(block)
    return out.reshape(32*rows, wide)

def sum_kernel(in_ref, out_ref, box, send, recv):
    z, y, x, c = place()
    hops = [peer(z,y,x,1-c), peer(z,y,1-x,c), peer(z,1-y,x,c), peer(z+1-2*(z%2),y,x,c), peer((z+2)%4,y,x,c)]
    greet(hops)
    out_ref[...] = in_ref[...]
    for k, to in enumerate(hops):
        box[k] = out_ref[...]
        d = pltpu.make_async_remote_copy(box.at[k], box.at[5+k], send.at[k], recv.at[k], device_id=to, device_id_type=MESH)
        d.start()
        d.wait()
        out_ref[...] += box[5+k]

def sum_call(v, cid):
    vm = pl.BlockSpec(memory_space=pltpu.VMEM)
    return pl.pallas_call(sum_kernel, out_shape=jax.ShapeDtypeStruct(v.shape, v.dtype), in_specs=[vm], out_specs=vm, name="sum_small",
        scratch_shapes=[pltpu.VMEM((10,)+v.shape, v.dtype), pltpu.SemaphoreType.DMA((5,)), pltpu.SemaphoreType.DMA((5,))],
        compiler_params=pltpu.CompilerParams(collective_id=cid, has_side_effects=True))(v)

def scatter_kernel(streams, g_ref, out_ref, r0, r1, r2, r3, send, recv):
    z, y, x, c = place()
    wide = out_ref.shape[1] // streams
    greet(partners())
    def rows(s): return pl.ds(s*wide, wide)
    def copies(s, p):
        first_x = s % 2 == 0
        if p == 0:
            src, dst, to = g_ref.at[:,:,:,:,1-c,rows(s)], r0.at[s], peer(z,y,x,1-c)
        elif p == 1:
            src, dst, to = (r0.at[s,:,:,:,1-x], r1.at[s], peer(z,y,1-x,c)) if first_x else (r0.at[s,:,:,1-y], r1.at[s], peer(z,1-y,x,c))
        elif p == 2:
            src, dst = r1.at[s,:,:,1-y if first_x else 1-x], r2.at[s]
            to = peer(z,1-y,x,c) if first_x else peer(z,y,1-x,c)
        else:
            return [pltpu.make_async_remote_copy(r2.at[s,:,(z+o)%4], r3.at[s,3-o], send.at[s,2+o], recv.at[s,6-o],
                    device_id=peer((z+o)%4,y,x,c), device_id_type=MESH) for o in (1,2,3)]
        return [pltpu.make_async_remote_copy(src, dst, send.at[s,p], recv.at[s,p], device_id=to, device_id_type=MESH)]
    def add(s, p):
        first_x = s % 2 == 0
        def one(m, _):
            if p == 0:
                r0[s,m] += g_ref[m,:,:,:,c,rows(s)]
            elif p == 1:
                r1[s,m] += r0[s,m,:,:,x] if first_x else r0[s,m,:,y]
            elif p == 2:
                r2[s,m] += r1[s,m,:,y] if first_x else r1[s,m,:,x]
            else:
                out_ref[m,rows(s)] = r2[s,m,z] + r3[s,0,m] + r3[s,1,m] + r3[s,2,m]
            return 0
        lax.fori_loop(0, 8, one, 0)
    live = {}
    for step in range(streams + 4):
        for s in range(streams):
            p = step - s
            if 1 <= p <= 4:
                for d in live[s,p-1]: d.wait_recv()
                add(s, p-1)
            if 0 <= p <= 3:
                live[s,p] = copies(s,p)
                for d in live[s,p]: d.start()
    for s in range(streams):
        for p in range(4):
            for d in live[s,p]: d.wait_send()

def scatter_call(g, cid, streams=4):
    T = g.shape[0] // 256
    g = g.reshape(8,4,2,2,2,T,128)
    w = T // streams
    vm = pl.BlockSpec(memory_space=pltpu.VMEM)
    V = pltpu.VMEM
    out = pl.pallas_call(lambda *r: scatter_kernel(streams, *r), out_shape=jax.ShapeDtypeStruct((8,T,128), F32), in_specs=[vm], out_specs=vm,
        scratch_shapes=[V((streams,8,4,2,2,w,128),F32), V((streams,8,4,2,w,128),F32), V((streams,8,4,w,128),F32), V((streams,3,8,w,128),F32),
                        pltpu.SemaphoreType.DMA((streams,6)), pltpu.SemaphoreType.DMA((streams,6))], name="scatter_gradient",
        compiler_params=pltpu.CompilerParams(collective_id=cid, has_side_effects=True, vmem_limit_bytes=40<<20))(g)
    return out.reshape(8, T*128)


def segments():
    matrices = [("w_in", 27, C1), ("w_down", 9 * C1, C2), ("w_res1", 9 * C2, C2), ("w_res2", 9 * C2, C2), ("w_time", C1, C2),
                ("w_qkv", C2, 3 * C2), ("w_proj", C2, C2), ("w_up", 9 * C2, C1), ("w_final", 9 * C1, 3)]
    vectors = [("g1", C2), ("s1", C2), ("g2", C2), ("s2", C2), ("g3", C2), ("s3", C2), ("g4", C1), ("s4", C1), ("b_in", C1),
               ("b_down", C2), ("b_res1", C2), ("b_res2", C2), ("b_time", C2), ("b_query", C2), ("b_value", C2), ("b_proj", C2),
               ("b_up", C1), ("b_final", 3)]
    listing, cursor = [], 0
    for name, height, breadth in matrices:
        listing.append((name, cursor, (height, breadth), "matrix"))
        cursor += height * breadth
    for name, length in vectors:
        listing.append((name, cursor, (length,), "gain" if name[0] != "b" else "bias"))
        cursor += length
    return listing

def rates(position):
    learn = jnp.zeros(position.shape, F32)
    decay = jnp.zeros(position.shape, F32)
    for name, offset, shape, kind in segments():
        inside = (position >= offset) & (position < offset + math.prod(shape))
        if kind == "matrix":
            spread = shape[0] ** (-0.5) * ((SIDE * SIDE / 4.0) ** 0.5 if name == "w_proj" else 1.0)
            learn = jnp.where(inside, 0.5 * spread, learn)
            decay = jnp.where(inside, 0.01, decay)
        elif kind == "gain":
            learn = jnp.where(inside, 0.2, learn)
        else:
            learn = jnp.where(inside, 0.05, learn)
    return learn, decay

def angle_of(step):
    return 0.1 + 1.35 * step.astype(F32) / TGRID

def time_features(step):
    half = C1 // 2
    freqs = jnp.exp(-math.log(1000.0) * jnp.arange(half).astype(F32) / half)
    phases = step.astype(F32)[..., None] * freqs
    return jnp.concatenate([jnp.sin(phases), jnp.cos(phases)], axis=-1)

def to_columns(shard, start, D):
    R, L = 256 // D, shard.shape[0]
    body = R * MID
    if HEAD % D == 0:
        parts = [shard[start:start+body], shard[:start], shard[start+body:]]
    else:
        at = jnp.arange(L - body)
        parts = [lax.dynamic_slice(shard, (start,), (body,)), jnp.where(at < start, shard[:L-body], shard[body:])]
    cols = jnp.concatenate(parts).reshape(-1, R).T
    return jnp.pad(cols, ((0,0),(0,MID+128-cols.shape[1])))

def from_columns(cols, start, D, L):
    R = 256 // D
    body = R * MID
    q = cols[:, O_QKV:O_QKV+768].reshape(R,3,256).transpose(0,2,1).reshape(R,768)
    cols = jnp.concatenate([cols[:, :O_QKV], q, cols[:, O_PROJ:L//R]], axis=1)
    flat = cols.T.reshape(-1)
    if HEAD % D == 0:
        return jnp.concatenate([flat[body:body+start], flat[:body], flat[body+start:]])
    rest = flat[body:]
    at = jnp.arange(L)
    mid = lax.dynamic_update_slice(jnp.zeros((L,), F32), flat[:body], (start,))
    low = jnp.pad(rest, (0, body)); high = jnp.pad(rest, (body, 0))
    return jnp.where(at < start, low, jnp.where(at < start + body, mid, high))

def lanes(images):
    v = jnp.repeat(images.transpose(1,2,0,3).reshape(256,N,3), 9, axis=2)
    return jnp.pad(v, ((0,0),(0,0),(0,101)))

def local(images, noise, timestep, stride, bucket, steps_table, master, first_moment, second_moment, teacher, step_count):
    axes = ("dp", "mp")
    D = lax.axis_size("dp") * lax.axis_size("mp")
    me = lax.axis_index(axes)
    R, L = 256 // D, master.shape[0]
    start = HEAD // D if HEAD % D == 0 else (HEAD - me + D - 1) // D
    near = lax.axis_size("dp") == 16 and lax.axis_size("mp") == 2
    teacher_cols = to_columns(teacher, start, D)
    teacher_all = gather_call(teacher_cols, 1) if near else lax.all_gather(teacher_cols, axes, axis=0, tiled=True)
    student_all = lax.all_gather(to_columns(master.astype(BF), start, D), axes, axis=0, tiled=True)
    wide = lambda v: jnp.broadcast_to(v[..., None], v.shape + (128,))
    angle = angle_of(timestep)
    noisy = lanes(jnp.cos(angle)[:,None,None,None] * images + jnp.sin(angle)[:,None,None,None] * noise)
    picked = jnp.sum(jnp.where(jnp.arange(steps_table.shape[0]) == bucket[0], steps_table, 0))
    turn = jnp.arange(KMAX)[:, None]
    current = timestep[None] - turn * stride[None]
    later = current - stride[None]
    keep = jnp.sin(angle_of(later)) / jnp.sin(angle_of(current))
    take = jnp.cos(angle_of(later)) - keep * jnp.cos(angle_of(current))
    features = jax.nn.silu(time_features(current)).astype(BF)
    final_t = timestep - picked * stride
    below = jnp.sin(angle - angle_of(final_t))
    target = teacher_call(D, picked.reshape(1), noisy, features, wide(take), wide(keep), wide(jnp.sin(angle)/below),
                          wide(-jnp.sin(angle_of(final_t))/below), teacher_all)
    snr = wide(jnp.maximum(jnp.square(jnp.cos(angle)/jnp.sin(angle)), 1.0))
    out, sums, kept = student_call(D, noisy, target, snr, features[0], student_all)
    sums = sum_call(sums, 2) if near else lax.psum(sums, axes)
    total = images.shape[0] * D
    pick = sums[:5, 0:27:9]
    mean_t, mean_o = pick[0]/(256*total), pick[2]/(256*total)
    var_t, var_o = pick[1]/(256*total) - jnp.square(mean_t), pick[3]/(256*total) - jnp.square(mean_o)
    loss = jnp.sum(pick[4])/(768*total) + jnp.sum(jnp.square(mean_o-mean_t) + jnp.square(var_o-var_t))
    grads = bwd_call(dict(kept, out=out, tgt=target, snr=snr, stat=sums, feat=features[0]), total)
    if near:
        part = scatter_call(grads, 3)
    else:
        order = grads.reshape(R, D, MID+128)
        if HEAD % D:
            order = jnp.concatenate([jnp.roll(order[:, :, :MID], HEAD % D, axis=1), order[:, :, MID:]], axis=2)
        part = lax.psum_scatter(order, axes, scatter_dimension=1, tiled=True).reshape(R, MID+128)
    grad = from_columns(part, start, D, L)
    learn, decay = rates(jnp.arange(L, dtype=jnp.int32) * D + me)
    steps_done = step_count[0].astype(F32)
    new_first = 0.5 * first_moment + 0.5 * grad
    new_second = 0.5 * second_moment + 0.5 * jnp.square(grad)
    fix_rate = 1.0 - jnp.power(0.5, steps_done)
    new_master = master - learn * (new_first / fix_rate / (jnp.sqrt(new_second / fix_rate) + 1e-08) + decay * master)
    return loss, new_master, new_first, new_second

def solution(mesh):
    s = P(("dp", "mp"))
    i = P(("dp", "mp"), None, None, None)
    return jax.shard_map(local, mesh=mesh, in_specs=(i, i, s, s, s, P(), s, s, s, s, P()), out_specs=(P(), s, s, s), check_vma=False)
```

```python
import math
import jax
import jax.numpy as jnp
from jax import lax
from jax.experimental import pallas as pl
from jax.experimental.pallas import tpu as pltpu
from jax.sharding import PartitionSpec as P

C1, C2, N = 128, 256, 16
SIDE, TGRID, KMAX = 16, 64, 4
F32, BF = jnp.float32, jnp.bfloat16
O_DOWN, O_R1, O_R2, O_TIME, O_QKV, O_PROJ, O_UP, MID = 0, 1152, 3456, 5760, 5888, 6656, 6912, 8064
HEAD = 3456
BLOCK = {}
_at = 54
for _name, _wide in (("g1",2),("s1",2),("g2",2),("s2",2),("g3",2),("s3",2),("g4",1),("s4",1),("b_in",1),("b_down",2),("b_res1",2),
                     ("b_res2",2),("b_time",2),("b_query",2),("b_value",2),("b_proj",2),("b_up",1),("b_final",1)):
    BLOCK[_name] = (_at, _wide)
    _at += _wide

def iota(shape, d): return lax.broadcasted_iota(jnp.int32, shape, d)

def nt(a, b): return lax.dot_general(a, b, (((1,),(1,)),((),())), preferred_element_type=F32)
def nn(a, b): return lax.dot_general(a, b, (((1,),(0,)),((),())), preferred_element_type=F32)

def one_hot(cond): return jnp.where(cond, 1.0, 0.0).astype(BF)

def split3(v):
    hi = v.astype(BF); r = v - hi.astype(F32)
    mid = r.astype(BF); lo = (r - mid.astype(F32)).astype(BF)
    return jnp.concatenate([hi, mid, lo], axis=0)

def group_sum(v, per):
    C = v.shape[1]
    G = one_hot(iota((C,C),0)//per == iota((C,C),1)//per)
    r = nn(split3(v), G)
    return r[0:N] + r[N:2*N] + r[2*N:3*N]

def prep(tg_ref, wt_ref, wup_ref, win_ref, wfin_ref, wfb_ref, sm_ref, D):
    R = 256 // D
    row, o = iota((256,256),1), iota((256,256),0)
    dev, m = row // R, row % R
    perm = one_hot(o == (dev + ((-HEAD) % D)) % D + D * m)
    CH = 1152
    for c in range(7):
        wt_ref[:, c*CH:(c+1)*CH] = nn(perm, tg_ref[:, c*CH:(c+1)*CH]).astype(BF)
    kk, ci = iota((256,256),0), iota((256,256),1)
    peo = one_hot(ci == 2*(kk % 128) + kk // 128)
    for t in range(9):
        cs = O_UP + t*128
        both = jnp.concatenate([wt_ref[0:128, cs:cs+128], wt_ref[128:256, cs:cs+128]], axis=1)
        wup_ref[t] = nn(both, peo).astype(BF)
    kq, lq = iota((768,768),0), iota((768,768),1)
    pq = one_hot(kq == 3*(lq % 256) + lq // 256)
    wt_ref[:, O_QKV:O_QKV+768] = nn(wt_ref[:, O_QKV:O_QKV+768], pq).astype(BF)
    perm0 = one_hot(o == dev + D * m)
    sm_ref[...] = nn(perm0, tg_ref[:, MID:MID+128]).T
    halves = jnp.concatenate([sm_ref[0:32, 0:128], sm_ref[0:32, 128:256]], axis=0).astype(BF)
    l, r = iota((128,64),0), iota((128,64),1)
    k = 3*(l % 9) + l // 9
    win_ref[...] = nn(one_hot((l < 27) & (r == 32*(k % 2) + k // 2)), halves).astype(BF)
    t16, r16 = iota((16,64),0), iota((16,64),1)
    pieces = []
    for h in range(3):
        blk = 27 + 3*t16 + h
        pieces.append(nn(one_hot((t16 < 9) & (r16 == 32*(blk % 2) + blk // 2)), halves))
    flat = jnp.concatenate(pieces, axis=1).astype(BF)
    acc = jnp.zeros((128,128), F32)
    for c in range(3):
        wc = nn(flat, one_hot(iota((384,128),0) == 3*iota((384,128),1) + c)).astype(BF)
        acc += nn(one_hot((iota((128,16),1) < 9) & (iota((128,16),0) == 9*c + iota((128,16),1))), wc)
    wfb = acc.astype(BF)
    wfb_ref[...] = wfb
    a, z = iota((128,128),0), iota((128,128),1)
    for t in range(9):
        wfin_ref[:, 128*t:128*t+128] = nn(one_hot((a < 27) & (z == 9*(a // 9) + t)), wfb).astype(BF)

def final_bias(sm_ref):
    b = sm_ref[42:43, 0:128].astype(BF)
    return nn(b, one_hot((iota((128,128),1) < 27) & (iota((128,128),0) == iota((128,128),1) // 9)))

def gn_stats(load, rows, per, C, count):
    def s1(i, acc): return acc + jnp.sum(load(i), axis=0)
    m = group_sum(lax.fori_loop(0, rows, s1, jnp.zeros((N,C),F32)), per) * (1.0/count)
    def s2(i, acc): return acc + jnp.sum(jnp.square(load(i) - m), axis=0)
    v = group_sum(lax.fori_loop(0, rows, s2, jnp.zeros((N,C),F32)), per) * (1.0/count)
    return m, lax.rsqrt(v + 1e-5)

def sigmoid(x): return 1.0 / (1.0 + jnp.exp(-x))

def vec(v_ref, name, C=C2):
    at, wide = BLOCK[name]
    return jnp.concatenate([v_ref[b//2:b//2+1, 128*(b%2):128*(b%2)+128] for b in range(at, at+wide)], axis=1)

def net(x_ref, feat, wt, wup, win, wfin, v_ref, sc):
    xp, tp, top, low, ap, mid, res, qkv, ob, yp, up, ep = (sc[k] for k in ("xp","tp","top","low","ap","mid","res","qkv","ob","yp","up","ep"))
    lane = iota((1,1,128),2)
    def save(si, m, inv):
        if "st" in sc:
            C = m.shape[1]
            sc["st"][2*si,:,0:C] = m
            sc["st"][2*si+1,:,0:C] = inv
    bfin = final_bias(v_ref)
    def a0(y, _):
        xp[y+1, 1:17] = x_ref[pl.ds(y*16,16)].astype(BF)
        return 0
    lax.fori_loop(0,16,a0,0)
    def a1(y2, _):
        pieces=[]
        for k in range(4):
            y = y2*4+k
            cols = jnp.zeros((16,16,128),BF)
            for t in range(9):
                w = xp[y+t//3, t%3:t%3+16]
                cols = jnp.where((lane%9==t)&(lane<27), w, cols) if t else jnp.where((lane%9==0)&(lane<27), w, jnp.zeros_like(w))
            if "cols" in sc: sc["cols"][pl.ds(y*16,16)] = cols
            pieces.append(cols.reshape(256,128))
        r = nn(jnp.concatenate(pieces,axis=0), win[...]) + vec(v_ref,"b_in",C1)
        top[pl.ds(y2*64,64)] = r.reshape(64,16,128)
        rb = r.astype(BF).reshape(4,8,2,16,128)
        for k in range(4):
            p = y2*4+k+1
            tp[p//2, p%2, 0:8, 1] = rb[k,:,0]
            tp[p//2, p%2, 1:9, 0] = rb[k,:,1]
        return 0
    lax.fori_loop(0,4,a1,0)
    taps=[]
    for t in range(9):
        ty,tx=t//3,t%3
        taps.append(tp[ty//2:ty//2+8, ty%2, tx//2:tx//2+8, tx%2].reshape(1024,128))
    low[...] = (nt(jnp.concatenate(taps,axis=1), wt[:,O_DOWN:O_DOWN+1152]) + vec(v_ref,"b_down")).reshape(64,16,256)
    def norm_act(src, g, s, si):
        m, inv = gn_stats(lambda i: src[pl.ds(i*8,8)], 8, 8, 256, 512.0)
        save(si, m, inv)
        def b(y,_):
            z = (src[pl.ds(y*8,8)] - m)*inv*vec(v_ref,g) + vec(v_ref,s)
            ap[y+1,1:9] = (z*sigmoid(z)).astype(BF)
            return 0
        lax.fori_loop(0,8,b,0)
    def conv3(off):
        return nt(jnp.concatenate([ap[t//3:t//3+8, t%3:t%3+8].reshape(1024,256) for t in range(9)],axis=1), wt[:,off:off+2304])
    norm_act(low,"g1","s1",0)
    emb = nt(feat, wt[:,O_TIME:O_TIME+128]) + vec(v_ref,"b_time")
    mid[...] = (conv3(O_R1) + vec(v_ref,"b_res1")).reshape(64,16,256) + emb
    norm_act(mid,"g2","s2",1)
    res[...] = low[...] + (conv3(O_R2) + vec(v_ref,"b_res2")).reshape(64,16,256)
    m, inv = gn_stats(lambda i: res[pl.ds(i*8,8)], 8, 8, 256, 512.0)
    save(2, m, inv)
    nb = ((res[...]-m)*inv*vec(v_ref,"g3") + vec(v_ref,"s3")).astype(BF).reshape(1024,256)
    q = nt(nb, wt[:,O_QKV:O_QKV+256]) + vec(v_ref,"b_query")
    k_ = nt(nb, wt[:,O_QKV+256:O_QKV+512])
    v_ = nt(nb, wt[:,O_QKV+512:O_QKV+768])+vec(v_ref,"b_value")
    for i, z in enumerate((q, k_, v_)):
        z = z.astype(BF).astype(F32)
        qkv[2*i] = z[:,0:128]
        qkv[2*i+1] = z[:,128:256]
    def att(n,_):
        x = [jnp.concatenate([qkv[h,pl.ds(n,64,stride=16),:] for h in (2*k,2*k+1)],axis=1).astype(BF) for k in range(3)]
        s = nt(x[0],x[1])*(C2**-0.5)
        e = jnp.exp(s - jnp.max(s,axis=1,keepdims=True))
        p = e/jnp.sum(e,axis=1,keepdims=True)
        o = nn(p.astype(BF), x[2]).astype(BF).astype(F32)
        ob[0,pl.ds(n,64,stride=16),:] = o[:,0:128]
        ob[1,pl.ds(n,64,stride=16),:] = o[:,128:256]
        return 0
    lax.fori_loop(0,16,att,0,unroll=4)
    obb = jnp.concatenate([ob[0],ob[1]],axis=1).astype(BF)
    if "obb" in sc: sc["obb"][...] = obb
    att_out = res[...].reshape(1024,256) + (nt(obb, wt[:,O_PROJ:O_PROJ+256]) + vec(v_ref,"b_proj"))
    attb = att_out.astype(BF)
    if "attb" in sc: sc["attb"][...] = attb
    for t in range(9):
        yp[t,1:9,1:9] = nt(attb, wup[t]).reshape(8,8,16,128)
    def u(i,_):
        for a in range(2):
            for b in range(2):
                acc=None
                for t in range(9):
                    r,c=t//3-1,t%3-1
                    dr=(a+r)//2; dc=(b+c)//2
                    v=yp[t, i+dr+1, 1+dc:9+dc]
                    acc = v if acc is None else acc+v
                up[i,a,:,b] = acc + vec(v_ref,"b_up",C1) + sc["top6"][i,a,:,b]
        return 0
    lax.fori_loop(0,8,u,0)
    upf = sc["up3"]
    m, inv = gn_stats(lambda i: upf[pl.ds(i*16,16)], 16, 4, 128, 1024.0)
    save(3, m, inv)
    def b4(y,_):
        z = (upf[pl.ds(y*16,16)]-m)*inv*vec(v_ref,"g4",C1)+vec(v_ref,"s4",C1)
        ep[y+1,1:17] = (z*sigmoid(z)).astype(BF)
        return 0
    lax.fori_loop(0,16,b4,0)
    def fin(put):
        def f(y4,_):
            cols=jnp.concatenate([ep[pl.ds(y4*8+t//3,8), t%3:t%3+16].reshape(2048,128) for t in range(9)],axis=1)
            put(y4, (nt(cols, wfin[...])+bfin).reshape(128,16,128))
            return 0
        lax.fori_loop(0,2,f,0)
    return fin

def scratch():
    V=pltpu.VMEM
    return dict(wt=V((256,MID),BF), wup=V((9,128,256),BF), win=V((128,128),BF), wfin=V((128,1152),BF), wfb=V((128,128),BF), sm=V((128,256),F32), xp=V((18,18,16,128),BF), tp=V((9,2,9,2,16,128),BF),
      top=V((256,16,128),F32), low=V((64,16,256),F32), ap=V((10,10,16,256),BF), mid=V((64,16,256),F32), res=V((64,16,256),F32),
      qkv=V((6,1024,128),F32), ob=V((2,1024,128),F32), yp=V((9,10,10,16,128),F32), up=V((8,2,8,2,16,128),F32), ep=V((18,18,16,128),BF))
KEYS=list(scratch().keys())

def zero_borders(sc):
    for k in ("xp","ep","tp","ap","yp"):
        sc[k][...] = jnp.zeros(sc[k].shape, sc[k].dtype)

def views(sc):
    sc=dict(sc)
    sc["top6"]=sc["top"].reshape(8,2,8,2,16,128)
    sc["up3"]=sc["up"].reshape(256,16,128)
    return sc

def teacher_call(D, cnt, x, feat, ce, cl, tc, nc, tg):
    def kern(cnt_ref, x_ref, feat_ref, ce_ref, cl_ref, tc_ref, nc_ref, tg_ref, out_ref, *scr):
        sc = views(dict(zip(KEYS, scr)))
        zero_borders(sc)
        prep(tg_ref, *(sc[k] for k in WKEYS), D)
        out_ref[...] = x_ref[...]
        def step(j, _):
            fin = net(out_ref, feat_ref[j], sc["wt"], sc["wup"], sc["win"], sc["wfin"], sc["sm"], sc)
            ce_, cl_ = ce_ref[j], cl_ref[j]
            def put(y4, e):
                out_ref[pl.ds(y4*128,128)] = ce_*e + cl_*out_ref[pl.ds(y4*128,128)]
            fin(put)
            return 0
        lax.fori_loop(0, cnt_ref[0], step, 0)
        def tgt(i, _):
            out_ref[pl.ds(i*16,16)] = tc_ref[...]*out_ref[pl.ds(i*16,16)] + nc_ref[...]*x_ref[pl.ds(i*16,16)]
            return 0
        lax.fori_loop(0, 16, tgt, 0)
    vm = pl.BlockSpec(memory_space=pltpu.VMEM)
    return pl.pallas_call(kern, out_shape=jax.ShapeDtypeStruct((256,16,128),F32),
        in_specs=[pl.BlockSpec(memory_space=pltpu.SMEM)]+[vm]*7, out_specs=vm, scratch_shapes=list(scratch().values()), name="teacher_steps",
        compiler_params=pltpu.CompilerParams(vmem_limit_bytes=60<<20))(cnt, x, feat, ce, cl, tc, nc, tg)

WKEYS = ["wt","wup","win","wfin","wfb","sm"]
RES = ["wt","wup","wfb","sm","tp","low","mid","res","qkv","up"]
def student_call(D, x, tgt, snr, feat, tg):
    vm=pl.BlockSpec(memory_space=pltpu.VMEM)
    sh=scratch()
    extra=dict(st=pltpu.VMEM((8,16,256),F32),cols=pltpu.VMEM((256,16,128),BF),attb=pltpu.VMEM((1024,256),BF),obb=pltpu.VMEM((1024,256),BF))
    outs={k:sh[k] for k in RES}; outs.update(extra)
    scr={k:v for k,v in sh.items() if k not in outs}
    ok,sk=list(outs),list(scr)
    def kern(x_ref,t_ref,snr_ref,feat_ref,tg_ref,out_ref,sum_ref,*refs):
        sc=views(dict(zip(ok+sk,refs)))
        zero_borders(sc)
        prep(tg_ref,*(sc[k] for k in WKEYS),D)
        fin=net(x_ref,feat_ref[...],sc["wt"],sc["wup"],sc["win"],sc["wfin"],sc["sm"],sc)
        def put(y4,e): out_ref[pl.ds(y4*128,128)]=e
        fin(put)
        def s(i,c):
            t,o=t_ref[pl.ds(i*16,16)],out_ref[pl.ds(i*16,16)]
            d=o-t
            return tuple(a+jnp.sum(b,axis=0) for a,b in zip(c,(t,t*t,o,o*o,d*d)))
        z=jnp.zeros((N,128),F32)
        r=lax.fori_loop(0,16,s,(z,)*5)
        r=r[:4]+(r[4]*snr_ref[...],)
        sum_ref[...]=jnp.concatenate([jnp.sum(a,axis=0,keepdims=True) for a in r]+[jnp.zeros((3,128),F32)],axis=0)
    res=pl.pallas_call(kern,
        out_shape=(jax.ShapeDtypeStruct((256,16,128),F32),jax.ShapeDtypeStruct((8,128),F32))+tuple(jax.ShapeDtypeStruct(outs[k].shape,outs[k].dtype) for k in ok),
        in_specs=[vm]*5,out_specs=(vm,)*(2+len(ok)),scratch_shapes=[scr[k] for k in sk], name="student_forward",
        compiler_params=pltpu.CompilerParams(vmem_limit_bytes=62<<20))(x,tgt,snr,feat,tg)
    return res[0],res[1],dict(zip(ok,res[2:]))

def tn(a, b): return lax.dot_general(a, b, (((0,),(0,)),((),())), preferred_element_type=F32)

def bwd_kernel(x_refs, o_refs, sc):
    X, S = x_refs, sc
    (G,) = o_refs
    sg, sn_total = S["sg"], X["total"]
    v_ref, wt, wup, st = X["v"], X["wt"], X["wup"], X["st"]
    gp18, gcols, big, ep, dp, s_hi, s_lo, gp, ap, da, gres, gqkv, gmx, yd = (S[k] for k in ("gp18","gcols","big","ep","dp","s_hi","s_lo","gp","ap","da","gres","gqkv","gmx","yd"))
    lane = iota((1,1,128),2)
    for k in ("gp18","dp","gp","ap","yd"):
        S[k][...] = jnp.zeros(S[k].shape, S[k].dtype)
    sg[...] = jnp.zeros((128,256),F32)
    def put_block(b, val):
        sg[b//2:b//2+1, 128*(b%2):128*(b%2)+128] = val
    def put_vec(name, val, C=C2):
        at, wide = BLOCK[name]
        for k in range(wide):
            put_block(at+k, val[:, 128*k:128*k+128])
    def rowsum(a): return jnp.sum(a, axis=0, keepdims=True)
    def put_g(val, col, row0=0):
        rows, width = val.shape
        for c in range(width//128):
            for r in range(0, rows, 8):
                G[pl.ds((row0+r)*64+col//128+c, 8, stride=64),:] = val[r:r+8, c*128:c*128+128]
    pixels = 256.0*sn_total
    so = X["stat"][...]
    mt, mo = so[0:1]/pixels, so[2:3]/pixels
    vt_, vo = so[1:2]/pixels-mt*mt, so[3:4]/pixels-mo*mo
    cb = 4.0*(vo-vt_)/pixels
    ca = 2.0*(mo-mt)/pixels-cb*mo
    sn = X["snr"][...]*(2.0/(768.0*sn_total))
    acc=jnp.zeros((N,128),F32)
    def g0(y,acc):
        o=X["out"][pl.ds(y*16,16)]
        go = sn*(o-X["tgt"][pl.ds(y*16,16)]) + ca + cb*o
        gp18[y+1,1:17]=go.astype(BF)
        return acc+jnp.sum(go,axis=0)
    acc=lax.fori_loop(0,16,g0,acc)
    acc=rowsum(acc)
    lane2=iota((1,128),1)
    put_block(84, sum(jnp.where(lane2==c, jnp.sum(jnp.where(lane2==9*c,acc,0.0),axis=1,keepdims=True),0.0) for c in range(3)))
    def g1(y,_):
        for t in range(9):
            w = gp18[y+2-t//3, 2-t%3:18-t%3]
            cols = jnp.where((lane%9==t)&(lane<27), w, cols) if t else jnp.where((lane%9==0)&(lane<27), w, jnp.zeros_like(w))
        gcols[pl.ds(y*16,16)] = cols
        return 0
    lax.fori_loop(0,16,g1,0)
    big[...] = nn(gcols[...].reshape(4096,128), X["wfb"][...]).reshape(256,16,128)
    def gn_bwd(src, dref, si, gname, sname, C, per, rows, k, act_put, dx_put, silu=True):
        m, inv = st[2*si,:,0:C], st[2*si+1,:,0:C]
        g, s = vec(v_ref,gname,C), vec(v_ref,sname,C)
        def p1(y,c):
            A,B=c
            xh=(src[pl.ds(y*k,k)]-m)*inv
            d=dref[pl.ds(y*k,k)]
            z=xh*g+s
            if silu:
                sg=sigmoid(z); act=z*sg
                act_put(y,act.astype(BF))
                d=d*(sg+act*(1.0-sg))
                dref[pl.ds(y*k,k)]=d
            else:
                act_put(y,z.astype(BF))
            return A+jnp.sum(d,axis=0), B+jnp.sum(d*xh,axis=0)
        A,B=lax.fori_loop(0,rows,p1,(jnp.zeros((N,C),F32),jnp.zeros((N,C),F32)))
        put_vec(gname,rowsum(B),C); put_vec(sname,rowsum(A),C)
        cnt=1.0/(per*rows*k)
        ga=group_sum(g*A,per)*cnt; gb=group_sum(g*B,per)*cnt
        def p2(y,acc):
            xh=(src[pl.ds(y*k,k)]-m)*inv
            dx=inv*(g*dref[pl.ds(y*k,k)]-ga-xh*gb)
            return acc+jnp.sum(dx_put(y,dx),axis=0)
        return lambda: lax.fori_loop(0,rows,p2,jnp.zeros((N,C),F32))
    def act4(y,a): ep[pl.ds(y*16,16)]=a
    def dx4(y,dx):
        big[pl.ds(y*16,16)]=dx
        b=dx.astype(BF).reshape(8,2,16,128)
        p=y+1
        dp[p//2,p%2,0:8,1]=b[:,0]
        dp[p//2,p%2,1:9,0]=b[:,1]
        return dx
    fin=gn_bwd(X["up"].reshape(256,16,128),big,3,"g4","s4",128,4,16,16,act4,dx4)
    dwf = tn(gcols[...].reshape(4096,128), ep[...].reshape(4096,128))
    flat = jnp.zeros((9,384),F32)
    for c in range(3):
        p3 = one_hot(iota((128,384),1) == 3*iota((128,384),0) + c)
        piece = dwf[9*c:9*c+9]
        hi = piece.astype(BF); rest = piece-hi.astype(F32)
        mi = rest.astype(BF); lo = (rest-mi.astype(F32)).astype(BF)
        flat += nn(hi,p3)+nn(mi,p3)+nn(lo,p3)
    for t in range(9):
        for h in range(3):
            put_block(27+3*t+h, flat[t:t+1,128*h:128*h+128])
    put_vec("b_up",rowsum(fin()),128)
    PAIR={-1:((1,0),(1,1)),0:((0,1),(1,0)),1:((0,0),(0,1))}
    def su(i,_):
        for r in (-1,0,1):
            (ra,pa),(rb,pb)=PAIR[r]
            V={}
            for cp in range(2):
                V[cp]=dp[i+ra,pa,:,cp].astype(F32)+dp[i+rb,pb,:,cp].astype(F32)
            for c in (-1,0,1):
                (ca_,qa),(cb_,qb)=PAIR[c]
                s=V[qa][ca_:ca_+8]+V[qb][cb_:cb_+8]
                t=(r+1)*3+c+1
                hi=s.astype(BF)
                s_hi[t,pl.ds(i*8,8)]=hi
                s_lo[t,pl.ds(i*8,8)]=(s-hi.astype(F32)).astype(BF)
        return 0
    lax.fori_loop(0,8,su,0)
    cat=lambda ref: jnp.concatenate([ref[t].reshape(1024,128) for t in range(9)],axis=1)
    wu=wup[...].reshape(1152,256)
    gatt=nn(cat(s_hi),wu)+nn(cat(s_lo),wu)
    gres[...]=gatt.reshape(64,16,256)
    put_vec("b_proj",rowsum(gatt))
    gab=gatt.astype(BF)
    attb=X["attb"][...]
    kk, ci = iota((256,256),1), iota((256,256),0)
    peo=one_hot(ci == 2*(kk % 128) + kk // 128)
    aeo=nn(attb,peo).astype(BF)
    for t in range(9):
        r=tn(s_hi[t].reshape(1024,128),aeo)+tn(s_lo[t].reshape(1024,128),aeo)
        put_g(r[:,0:128],O_UP+t*128,0); put_g(r[:,128:256],O_UP+t*128,128)
    obb=X["ob"][...]
    put_g(tn(gab,obb),O_PROJ)
    gm=nn(gab,wt[:,O_PROJ:O_PROJ+256]).astype(BF).astype(F32)
    gmx[0]=gm[:,0:128]; gmx[1]=gm[:,128:256]
    qkv=X["qkv"]
    sc_=C2**-0.5
    def att(n,_):
        q,k,v=[jnp.concatenate([qkv[h,pl.ds(n,64,stride=16),:] for h in (2*j,2*j+1)],axis=1).astype(BF) for j in range(3)]
        gmn=jnp.concatenate([gmx[h,pl.ds(n,64,stride=16),:] for h in (0,1)],axis=1).astype(BF)
        s=nt(q,k)*sc_
        e=jnp.exp(s-jnp.max(s,axis=1,keepdims=True))
        p=e/jnp.sum(e,axis=1,keepdims=True)
        ga=nt(gmn,v)
        gs=(p*(ga-jnp.sum(ga*p,axis=1,keepdims=True))).astype(BF)
        outs=(nn(gs,k)*sc_, tn(gs,q)*sc_, tn(p.astype(BF),gmn))
        for j,o in enumerate(outs):
            o=o.astype(BF).astype(F32)
            gqkv[2*j,pl.ds(n,64,stride=16),:]=o[:,0:128]
            gqkv[2*j+1,pl.ds(n,64,stride=16),:]=o[:,128:256]
        return 0
    lax.fori_loop(0,16,att,0,unroll=4)
    gq=[jnp.concatenate([gqkv[2*j],gqkv[2*j+1]],axis=1) for j in range(3)]
    put_vec("b_query",rowsum(gq[0])); put_vec("b_value",rowsum(gq[2]))
    gqb=[g.astype(BF) for g in gq]
    da[...]=nn(jnp.concatenate(gqb,axis=1),jnp.concatenate([wt[:,O_QKV+256*j:O_QKV+256*j+256] for j in range(3)],axis=0)).reshape(64,16,256)
    nbs=S["nb"]
    def act3(y,a): nbs[pl.ds(y*8,8)]=a
    def dx3(y,dx):
        z=gres[pl.ds(y*8,8)]+dx
        gres[pl.ds(y*8,8)]=z
        gp[y+1,1:9]=z.astype(BF)
        return z
    fin=gn_bwd(X["res"],da,2,"g3","s3",256,8,8,8,act3,dx3,silu=False)
    nb=nbs[...].reshape(1024,256)
    for j in range(3): put_g(tn(gqb[j],nb),O_QKV+256*j)
    put_vec("b_res2",rowsum(fin()))
    def conv_dgrad(off):
        return nn(jnp.concatenate([gp[2-t//3:10-t//3,2-t%3:10-t%3].reshape(1024,256) for t in range(9)],axis=1),
                  jnp.concatenate([wt[:,off+256*t:off+256*t+256] for t in range(9)],axis=0))
    def conv_wgrad(g,off):
        gt=g.T
        for t in range(9):
            put_g(nn(gt,ap[t//3:t//3+8,t%3:t%3+8].reshape(1024,256)),off+256*t)
    def act_(y,a): ap[y+1,1:9]=a
    da[...]=conv_dgrad(O_R2).reshape(64,16,256)
    def dxm(y,dx):
        gp[y+1,1:9]=dx.astype(BF)
        return dx
    fin=gn_bwd(X["mid"],da,1,"g2","s2",256,8,8,8,act_,dxm)
    conv_wgrad(gp[1:9,1:9].reshape(1024,256),O_R2)
    gemb=fin()
    put_vec("b_time",rowsum(gemb)); put_vec("b_res1",rowsum(gemb))
    put_g(tn(gemb.astype(BF),X["feat"][...]),O_TIME)
    da[...]=conv_dgrad(O_R1).reshape(64,16,256)
    def dxl(y,dx):
        z=gres[pl.ds(y*8,8)]+dx
        gp[y+1,1:9]=z.astype(BF)
        return z
    fin=gn_bwd(X["low"],da,0,"g1","s1",256,8,8,8,act_,dxl)
    conv_wgrad(gp[1:9,1:9].reshape(1024,256),O_R1)
    put_vec("b_down",rowsum(fin()))
    glb=gp[1:9,1:9].reshape(1024,256)
    glt=glb.T
    tp=X["tp"]
    for t in range(9):
        ty,tx=t//3,t%3
        yd[t,0:8,0:8]=nn(glb,wt[:,O_DOWN+128*t:O_DOWN+128*t+128]).reshape(8,8,16,128)
        put_g(nn(glt,tp[ty//2:ty//2+8,ty%2,tx//2:tx//2+8,tx%2].reshape(1024,128)),O_DOWN+128*t)
    big6=big.reshape(8,2,8,2,16,128)
    SRC={0:((1,0),),1:((0,1),(2,0))}
    def dt(i,acc):
        for a in range(2):
            for b in range(2):
                z=big6[i,a,:,b]
                for ty,oy in SRC[a]:
                    for tx,ox in SRC[b]:
                        z=z+yd[ty*3+tx,i+oy,ox:ox+8]
                S["dt"].reshape(8,2,8,2,16,128)[i,a,:,b]=z.astype(BF)
                acc=acc+jnp.sum(z,axis=0)
        return acc
    put_vec("b_in",rowsum(lax.fori_loop(0,8,dt,jnp.zeros((N,128),F32))),128)
    dwi=tn(X["cols"][...].reshape(4096,128),S["dt"][...].reshape(4096,128))
    for k in range(27):
        put_block(k, dwi[9*(k%3)+k//3:9*(k%3)+k//3+1])
    put_g(sg[...].T, MID)

def bwd_scratch():
    V=pltpu.VMEM
    return dict(gp18=V((18,18,16,128),BF),gcols=V((256,16,128),BF),big=V((256,16,128),F32),ep=V((256,16,128),BF),dp=V((9,2,9,2,16,128),BF),
      s_hi=V((9,64,16,128),BF),s_lo=V((9,64,16,128),BF),gp=V((10,10,16,256),BF),ap=V((10,10,16,256),BF),da=V((64,16,256),F32),gres=V((64,16,256),F32),
      gqkv=V((6,1024,128),F32),gmx=V((2,1024,128),F32),yd=V((9,9,9,16,128),F32),nb=V((64,16,256),BF),dt=V((256,16,128),BF),sg=V((128,256),F32))
BIN=["out","tgt","snr","stat","cols","tp","low","mid","res","qkv","obb","attb","up","st","feat","wt","wup","wfb","sm"]
def bwd_call(ins, total, near):
    vm=pl.BlockSpec(memory_space=pltpu.VMEM)
    sc=bwd_scratch()
    if near:
        sc.update(box=pltpu.VMEM((10,8,128),F32), send=pltpu.SemaphoreType.DMA((5,)), recv=pltpu.SemaphoreType.DMA((5,)))
    keys=list(sc)
    def k(*refs):
        a=dict(zip(BIN,refs[:len(BIN)])); a["v"]=a["sm"]; a["ob"]=a["obb"]; a["total"]=float(total)
        s=dict(zip(keys,refs[len(BIN)+2:]))
        sum_ref=refs[len(BIN)+1]
        if near:
            sum_kernel(a["stat"],sum_ref,s["box"],s["send"],s["recv"])
        else:
            sum_ref[...]=a["stat"][...]
        a["stat"]=sum_ref
        bwd_kernel(a,refs[len(BIN):len(BIN)+1],s)
    extra=dict(collective_id=2, has_side_effects=True) if near else {}
    return pl.pallas_call(k,out_shape=(jax.ShapeDtypeStruct((256*64,128),F32),jax.ShapeDtypeStruct((8,128),F32)),
        in_specs=[vm]*len(BIN),out_specs=(vm,vm),scratch_shapes=list(sc.values()), name="student_backward",
        compiler_params=pltpu.CompilerParams(vmem_limit_bytes=62<<20, **extra))(*[ins[k] for k in BIN])

MESH = pl.DeviceIdType.MESH

def place():
    dp = lax.axis_index("dp")
    return dp // 4, dp // 2 % 2, dp % 2, lax.axis_index("mp")

def peer(z, y, x, c):
    return {"dp": z*4 + y*2 + x, "mp": c}

def greet(peers):
    barrier = pltpu.get_barrier_semaphore()
    for p in peers:
        pl.semaphore_signal(barrier, inc=1, device_id=p, device_id_type=MESH)
    pl.semaphore_wait(barrier, len(peers))

def partners():
    z, y, x, c = place()
    return [peer(z,y,x,1-c), peer(z,y,1-x,c), peer(z,1-y,x,c)] + [peer((z+o)%4,y,x,c) for o in (1,2,3)]

def gather_kernel(streams, in_ref, out_ref, send, recv, keep):
    z, y, x, c = place()
    wide = in_ref.shape[1] // streams
    greet(partners())
    own = pltpu.make_async_copy(in_ref, out_ref.at[z,y,x,c], keep)
    own.start()
    def cols(s): return pl.ds(s*wide, wide)
    def copies(s, p):
        if p == 0:
            return [pltpu.make_async_remote_copy(in_ref.at[:,cols(s)], out_ref.at[z,y,x,c,:,cols(s)], send.at[s,o-1], recv.at[s,3-o],
                    device_id=peer((z+o)%4,y,x,c), device_id_type=MESH) for o in (1,2,3)]
        first_x = s % 2 == 0
        if p == 1:
            part = out_ref.at[:,y,x,c,:,cols(s)]
            to = peer(z,y,1-x,c) if first_x else peer(z,1-y,x,c)
        elif p == 2:
            part = out_ref.at[:,y,:,c,:,cols(s)] if first_x else out_ref.at[:,:,x,c,:,cols(s)]
            to = peer(z,1-y,x,c) if first_x else peer(z,y,1-x,c)
        else:
            part = out_ref.at[:,:,:,c,:,cols(s)]
            to = peer(z,y,x,1-c)
        return [pltpu.make_async_remote_copy(part, part, send.at[s,p+2], recv.at[s,p+2], device_id=to, device_id_type=MESH)]
    own.wait()
    live = {}
    for step in range(streams + 4):
        for s in range(streams):
            p = step - s
            if 1 <= p <= 4:
                for d in live[s,p-1]: d.wait_recv()
            if 0 <= p <= 3:
                live[s,p] = copies(s,p)
                for d in live[s,p]: d.start()
    for s in range(streams):
        for p in range(4):
            for d in live[s,p]: d.wait_send()

def gather_call(block, cid, streams=4):
    rows, wide = block.shape
    any_ = pl.BlockSpec(memory_space=pl.ANY)
    out = pl.pallas_call(lambda *r: gather_kernel(streams, *r), out_shape=jax.ShapeDtypeStruct((4,2,2,2,rows,wide), block.dtype),
        in_specs=[any_], out_specs=any_, name="gather_columns",
        scratch_shapes=[pltpu.SemaphoreType.DMA((streams,6)), pltpu.SemaphoreType.DMA((streams,6)), pltpu.SemaphoreType.DMA],
        compiler_params=pltpu.CompilerParams(collective_id=cid, has_side_effects=True))(block)
    return out.reshape(32*rows, wide)

def sum_kernel(in_ref, out_ref, box, send, recv):
    z, y, x, c = place()
    hops = [peer(z,y,x,1-c), peer(z,y,1-x,c), peer(z,1-y,x,c), peer(z+1-2*(z%2),y,x,c), peer((z+2)%4,y,x,c)]
    greet(hops)
    out_ref[...] = in_ref[...]
    for k, to in enumerate(hops):
        box[k] = out_ref[...]
        d = pltpu.make_async_remote_copy(box.at[k], box.at[5+k], send.at[k], recv.at[k], device_id=to, device_id_type=MESH)
        d.start()
        d.wait()
        out_ref[...] += box[5+k]

def scatter_kernel(streams, g_ref, out_ref, r0, r1, r2, r3, send, recv):
    z, y, x, c = place()
    wide = out_ref.shape[1] // streams
    greet(partners())
    def rows(s): return pl.ds(s*wide, wide)
    def copies(s, p):
        first_x = s % 2 == 0
        if p == 0:
            src, dst, to = g_ref.at[:,:,:,:,1-c,rows(s)], r0.at[s], peer(z,y,x,1-c)
        elif p == 1:
            src, dst, to = (r0.at[s,:,:,:,1-x], r1.at[s], peer(z,y,1-x,c)) if first_x else (r0.at[s,:,:,1-y], r1.at[s], peer(z,1-y,x,c))
        elif p == 2:
            src, dst = r1.at[s,:,:,1-y if first_x else 1-x], r2.at[s]
            to = peer(z,1-y,x,c) if first_x else peer(z,y,1-x,c)
        else:
            return [pltpu.make_async_remote_copy(r2.at[s,:,(z+o)%4], r3.at[s,3-o], send.at[s,2+o], recv.at[s,6-o],
                    device_id=peer((z+o)%4,y,x,c), device_id_type=MESH) for o in (1,2,3)]
        return [pltpu.make_async_remote_copy(src, dst, send.at[s,p], recv.at[s,p], device_id=to, device_id_type=MESH)]
    def add(s, p):
        first_x = s % 2 == 0
        def one(m, _):
            if p == 0:
                r0[s,m] += g_ref[m,:,:,:,c,rows(s)]
            elif p == 1:
                r1[s,m] += r0[s,m,:,:,x] if first_x else r0[s,m,:,y]
            elif p == 2:
                r2[s,m] += r1[s,m,:,y] if first_x else r1[s,m,:,x]
            else:
                out_ref[m,rows(s)] = r2[s,m,z] + r3[s,0,m] + r3[s,1,m] + r3[s,2,m]
            return 0
        lax.fori_loop(0, 8, one, 0)
    live = {}
    for step in range(streams + 4):
        for s in range(streams):
            p = step - s
            if 1 <= p <= 4:
                for d in live[s,p-1]: d.wait_recv()
                add(s, p-1)
            if 0 <= p <= 3:
                live[s,p] = copies(s,p)
                for d in live[s,p]: d.start()
    for s in range(streams):
        for p in range(4):
            for d in live[s,p]: d.wait_send()

def scatter_call(g, cid, streams=4):
    T = g.shape[0] // 256
    g = g.reshape(8,4,2,2,2,T,128)
    w = T // streams
    vm = pl.BlockSpec(memory_space=pltpu.VMEM)
    V = pltpu.VMEM
    out = pl.pallas_call(lambda *r: scatter_kernel(streams, *r), out_shape=jax.ShapeDtypeStruct((8,T,128), F32), in_specs=[vm], out_specs=vm,
        scratch_shapes=[V((streams,8,4,2,2,w,128),F32), V((streams,8,4,2,w,128),F32), V((streams,8,4,w,128),F32), V((streams,3,8,w,128),F32),
                        pltpu.SemaphoreType.DMA((streams,6)), pltpu.SemaphoreType.DMA((streams,6))], name="scatter_gradient",
        compiler_params=pltpu.CompilerParams(collective_id=cid, has_side_effects=True, vmem_limit_bytes=40<<20))(g)
    return out.reshape(8, T*128)


def segments():
    matrices = [("w_in", 27, C1), ("w_down", 9 * C1, C2), ("w_res1", 9 * C2, C2), ("w_res2", 9 * C2, C2), ("w_time", C1, C2),
                ("w_qkv", C2, 3 * C2), ("w_proj", C2, C2), ("w_up", 9 * C2, C1), ("w_final", 9 * C1, 3)]
    vectors = [("g1", C2), ("s1", C2), ("g2", C2), ("s2", C2), ("g3", C2), ("s3", C2), ("g4", C1), ("s4", C1), ("b_in", C1),
               ("b_down", C2), ("b_res1", C2), ("b_res2", C2), ("b_time", C2), ("b_query", C2), ("b_value", C2), ("b_proj", C2),
               ("b_up", C1), ("b_final", 3)]
    listing, cursor = [], 0
    for name, height, breadth in matrices:
        listing.append((name, cursor, (height, breadth), "matrix"))
        cursor += height * breadth
    for name, length in vectors:
        listing.append((name, cursor, (length,), "gain" if name[0] != "b" else "bias"))
        cursor += length
    return listing

def rates(position):
    learn = jnp.zeros(position.shape, F32)
    decay = jnp.zeros(position.shape, F32)
    for name, offset, shape, kind in segments():
        inside = (position >= offset) & (position < offset + math.prod(shape))
        if kind == "matrix":
            spread = shape[0] ** (-0.5) * ((SIDE * SIDE / 4.0) ** 0.5 if name == "w_proj" else 1.0)
            learn = jnp.where(inside, 0.5 * spread, learn)
            decay = jnp.where(inside, 0.01, decay)
        elif kind == "gain":
            learn = jnp.where(inside, 0.2, learn)
        else:
            learn = jnp.where(inside, 0.05, learn)
    return learn, decay

def angle_of(step):
    return 0.1 + 1.35 * step.astype(F32) / TGRID

def time_features(step):
    half = C1 // 2
    freqs = jnp.exp(-math.log(1000.0) * jnp.arange(half).astype(F32) / half)
    phases = step.astype(F32)[..., None] * freqs
    return jnp.concatenate([jnp.sin(phases), jnp.cos(phases)], axis=-1)

def to_columns(shard, start, D):
    R, L = 256 // D, shard.shape[0]
    body = R * MID
    if HEAD % D == 0:
        parts = [shard[start:start+body], shard[:start], shard[start+body:]]
    else:
        at = jnp.arange(L - body)
        parts = [lax.dynamic_slice(shard, (start,), (body,)), jnp.where(at < start, shard[:L-body], shard[body:])]
    cols = jnp.concatenate(parts).reshape(-1, R).T
    return jnp.pad(cols, ((0,0),(0,MID+128-cols.shape[1])))

def from_columns(cols, start, D, L):
    R = 256 // D
    body = R * MID
    q = cols[:, O_QKV:O_QKV+768].reshape(R,3,256).transpose(0,2,1).reshape(R,768)
    cols = jnp.concatenate([cols[:, :O_QKV], q, cols[:, O_PROJ:L//R]], axis=1)
    flat = cols.T.reshape(-1)
    if HEAD % D == 0:
        return jnp.concatenate([flat[body:body+start], flat[:body], flat[body+start:]])
    rest = flat[body:]
    at = jnp.arange(L)
    mid = lax.dynamic_update_slice(jnp.zeros((L,), F32), flat[:body], (start,))
    low = jnp.pad(rest, (0, body)); high = jnp.pad(rest, (body, 0))
    return jnp.where(at < start, low, jnp.where(at < start + body, mid, high))

def lanes(images):
    v = jnp.repeat(images.transpose(1,2,0,3).reshape(256,N,3), 9, axis=2)
    return jnp.pad(v, ((0,0),(0,0),(0,101)))

def local(images, noise, timestep, stride, bucket, steps_table, master, first_moment, second_moment, teacher, step_count):
    axes = ("dp", "mp")
    D = lax.axis_size("dp") * lax.axis_size("mp")
    me = lax.axis_index(axes)
    R, L = 256 // D, master.shape[0]
    start = HEAD // D if HEAD % D == 0 else (HEAD - me + D - 1) // D
    near = lax.axis_size("dp") == 16 and lax.axis_size("mp") == 2
    teacher_cols = to_columns(teacher, start, D)
    teacher_all = gather_call(teacher_cols, 1) if near else lax.all_gather(teacher_cols, axes, axis=0, tiled=True)
    student_all = lax.all_gather(to_columns(master.astype(BF), start, D), axes, axis=0, tiled=True)
    wide = lambda v: jnp.broadcast_to(v[..., None], v.shape + (128,))
    angle = angle_of(timestep)
    noisy = lanes(jnp.cos(angle)[:,None,None,None] * images + jnp.sin(angle)[:,None,None,None] * noise)
    picked = jnp.sum(jnp.where(jnp.arange(steps_table.shape[0]) == bucket[0], steps_table, 0))
    turn = jnp.arange(KMAX)[:, None]
    current = timestep[None] - turn * stride[None]
    later = current - stride[None]
    keep = jnp.sin(angle_of(later)) / jnp.sin(angle_of(current))
    take = jnp.cos(angle_of(later)) - keep * jnp.cos(angle_of(current))
    features = jax.nn.silu(time_features(current)).astype(BF)
    final_t = timestep - picked * stride
    below = jnp.sin(angle - angle_of(final_t))
    target = teacher_call(D, picked.reshape(1), noisy, features, wide(take), wide(keep), wide(jnp.sin(angle)/below),
                          wide(-jnp.sin(angle_of(final_t))/below), teacher_all)
    snr = wide(jnp.maximum(jnp.square(jnp.cos(angle)/jnp.sin(angle)), 1.0))
    out, sums, kept = student_call(D, noisy, target, snr, features[0], student_all)
    if not near:
        sums = lax.psum(sums, axes)
    total = images.shape[0] * D
    grads, sums = bwd_call(dict(kept, out=out, tgt=target, snr=snr, stat=sums, feat=features[0]), total, near)
    pick = sums[:5, 0:27:9]
    mean_t, mean_o = pick[0]/(256*total), pick[2]/(256*total)
    var_t, var_o = pick[1]/(256*total) - jnp.square(mean_t), pick[3]/(256*total) - jnp.square(mean_o)
    loss = jnp.sum(pick[4])/(768*total) + jnp.sum(jnp.square(mean_o-mean_t) + jnp.square(var_o-var_t))
    if near:
        part = scatter_call(grads, 3)
    else:
        order = grads.reshape(R, D, MID+128)
        if HEAD % D:
            order = jnp.concatenate([jnp.roll(order[:, :, :MID], HEAD % D, axis=1), order[:, :, MID:]], axis=2)
        part = lax.psum_scatter(order, axes, scatter_dimension=1, tiled=True).reshape(R, MID+128)
    grad = from_columns(part, start, D, L)
    learn, decay = rates(jnp.arange(L, dtype=jnp.int32) * D + me)
    steps_done = step_count[0].astype(F32)
    new_first = 0.5 * first_moment + 0.5 * grad
    new_second = 0.5 * second_moment + 0.5 * jnp.square(grad)
    fix_rate = 1.0 - jnp.power(0.5, steps_done)
    new_master = master - learn * (new_first / fix_rate / (jnp.sqrt(new_second / fix_rate) + 1e-08) + decay * master)
    return loss, new_master, new_first, new_second

def solution(mesh):
    s = P(("dp", "mp"))
    i = P(("dp", "mp"), None, None, None)
    return jax.shard_map(local, mesh=mesh, in_specs=(i, i, s, s, s, P(), s, s, s, s, P()), out_specs=(P(), s, s, s), check_vma=False)
```

```python
import math
import jax
import jax.numpy as jnp
from jax import lax
from jax.experimental import pallas as pl
from jax.experimental.pallas import tpu as pltpu
from jax.sharding import PartitionSpec as P

C1, C2, N = 128, 256, 16
SIDE, TGRID, KMAX = 16, 64, 4
F32, BF = jnp.float32, jnp.bfloat16
O_DOWN, O_R1, O_R2, O_TIME, O_QKV, O_PROJ, O_UP, MID = 0, 1152, 3456, 5760, 5888, 6656, 6912, 8064
HEAD = 3456
BLOCK = {}
_at = 54
for _name, _wide in (("g1",2),("s1",2),("g2",2),("s2",2),("g3",2),("s3",2),("g4",1),("s4",1),("b_in",1),("b_down",2),("b_res1",2),
                     ("b_res2",2),("b_time",2),("b_query",2),("b_value",2),("b_proj",2),("b_up",1),("b_final",1)):
    BLOCK[_name] = (_at, _wide)
    _at += _wide

def iota(shape, d): return lax.broadcasted_iota(jnp.int32, shape, d)

def nt(a, b): return lax.dot_general(a, b, (((1,),(1,)),((),())), preferred_element_type=F32)
def nn(a, b): return lax.dot_general(a, b, (((1,),(0,)),((),())), preferred_element_type=F32)

def one_hot(cond): return jnp.where(cond, 1.0, 0.0).astype(BF)

def split3(v):
    hi = v.astype(BF); r = v - hi.astype(F32)
    mid = r.astype(BF); lo = (r - mid.astype(F32)).astype(BF)
    return jnp.concatenate([hi, mid, lo], axis=0)

def pile(v, k):
    return jnp.sum(jnp.sum(v.reshape((-1, k) + v.shape[1:]), axis=0), axis=0)

def group_sum(v, same):
    r = nn(split3(v), same)
    return r[0:N] + r[N:2*N] + r[2*N:3*N]

def prep(tg_ref, wt_ref, wup_ref, win_ref, wfin_ref, wfb_ref, sm_ref, D):
    R = 256 // D
    row, o = iota((256,256),1), iota((256,256),0)
    dev, m = row // R, row % R
    perm = one_hot(o == (dev + ((-HEAD) % D)) % D + D * m)
    CH = 1152
    for c in range(7):
        wt_ref[:, c*CH:(c+1)*CH] = nn(perm, tg_ref[:, c*CH:(c+1)*CH]).astype(BF)
    kk, ci = iota((256,256),0), iota((256,256),1)
    peo = one_hot(ci == 2*(kk % 128) + kk // 128)
    for t in range(9):
        cs = O_UP + t*128
        both = jnp.concatenate([wt_ref[0:128, cs:cs+128], wt_ref[128:256, cs:cs+128]], axis=1)
        wup_ref[t] = nn(both, peo).astype(BF)
    kq, lq = iota((768,768),0), iota((768,768),1)
    pq = one_hot(kq == 3*(lq % 256) + lq // 256)
    wt_ref[:, O_QKV:O_QKV+768] = nn(wt_ref[:, O_QKV:O_QKV+768], pq).astype(BF)
    perm0 = one_hot(o == dev + D * m)
    sm_ref[...] = nn(perm0, tg_ref[:, MID:MID+128]).T
    halves = jnp.concatenate([sm_ref[0:32, 0:128], sm_ref[0:32, 128:256]], axis=0).astype(BF)
    l, r = iota((128,64),0), iota((128,64),1)
    k = 3*(l % 9) + l // 9
    win_ref[...] = nn(one_hot((l < 27) & (r == 32*(k % 2) + k // 2)), halves).astype(BF)
    t16, r16 = iota((16,64),0), iota((16,64),1)
    pieces = []
    for h in range(3):
        blk = 27 + 3*t16 + h
        pieces.append(nn(one_hot((t16 < 9) & (r16 == 32*(blk % 2) + blk // 2)), halves))
    flat = jnp.concatenate(pieces, axis=1).astype(BF)
    acc = jnp.zeros((128,128), F32)
    for c in range(3):
        wc = nn(flat, one_hot(iota((384,128),0) == 3*iota((384,128),1) + c)).astype(BF)
        acc += nn(one_hot((iota((128,16),1) < 9) & (iota((128,16),0) == 9*c + iota((128,16),1))), wc)
    wfb = acc.astype(BF)
    wfb_ref[...] = wfb
    a, z = iota((128,128),0), iota((128,128),1)
    for r in range(3):
        wfin_ref[:, 128*r:128*r+128] = nn(one_hot((a < 81) & (z == 9*(a % 27 // 9) + 3*r + a // 27)), wfb).astype(BF)

def final_bias(sm_ref):
    b = sm_ref[42:43, 0:128].astype(BF)
    return nn(b, one_hot((iota((128,128),1) < 27) & (iota((128,128),0) == iota((128,128),1) // 9)))

def gn_stats(src, P, per, same):
    k = 4
    B = 16
    s = [pile(src[pl.ds(i,B)], k) for i in range(0,P,B)]
    m = sum(s[1:], s[0]) * (1.0/P)
    q = [pile(jnp.square(src[pl.ds(i,B)] - m), k) for i in range(0,P,B)]
    mean = group_sum(m, same) * (1.0/per)
    spread = sum(q[1:], q[0]) * (1.0/P) + jnp.square(m - mean)
    return mean, lax.rsqrt(group_sum(spread, same) * (1.0/per) + 1e-5)

def vec(v_ref, name, C=C2):
    at, wide = BLOCK[name]
    return jnp.concatenate([v_ref[b//2:b//2+1, 128*(b%2):128*(b%2)+128] for b in range(at, at+wide)], axis=1)

def net(x_ref, feat, wt, wup, win, wfin, v_ref, sc):
    xp, tp, top, low, ap, mid, res, qkv, ob, yp, up, ep = (sc[k] for k in ("xp","tp","top","low","ap","mid","res","qkv","ob","yp","up","ep"))
    lane = iota((1,1,128),2)
    def save(si, m, inv):
        if "st" in sc:
            C = m.shape[1]
            sc["st"][2*si,:,0:C] = m
            sc["st"][2*si+1,:,0:C] = inv
    bfin = final_bias(v_ref)
    def a0(y, _):
        xp[y+1, 1:17] = x_ref[pl.ds(y*16,16)].astype(BF)
        return 0
    lax.fori_loop(0,16,a0,0)
    def a1(y2, _):
        pieces=[]
        for k in range(4):
            y = y2*4+k
            cols = jnp.zeros((16,16,128),BF)
            for t in range(9):
                w = xp[y+t//3, t%3:t%3+16]
                cols = jnp.where((lane%9==t)&(lane<27), w, cols) if t else jnp.where((lane%9==0)&(lane<27), w, jnp.zeros_like(w))
            if "cols" in sc: sc["cols"][pl.ds(y*16,16)] = cols
            pieces.append(cols.reshape(256,128))
        r = nn(jnp.concatenate(pieces,axis=0), win[...]) + vec(v_ref,"b_in",C1)
        top[pl.ds(y2*64,64)] = r.reshape(64,16,128)
        rb = r.astype(BF).reshape(4,8,2,16,128)
        for k in range(4):
            p = y2*4+k+1
            tp[p//2, p%2, 0:8, 1] = rb[k,:,0]
            tp[p//2, p%2, 1:9, 0] = rb[k,:,1]
        return 0
    lax.fori_loop(0,4,a1,0)
    taps=[]
    for t in range(9):
        ty,tx=t//3,t%3
        taps.append(tp[ty//2:ty//2+8, ty%2, tx//2:tx//2+8, tx%2].reshape(1024,128))
    low[...] = (nt(jnp.concatenate(taps,axis=1), wt[:,O_DOWN:O_DOWN+1152]) + vec(v_ref,"b_down")).reshape(64,16,256)
    def norm_act(src, g, s, si):
        m, inv = gn_stats(src, 64, 8, sc["same8"][...])
        save(si, m, inv)
        half = 0.5*inv*vec(v_ref,g)
        shift = 0.5*vec(v_ref,s) - m*half
        for y in range(8):
            h = src[y*8:y*8+8]*half + shift
            ap[y+1,1:9] = (h + h*jnp.tanh(h)).astype(BF)
    def conv3(off):
        return nt(jnp.concatenate([ap[t//3:t//3+8, t%3:t%3+8].reshape(1024,256) for t in range(9)],axis=1), wt[:,off:off+2304])
    norm_act(low,"g1","s1",0)
    emb = nt(feat, wt[:,O_TIME:O_TIME+128]) + vec(v_ref,"b_time")
    mid[...] = (conv3(O_R1) + vec(v_ref,"b_res1")).reshape(64,16,256) + emb
    norm_act(mid,"g2","s2",1)
    res[...] = low[...] + (conv3(O_R2) + vec(v_ref,"b_res2")).reshape(64,16,256)
    m, inv = gn_stats(res, 64, 8, sc["same8"][...])
    save(2, m, inv)
    gain = inv*vec(v_ref,"g3")
    nb = (res[...]*gain + (vec(v_ref,"s3") - m*gain)).astype(BF).reshape(1024,256)
    q = nt(nb, wt[:,O_QKV:O_QKV+256]) + vec(v_ref,"b_query")
    k_ = nt(nb, wt[:,O_QKV+256:O_QKV+512])
    v_ = nt(nb, wt[:,O_QKV+512:O_QKV+768])+vec(v_ref,"b_value")
    for i, z in enumerate((q, k_, v_)):
        z = z.astype(BF).astype(F32)
        qkv[2*i] = z[:,0:128]
        qkv[2*i+1] = z[:,128:256]
    def head(j, n):
        return jnp.concatenate([qkv[2*j,pl.ds(n,64,stride=16),:], qkv[2*j+1,pl.ds(n,64,stride=16),:]], axis=1).astype(BF)
    s = jnp.concatenate([nt(head(0,n), head(1,n)) for n in range(N)], axis=0)*(C2**-0.5)
    e = jnp.exp(s - jnp.max(s,axis=1,keepdims=True))
    p = (e/jnp.sum(e,axis=1,keepdims=True)).astype(BF)
    for n in range(N):
        o = nn(p[64*n:64*n+64], head(2,n)).astype(BF).astype(F32)
        ob[0,pl.ds(n,64,stride=16),:] = o[:,0:128]
        ob[1,pl.ds(n,64,stride=16),:] = o[:,128:256]
    obb = jnp.concatenate([ob[0],ob[1]],axis=1).astype(BF)
    if "obb" in sc: sc["obb"][...] = obb
    att_out = res[...].reshape(1024,256) + (nt(obb, wt[:,O_PROJ:O_PROJ+256]) + vec(v_ref,"b_proj"))
    attb = att_out.astype(BF)
    if "attb" in sc: sc["attb"][...] = attb
    for t in range(0,9,2):
        k = min(2, 9-t)
        r = nt(attb, wup[t:t+k].reshape(128*k,256))
        for i in range(k):
            yp[t+i,1:9,1:9] = r[:,128*i:128*i+128].reshape(8,8,16,128)
    def u(i,_):
        for a in range(2):
            for b in range(2):
                acc=None
                for t in range(9):
                    r,c=t//3-1,t%3-1
                    dr=(a+r)//2; dc=(b+c)//2
                    v=yp[t, i+dr+1, 1+dc:9+dc]
                    acc = v if acc is None else acc+v
                up[i,a,:,b] = acc + vec(v_ref,"b_up",C1) + sc["top6"][i,a,:,b]
        return 0
    lax.fori_loop(0,8,u,0)
    upf = sc["up3"]
    m, inv = gn_stats(upf, 256, 4, sc["same4"][...])
    save(3, m, inv)
    half = 0.5*inv*vec(v_ref,"g4",C1)
    shift = 0.5*vec(v_ref,"s4",C1) - m*half
    def b4(y,_):
        h = upf[pl.ds(y*16,16)]*half + shift
        ep[y+1,1:17] = (h + h*jnp.tanh(h)).astype(BF)
        return 0
    lax.fori_loop(0,16,b4,0,unroll=4)
    def fin(put):
        def f(y4,_):
            cols=jnp.concatenate([ep[pl.ds(y4*8+r,8)].reshape(2304,128) for r in range(3)],axis=1)
            d=nt(cols, wfin[...]).reshape(8,18,16,128)
            put(y4, (d[:,0:16] + pltpu.roll(d[:,1:17].reshape(2048,128),101,1).reshape(8,16,16,128)
                     + pltpu.roll(d[:,2:18].reshape(2048,128),74,1).reshape(8,16,16,128)).reshape(128,16,128) + bfin)
            return 0
        lax.fori_loop(0,2,f,0)
    return fin

def scratch():
    V=pltpu.VMEM
    return dict(wt=V((256,MID),BF), wup=V((9,128,256),BF), win=V((128,128),BF), wfin=V((128,384),BF), wfb=V((128,128),BF), sm=V((128,256),F32), xp=V((18,18,16,128),BF), tp=V((9,2,9,2,16,128),BF),
      top=V((256,16,128),F32), low=V((64,16,256),F32), ap=V((10,10,16,256),BF), mid=V((64,16,256),F32), res=V((64,16,256),F32),
      qkv=V((6,1024,128),F32), ob=V((2,1024,128),F32), yp=V((9,10,10,16,128),F32), up=V((8,2,8,2,16,128),F32), ep=V((18,18,16,128),BF), same8=V((256,256),BF), same4=V((128,128),BF))
KEYS=list(scratch().keys())

def zero_borders(sc):
    for k in ("xp","ep","tp","ap"):
        sc[k][...] = jnp.zeros(sc[k].shape, sc[k].dtype)
    yp = sc["yp"]
    edge = jnp.zeros((9,10,16,128), F32)
    for k in (0,9):
        yp[:,k] = edge
        yp[:,:,k] = edge
    for k, C, per in (("same8",256,8), ("same4",128,4)):
        sc[k][...] = one_hot(iota((C,C),0)//per == iota((C,C),1)//per)

def views(sc):
    sc=dict(sc)
    sc["top6"]=sc["top"].reshape(8,2,8,2,16,128)
    sc["up3"]=sc["up"].reshape(256,16,128)
    return sc

def teacher_call(D, cnt, x, feat, ce, cl, tc, nc, tg):
    def kern(cnt_ref, x_ref, feat_ref, ce_ref, cl_ref, tc_ref, nc_ref, tg_ref, out_ref, *scr):
        sc = views(dict(zip(KEYS, scr)))
        zero_borders(sc)
        prep(tg_ref, *(sc[k] for k in WKEYS), D)
        out_ref[...] = x_ref[...]
        def step(j, _):
            fin = net(out_ref, feat_ref[j], sc["wt"], sc["wup"], sc["win"], sc["wfin"], sc["sm"], sc)
            ce_, cl_ = ce_ref[j], cl_ref[j]
            def put(y4, e):
                out_ref[pl.ds(y4*128,128)] = ce_*e + cl_*out_ref[pl.ds(y4*128,128)]
            fin(put)
            return 0
        lax.fori_loop(0, cnt_ref[0], step, 0)
        def tgt(i, _):
            out_ref[pl.ds(i*16,16)] = tc_ref[...]*out_ref[pl.ds(i*16,16)] + nc_ref[...]*x_ref[pl.ds(i*16,16)]
            return 0
        lax.fori_loop(0, 16, tgt, 0)
    vm = pl.BlockSpec(memory_space=pltpu.VMEM)
    return pl.pallas_call(kern, out_shape=jax.ShapeDtypeStruct((256,16,128),F32),
        in_specs=[pl.BlockSpec(memory_space=pltpu.SMEM)]+[vm]*7, out_specs=vm, scratch_shapes=list(scratch().values()), name="teacher_steps",
        compiler_params=pltpu.CompilerParams(vmem_limit_bytes=60<<20))(cnt, x, feat, ce, cl, tc, nc, tg)

WKEYS = ["wt","wup","win","wfin","wfb","sm"]
RES = ["wt","wup","wfb","sm","tp","low","mid","res","qkv","up"]
def student_call(D, x, tgt, snr, feat, tg):
    vm=pl.BlockSpec(memory_space=pltpu.VMEM)
    sh=scratch()
    extra=dict(st=pltpu.VMEM((8,16,256),F32),cols=pltpu.VMEM((256,16,128),BF),attb=pltpu.VMEM((1024,256),BF),obb=pltpu.VMEM((1024,256),BF))
    outs={k:sh[k] for k in RES}; outs.update(extra)
    scr={k:v for k,v in sh.items() if k not in outs}
    ok,sk=list(outs),list(scr)
    def kern(x_ref,t_ref,snr_ref,feat_ref,tg_ref,out_ref,sum_ref,*refs):
        sc=views(dict(zip(ok+sk,refs)))
        zero_borders(sc)
        prep(tg_ref,*(sc[k] for k in WKEYS),D)
        fin=net(x_ref,feat_ref[...],sc["wt"],sc["wup"],sc["win"],sc["wfin"],sc["sm"],sc)
        def put(y4,e): out_ref[pl.ds(y4*128,128)]=e
        fin(put)
        def s(i,c):
            t,o=t_ref[pl.ds(i*16,16)],out_ref[pl.ds(i*16,16)]
            d=o-t
            return tuple(a+jnp.sum(b,axis=0) for a,b in zip(c,(t,t*t,o,o*o,d*d)))
        z=jnp.zeros((N,128),F32)
        r=lax.fori_loop(0,16,s,(z,)*5)
        r=r[:4]+(r[4]*snr_ref[...],)
        sum_ref[...]=jnp.concatenate([jnp.sum(a,axis=0,keepdims=True) for a in r]+[jnp.zeros((3,128),F32)],axis=0)
    res=pl.pallas_call(kern,
        out_shape=(jax.ShapeDtypeStruct((256,16,128),F32),jax.ShapeDtypeStruct((8,128),F32))+tuple(jax.ShapeDtypeStruct(outs[k].shape,outs[k].dtype) for k in ok),
        in_specs=[vm]*5,out_specs=(vm,)*(2+len(ok)),scratch_shapes=[scr[k] for k in sk], name="student_forward",
        compiler_params=pltpu.CompilerParams(vmem_limit_bytes=62<<20))(x,tgt,snr,feat,tg)
    return res[0],res[1],dict(zip(ok,res[2:]))

MESH = pl.DeviceIdType.MESH

def place():
    dp = lax.axis_index("dp")
    return dp // 4, dp // 2 % 2, dp % 2, lax.axis_index("mp")

def peer(z, y, x, c):
    return {"dp": z*4 + y*2 + x, "mp": c}

def greet(peers):
    barrier = pltpu.get_barrier_semaphore()
    for p in peers:
        pl.semaphore_signal(barrier, inc=1, device_id=p, device_id_type=MESH)
    pl.semaphore_wait(barrier, len(peers))

def partners():
    z, y, x, c = place()
    return [peer(z,y,x,1-c), peer(z,y,1-x,c), peer(z,1-y,x,c)] + [peer((z+o)%4,y,x,c) for o in (1,2,3)]

def gather_kernel(streams, in_ref, out_ref, send, recv, keep):
    z, y, x, c = place()
    wide = in_ref.shape[1] // streams
    greet(partners())
    own = pltpu.make_async_copy(in_ref, out_ref.at[z,y,x,c], keep)
    own.start()
    def cols(s): return pl.ds(s*wide, wide)
    def copies(s, p):
        if p == 0:
            return [pltpu.make_async_remote_copy(in_ref.at[:,cols(s)], out_ref.at[z,y,x,c,:,cols(s)], send.at[s,o-1], recv.at[s,3-o],
                    device_id=peer((z+o)%4,y,x,c), device_id_type=MESH) for o in (1,2,3)]
        first_x = s % 2 == 0
        if p == 1:
            part = out_ref.at[:,y,x,c,:,cols(s)]
            to = peer(z,y,1-x,c) if first_x else peer(z,1-y,x,c)
        elif p == 2:
            part = out_ref.at[:,y,:,c,:,cols(s)] if first_x else out_ref.at[:,:,x,c,:,cols(s)]
            to = peer(z,1-y,x,c) if first_x else peer(z,y,1-x,c)
        else:
            part = out_ref.at[:,:,:,c,:,cols(s)]
            to = peer(z,y,x,1-c)
        return [pltpu.make_async_remote_copy(part, part, send.at[s,p+2], recv.at[s,p+2], device_id=to, device_id_type=MESH)]
    own.wait()
    live = {}
    for step in range(streams + 4):
        for s in range(streams):
            p = step - s
            if 1 <= p <= 4:
                for d in live[s,p-1]: d.wait_recv()
            if 0 <= p <= 3:
                live[s,p] = copies(s,p)
                for d in live[s,p]: d.start()
    for s in range(streams):
        for p in range(4):
            for d in live[s,p]: d.wait_send()

def gather_call(block, cid, streams=4):
    rows, wide = block.shape
    any_ = pl.BlockSpec(memory_space=pl.ANY)
    out = pl.pallas_call(lambda *r: gather_kernel(streams, *r), out_shape=jax.ShapeDtypeStruct((4,2,2,2,rows,wide), block.dtype),
        in_specs=[any_], out_specs=any_, name="gather_columns",
        scratch_shapes=[pltpu.SemaphoreType.DMA((streams,6)), pltpu.SemaphoreType.DMA((streams,6)), pltpu.SemaphoreType.DMA],
        compiler_params=pltpu.CompilerParams(collective_id=cid, has_side_effects=True))(block)
    return out.reshape(32*rows, wide)

def sum_kernel(in_ref, out_ref, box, send, recv):
    z, y, x, c = place()
    hops = [peer(z,y,x,1-c), peer(z,y,1-x,c), peer(z,1-y,x,c), peer(z+1-2*(z%2),y,x,c), peer((z+2)%4,y,x,c)]
    out_ref[...] = in_ref[...]
    for k, to in enumerate(hops):
        box[k] = out_ref[...]
        d = pltpu.make_async_remote_copy(box.at[k], box.at[5+k], send.at[k], recv.at[k], device_id=to, device_id_type=MESH)
        d.start()
        d.wait()
        out_ref[...] += box[5+k]

STREAMS = ((0,8), (8,8), (16,16), (32,8), (40,8), (48,8), (56,8))

def scatter_scratch():
    V = pltpu.VMEM
    sc = {}
    for s, (_, w) in enumerate(STREAMS):
        sc[f"c{s}"] = V((8,4,2,2,w,128),F32)
        sc[f"h{s}"] = V((8,4,2,w,128),F32)
        sc[f"q{s}"] = V((8,4,w,128),F32)
        sc[f"z{s}"] = V((3,8,w,128),F32)
    sc["ssem"] = pltpu.SemaphoreType.DMA((len(STREAMS),6))
    sc["rsem"] = pltpu.SemaphoreType.DMA((len(STREAMS),6))
    return sc

def scatter_steps(g_ref, out_ref, sc):
    z, y, x, c = place()
    send, recv = sc["ssem"], sc["rsem"]
    live = {}
    def bufs(s): return tuple(sc[f"{k}{s}"] for k in "chqz") + (pl.ds(*STREAMS[s]),)
    def copies(s, p):
        r0, r1, r2, r3, rows = bufs(s)
        first_x = s % 2 == 0
        if p == 0:
            src, dst, to = g_ref.at[:,:,:,:,1-c,rows], r0, peer(z,y,x,1-c)
        elif p == 1:
            src, dst, to = (r0.at[:,:,:,1-x], r1, peer(z,y,1-x,c)) if first_x else (r0.at[:,:,1-y], r1, peer(z,1-y,x,c))
        elif p == 2:
            src, dst = r1.at[:,:,1-y if first_x else 1-x], r2
            to = peer(z,1-y,x,c) if first_x else peer(z,y,1-x,c)
        else:
            return [pltpu.make_async_remote_copy(r2.at[:,(z+o)%4], r3.at[3-o], send.at[s,2+o], recv.at[s,6-o],
                    device_id=peer((z+o)%4,y,x,c), device_id_type=MESH) for o in (1,2,3)]
        return [pltpu.make_async_remote_copy(src, dst, send.at[s,p], recv.at[s,p], device_id=to, device_id_type=MESH)]
    def add(s, p):
        r0, r1, r2, r3, rows = bufs(s)
        first_x = s % 2 == 0
        def one(m, _):
            if p == 0:
                r0[m] += g_ref[m,:,:,:,c,rows]
            elif p == 1:
                r1[m] += r0[m,:,:,x] if first_x else r0[m,:,y]
            elif p == 2:
                r2[m] += r1[m,:,y] if first_x else r1[m,:,x]
            else:
                out_ref[m,rows] = r2[m,z] + r3[0,m] + r3[1,m] + r3[2,m]
            return 0
        lax.fori_loop(0, 8, one, 0)
    def advance(s, p):
        if p:
            for d in live[s,p-1]: d.wait_recv()
            add(s, p-1)
        if p < 4:
            live[s,p] = copies(s,p)
            for d in live[s,p]: d.start()
    def finish():
        for ds in live.values():
            for d in ds: d.wait_send()
    return advance, finish

def tn(a, b): return lax.dot_general(a, b, (((0,),(0,)),((),())), preferred_element_type=F32)

def bwd_kernel(x_refs, o_refs, sc):
    X, S = x_refs, sc
    (G,) = o_refs
    sg, sn_total = S["sg"], X["total"]
    v_ref, wt, wup, st = X["v"], X["wt"], X["wup"], X["st"]
    gp18, gcols, big, ep, dp, s_hi, s_lo, gp, ap, da, gres, gqkv, gmx = (S[k] for k in ("gp18","gcols","big","ep","dp","s_hi","s_lo","gp","ap","da","gres","gqkv","gmx"))
    lane = iota((1,1,128),2)
    for k, C, per in (("same8",256,8), ("same4",128,4)):
        S[k][...] = one_hot(iota((C,C),0)//per == iota((C,C),1)//per)
    for k in ("gp18","dp","gp","ap"):
        S[k][...] = jnp.zeros(S[k].shape, S[k].dtype)
    sg[...] = jnp.zeros((128,256),F32)
    def put_block(b, val):
        sg[b//2:b//2+1, 128*(b%2):128*(b%2)+128] = val
    def put_vec(name, val, C=C2):
        at, wide = BLOCK[name]
        for k in range(wide):
            put_block(at+k, val[:, 128*k:128*k+128])
    def rowsum(a): return jnp.sum(a, axis=0, keepdims=True)
    step = S["step"]
    def put_g(val, col, row0=0):
        rows, width = val.shape
        col = 128*next(GROUP[o] + (col-o)//128 for o in sorted(GROUP, reverse=True) if col >= o)
        for c in range(width//128):
            for r in range(0, rows, 8):
                G[pl.ds((row0+r)*64+col//128+c, 8, stride=64),:] = val[r:r+8, c*128:c*128+128]
    pixels = 256.0*sn_total
    so = X["stat"][...]
    mt, mo = so[0:1]/pixels, so[2:3]/pixels
    vt_, vo = so[1:2]/pixels-mt*mt, so[3:4]/pixels-mo*mo
    cb = 4.0*(vo-vt_)/pixels
    ca = 2.0*(mo-mt)/pixels-cb*mo
    sn = X["snr"][...]*(2.0/(768.0*sn_total))
    acc=jnp.zeros((N,128),F32)
    def g0(y,acc):
        o=X["out"][pl.ds(y*16,16)]
        go = sn*(o-X["tgt"][pl.ds(y*16,16)]) + ca + cb*o
        gp18[y+1,1:17]=go.astype(BF)
        return acc+jnp.sum(go,axis=0)
    acc=lax.fori_loop(0,16,g0,acc)
    acc=rowsum(acc)
    lane2=iota((1,128),1)
    put_block(84, sum(jnp.where(lane2==c, jnp.sum(jnp.where(lane2==9*c,acc,0.0),axis=1,keepdims=True),0.0) for c in range(3)))
    def g1(y,_):
        for t in range(9):
            w = gp18[y+2-t//3, 2-t%3:18-t%3]
            cols = jnp.where((lane%9==t)&(lane<27), w, cols) if t else jnp.where((lane%9==0)&(lane<27), w, jnp.zeros_like(w))
        gcols[pl.ds(y*16,16)] = cols
        return 0
    lax.fori_loop(0,16,g1,0)
    big[...] = nn(gcols[...].reshape(4096,128), X["wfb"][...]).reshape(256,16,128)
    def gn_bwd(src, dref, si, gname, sname, C, per, same, rows, k, act_put, dx_put, silu=True):
        m, inv = st[2*si,:,0:C], st[2*si+1,:,0:C]
        g, s = vec(v_ref,gname,C), vec(v_ref,sname,C)
        w = 512//C
        zero = jnp.zeros((w,N,C),F32)
        def pick(v): return jnp.sum(v.reshape((-1,w)+v.shape[1:]),axis=0)
        def p1(y,c):
            A,B=c
            xh=(src[pl.ds(y*k,k)]-m)*inv
            d=dref[pl.ds(y*k,k)]
            if silu:
                h=xh*(0.5*g)+0.5*s
                th=jnp.tanh(h); sg=0.5+0.5*th; act=h+h*th
                act_put(y,act.astype(BF))
                d=d*(sg+act*(1.0-sg))
                dref[pl.ds(y*k,k)]=d
            else:
                act_put(y,(xh*g+s).astype(BF))
            return A+pick(d), B+pick(d*xh)
        A,B=lax.fori_loop(0,rows,p1,(zero,zero),unroll=4)
        A,B=jnp.sum(A,axis=0),jnp.sum(B,axis=0)
        put_vec(gname,rowsum(B),C); put_vec(sname,rowsum(A),C)
        cnt=1.0/(per*rows*k)
        ga=group_sum(g*A,same)*cnt; gb=group_sum(g*B,same)*cnt
        ig=inv*g; ib=inv*inv*gb; ic=m*ib-inv*ga
        def p2(y,acc):
            dx=ig*dref[pl.ds(y*k,k)]-ib*src[pl.ds(y*k,k)]+ic
            return acc+pick(dx_put(y,dx))
        return lambda: jnp.sum(lax.fori_loop(0,rows,p2,zero,unroll=4),axis=0)
    def act4(y,a): ep[pl.ds(y*16,16)]=a
    def dx4(y,dx):
        big[pl.ds(y*16,16)]=dx
        b=dx.astype(BF).reshape(8,2,16,128)
        p=y+1
        dp[p//2,p%2,0:8,1]=b[:,0]
        dp[p//2,p%2,1:9,0]=b[:,1]
        return dx
    fin=gn_bwd(X["up"].reshape(256,16,128),big,3,"g4","s4",128,4,S["same4"][...],16,16,act4,dx4)
    dwf = tn(gcols[...].reshape(4096,128), ep[...].reshape(4096,128))
    flat = jnp.zeros((9,384),F32)
    for c in range(3):
        p3 = one_hot(iota((128,384),1) == 3*iota((128,384),0) + c)
        piece = dwf[9*c:9*c+9]
        hi = piece.astype(BF); rest = piece-hi.astype(F32)
        mi = rest.astype(BF); lo = (rest-mi.astype(F32)).astype(BF)
        flat += nn(hi,p3)+nn(mi,p3)+nn(lo,p3)
    for t in range(9):
        for h in range(3):
            put_block(27+3*t+h, flat[t:t+1,128*h:128*h+128])
    put_vec("b_up",rowsum(fin()),128)
    PAIR={-1:((1,0),(1,1)),0:((0,1),(1,0)),1:((0,0),(0,1))}
    def su(i,_):
        for r in (-1,0,1):
            (ra,pa),(rb,pb)=PAIR[r]
            V={}
            for cp in range(2):
                V[cp]=dp[i+ra,pa,:,cp].astype(F32)+dp[i+rb,pb,:,cp].astype(F32)
            for c in (-1,0,1):
                (ca_,qa),(cb_,qb)=PAIR[c]
                s=V[qa][ca_:ca_+8]+V[qb][cb_:cb_+8]
                t=(r+1)*3+c+1
                hi=s.astype(BF)
                s_hi[t,pl.ds(i*8,8)]=hi
                s_lo[t,pl.ds(i*8,8)]=(s-hi.astype(F32)).astype(BF)
        return 0
    lax.fori_loop(0,8,su,0)
    cat=lambda ref: jnp.concatenate([ref[t].reshape(1024,128) for t in range(9)],axis=1)
    wu=wup[...].reshape(1152,256)
    gatt=nn(cat(s_hi),wu)+nn(cat(s_lo),wu)
    gres[...]=gatt.reshape(64,16,256)
    put_vec("b_proj",rowsum(gatt))
    gab=gatt.astype(BF)
    attb=X["attb"][...]
    kk, ci = iota((256,256),1), iota((256,256),0)
    peo=one_hot(ci == 2*(kk % 128) + kk // 128)
    aeo=nn(attb,peo).astype(BF)
    for t in range(9):
        r=tn(s_hi[t].reshape(1024,128),aeo)+tn(s_lo[t].reshape(1024,128),aeo)
        put_g(r[:,0:128],O_UP+t*128,0); put_g(r[:,128:256],O_UP+t*128,128)
    step((0,0))
    obb=X["ob"][...]
    put_g(tn(gab,obb),O_PROJ)
    gm=nn(gab,wt[:,O_PROJ:O_PROJ+256]).astype(BF).astype(F32)
    gmx[0]=gm[:,0:128]; gmx[1]=gm[:,128:256]
    qkv=X["qkv"]
    sc_=C2**-0.5
    def pair(ref,j,n): return jnp.concatenate([ref[2*j,pl.ds(n,64,stride=16),:],ref[2*j+1,pl.ds(n,64,stride=16),:]],axis=1).astype(BF)
    s=jnp.concatenate([nt(pair(qkv,0,n),pair(qkv,1,n)) for n in range(N)],axis=0)*sc_
    e=jnp.exp(s-jnp.max(s,axis=1,keepdims=True))
    p=e/jnp.sum(e,axis=1,keepdims=True)
    ga=jnp.concatenate([nt(pair(gmx,0,n),pair(qkv,2,n)) for n in range(N)],axis=0)
    gs=(p*(ga-jnp.sum(ga*p,axis=1,keepdims=True))).astype(BF)
    pb=p.astype(BF)
    for n in range(N):
        gsn,pn=gs[64*n:64*n+64],pb[64*n:64*n+64]
        for j,o in enumerate((nn(gsn,pair(qkv,1,n))*sc_, tn(gsn,pair(qkv,0,n))*sc_, tn(pn,pair(gmx,0,n)))):
            o=o.astype(BF).astype(F32)
            gqkv[2*j,pl.ds(n,64,stride=16),:]=o[:,0:128]
            gqkv[2*j+1,pl.ds(n,64,stride=16),:]=o[:,128:256]
    step((0,1))
    gq=[jnp.concatenate([gqkv[2*j],gqkv[2*j+1]],axis=1) for j in range(3)]
    put_vec("b_query",rowsum(gq[0])); put_vec("b_value",rowsum(gq[2]))
    gqb=[g.astype(BF) for g in gq]
    da[...]=nn(jnp.concatenate(gqb,axis=1),jnp.concatenate([wt[:,O_QKV+256*j:O_QKV+256*j+256] for j in range(3)],axis=0)).reshape(64,16,256)
    nbs=S["nb"]
    def act3(y,a): nbs[pl.ds(y*8,8)]=a
    def dx3(y,dx):
        z=gres[pl.ds(y*8,8)]+dx
        gres[pl.ds(y*8,8)]=z
        gp[y+1,1:9]=z.astype(BF)
        return z
    fin=gn_bwd(X["res"],da,2,"g3","s3",256,8,S["same8"][...],8,8,act3,dx3,silu=False)
    nb=nbs[...].reshape(1024,256)
    for j in range(3): put_g(tn(gqb[j],nb),O_QKV+256*j)
    step((1,0))
    put_vec("b_res2",rowsum(fin()))
    step((0,2),(1,1))
    def conv_dgrad(off):
        return nn(jnp.concatenate([gp[2-t//3:10-t//3,2-t%3:10-t%3].reshape(1024,256) for t in range(9)],axis=1),
                  jnp.concatenate([wt[:,off+256*t:off+256*t+256] for t in range(9)],axis=0))
    def conv_wgrad(g,off,steps):
        gt=g.T
        for t in range(9):
            put_g(nn(gt,ap[t//3:t//3+8,t%3:t%3+8].reshape(1024,256)),off+256*t)
            step(*steps.get(t,()))
    def act_(y,a): ap[y+1,1:9]=a
    da[...]=conv_dgrad(O_R2).reshape(64,16,256)
    step((0,3))
    def dxm(y,dx):
        gp[y+1,1:9]=dx.astype(BF)
        return dx
    fin=gn_bwd(X["mid"],da,1,"g2","s2",256,8,S["same8"][...],8,8,act_,dxm)
    conv_wgrad(gp[1:9,1:9].reshape(1024,256),O_R2,{7:((2,0),)})
    gemb=fin()
    step((1,2),(2,1))
    put_vec("b_time",rowsum(gemb)); put_vec("b_res1",rowsum(gemb))
    put_g(tn(gemb.astype(BF),X["feat"][...]),O_TIME)
    da[...]=conv_dgrad(O_R1).reshape(64,16,256)
    step((1,3))
    def dxl(y,dx):
        z=gres[pl.ds(y*8,8)]+dx
        gp[y+1,1:9]=z.astype(BF)
        return z
    fin=gn_bwd(X["low"],da,0,"g1","s1",256,8,S["same8"][...],8,8,act_,dxl)
    conv_wgrad(gp[1:9,1:9].reshape(1024,256),O_R1,{1:((3,0),),3:((2,2),),5:((4,0),(3,1))})
    put_vec("b_down",rowsum(fin()))
    step((4,1),(3,2))
    glb=gp[1:9,1:9].reshape(1024,256)
    glt=glb.T
    tp=X["tp"]
    for t in range(9):
        ty,tx=t//3,t%3
        put_g(nn(glt,tp[ty//2:ty//2+8,ty%2,tx//2:tx//2+8,tx%2].reshape(1024,128)),O_DOWN+128*t)
        if t==1: step((5,0),(2,3))
    step((5,1),(4,2),(3,3))
    big6=big.reshape(8,2,8,2,16,128)
    dt6=S["dt"].reshape(8,2,8,2,16,128)
    SRC={0:((1,0),),1:((0,1),(2,0))}
    total=jnp.zeros((N,128),F32)
    for a in range(2):
        for b in range(2):
            taps=[(3*ty+tx,1+oy,1+ox) for ty,oy in SRC[a] for tx,ox in SRC[b]]
            z=nn(jnp.concatenate([gp[oy:oy+8,ox:ox+8].reshape(1024,256) for _,oy,ox in taps],axis=1),
                 jnp.concatenate([wt[:,O_DOWN+128*t:O_DOWN+128*t+128] for t,_,_ in taps],axis=0)).reshape(8,8,16,128)
            z=z+big6[:,a,:,b]
            dt6[:,a,:,b]=z.astype(BF)
            total=total+jnp.sum(jnp.sum(z,axis=0),axis=0)
    put_vec("b_in",rowsum(total),128)
    dwi=tn(X["cols"][...].reshape(4096,128),S["dt"][...].reshape(4096,128))
    for k in range(27):
        put_block(k, dwi[9*(k%3)+k//3:9*(k%3)+k//3+1])
    put_g(sg[...].T, MID)

def bwd_scratch():
    V=pltpu.VMEM
    return dict(gp18=V((18,18,16,128),BF),gcols=V((256,16,128),BF),big=V((256,16,128),F32),ep=V((256,16,128),BF),dp=V((9,2,9,2,16,128),BF),
      s_hi=V((9,64,16,128),BF),s_lo=V((9,64,16,128),BF),gp=V((10,10,16,256),BF),ap=V((10,10,16,256),BF),da=V((64,16,256),F32),gres=V((64,16,256),F32),
      gqkv=V((6,1024,128),F32),gmx=V((2,1024,128),F32),nb=V((64,16,256),BF),dt=V((256,16,128),BF),sg=V((128,256),F32),same8=V((256,256),BF),same4=V((128,128),BF))
BIN=["out","tgt","snr","stat","cols","tp","low","mid","res","qkv","obb","attb","up","st","feat","wt","wup","wfb","sm"]
GROUP = {O_UP:0, O_PROJ:9, O_QKV:11, O_R2:17, O_TIME:35, O_R1:36, O_DOWN:54, MID:63}
def bwd_call(ins, total, near):
    vm=pl.BlockSpec(memory_space=pltpu.VMEM)
    sc=bwd_scratch()
    if near:
        sc.update(box=pltpu.VMEM((10,8,128),F32), send=pltpu.SemaphoreType.DMA((5,)), recv=pltpu.SemaphoreType.DMA((5,)), g=pltpu.VMEM((256*64,128),F32))
        sc.update(scatter_scratch())
    keys=list(sc)
    def k(*refs):
        a=dict(zip(BIN,refs[:len(BIN)])); a["v"]=a["sm"]; a["ob"]=a["obb"]; a["total"]=float(total)
        s=dict(zip(keys,refs[len(BIN)+2:]))
        grad_ref,sum_ref=refs[len(BIN):len(BIN)+2]
        if not near:
            sum_ref[...]=a["stat"][...]
            s["step"]=lambda *_: None
            a["stat"]=sum_ref
            bwd_kernel(a,(grad_ref,),s)
            return
        greet(partners())
        sum_kernel(a["stat"],sum_ref,s["box"],s["send"],s["recv"])
        a["stat"]=sum_ref
        advance,finish=scatter_steps(s["g"].reshape(8,4,2,2,2,64,128),grad_ref,s)
        def step(*moves):
            for m in moves: advance(*m)
        s["step"]=step
        bwd_kernel(a,(s["g"],),s)
        step((6,0),(5,2),(4,3),(6,1),(5,3),(2,4),(0,4),(1,4),(3,4),(6,2),(4,4),(6,3),(5,4),(6,4))
        finish()
    extra=dict(collective_id=2, has_side_effects=True) if near else {}
    shape=(8,64,128) if near else (256*64,128)
    return pl.pallas_call(k,out_shape=(jax.ShapeDtypeStruct(shape,F32),jax.ShapeDtypeStruct((8,128),F32)),
        in_specs=[vm]*len(BIN),out_specs=(vm,vm),scratch_shapes=list(sc.values()), name="student_backward",
        compiler_params=pltpu.CompilerParams(vmem_limit_bytes=63<<20, **extra))(*[ins[k] for k in BIN])

def segments():
    matrices = [("w_in", 27, C1), ("w_down", 9 * C1, C2), ("w_res1", 9 * C2, C2), ("w_res2", 9 * C2, C2), ("w_time", C1, C2),
                ("w_qkv", C2, 3 * C2), ("w_proj", C2, C2), ("w_up", 9 * C2, C1), ("w_final", 9 * C1, 3)]
    vectors = [("g1", C2), ("s1", C2), ("g2", C2), ("s2", C2), ("g3", C2), ("s3", C2), ("g4", C1), ("s4", C1), ("b_in", C1),
               ("b_down", C2), ("b_res1", C2), ("b_res2", C2), ("b_time", C2), ("b_query", C2), ("b_value", C2), ("b_proj", C2),
               ("b_up", C1), ("b_final", 3)]
    listing, cursor = [], 0
    for name, height, breadth in matrices:
        listing.append((name, cursor, (height, breadth), "matrix"))
        cursor += height * breadth
    for name, length in vectors:
        listing.append((name, cursor, (length,), "gain" if name[0] != "b" else "bias"))
        cursor += length
    return listing

def rates(position):
    learn = jnp.zeros(position.shape, F32)
    decay = jnp.zeros(position.shape, F32)
    for name, offset, shape, kind in segments():
        inside = (position >= offset) & (position < offset + math.prod(shape))
        if kind == "matrix":
            spread = shape[0] ** (-0.5) * ((SIDE * SIDE / 4.0) ** 0.5 if name == "w_proj" else 1.0)
            learn = jnp.where(inside, 0.5 * spread, learn)
            decay = jnp.where(inside, 0.01, decay)
        elif kind == "gain":
            learn = jnp.where(inside, 0.2, learn)
        else:
            learn = jnp.where(inside, 0.05, learn)
    return learn, decay

def angle_of(step):
    return 0.1 + 1.35 * step.astype(F32) / TGRID

def time_features(step):
    half = C1 // 2
    freqs = jnp.exp(-math.log(1000.0) * jnp.arange(half).astype(F32) / half)
    phases = step.astype(F32)[..., None] * freqs
    return jnp.concatenate([jnp.sin(phases), jnp.cos(phases)], axis=-1)

def to_columns(shard, start, D):
    R, L = 256 // D, shard.shape[0]
    body = R * MID
    if HEAD % D == 0:
        parts = [shard[start:start+body], shard[:start], shard[start+body:]]
    else:
        at = jnp.arange(L - body)
        parts = [lax.dynamic_slice(shard, (start,), (body,)), jnp.where(at < start, shard[:L-body], shard[body:])]
    cols = jnp.concatenate(parts).reshape(-1, R).T
    return jnp.pad(cols, ((0,0),(0,MID+128-cols.shape[1])))

def from_columns(cols, start, D, L):
    R = 256 // D
    body = R * MID
    def piece(at, width): return cols[:, 128*GROUP[at]:128*GROUP[at]+width]
    q = piece(O_QKV,768).reshape(R,3,256).transpose(0,2,1).reshape(R,768)
    cols = jnp.concatenate([piece(O_DOWN,1152), piece(O_R1,2304), piece(O_R2,2304), piece(O_TIME,128), q, piece(O_PROJ,256), piece(O_UP,1152),
                            piece(MID,L//R-MID)], axis=1)
    flat = cols.T.reshape(-1)
    if HEAD % D == 0:
        return jnp.concatenate([flat[body:body+start], flat[:body], flat[body+start:]])
    rest = flat[body:]
    at = jnp.arange(L)
    mid = lax.dynamic_update_slice(jnp.zeros((L,), F32), flat[:body], (start,))
    low = jnp.pad(rest, (0, body)); high = jnp.pad(rest, (body, 0))
    return jnp.where(at < start, low, jnp.where(at < start + body, mid, high))

def lanes(images):
    v = jnp.repeat(images.transpose(1,2,0,3).reshape(256,N,3), 9, axis=2)
    return jnp.pad(v, ((0,0),(0,0),(0,101)))

def local(images, noise, timestep, stride, bucket, steps_table, master, first_moment, second_moment, teacher, step_count):
    axes = ("dp", "mp")
    D = lax.axis_size("dp") * lax.axis_size("mp")
    me = lax.axis_index(axes)
    R, L = 256 // D, master.shape[0]
    start = HEAD // D if HEAD % D == 0 else (HEAD - me + D - 1) // D
    near = lax.axis_size("dp") == 16 and lax.axis_size("mp") == 2
    teacher_cols = to_columns(teacher, start, D)
    teacher_all = gather_call(teacher_cols, 1) if near else lax.all_gather(teacher_cols, axes, axis=0, tiled=True)
    student_all = lax.all_gather(to_columns(master.astype(BF), start, D), axes, axis=0, tiled=True)
    wide = lambda v: jnp.where(jnp.arange(128) < 27, v[..., None], 0.0)
    angle = angle_of(timestep)
    noisy = lanes(jnp.cos(angle)[:,None,None,None] * images + jnp.sin(angle)[:,None,None,None] * noise)
    picked = jnp.sum(jnp.where(jnp.arange(steps_table.shape[0]) == bucket[0], steps_table, 0))
    turn = jnp.arange(KMAX)[:, None]
    current = timestep[None] - turn * stride[None]
    later = current - stride[None]
    keep = jnp.sin(angle_of(later)) / jnp.sin(angle_of(current))
    take = jnp.cos(angle_of(later)) - keep * jnp.cos(angle_of(current))
    features = jax.nn.silu(time_features(current)).astype(BF)
    final_t = timestep - picked * stride
    below = jnp.sin(angle - angle_of(final_t))
    target = teacher_call(D, picked.reshape(1), noisy, features, wide(take), wide(keep), wide(jnp.sin(angle)/below),
                          wide(-jnp.sin(angle_of(final_t))/below), teacher_all)
    snr = wide(jnp.maximum(jnp.square(jnp.cos(angle)/jnp.sin(angle)), 1.0))
    out, sums, kept = student_call(D, noisy, target, snr, features[0], student_all)
    if not near:
        sums = lax.psum(sums, axes)
    total = images.shape[0] * D
    grads, sums = bwd_call(dict(kept, out=out, tgt=target, snr=snr, stat=sums, feat=features[0]), total, near)
    pick = sums[:5, 0:27:9]
    mean_t, mean_o = pick[0]/(256*total), pick[2]/(256*total)
    var_t, var_o = pick[1]/(256*total) - jnp.square(mean_t), pick[3]/(256*total) - jnp.square(mean_o)
    loss = jnp.sum(pick[4])/(768*total) + jnp.sum(jnp.square(mean_o-mean_t) + jnp.square(var_o-var_t))
    if near:
        part = grads.reshape(R, MID+128)
    else:
        order = grads.reshape(R, D, MID+128)
        if HEAD % D:
            order = jnp.concatenate([jnp.roll(order[:, :, :MID], HEAD % D, axis=1), order[:, :, MID:]], axis=2)
        part = lax.psum_scatter(order, axes, scatter_dimension=1, tiled=True).reshape(R, MID+128)
    grad = from_columns(part, start, D, L)
    learn, decay = rates(jnp.arange(L, dtype=jnp.int32) * D + me)
    steps_done = step_count[0].astype(F32)
    new_first = 0.5 * first_moment + 0.5 * grad
    new_second = 0.5 * second_moment + 0.5 * jnp.square(grad)
    fix_rate = 1.0 - jnp.power(0.5, steps_done)
    new_master = master - learn * (new_first / fix_rate / (jnp.sqrt(new_second / fix_rate) + 1e-08) + decay * master)
    return loss, new_master, new_first, new_second

def solution(mesh):
    s = P(("dp", "mp"))
    i = P(("dp", "mp"), None, None, None)
    return jax.shard_map(local, mesh=mesh, in_specs=(i, i, s, s, s, P(), s, s, s, s, P()), out_specs=(P(), s, s, s), check_vma=False)
```

```python
import math
import jax
import jax.numpy as jnp
from jax import lax
from jax.experimental import pallas as pl
from jax.experimental.pallas import tpu as pltpu
from jax.sharding import PartitionSpec as P

C1, C2, N = 128, 256, 16
SIDE, TGRID, KMAX = 16, 64, 4
F32, BF = jnp.float32, jnp.bfloat16
O_DOWN, O_R1, O_R2, O_TIME, O_QKV, O_PROJ, O_UP, MID = 0, 1152, 3456, 5760, 5888, 6656, 6912, 8064
HEAD = 3456
BLOCK = {}
_at = 54
for _name, _wide in (("g1",2),("s1",2),("g2",2),("s2",2),("g3",2),("s3",2),("g4",1),("s4",1),("b_in",1),("b_down",2),("b_res1",2),
                     ("b_res2",2),("b_time",2),("b_query",2),("b_value",2),("b_proj",2),("b_up",1),("b_final",1)):
    BLOCK[_name] = (_at, _wide)
    _at += _wide

def iota(shape, d): return lax.broadcasted_iota(jnp.int32, shape, d)

def nt(a, b): return lax.dot_general(a, b, (((1,),(1,)),((),())), preferred_element_type=F32)
def nn(a, b): return lax.dot_general(a, b, (((1,),(0,)),((),())), preferred_element_type=F32)

def one_hot(cond): return jnp.where(cond, 1.0, 0.0).astype(BF)

def split3(v):
    hi = v.astype(BF); r = v - hi.astype(F32)
    mid = r.astype(BF); lo = (r - mid.astype(F32)).astype(BF)
    return jnp.concatenate([hi, mid, lo], axis=0)

def pile(v, k):
    return jnp.sum(jnp.sum(v.reshape((-1, k) + v.shape[1:]), axis=0), axis=0)

def group_sum(v, same):
    r = nn(split3(v), same)
    return r[0:N] + r[N:2*N] + r[2*N:3*N]

def prep(tg_ref, wt_ref, wup_ref, win_ref, wfin_ref, wfb_ref, sm_ref, D):
    R = 256 // D
    row, o = iota((256,256),1), iota((256,256),0)
    dev, m = row // R, row % R
    perm = one_hot(o == (dev + ((-HEAD) % D)) % D + D * m)
    CH = 1152
    for c in range(7):
        wt_ref[:, c*CH:(c+1)*CH] = nn(perm, tg_ref[:, c*CH:(c+1)*CH]).astype(BF)
    kk, ci = iota((256,256),0), iota((256,256),1)
    peo = one_hot(ci == 2*(kk % 128) + kk // 128)
    for t in range(9):
        cs = O_UP + t*128
        both = jnp.concatenate([wt_ref[0:128, cs:cs+128], wt_ref[128:256, cs:cs+128]], axis=1)
        wup_ref[t] = nn(both, peo).astype(BF)
    kq, lq = iota((768,768),0), iota((768,768),1)
    pq = one_hot(kq == 3*(lq % 256) + lq // 256)
    wt_ref[:, O_QKV:O_QKV+768] = nn(wt_ref[:, O_QKV:O_QKV+768], pq).astype(BF)
    perm0 = one_hot(o == dev + D * m)
    sm_ref[...] = nn(perm0, tg_ref[:, MID:MID+128]).T
    halves = jnp.concatenate([sm_ref[0:32, 0:128], sm_ref[0:32, 128:256]], axis=0).astype(BF)
    l, r = iota((128,64),0), iota((128,64),1)
    k = 3*(l % 9) + l // 9
    win_ref[...] = nn(one_hot((l < 27) & (r == 32*(k % 2) + k // 2)), halves).astype(BF)
    t16, r16 = iota((16,64),0), iota((16,64),1)
    pieces = []
    for h in range(3):
        blk = 27 + 3*t16 + h
        pieces.append(nn(one_hot((t16 < 9) & (r16 == 32*(blk % 2) + blk // 2)), halves))
    flat = jnp.concatenate(pieces, axis=1).astype(BF)
    acc = jnp.zeros((128,128), F32)
    for c in range(3):
        wc = nn(flat, one_hot(iota((384,128),0) == 3*iota((384,128),1) + c)).astype(BF)
        acc += nn(one_hot((iota((128,16),1) < 9) & (iota((128,16),0) == 9*c + iota((128,16),1))), wc)
    wfb = acc.astype(BF)
    wfb_ref[...] = wfb
    a, z = iota((128,128),0), iota((128,128),1)
    for r in range(3):
        wfin_ref[:, 128*r:128*r+128] = nn(one_hot((a < 81) & (z == 9*(a % 27 // 9) + 3*r + a // 27)), wfb).astype(BF)

def final_bias(sm_ref):
    b = sm_ref[42:43, 0:128].astype(BF)
    return nn(b, one_hot((iota((128,128),1) < 27) & (iota((128,128),0) == iota((128,128),1) // 9)))

def gn_stats(src, P, per, same):
    k = 4
    B = 16
    s = [pile(src[pl.ds(i,B)], k) for i in range(0,P,B)]
    m = sum(s[1:], s[0]) * (1.0/P)
    q = [pile(jnp.square(src[pl.ds(i,B)] - m), k) for i in range(0,P,B)]
    mean = group_sum(m, same) * (1.0/per)
    spread = sum(q[1:], q[0]) * (1.0/P) + jnp.square(m - mean)
    return mean, lax.rsqrt(group_sum(spread, same) * (1.0/per) + 1e-5)

def vec(v_ref, name, C=C2):
    at, wide = BLOCK[name]
    return jnp.concatenate([v_ref[b//2:b//2+1, 128*(b%2):128*(b%2)+128] for b in range(at, at+wide)], axis=1)

def net(x_ref, feat, wt, wup, win, wfin, v_ref, sc):
    xp, tp, top, low, ap, mid, res, qkv, ob, yp, up, ep = (sc[k] for k in ("xp","tp","top","low","ap","mid","res","qkv","ob","yp","up","ep"))
    lane = iota((1,1,128),2)
    def save(si, m, inv):
        if "st" in sc:
            C = m.shape[1]
            sc["st"][2*si,:,0:C] = m
            sc["st"][2*si+1,:,0:C] = inv
    bfin = final_bias(v_ref)
    def a0(y, _):
        xp[y+1, 1:17] = x_ref[pl.ds(y*16,16)].astype(BF)
        return 0
    lax.fori_loop(0,16,a0,0)
    def a1(y2, _):
        pieces=[]
        for k in range(4):
            y = y2*4+k
            cols = jnp.zeros((16,16,128),BF)
            for t in range(9):
                w = xp[y+t//3, t%3:t%3+16]
                cols = jnp.where((lane%9==t)&(lane<27), w, cols) if t else jnp.where((lane%9==0)&(lane<27), w, jnp.zeros_like(w))
            if "cols" in sc: sc["cols"][pl.ds(y*16,16)] = cols
            pieces.append(cols.reshape(256,128))
        r = nn(jnp.concatenate(pieces,axis=0), win[...]) + vec(v_ref,"b_in",C1)
        top[pl.ds(y2*64,64)] = r.reshape(64,16,128)
        rb = r.astype(BF).reshape(4,8,2,16,128)
        for k in range(4):
            p = y2*4+k+1
            tp[p//2, p%2, 0:8, 1] = rb[k,:,0]
            tp[p//2, p%2, 1:9, 0] = rb[k,:,1]
        return 0
    lax.fori_loop(0,4,a1,0)
    taps=[]
    for t in range(9):
        ty,tx=t//3,t%3
        taps.append(tp[ty//2:ty//2+8, ty%2, tx//2:tx//2+8, tx%2].reshape(1024,128))
    low[...] = (nt(jnp.concatenate(taps,axis=1), wt[:,O_DOWN:O_DOWN+1152]) + vec(v_ref,"b_down")).reshape(64,16,256)
    def norm_act(src, g, s, si):
        m, inv = gn_stats(src, 64, 8, sc["same8"][...])
        save(si, m, inv)
        half = 0.5*inv*vec(v_ref,g)
        shift = 0.5*vec(v_ref,s) - m*half
        for y in range(8):
            h = src[y*8:y*8+8]*half + shift
            ap[y+1,1:9] = (h + h*jnp.tanh(h)).astype(BF)
    def conv3(off):
        return nt(jnp.concatenate([ap[t//3:t//3+8, t%3:t%3+8].reshape(1024,256) for t in range(9)],axis=1), wt[:,off:off+2304])
    norm_act(low,"g1","s1",0)
    emb = nt(feat, wt[:,O_TIME:O_TIME+128]) + vec(v_ref,"b_time")
    mid[...] = (conv3(O_R1) + vec(v_ref,"b_res1")).reshape(64,16,256) + emb
    norm_act(mid,"g2","s2",1)
    res[...] = low[...] + (conv3(O_R2) + vec(v_ref,"b_res2")).reshape(64,16,256)
    m, inv = gn_stats(res, 64, 8, sc["same8"][...])
    save(2, m, inv)
    gain = inv*vec(v_ref,"g3")
    nb = (res[...]*gain + (vec(v_ref,"s3") - m*gain)).astype(BF).reshape(1024,256)
    q = nt(nb, wt[:,O_QKV:O_QKV+256]) + vec(v_ref,"b_query")
    k_ = nt(nb, wt[:,O_QKV+256:O_QKV+512])
    v_ = nt(nb, wt[:,O_QKV+512:O_QKV+768])+vec(v_ref,"b_value")
    for i, z in enumerate((q, k_, v_)):
        z = z.astype(BF).astype(F32)
        qkv[2*i] = z[:,0:128]
        qkv[2*i+1] = z[:,128:256]
    def head(j, n):
        return jnp.concatenate([qkv[2*j,pl.ds(n,64,stride=16),:], qkv[2*j+1,pl.ds(n,64,stride=16),:]], axis=1).astype(BF)
    s = jnp.concatenate([nt(head(0,n), head(1,n)) for n in range(N)], axis=0)*(C2**-0.5)
    e = jnp.exp(s - jnp.max(s,axis=1,keepdims=True))
    p = (e/jnp.sum(e,axis=1,keepdims=True)).astype(BF)
    for n in range(N):
        o = nn(p[64*n:64*n+64], head(2,n)).astype(BF).astype(F32)
        ob[0,pl.ds(n,64,stride=16),:] = o[:,0:128]
        ob[1,pl.ds(n,64,stride=16),:] = o[:,128:256]
    obb = jnp.concatenate([ob[0],ob[1]],axis=1).astype(BF)
    if "obb" in sc: sc["obb"][...] = obb
    att_out = res[...].reshape(1024,256) + (nt(obb, wt[:,O_PROJ:O_PROJ+256]) + vec(v_ref,"b_proj"))
    attb = att_out.astype(BF)
    if "attb" in sc: sc["attb"][...] = attb
    for t in range(0,9,2):
        k = min(2, 9-t)
        r = nt(attb, wup[t:t+k].reshape(128*k,256))
        for i in range(k):
            yp[t+i,1:9,1:9] = r[:,128*i:128*i+128].reshape(8,8,16,128)
    def u(i,_):
        for a in range(2):
            for b in range(2):
                acc=None
                for t in range(9):
                    r,c=t//3-1,t%3-1
                    dr=(a+r)//2; dc=(b+c)//2
                    v=yp[t, i+dr+1, 1+dc:9+dc]
                    acc = v if acc is None else acc+v
                up[i,a,:,b] = acc + vec(v_ref,"b_up",C1) + sc["top6"][i,a,:,b]
        return 0
    lax.fori_loop(0,8,u,0)
    upf = sc["up3"]
    m, inv = gn_stats(upf, 256, 4, sc["same4"][...])
    save(3, m, inv)
    half = 0.5*inv*vec(v_ref,"g4",C1)
    shift = 0.5*vec(v_ref,"s4",C1) - m*half
    def b4(y,_):
        h = upf[pl.ds(y*16,16)]*half + shift
        ep[y+1,1:17] = (h + h*jnp.tanh(h)).astype(BF)
        return 0
    lax.fori_loop(0,16,b4,0,unroll=4)
    def fin(put):
        def f(y4,_):
            cols=jnp.concatenate([ep[pl.ds(y4*8+r,8)].reshape(2304,128) for r in range(3)],axis=1)
            d=nt(cols, wfin[...]).reshape(8,18,16,128)
            put(y4, (d[:,0:16] + pltpu.roll(d[:,1:17].reshape(2048,128),101,1).reshape(8,16,16,128)
                     + pltpu.roll(d[:,2:18].reshape(2048,128),74,1).reshape(8,16,16,128)).reshape(128,16,128) + bfin)
            return 0
        lax.fori_loop(0,2,f,0)
    return fin

def scratch():
    V=pltpu.VMEM
    return dict(wt=V((256,MID),BF), wup=V((9,128,256),BF), win=V((128,128),BF), wfin=V((128,384),BF), wfb=V((128,128),BF), sm=V((128,256),F32), xp=V((18,18,16,128),BF), tp=V((9,2,9,2,16,128),BF),
      top=V((256,16,128),F32), low=V((64,16,256),F32), ap=V((10,10,16,256),BF), mid=V((64,16,256),F32), res=V((64,16,256),F32),
      qkv=V((6,1024,128),F32), ob=V((2,1024,128),F32), yp=V((9,10,10,16,128),F32), up=V((8,2,8,2,16,128),F32), ep=V((18,18,16,128),BF), same8=V((256,256),BF), same4=V((128,128),BF))
KEYS=list(scratch().keys())

def zero_borders(sc):
    for k in ("xp","ep","tp","ap"):
        sc[k][...] = jnp.zeros(sc[k].shape, sc[k].dtype)
    yp = sc["yp"]
    edge = jnp.zeros((9,10,16,128), F32)
    for k in (0,9):
        yp[:,k] = edge
        yp[:,:,k] = edge
    for k, C, per in (("same8",256,8), ("same4",128,4)):
        sc[k][...] = one_hot(iota((C,C),0)//per == iota((C,C),1)//per)

def views(sc):
    sc=dict(sc)
    sc["top6"]=sc["top"].reshape(8,2,8,2,16,128)
    sc["up3"]=sc["up"].reshape(256,16,128)
    return sc

def teacher_call(D, cnt, x, feat, ce, cl, tc, nc, tg):
    def kern(cnt_ref, x_ref, feat_ref, ce_ref, cl_ref, tc_ref, nc_ref, tg_ref, out_ref, *scr):
        sc = views(dict(zip(KEYS, scr)))
        zero_borders(sc)
        prep(tg_ref, *(sc[k] for k in WKEYS), D)
        out_ref[...] = x_ref[...]
        def step(j, _):
            fin = net(out_ref, feat_ref[j], sc["wt"], sc["wup"], sc["win"], sc["wfin"], sc["sm"], sc)
            ce_, cl_ = ce_ref[j], cl_ref[j]
            def put(y4, e):
                out_ref[pl.ds(y4*128,128)] = ce_*e + cl_*out_ref[pl.ds(y4*128,128)]
            fin(put)
            return 0
        lax.fori_loop(0, cnt_ref[0], step, 0)
        def tgt(i, _):
            out_ref[pl.ds(i*16,16)] = tc_ref[...]*out_ref[pl.ds(i*16,16)] + nc_ref[...]*x_ref[pl.ds(i*16,16)]
            return 0
        lax.fori_loop(0, 16, tgt, 0)
    vm = pl.BlockSpec(memory_space=pltpu.VMEM)
    return pl.pallas_call(kern, out_shape=jax.ShapeDtypeStruct((256,16,128),F32),
        in_specs=[pl.BlockSpec(memory_space=pltpu.SMEM)]+[vm]*7, out_specs=vm, scratch_shapes=list(scratch().values()), name="teacher_steps",
        compiler_params=pltpu.CompilerParams(vmem_limit_bytes=60<<20))(cnt, x, feat, ce, cl, tc, nc, tg)

WKEYS = ["wt","wup","win","wfin","wfb","sm"]
RES = ["wt","wup","wfb","sm","tp","low","mid","res","qkv","up"]
def student_call(D, x, tgt, snr, feat, tg):
    vm=pl.BlockSpec(memory_space=pltpu.VMEM)
    sh=scratch()
    extra=dict(st=pltpu.VMEM((8,16,256),F32),cols=pltpu.VMEM((256,16,128),BF),attb=pltpu.VMEM((1024,256),BF),obb=pltpu.VMEM((1024,256),BF))
    outs={k:sh[k] for k in RES}; outs.update(extra)
    scr={k:v for k,v in sh.items() if k not in outs}
    ok,sk=list(outs),list(scr)
    def kern(x_ref,t_ref,snr_ref,feat_ref,tg_ref,out_ref,sum_ref,*refs):
        sc=views(dict(zip(ok+sk,refs)))
        zero_borders(sc)
        prep(tg_ref,*(sc[k] for k in WKEYS),D)
        fin=net(x_ref,feat_ref[...],sc["wt"],sc["wup"],sc["win"],sc["wfin"],sc["sm"],sc)
        def put(y4,e): out_ref[pl.ds(y4*128,128)]=e
        fin(put)
        def s(i,c):
            t,o=t_ref[pl.ds(i*16,16)],out_ref[pl.ds(i*16,16)]
            d=o-t
            return tuple(a+jnp.sum(b,axis=0) for a,b in zip(c,(t,t*t,o,o*o,d*d)))
        z=jnp.zeros((N,128),F32)
        r=lax.fori_loop(0,16,s,(z,)*5)
        r=r[:4]+(r[4]*snr_ref[...],)
        sum_ref[...]=jnp.concatenate([jnp.sum(a,axis=0,keepdims=True) for a in r]+[jnp.zeros((3,128),F32)],axis=0)
    res=pl.pallas_call(kern,
        out_shape=(jax.ShapeDtypeStruct((256,16,128),F32),jax.ShapeDtypeStruct((8,128),F32))+tuple(jax.ShapeDtypeStruct(outs[k].shape,outs[k].dtype) for k in ok),
        in_specs=[vm]*5,out_specs=(vm,)*(2+len(ok)),scratch_shapes=[scr[k] for k in sk], name="student_forward",
        compiler_params=pltpu.CompilerParams(vmem_limit_bytes=62<<20))(x,tgt,snr,feat,tg)
    return res[0],res[1],dict(zip(ok,res[2:]))

MESH = pl.DeviceIdType.MESH

def place():
    dp = lax.axis_index("dp")
    return dp // 4, dp // 2 % 2, dp % 2, lax.axis_index("mp")

def peer(z, y, x, c):
    return {"dp": z*4 + y*2 + x, "mp": c}

def greet(peers):
    barrier = pltpu.get_barrier_semaphore()
    for p in peers:
        pl.semaphore_signal(barrier, inc=1, device_id=p, device_id_type=MESH)
    pl.semaphore_wait(barrier, len(peers))

def partners():
    z, y, x, c = place()
    return [peer(z,y,x,1-c), peer(z,y,1-x,c), peer(z,1-y,x,c)] + [peer((z+o)%4,y,x,c) for o in (1,2,3)]

def gather_copies(s, p, streams, in_ref, out_ref, send, recv):
    z, y, x, c = place()
    wide = in_ref.shape[1] // streams
    all_, lo, hi = pl.ds(s*wide, wide), pl.ds(s*wide, wide//2), pl.ds(s*wide + wide//2, wide//2)
    to_x, to_y = peer(z,y,1-x,c), peer(z,1-y,x,c)
    if p == 0:
        return [pltpu.make_async_remote_copy(in_ref.at[:,all_], out_ref.at[z,y,x,c,:,all_], send.at[s,o-1], recv.at[s,3-o],
                device_id=peer((z+o)%4,y,x,c), device_id_type=MESH) for o in (2,1,3)]
    if p == 1:
        moves = [(out_ref.at[:,y,x,c,:,lo], to_x, 3), (out_ref.at[:,y,x,c,:,hi], to_y, 4)]
    elif p == 2:
        moves = [(out_ref.at[:,y,:,c,:,lo], to_y, 5), (out_ref.at[:,:,x,c,:,hi], to_x, 6)]
    else:
        moves = [(out_ref.at[:,:,:,c,:,all_], peer(z,y,x,1-c), 7)]
    return [pltpu.make_async_remote_copy(part, part, send.at[s,i], recv.at[s,i], device_id=to, device_id_type=MESH) for part, to, i in moves]

def gather_kernel(streams, in_ref, out_ref, send, recv, keep):
    z, y, x, c = place()
    greet(partners())
    own = pltpu.make_async_copy(in_ref, out_ref.at[z,y,x,c], keep)
    own.start()
    live = {(s,p): gather_copies(s,p,streams,in_ref,out_ref,send,recv) for s in range(streams) for p in range(4)}
    for s in range(streams):
        for d in live[s,0]: d.start()
    own.wait()
    for step in range(streams + 3):
        for s in range(streams):
            p = step - s
            if 0 <= p <= 3:
                for d in live[s,p]: d.wait_recv()
                if p < 3:
                    for d in live[s,p+1]: d.start()
    for ds in live.values():
        for d in ds: d.wait_send()

def gather_call(block, cid, streams=4):
    rows, wide = block.shape
    any_ = pl.BlockSpec(memory_space=pl.ANY)
    out = pl.pallas_call(lambda *r: gather_kernel(streams, *r), out_shape=jax.ShapeDtypeStruct((4,2,2,2,rows,wide), block.dtype),
        in_specs=[any_], out_specs=any_, name="gather_columns",
        scratch_shapes=[pltpu.SemaphoreType.DMA((streams,8)), pltpu.SemaphoreType.DMA((streams,8)), pltpu.SemaphoreType.DMA],
        compiler_params=pltpu.CompilerParams(collective_id=cid, has_side_effects=True))(block)
    return out.reshape(32*rows, wide)

def sum_kernel(in_ref, out_ref, box, send, recv):
    z, y, x, c = place()
    hops = [peer(z,y,x,1-c), peer(z,y,1-x,c), peer(z,1-y,x,c), peer(z+1-2*(z%2),y,x,c), peer((z+2)%4,y,x,c)]
    out_ref[...] = in_ref[...]
    for k, to in enumerate(hops):
        box[k] = out_ref[...]
        d = pltpu.make_async_remote_copy(box.at[k], box.at[5+k], send.at[k], recv.at[k], device_id=to, device_id_type=MESH)
        d.start()
        d.wait()
        out_ref[...] += box[5+k]

STREAMS = 8

def row_of(r):
    return 128*(r//128) + 32*(r//8%4) + 8*(r//32%4) + 4*(r%2) + 2*(r//2%2) + r//4%2

def scatter_scratch():
    V = pltpu.VMEM
    sc = {}
    for s in range(STREAMS):
        sc[f"c{s}"] = V((2,2,2,4,4,8,128),F32)
        sc[f"h{s}"] = V((2,2,4,4,8,128),F32)
        sc[f"q{s}"] = V((2,4,4,8,128),F32)
        sc[f"z{s}"] = V((3,2,4,8,128),F32)
    sc["ssem"] = pltpu.SemaphoreType.DMA((STREAMS,8))
    sc["rsem"] = pltpu.SemaphoreType.DMA((STREAMS,8))
    return sc

def scatter_steps(g_ref, out_ref, sc):
    z, y, x, c = place()
    send, recv = sc["ssem"], sc["rsem"]
    live = {}
    def bufs(s): return tuple(sc[f"{k}{s}"] for k in "chqz")
    def copies(s, p):
        r0, r1, r2, r3 = bufs(s)
        to_x, to_y = peer(z,y,1-x,c), peer(z,1-y,x,c)
        if p == 0:
            moves = [(g_ref.at[s,:,1-c], r0, peer(z,y,x,1-c), 0, 0)]
        elif p == 1:
            moves = [(r0.at[0,1-x], r1.at[0], to_x, 1, 1), (r0.at[1,:,1-y], r1.at[1], to_y, 2, 2)]
        elif p == 2:
            moves = [(r1.at[0,1-y], r2.at[0], to_y, 3, 3), (r1.at[1,1-x], r2.at[1], to_x, 4, 4)]
        else:
            moves = [(r2.at[:,(z+o)%4], r3.at[3-o], peer((z+o)%4,y,x,c), 4+o, 8-o) for o in (2,1,3)]
        return [pltpu.make_async_remote_copy(src, dst, send.at[s,i], recv.at[s,k], device_id=to, device_id_type=MESH) for src, dst, to, i, k in moves]
    def add(s, p):
        r0, r1, r2, r3 = bufs(s)
        if p == 0:
            for h in range(2):
                for i in range(2):
                    r0[h,i] += g_ref[s,h,c,i]
        elif p == 1:
            r1[0] += r0[0,x]
            r1[1] += r0[1,:,y]
        elif p == 2:
            r2[0] += r1[0,y]
            r2[1] += r1[1,x]
        else:
            out_ref[:,:,8*s:8*s+8] = r2[:,z] + r3[0] + r3[1] + r3[2]
    def advance(s, p):
        if p:
            for d in live[s,p-1]: d.wait_recv()
            add(s, p-1)
        if p < 4:
            live[s,p] = copies(s,p)
            for d in live[s,p]: d.start()
    def finish():
        for ds in live.values():
            for d in ds: d.wait_send()
    return advance, finish

def tn(a, b): return lax.dot_general(a, b, (((0,),(0,)),((),())), preferred_element_type=F32)

def bwd_kernel(x_refs, o_refs, sc):
    X, S = x_refs, sc
    (G,) = o_refs
    sg, sn_total = S["sg"], X["total"]
    v_ref, wt, wup, st = X["v"], X["wt"], X["wup"], X["st"]
    gp18, gcols, big, ep, dp, s_hi, s_lo, gp, ap, da, gres, gqkv, gmx = (S[k] for k in ("gp18","gcols","big","ep","dp","s_hi","s_lo","gp","ap","da","gres","gqkv","gmx"))
    lane = iota((1,1,128),2)
    for k, C, per in (("same8",256,8), ("same4",128,4)):
        S[k][...] = one_hot(iota((C,C),0)//per == iota((C,C),1)//per)
    for k in ("gp18","dp","gp","ap"):
        S[k][...] = jnp.zeros(S[k].shape, S[k].dtype)
    sg[...] = jnp.zeros((128,256),F32)
    def put_block(b, val):
        sg[b//2:b//2+1, 128*(b%2):128*(b%2)+128] = val
    def put_vec(name, val, C=C2):
        at, wide = BLOCK[name]
        for k in range(wide):
            put_block(at+k, val[:, 128*k:128*k+128])
    def rowsum(a): return jnp.sum(a, axis=0, keepdims=True)
    step, near = S["step"], S["near"]
    def put_g(val, col, row0=0):
        rows, width = val.shape
        col = 128*next(GROUP[o] + (col-o)//128 for o in sorted(GROUP, reverse=True) if col >= o)
        for c in range(width//128):
            at = col//128+c
            for r in range(row0, row0+rows, 8):
                if near: to = pl.ds(2048*(at//8) + 1024*(r//128) + 32*(r//32%4) + 8*(r//8%4) + at%8, 8, stride=128)
                else: to = pl.ds(64*r+at, 8, stride=64)
                G[to,:] = val[r-row0:r-row0+8, c*128:c*128+128]
    pm = S["pm"]
    pm[...] = one_hot(iota((256,256),1) == (row_of(iota((256,256),0)) if near else iota((256,256),0)))
    def turn(g): return nt(pm[...], g).astype(BF)
    pixels = 256.0*sn_total
    so = X["stat"][...]
    mt, mo = so[0:1]/pixels, so[2:3]/pixels
    vt_, vo = so[1:2]/pixels-mt*mt, so[3:4]/pixels-mo*mo
    cb = 4.0*(vo-vt_)/pixels
    ca = 2.0*(mo-mt)/pixels-cb*mo
    sn = X["snr"][...]*(2.0/(768.0*sn_total))
    acc=jnp.zeros((N,128),F32)
    def g0(y,acc):
        o=X["out"][pl.ds(y*16,16)]
        go = sn*(o-X["tgt"][pl.ds(y*16,16)]) + ca + cb*o
        gp18[y+1,1:17]=go.astype(BF)
        return acc+jnp.sum(go,axis=0)
    acc=lax.fori_loop(0,16,g0,acc)
    acc=rowsum(acc)
    lane2=iota((1,128),1)
    put_block(84, sum(jnp.where(lane2==c, jnp.sum(jnp.where(lane2==9*c,acc,0.0),axis=1,keepdims=True),0.0) for c in range(3)))
    def g1(y,_):
        for t in range(9):
            w = gp18[y+2-t//3, 2-t%3:18-t%3]
            cols = jnp.where((lane%9==t)&(lane<27), w, cols) if t else jnp.where((lane%9==0)&(lane<27), w, jnp.zeros_like(w))
        gcols[pl.ds(y*16,16)] = cols
        return 0
    lax.fori_loop(0,16,g1,0)
    big[...] = nn(gcols[...].reshape(4096,128), X["wfb"][...]).reshape(256,16,128)
    def gn_bwd(src, dref, si, gname, sname, C, per, same, rows, k, act_put, dx_put, silu=True):
        m, inv = st[2*si,:,0:C], st[2*si+1,:,0:C]
        g, s = vec(v_ref,gname,C), vec(v_ref,sname,C)
        w = 512//C
        zero = jnp.zeros((w,N,C),F32)
        def pick(v): return jnp.sum(v.reshape((-1,w)+v.shape[1:]),axis=0)
        def p1(y,c):
            A,B=c
            xh=(src[pl.ds(y*k,k)]-m)*inv
            d=dref[pl.ds(y*k,k)]
            if silu:
                h=xh*(0.5*g)+0.5*s
                th=jnp.tanh(h); sg=0.5+0.5*th; act=h+h*th
                act_put(y,act.astype(BF))
                d=d*(sg+act*(1.0-sg))
                dref[pl.ds(y*k,k)]=d
            else:
                act_put(y,(xh*g+s).astype(BF))
            return A+pick(d), B+pick(d*xh)
        A,B=lax.fori_loop(0,rows,p1,(zero,zero),unroll=4)
        A,B=jnp.sum(A,axis=0),jnp.sum(B,axis=0)
        put_vec(gname,rowsum(B),C); put_vec(sname,rowsum(A),C)
        cnt=1.0/(per*rows*k)
        ga=group_sum(g*A,same)*cnt; gb=group_sum(g*B,same)*cnt
        ig=inv*g; ib=inv*inv*gb; ic=m*ib-inv*ga
        def p2(y,acc):
            dx=ig*dref[pl.ds(y*k,k)]-ib*src[pl.ds(y*k,k)]+ic
            return acc+pick(dx_put(y,dx))
        return lambda: jnp.sum(lax.fori_loop(0,rows,p2,zero,unroll=4),axis=0)
    def act4(y,a): ep[pl.ds(y*16,16)]=a
    def dx4(y,dx):
        big[pl.ds(y*16,16)]=dx
        b=dx.astype(BF).reshape(8,2,16,128)
        p=y+1
        dp[p//2,p%2,0:8,1]=b[:,0]
        dp[p//2,p%2,1:9,0]=b[:,1]
        return dx
    fin=gn_bwd(X["up"].reshape(256,16,128),big,3,"g4","s4",128,4,S["same4"][...],16,16,act4,dx4)
    dwf = tn(gcols[...].reshape(4096,128), ep[...].reshape(4096,128))
    flat = jnp.zeros((9,384),F32)
    for c in range(3):
        p3 = one_hot(iota((128,384),1) == 3*iota((128,384),0) + c)
        piece = dwf[9*c:9*c+9]
        hi = piece.astype(BF); rest = piece-hi.astype(F32)
        mi = rest.astype(BF); lo = (rest-mi.astype(F32)).astype(BF)
        flat += nn(hi,p3)+nn(mi,p3)+nn(lo,p3)
    for t in range(9):
        for h in range(3):
            put_block(27+3*t+h, flat[t:t+1,128*h:128*h+128])
    put_vec("b_up",rowsum(fin()),128)
    PAIR={-1:((1,0),(1,1)),0:((0,1),(1,0)),1:((0,0),(0,1))}
    def su(i,_):
        for r in (-1,0,1):
            (ra,pa),(rb,pb)=PAIR[r]
            V={}
            for cp in range(2):
                V[cp]=dp[i+ra,pa,:,cp].astype(F32)+dp[i+rb,pb,:,cp].astype(F32)
            for c in (-1,0,1):
                (ca_,qa),(cb_,qb)=PAIR[c]
                s=V[qa][ca_:ca_+8]+V[qb][cb_:cb_+8]
                t=(r+1)*3+c+1
                hi=s.astype(BF)
                s_hi[t,pl.ds(i*8,8)]=hi
                s_lo[t,pl.ds(i*8,8)]=(s-hi.astype(F32)).astype(BF)
        return 0
    lax.fori_loop(0,8,su,0)
    cat=lambda ref: jnp.concatenate([ref[t].reshape(1024,128) for t in range(9)],axis=1)
    wu=wup[...].reshape(1152,256)
    gatt=nn(cat(s_hi),wu)+nn(cat(s_lo),wu)
    gres[...]=gatt.reshape(64,16,256)
    put_vec("b_proj",rowsum(gatt))
    gab=gatt.astype(BF)
    attb=X["attb"][...]
    kk, ci = iota((256,256),1), iota((256,256),0)
    peo=one_hot(ci == 2*(kk % 128) + kk // 128)
    aeo=nn(attb,peo).astype(BF)
    for t in range(9):
        hi,lo=[nt(pm[0:128,0:128],v[t].reshape(1024,128)).astype(BF) for v in (s_hi,s_lo)]
        r=nn(hi,aeo)+nn(lo,aeo)
        put_g(r[:,0:128],O_UP+t*128,0); put_g(r[:,128:256],O_UP+t*128,128)
    step((0,0))
    obb=X["ob"][...]
    put_g(nn(turn(gab),obb),O_PROJ)
    gm=nn(gab,wt[:,O_PROJ:O_PROJ+256]).astype(BF).astype(F32)
    gmx[0]=gm[:,0:128]; gmx[1]=gm[:,128:256]
    qkv=X["qkv"]
    sc_=C2**-0.5
    def pair(ref,j,n): return jnp.concatenate([ref[2*j,pl.ds(n,64,stride=16),:],ref[2*j+1,pl.ds(n,64,stride=16),:]],axis=1).astype(BF)
    s=jnp.concatenate([nt(pair(qkv,0,n),pair(qkv,1,n)) for n in range(N)],axis=0)*sc_
    e=jnp.exp(s-jnp.max(s,axis=1,keepdims=True))
    p=e/jnp.sum(e,axis=1,keepdims=True)
    ga=jnp.concatenate([nt(pair(gmx,0,n),pair(qkv,2,n)) for n in range(N)],axis=0)
    gs=(p*(ga-jnp.sum(ga*p,axis=1,keepdims=True))).astype(BF)
    pb=p.astype(BF)
    for n in range(N):
        gsn,pn=gs[64*n:64*n+64],pb[64*n:64*n+64]
        for j,o in enumerate((nn(gsn,pair(qkv,1,n))*sc_, tn(gsn,pair(qkv,0,n))*sc_, tn(pn,pair(gmx,0,n)))):
            o=o.astype(BF).astype(F32)
            gqkv[2*j,pl.ds(n,64,stride=16),:]=o[:,0:128]
            gqkv[2*j+1,pl.ds(n,64,stride=16),:]=o[:,128:256]
    step((0,1))
    gq=[jnp.concatenate([gqkv[2*j],gqkv[2*j+1]],axis=1) for j in range(3)]
    put_vec("b_query",rowsum(gq[0])); put_vec("b_value",rowsum(gq[2]))
    gqb=[g.astype(BF) for g in gq]
    da[...]=nn(jnp.concatenate(gqb,axis=1),jnp.concatenate([wt[:,O_QKV+256*j:O_QKV+256*j+256] for j in range(3)],axis=0)).reshape(64,16,256)
    nbs=S["nb"]
    def act3(y,a): nbs[pl.ds(y*8,8)]=a
    def dx3(y,dx):
        z=gres[pl.ds(y*8,8)]+dx
        gres[pl.ds(y*8,8)]=z
        gp[y+1,1:9]=z.astype(BF)
        return z
    fin=gn_bwd(X["res"],da,2,"g3","s3",256,8,S["same8"][...],8,8,act3,dx3,silu=False)
    nb=nbs[...].reshape(1024,256)
    for j in range(3): put_g(nn(turn(gqb[j]),nb),O_QKV+256*j)
    step((1,0))
    put_vec("b_res2",rowsum(fin()))
    step((0,2))
    def conv_dgrad(off):
        return nn(jnp.concatenate([gp[2-t//3:10-t//3,2-t%3:10-t%3].reshape(1024,256) for t in range(9)],axis=1),
                  jnp.concatenate([wt[:,off+256*t:off+256*t+256] for t in range(9)],axis=0))
    def conv_wgrad(g,off,steps):
        gt=turn(g)
        for t in range(9):
            put_g(nn(gt,ap[t//3:t//3+8,t%3:t%3+8].reshape(1024,256)),off+256*t)
            step(*steps.get(t,()))
    def act_(y,a): ap[y+1,1:9]=a
    da[...]=conv_dgrad(O_R2).reshape(64,16,256)
    step((0,3),(1,1))
    def dxm(y,dx):
        gp[y+1,1:9]=dx.astype(BF)
        return dx
    fin=gn_bwd(X["mid"],da,1,"g2","s2",256,8,S["same8"][...],8,8,act_,dxm)
    step((1,2))
    conv_wgrad(gp[1:9,1:9].reshape(1024,256),O_R2,{3:((2,0),),7:((3,0),),8:((1,3),)})
    gemb=fin()
    step((2,1),(0,4))
    put_vec("b_time",rowsum(gemb)); put_vec("b_res1",rowsum(gemb))
    put_g(nn(turn(gemb.astype(BF)),X["feat"][...]),O_TIME)
    da[...]=conv_dgrad(O_R1).reshape(64,16,256)
    step((2,2),(3,1),(1,4))
    def dxl(y,dx):
        z=gres[pl.ds(y*8,8)]+dx
        gp[y+1,1:9]=z.astype(BF)
        return z
    fin=gn_bwd(X["low"],da,0,"g1","s1",256,8,S["same8"][...],8,8,act_,dxl)
    conv_wgrad(gp[1:9,1:9].reshape(1024,256),O_R1,{1:((4,0),),3:((2,3),),5:((5,0),),8:((3,2),)})
    put_vec("b_down",rowsum(fin()))
    step((4,1),(3,3))
    glb=gp[1:9,1:9].reshape(1024,256)
    glt=turn(glb)
    tp=X["tp"]
    for t in range(9):
        ty,tx=t//3,t%3
        put_g(nn(glt,tp[ty//2:ty//2+8,ty%2,tx//2:tx//2+8,tx%2].reshape(1024,128)),O_DOWN+128*t)
        step(*{1:((6,0),),8:((5,1),(2,4))}.get(t,()))
    big6=big.reshape(8,2,8,2,16,128)
    dt6=S["dt"].reshape(8,2,8,2,16,128)
    SRC={0:((1,0),),1:((0,1),(2,0))}
    total=jnp.zeros((N,128),F32)
    for a in range(2):
        for b in range(2):
            taps=[(3*ty+tx,1+oy,1+ox) for ty,oy in SRC[a] for tx,ox in SRC[b]]
            z=nn(jnp.concatenate([gp[oy:oy+8,ox:ox+8].reshape(1024,256) for _,oy,ox in taps],axis=1),
                 jnp.concatenate([wt[:,O_DOWN+128*t:O_DOWN+128*t+128] for t,_,_ in taps],axis=0)).reshape(8,8,16,128)
            z=z+big6[:,a,:,b]
            dt6[:,a,:,b]=z.astype(BF)
            total=total+jnp.sum(jnp.sum(z,axis=0),axis=0)
    put_vec("b_in",rowsum(total),128)
    step((4,2),(6,1))
    dwi=tn(X["cols"][...].reshape(4096,128),S["dt"][...].reshape(4096,128))
    for k in range(27):
        put_block(k, dwi[9*(k%3)+k//3:9*(k%3)+k//3+1])
    kept = nt(split3(sg[...]), pm[...])
    put_g((kept[0:128]+kept[128:256]+kept[256:384]).T, MID)

def bwd_scratch():
    V=pltpu.VMEM
    return dict(gp18=V((18,18,16,128),BF),gcols=V((256,16,128),BF),big=V((256,16,128),F32),ep=V((256,16,128),BF),dp=V((9,2,9,2,16,128),BF),
      s_hi=V((9,64,16,128),BF),s_lo=V((9,64,16,128),BF),gp=V((10,10,16,256),BF),ap=V((10,10,16,256),BF),da=V((64,16,256),F32),gres=V((64,16,256),F32),
      gqkv=V((6,1024,128),F32),gmx=V((2,1024,128),F32),nb=V((64,16,256),BF),dt=V((256,16,128),BF),sg=V((128,256),F32),pm=V((256,256),BF),same8=V((256,256),BF),same4=V((128,128),BF))
BIN=["out","tgt","snr","stat","cols","tp","low","mid","res","qkv","obb","attb","up","st","feat","wt","wup","wfb","sm"]
GROUP = {O_UP:0, O_PROJ:9, O_QKV:11, O_R2:17, O_TIME:35, O_R1:36, O_DOWN:54, MID:63}
def bwd_call(ins, total, near):
    vm=pl.BlockSpec(memory_space=pltpu.VMEM)
    sc=bwd_scratch()
    if near:
        sc.update(box=pltpu.VMEM((10,8,128),F32), send=pltpu.SemaphoreType.DMA((5,)), recv=pltpu.SemaphoreType.DMA((5,)), g=pltpu.VMEM((256*64,128),F32))
        sc.update(scatter_scratch())
    keys=list(sc)
    def k(*refs):
        a=dict(zip(BIN,refs[:len(BIN)])); a["v"]=a["sm"]; a["ob"]=a["obb"]; a["total"]=float(total)
        s=dict(zip(keys,refs[len(BIN)+2:]))
        grad_ref,sum_ref=refs[len(BIN):len(BIN)+2]
        if not near:
            sum_ref[...]=a["stat"][...]
            s["step"],s["near"]=(lambda *_: None),False
            a["stat"]=sum_ref
            bwd_kernel(a,(grad_ref,),s)
            return
        greet(partners())
        sum_kernel(a["stat"],sum_ref,s["box"],s["send"],s["recv"])
        a["stat"]=sum_ref
        advance,finish=scatter_steps(s["g"].reshape(8,2,2,2,2,4,4,8,128),grad_ref.reshape(2,4,64,128),s)
        def step(*moves):
            for m in moves: advance(*m)
        s["step"],s["near"]=step,True
        bwd_kernel(a,(s["g"],),s)
        step((7,0),(4,3),(5,2),(7,1),(6,2),(3,4),(5,3),(4,4),(7,2),(6,3),(5,4),(7,3),(6,4),(7,4))
        finish()
    extra=dict(collective_id=2, has_side_effects=True) if near else {}
    shape=(8,64,128) if near else (256*64,128)
    return pl.pallas_call(k,out_shape=(jax.ShapeDtypeStruct(shape,F32),jax.ShapeDtypeStruct((8,128),F32)),
        in_specs=[vm]*len(BIN),out_specs=(vm,vm),scratch_shapes=list(sc.values()), name="student_backward",
        compiler_params=pltpu.CompilerParams(vmem_limit_bytes=63<<20, **extra))(*[ins[k] for k in BIN])

def segments():
    matrices = [("w_in", 27, C1), ("w_down", 9 * C1, C2), ("w_res1", 9 * C2, C2), ("w_res2", 9 * C2, C2), ("w_time", C1, C2),
                ("w_qkv", C2, 3 * C2), ("w_proj", C2, C2), ("w_up", 9 * C2, C1), ("w_final", 9 * C1, 3)]
    vectors = [("g1", C2), ("s1", C2), ("g2", C2), ("s2", C2), ("g3", C2), ("s3", C2), ("g4", C1), ("s4", C1), ("b_in", C1),
               ("b_down", C2), ("b_res1", C2), ("b_res2", C2), ("b_time", C2), ("b_query", C2), ("b_value", C2), ("b_proj", C2),
               ("b_up", C1), ("b_final", 3)]
    listing, cursor = [], 0
    for name, height, breadth in matrices:
        listing.append((name, cursor, (height, breadth), "matrix"))
        cursor += height * breadth
    for name, length in vectors:
        listing.append((name, cursor, (length,), "gain" if name[0] != "b" else "bias"))
        cursor += length
    return listing

def rates(position):
    learn = jnp.zeros(position.shape, F32)
    decay = jnp.zeros(position.shape, F32)
    for name, offset, shape, kind in segments():
        inside = (position >= offset) & (position < offset + math.prod(shape))
        if kind == "matrix":
            spread = shape[0] ** (-0.5) * ((SIDE * SIDE / 4.0) ** 0.5 if name == "w_proj" else 1.0)
            learn = jnp.where(inside, 0.5 * spread, learn)
            decay = jnp.where(inside, 0.01, decay)
        elif kind == "gain":
            learn = jnp.where(inside, 0.2, learn)
        else:
            learn = jnp.where(inside, 0.05, learn)
    return learn, decay

def angle_of(step):
    return 0.1 + 1.35 * step.astype(F32) / TGRID

def time_features(step):
    half = C1 // 2
    freqs = jnp.exp(-math.log(1000.0) * jnp.arange(half).astype(F32) / half)
    phases = step.astype(F32)[..., None] * freqs
    return jnp.concatenate([jnp.sin(phases), jnp.cos(phases)], axis=-1)

def to_columns(shard, start, D):
    R, L = 256 // D, shard.shape[0]
    body = R * MID
    if HEAD % D == 0:
        parts = [shard[start:start+body], shard[:start], shard[start+body:]]
    else:
        at = jnp.arange(L - body)
        parts = [lax.dynamic_slice(shard, (start,), (body,)), jnp.where(at < start, shard[:L-body], shard[body:])]
    cols = jnp.concatenate(parts).reshape(-1, R).T
    return jnp.pad(cols, ((0,0),(0,MID+128-cols.shape[1])))

def from_columns(cols, start, D, L):
    R = 256 // D
    body = R * MID
    def piece(at, width): return cols[:, 128*GROUP[at]:128*GROUP[at]+width]
    q = piece(O_QKV,768).reshape(R,3,256).transpose(0,2,1).reshape(R,768)
    cols = jnp.concatenate([piece(O_DOWN,1152), piece(O_R1,2304), piece(O_R2,2304), piece(O_TIME,128), q, piece(O_PROJ,256), piece(O_UP,1152),
                            piece(MID,L//R-MID)], axis=1)
    flat = cols.T.reshape(-1)
    if HEAD % D == 0:
        return jnp.concatenate([flat[body:body+start], flat[:body], flat[body+start:]])
    rest = flat[body:]
    at = jnp.arange(L)
    mid = lax.dynamic_update_slice(jnp.zeros((L,), F32), flat[:body], (start,))
    low = jnp.pad(rest, (0, body)); high = jnp.pad(rest, (body, 0))
    return jnp.where(at < start, low, jnp.where(at < start + body, mid, high))

def lanes(images):
    v = jnp.repeat(images.transpose(1,2,0,3).reshape(256,N,3), 9, axis=2)
    return jnp.pad(v, ((0,0),(0,0),(0,101)))

def local(images, noise, timestep, stride, bucket, steps_table, master, first_moment, second_moment, teacher, step_count):
    axes = ("dp", "mp")
    D = lax.axis_size("dp") * lax.axis_size("mp")
    me = lax.axis_index(axes)
    R, L = 256 // D, master.shape[0]
    start = HEAD // D if HEAD % D == 0 else (HEAD - me + D - 1) // D
    near = lax.axis_size("dp") == 16 and lax.axis_size("mp") == 2
    teacher_cols = to_columns(teacher, start, D)
    teacher_all = gather_call(teacher_cols, 1) if near else lax.all_gather(teacher_cols, axes, axis=0, tiled=True)
    student_all = lax.all_gather(to_columns(master.astype(BF), start, D), axes, axis=0, tiled=True)
    wide = lambda v: jnp.where(jnp.arange(128) < 27, v[..., None], 0.0)
    angle = angle_of(timestep)
    noisy = lanes(jnp.cos(angle)[:,None,None,None] * images + jnp.sin(angle)[:,None,None,None] * noise)
    picked = jnp.sum(jnp.where(jnp.arange(steps_table.shape[0]) == bucket[0], steps_table, 0))
    turn = jnp.arange(KMAX)[:, None]
    current = timestep[None] - turn * stride[None]
    later = current - stride[None]
    keep = jnp.sin(angle_of(later)) / jnp.sin(angle_of(current))
    take = jnp.cos(angle_of(later)) - keep * jnp.cos(angle_of(current))
    features = jax.nn.silu(time_features(current)).astype(BF)
    final_t = timestep - picked * stride
    below = jnp.sin(angle - angle_of(final_t))
    target = teacher_call(D, picked.reshape(1), noisy, features, wide(take), wide(keep), wide(jnp.sin(angle)/below),
                          wide(-jnp.sin(angle_of(final_t))/below), teacher_all)
    snr = wide(jnp.maximum(jnp.square(jnp.cos(angle)/jnp.sin(angle)), 1.0))
    out, sums, kept = student_call(D, noisy, target, snr, features[0], student_all)
    if not near:
        sums = lax.psum(sums, axes)
    total = images.shape[0] * D
    grads, sums = bwd_call(dict(kept, out=out, tgt=target, snr=snr, stat=sums, feat=features[0]), total, near)
    pick = sums[:5, 0:27:9]
    mean_t, mean_o = pick[0]/(256*total), pick[2]/(256*total)
    var_t, var_o = pick[1]/(256*total) - jnp.square(mean_t), pick[3]/(256*total) - jnp.square(mean_o)
    loss = jnp.sum(pick[4])/(768*total) + jnp.sum(jnp.square(mean_o-mean_t) + jnp.square(var_o-var_t))
    if near:
        part = grads.reshape(R, MID+128)
    else:
        order = grads.reshape(R, D, MID+128)
        if HEAD % D:
            order = jnp.concatenate([jnp.roll(order[:, :, :MID], HEAD % D, axis=1), order[:, :, MID:]], axis=2)
        part = lax.psum_scatter(order, axes, scatter_dimension=1, tiled=True).reshape(R, MID+128)
    grad = from_columns(part, start, D, L)
    learn, decay = rates(jnp.arange(L, dtype=jnp.int32) * D + me)
    steps_done = step_count[0].astype(F32)
    new_first = 0.5 * first_moment + 0.5 * grad
    new_second = 0.5 * second_moment + 0.5 * jnp.square(grad)
    fix_rate = 1.0 - jnp.power(0.5, steps_done)
    new_master = master - learn * (new_first / fix_rate / (jnp.sqrt(new_second / fix_rate) + 1e-08) + decay * master)
    return loss, new_master, new_first, new_second

def solution(mesh):
    s = P(("dp", "mp"))
    i = P(("dp", "mp"), None, None, None)
    return jax.shard_map(local, mesh=mesh, in_specs=(i, i, s, s, s, P(), s, s, s, s, P()), out_specs=(P(), s, s, s), check_vma=False)
```

```python
import math
import jax
import jax.numpy as jnp
from jax import lax
from jax.experimental import pallas as pl
from jax.experimental.pallas import tpu as pltpu
from jax.sharding import PartitionSpec as P

C1, C2, N = 128, 256, 16
SIDE, TGRID, KMAX = 16, 64, 4
F32, BF = jnp.float32, jnp.bfloat16
O_DOWN, O_R1, O_R2, O_TIME, O_QKV, O_PROJ, O_UP, MID = 0, 1152, 3456, 5760, 5888, 6656, 6912, 8064
HEAD = 3456
BLOCK = {}
_at = 54
for _name, _wide in (("g1",2),("s1",2),("g2",2),("s2",2),("g3",2),("s3",2),("g4",1),("s4",1),("b_in",1),("b_down",2),("b_res1",2),
                     ("b_res2",2),("b_time",2),("b_query",2),("b_value",2),("b_proj",2),("b_up",1),("b_final",1)):
    BLOCK[_name] = (_at, _wide)
    _at += _wide

def iota(shape, d): return lax.broadcasted_iota(jnp.int32, shape, d)

def nt(a, b): return lax.dot_general(a, b, (((1,),(1,)),((),())), preferred_element_type=F32)
def nn(a, b): return lax.dot_general(a, b, (((1,),(0,)),((),())), preferred_element_type=F32)

def one_hot(cond): return jnp.where(cond, 1.0, 0.0).astype(BF)

def split3(v):
    hi = v.astype(BF); r = v - hi.astype(F32)
    mid = r.astype(BF); lo = (r - mid.astype(F32)).astype(BF)
    return jnp.concatenate([hi, mid, lo], axis=0)

def pile(v, k):
    return jnp.sum(jnp.sum(v.reshape((-1, k) + v.shape[1:]), axis=0), axis=0)

def group_sum(v, same):
    r = nn(split3(v), same)
    return r[0:N] + r[N:2*N] + r[2*N:3*N]

def prep(tg_ref, wt_ref, wup_ref, win_ref, wfin_ref, wfb_ref, sm_ref, D):
    R = 256 // D
    row, rho = iota((256,256),1), iota((256,256),0)
    perm = one_hot(rho == row // R + D * (row % R))
    CH = 1152
    for c in range(7):
        wt_ref[0:128, c*CH:(c+1)*CH] = nn(perm[128:256], tg_ref[:, 13+c*CH:13+(c+1)*CH]).astype(BF)
        wt_ref[128:256, c*CH:(c+1)*CH] = nn(perm[0:128], tg_ref[:, 14+c*CH:14+(c+1)*CH]).astype(BF)
    kk, ci = iota((256,256),0), iota((256,256),1)
    peo = one_hot(ci == 2*(kk % 128) + kk // 128)
    for t in range(9):
        cs = O_UP + t*128
        both = jnp.concatenate([wt_ref[0:128, cs:cs+128], wt_ref[128:256, cs:cs+128]], axis=1)
        wup_ref[t] = nn(both, peo).astype(BF)
    kq, lq = iota((768,768),0), iota((768,768),1)
    pq = one_hot(kq == 3*(lq % 256) + lq // 256)
    wt_ref[:, O_QKV:O_QKV+768] = nn(wt_ref[:, O_QKV:O_QKV+768], pq).astype(BF)
    scol, srho = iota((256,128),1), iota((256,128),0)
    sm_ref[...] = jnp.where((scol < 13) | ((scol == 13) & (srho < 128)), nn(perm, tg_ref[:, 0:128]), nn(perm, tg_ref[:, MID:MID+128])).T
    halves = jnp.concatenate([sm_ref[0:32, 0:128], sm_ref[0:32, 128:256]], axis=0).astype(BF)
    l, r = iota((128,64),0), iota((128,64),1)
    k = 3*(l % 9) + l // 9
    win_ref[...] = nn(one_hot((l < 27) & (r == 32*(k % 2) + k // 2)), halves).astype(BF)
    t16, r16 = iota((16,64),0), iota((16,64),1)
    pieces = []
    for h in range(3):
        blk = 27 + 3*t16 + h
        pieces.append(nn(one_hot((t16 < 9) & (r16 == 32*(blk % 2) + blk // 2)), halves))
    flat = jnp.concatenate(pieces, axis=1).astype(BF)
    acc = jnp.zeros((128,128), F32)
    for c in range(3):
        wc = nn(flat, one_hot(iota((384,128),0) == 3*iota((384,128),1) + c)).astype(BF)
        acc += nn(one_hot((iota((128,16),1) < 9) & (iota((128,16),0) == 9*c + iota((128,16),1))), wc)
    wfb = acc.astype(BF)
    wfb_ref[...] = wfb
    a, z = iota((128,128),0), iota((128,128),1)
    for r in range(3):
        wfin_ref[:, 128*r:128*r+128] = nn(one_hot((a < 81) & (z == 9*(a % 27 // 9) + 3*r + a // 27)), wfb).astype(BF)

def final_bias(sm_ref):
    b = sm_ref[42:43, 0:128].astype(BF)
    return nn(b, one_hot((iota((128,128),1) < 27) & (iota((128,128),0) == iota((128,128),1) // 9)))

def gn_stats(src, P, per, same):
    k = 4
    B = 16
    s = [pile(src[pl.ds(i,B)], k) for i in range(0,P,B)]
    m = sum(s[1:], s[0]) * (1.0/P)
    q = [pile(jnp.square(src[pl.ds(i,B)] - m), k) for i in range(0,P,B)]
    mean = group_sum(m, same) * (1.0/per)
    spread = sum(q[1:], q[0]) * (1.0/P) + jnp.square(m - mean)
    return mean, lax.rsqrt(group_sum(spread, same) * (1.0/per) + 1e-5)

def vec(v_ref, name, C=C2):
    at, wide = BLOCK[name]
    return jnp.concatenate([v_ref[b//2:b//2+1, 128*(b%2):128*(b%2)+128] for b in range(at, at+wide)], axis=1)

def net(x_ref, feat, wt, wup, win, wfin, v_ref, sc):
    xp, tp, top, low, ap, mid, res, qkv, ob, yp, up, ep = (sc[k] for k in ("xp","tp","top","low","ap","mid","res","qkv","ob","yp","up","ep"))
    ap2 = sc.get("ap2", ap)
    lane = iota((1,1,128),2)
    def save(si, m, inv):
        if "st" in sc:
            C = m.shape[1]
            sc["st"][2*si,:,0:C] = m
            sc["st"][2*si+1,:,0:C] = inv
    bfin = final_bias(v_ref)
    def a0(y, _):
        xp[y+1, 1:17] = x_ref[pl.ds(y*16,16)].astype(BF)
        return 0
    lax.fori_loop(0,16,a0,0)
    def a1(y2, _):
        pieces=[]
        for k in range(4):
            y = y2*4+k
            cols = jnp.zeros((16,16,128),BF)
            for t in range(9):
                w = xp[y+t//3, t%3:t%3+16]
                cols = jnp.where((lane%9==t)&(lane<27), w, cols) if t else jnp.where((lane%9==0)&(lane<27), w, jnp.zeros_like(w))
            if "cols" in sc: sc["cols"][pl.ds(y*16,16)] = cols
            pieces.append(cols.reshape(256,128))
        r = nn(jnp.concatenate(pieces,axis=0), win[...]) + vec(v_ref,"b_in",C1)
        top[pl.ds(y2*64,64)] = r.reshape(64,16,128)
        rb = r.astype(BF).reshape(4,8,2,16,128)
        for k in range(4):
            p = y2*4+k+1
            tp[p//2, p%2, 0:8, 1] = rb[k,:,0]
            tp[p//2, p%2, 1:9, 0] = rb[k,:,1]
        return 0
    lax.fori_loop(0,4,a1,0)
    taps=[]
    for t in range(9):
        ty,tx=t//3,t%3
        taps.append(tp[ty//2:ty//2+8, ty%2, tx//2:tx//2+8, tx%2].reshape(1024,128))
    low[...] = (nt(jnp.concatenate(taps,axis=1), wt[:,O_DOWN:O_DOWN+1152]) + vec(v_ref,"b_down")).reshape(64,16,256)
    def norm_act(src, ap, g, s, si):
        m, inv = gn_stats(src, 64, 8, sc["same8"][...])
        save(si, m, inv)
        half = 0.5*inv*vec(v_ref,g)
        shift = 0.5*vec(v_ref,s) - m*half
        for y in range(8):
            h = src[y*8:y*8+8]*half + shift
            ap[y+1,1:9] = (h + h*jnp.tanh(h)).astype(BF)
    def conv3(ap, off):
        return nt(jnp.concatenate([ap[t//3:t//3+8, t%3:t%3+8].reshape(1024,256) for t in range(9)],axis=1), wt[:,off:off+2304])
    norm_act(low,ap,"g1","s1",0)
    emb = nt(feat, wt[:,O_TIME:O_TIME+128]) + vec(v_ref,"b_time")
    mid[...] = (conv3(ap,O_R1) + vec(v_ref,"b_res1")).reshape(64,16,256) + emb
    norm_act(mid,ap2,"g2","s2",1)
    res[...] = low[...] + (conv3(ap2,O_R2) + vec(v_ref,"b_res2")).reshape(64,16,256)
    m, inv = gn_stats(res, 64, 8, sc["same8"][...])
    save(2, m, inv)
    gain = inv*vec(v_ref,"g3")
    nb = (res[...]*gain + (vec(v_ref,"s3") - m*gain)).astype(BF).reshape(1024,256)
    q = nt(nb, wt[:,O_QKV:O_QKV+256]) + vec(v_ref,"b_query")
    k_ = nt(nb, wt[:,O_QKV+256:O_QKV+512])
    v_ = nt(nb, wt[:,O_QKV+512:O_QKV+768])+vec(v_ref,"b_value")
    for i, z in enumerate((q, k_, v_)):
        z = z.astype(BF).astype(F32)
        qkv[2*i] = z[:,0:128]
        qkv[2*i+1] = z[:,128:256]
    def head(j, n):
        return jnp.concatenate([qkv[2*j,pl.ds(n,64,stride=16),:], qkv[2*j+1,pl.ds(n,64,stride=16),:]], axis=1).astype(BF)
    s = jnp.concatenate([nt(head(0,n), head(1,n)) for n in range(N)], axis=0)*(C2**-0.5)
    e = jnp.exp(s - jnp.max(s,axis=1,keepdims=True))
    p = (e/jnp.sum(e,axis=1,keepdims=True)).astype(BF)
    for n in range(N):
        o = nn(p[64*n:64*n+64], head(2,n)).astype(BF).astype(F32)
        ob[0,pl.ds(n,64,stride=16),:] = o[:,0:128]
        ob[1,pl.ds(n,64,stride=16),:] = o[:,128:256]
    obb = jnp.concatenate([ob[0],ob[1]],axis=1).astype(BF)
    if "obb" in sc: sc["obb"][...] = obb
    att_out = res[...].reshape(1024,256) + (nt(obb, wt[:,O_PROJ:O_PROJ+256]) + vec(v_ref,"b_proj"))
    attb = att_out.astype(BF)
    if "attb" in sc: sc["attb"][...] = attb
    for t in range(0,9,2):
        k = min(2, 9-t)
        r = nt(attb, wup[t:t+k].reshape(128*k,256))
        for i in range(k):
            yp[t+i,1:9,1:9] = r[:,128*i:128*i+128].reshape(8,8,16,128)
    def u(i,_):
        for a in range(2):
            for b in range(2):
                acc=None
                for t in range(9):
                    r,c=t//3-1,t%3-1
                    dr=(a+r)//2; dc=(b+c)//2
                    v=yp[t, i+dr+1, 1+dc:9+dc]
                    acc = v if acc is None else acc+v
                up[i,a,:,b] = acc + vec(v_ref,"b_up",C1) + sc["top6"][i,a,:,b]
        return 0
    lax.fori_loop(0,8,u,0)
    upf = sc["up3"]
    m, inv = gn_stats(upf, 256, 4, sc["same4"][...])
    save(3, m, inv)
    half = 0.5*inv*vec(v_ref,"g4",C1)
    shift = 0.5*vec(v_ref,"s4",C1) - m*half
    def b4(y,_):
        h = upf[pl.ds(y*16,16)]*half + shift
        ep[y+1,1:17] = (h + h*jnp.tanh(h)).astype(BF)
        return 0
    lax.fori_loop(0,16,b4,0,unroll=4)
    def fin(put):
        def f(y4,_):
            cols=jnp.concatenate([ep[pl.ds(y4*8+r,8)].reshape(2304,128) for r in range(3)],axis=1)
            d=nt(cols, wfin[...]).reshape(8,18,16,128)
            put(y4, (d[:,0:16] + pltpu.roll(d[:,1:17].reshape(2048,128),101,1).reshape(8,16,16,128)
                     + pltpu.roll(d[:,2:18].reshape(2048,128),74,1).reshape(8,16,16,128)).reshape(128,16,128) + bfin)
            return 0
        lax.fori_loop(0,2,f,0)
    return fin

def scratch():
    V=pltpu.VMEM
    return dict(wt=V((256,MID),BF), wup=V((9,128,256),BF), win=V((128,128),BF), wfin=V((128,384),BF), wfb=V((128,128),BF), sm=V((128,256),F32), xp=V((18,18,16,128),BF), tp=V((9,2,9,2,16,128),BF),
      top=V((256,16,128),F32), low=V((64,16,256),F32), ap=V((10,10,16,256),BF), mid=V((64,16,256),F32), res=V((64,16,256),F32),
      qkv=V((6,1024,128),F32), ob=V((2,1024,128),F32), yp=V((9,10,10,16,128),F32), up=V((8,2,8,2,16,128),F32), ep=V((18,18,16,128),BF), same8=V((256,256),BF), same4=V((128,128),BF))
KEYS=list(scratch().keys())

def zero_borders(sc):
    for k in ("xp","ep","tp","ap","ap2"):
        if k in sc: sc[k][...] = jnp.zeros(sc[k].shape, sc[k].dtype)
    yp = sc["yp"]
    edge = jnp.zeros((9,10,16,128), F32)
    for k in (0,9):
        yp[:,k] = edge
        yp[:,:,k] = edge
    for k, C, per in (("same8",256,8), ("same4",128,4)):
        sc[k][...] = one_hot(iota((C,C),0)//per == iota((C,C),1)//per)

def views(sc):
    sc=dict(sc)
    sc["top6"]=sc["top"].reshape(8,2,8,2,16,128)
    sc["up3"]=sc["up"].reshape(256,16,128)
    return sc

def teacher_call(D, cnt, x, feat, ce, cl, tc, nc, tg):
    def kern(cnt_ref, x_ref, feat_ref, ce_ref, cl_ref, tc_ref, nc_ref, tg_ref, out_ref, *scr):
        sc = views(dict(zip(KEYS, scr)))
        zero_borders(sc)
        prep(tg_ref, *(sc[k] for k in WKEYS), D)
        out_ref[...] = x_ref[...]
        def step(j, _):
            fin = net(out_ref, feat_ref[j], sc["wt"], sc["wup"], sc["win"], sc["wfin"], sc["sm"], sc)
            ce_, cl_ = ce_ref[j], cl_ref[j]
            def put(y4, e):
                out_ref[pl.ds(y4*128,128)] = ce_*e + cl_*out_ref[pl.ds(y4*128,128)]
            fin(put)
            return 0
        lax.fori_loop(0, cnt_ref[0], step, 0)
        def tgt(i, _):
            out_ref[pl.ds(i*16,16)] = tc_ref[...]*out_ref[pl.ds(i*16,16)] + nc_ref[...]*x_ref[pl.ds(i*16,16)]
            return 0
        lax.fori_loop(0, 16, tgt, 0)
    vm = pl.BlockSpec(memory_space=pltpu.VMEM)
    return pl.pallas_call(kern, out_shape=jax.ShapeDtypeStruct((256,16,128),F32),
        in_specs=[pl.BlockSpec(memory_space=pltpu.SMEM)]+[vm]*7, out_specs=vm, scratch_shapes=list(scratch().values()), name="teacher_steps",
        compiler_params=pltpu.CompilerParams(vmem_limit_bytes=60<<20))(cnt, x, feat, ce, cl, tc, nc, tg)

WKEYS = ["wt","wup","win","wfin","wfb","sm"]
RES = ["wt","wup","wfb","sm","tp","low","ap","mid","res","qkv","up"]
def student_call(D, x, tgt, snr, feat, tg):
    vm=pl.BlockSpec(memory_space=pltpu.VMEM)
    sh=scratch()
    extra=dict(st=pltpu.VMEM((8,16,256),F32),cols=pltpu.VMEM((256,16,128),BF),attb=pltpu.VMEM((1024,256),BF),obb=pltpu.VMEM((1024,256),BF),ap2=pltpu.VMEM((10,10,16,256),BF))
    outs={k:sh[k] for k in RES}; outs.update(extra)
    scr={k:v for k,v in sh.items() if k not in outs}
    ok,sk=list(outs),list(scr)
    def kern(x_ref,t_ref,snr_ref,feat_ref,tg_ref,out_ref,sum_ref,*refs):
        sc=views(dict(zip(ok+sk,refs)))
        zero_borders(sc)
        prep(tg_ref,*(sc[k] for k in WKEYS),D)
        fin=net(x_ref,feat_ref[...],sc["wt"],sc["wup"],sc["win"],sc["wfin"],sc["sm"],sc)
        def put(y4,e): out_ref[pl.ds(y4*128,128)]=e
        fin(put)
        def s(i,c):
            t,o=t_ref[pl.ds(i*16,16)],out_ref[pl.ds(i*16,16)]
            d=o-t
            return tuple(a+jnp.sum(b,axis=0) for a,b in zip(c,(t,t*t,o,o*o,d*d)))
        z=jnp.zeros((N,128),F32)
        r=lax.fori_loop(0,16,s,(z,)*5)
        r=r[:4]+(r[4]*snr_ref[...],)
        sum_ref[...]=jnp.concatenate([jnp.sum(a,axis=0,keepdims=True) for a in r]+[jnp.zeros((3,128),F32)],axis=0)
    res=pl.pallas_call(kern,
        out_shape=(jax.ShapeDtypeStruct((256,16,128),F32),jax.ShapeDtypeStruct((8,128),F32))+tuple(jax.ShapeDtypeStruct(outs[k].shape,outs[k].dtype) for k in ok),
        in_specs=[vm]*5,out_specs=(vm,)*(2+len(ok)),scratch_shapes=[scr[k] for k in sk], name="student_forward",
        compiler_params=pltpu.CompilerParams(vmem_limit_bytes=62<<20))(x,tgt,snr,feat,tg)
    return res[0],res[1],dict(zip(ok,res[2:]))

MESH = pl.DeviceIdType.MESH

def place():
    dp = lax.axis_index("dp")
    return dp // 4, dp // 2 % 2, dp % 2, lax.axis_index("mp")

def peer(z, y, x, c):
    return {"dp": z*4 + y*2 + x, "mp": c}

def greet(peers):
    barrier = pltpu.get_barrier_semaphore()
    for p in peers:
        pl.semaphore_signal(barrier, inc=1, device_id=p, device_id_type=MESH)
    pl.semaphore_wait(barrier, len(peers))

def partners():
    z, y, x, c = place()
    return [peer(z,y,x,1-c), peer(z,y,1-x,c), peer(z,1-y,x,c)] + [peer((z+o)%4,y,x,c) for o in (1,2,3)]

def gather_copies(s, p, streams, in_ref, out_ref, send, recv):
    z, y, x, c = place()
    wide = in_ref.shape[1] // streams
    all_, lo, hi = pl.ds(s*wide, wide), pl.ds(s*wide, wide//2), pl.ds(s*wide + wide//2, wide//2)
    to_x, to_y = peer(z,y,1-x,c), peer(z,1-y,x,c)
    if p == 0:
        return [pltpu.make_async_remote_copy(in_ref.at[:,all_], out_ref.at[z,y,x,c,:,all_], send.at[s,o-1], recv.at[s,3-o],
                device_id=peer((z+o)%4,y,x,c), device_id_type=MESH) for o in (2,1,3)]
    if p == 1:
        moves = [(out_ref.at[:,y,x,c,:,lo], to_x, 3), (out_ref.at[:,y,x,c,:,hi], to_y, 4)]
    elif p == 2:
        moves = [(out_ref.at[:,y,:,c,:,lo], to_y, 5), (out_ref.at[:,:,x,c,:,hi], to_x, 6)]
    else:
        moves = [(out_ref.at[:,:,:,c,:,all_], peer(z,y,x,1-c), 7)]
    return [pltpu.make_async_remote_copy(part, part, send.at[s,i], recv.at[s,i], device_id=to, device_id_type=MESH) for part, to, i in moves]

def mix_images(ca_ref, sa_ref, im_ref, ns_ref, x_ref, flat, planes):
    flat[...] = jnp.zeros(flat.shape, F32)
    for n in range(N):
        for c in range(3):
            flat[16*n:16*n+16, 16*c:16*c+16] = ca_ref[n]*im_ref[n,c] + sa_ref[n]*ns_ref[n,c]
    parts = split3(flat[...])
    k, l = iota((128,512),0), iota((128,512),1)
    for q in range(4):
        r = nn(parts, one_hot((l % 128 < 27) & (k == 16*(l % 128 // 9) + 4*q + l // 128)))
        r = r[0:256] + r[256:512] + r[512:768]
        for i in range(4): planes[4*q+i] = r[:,128*i:128*i+128]
    for y in range(SIDE):
        for x in range(SIDE):
            x_ref[SIDE*y+x] = planes[x,pl.ds(y,N,stride=SIDE),:]

def gather_kernel(streams, ca_ref, sa_ref, im_ref, ns_ref, in_ref, out_ref, x_ref, send, recv, keep, flat, planes):
    z, y, x, c = place()
    greet(partners())
    own = pltpu.make_async_copy(in_ref, out_ref.at[z,y,x,c], keep)
    own.start()
    live = {(s,p): gather_copies(s,p,streams,in_ref,out_ref,send,recv) for s in range(streams) for p in range(4)}
    for s in range(streams):
        for d in live[s,0]: d.start()
    mix_images(ca_ref, sa_ref, im_ref, ns_ref, x_ref, flat, planes)
    own.wait()
    for step in range(streams + 3):
        for s in range(streams):
            p = step - s
            if 0 <= p <= 3:
                for d in live[s,p]: d.wait_recv()
                if p < 3:
                    for d in live[s,p+1]: d.start()
    for ds in live.values():
        for d in ds: d.wait_send()

def gather_call(block, ca, sa, images, noise, cid, streams=4):
    rows, wide = block.shape
    any_, vm, sm = (pl.BlockSpec(memory_space=m) for m in (pl.ANY, pltpu.VMEM, pltpu.SMEM))
    out, noisy = pl.pallas_call(lambda *r: gather_kernel(streams, *r),
        out_shape=(jax.ShapeDtypeStruct((4,2,2,2,rows,wide), block.dtype), jax.ShapeDtypeStruct((256,N,128), F32)),
        in_specs=[sm,sm,vm,vm,any_], out_specs=(any_,vm), name="gather_columns",
        scratch_shapes=[pltpu.SemaphoreType.DMA((streams,8)), pltpu.SemaphoreType.DMA((streams,8)), pltpu.SemaphoreType.DMA,
                        pltpu.VMEM((256,128),F32), pltpu.VMEM((16,256,128),F32)],
        compiler_params=pltpu.CompilerParams(collective_id=cid, has_side_effects=True, vmem_limit_bytes=24<<20))(
            ca, sa, images.transpose(0,3,1,2), noise.transpose(0,3,1,2), block)
    return out.reshape(32*rows, wide), noisy

def sum_kernel(in_ref, out_ref, box, send, recv):
    z, y, x, c = place()
    hops = [peer(z,y,x,1-c), peer(z,y,1-x,c), peer(z,1-y,x,c), peer(z+1-2*(z%2),y,x,c), peer((z+2)%4,y,x,c)]
    out_ref[...] = in_ref[...]
    for k, to in enumerate(hops):
        box[k] = out_ref[...]
        d = pltpu.make_async_remote_copy(box.at[k], box.at[5+k], send.at[k], recv.at[k], device_id=to, device_id_type=MESH)
        d.start()
        d.wait()
        out_ref[...] += box[5+k]

STREAMS = 8

def row_of(r):
    return 128*(r//128) + 32*(r//8%4) + 8*(r//32%4) + 4*(r%2) + 2*(r//2%2) + r//4%2

def scatter_scratch():
    V = pltpu.VMEM
    sc = {}
    for s in range(STREAMS):
        sc[f"c{s}"] = V((2,2,2,4,4,8,128),F32)
        sc[f"h{s}"] = V((2,2,4,4,8,128),F32)
        sc[f"q{s}"] = V((2,4,4,8,128),F32)
        sc[f"z{s}"] = V((3,2,4,8,128),F32)
    sc["ssem"] = pltpu.SemaphoreType.DMA((STREAMS,8))
    sc["rsem"] = pltpu.SemaphoreType.DMA((STREAMS,8))
    return sc

def scatter_steps(g_ref, out_ref, sc):
    z, y, x, c = place()
    send, recv = sc["ssem"], sc["rsem"]
    live = {}
    def bufs(s): return tuple(sc[f"{k}{s}"] for k in "chqz")
    def copies(s, p):
        r0, r1, r2, r3 = bufs(s)
        to_x, to_y = peer(z,y,1-x,c), peer(z,1-y,x,c)
        if p == 0:
            moves = [(g_ref.at[s,:,1-c], r0, peer(z,y,x,1-c), 0, 0)]
        elif p == 1:
            moves = [(r0.at[0,1-x], r1.at[0], to_x, 1, 1), (r0.at[1,:,1-y], r1.at[1], to_y, 2, 2)]
        elif p == 2:
            moves = [(r1.at[0,1-y], r2.at[0], to_y, 3, 3), (r1.at[1,1-x], r2.at[1], to_x, 4, 4)]
        else:
            moves = [(r2.at[:,(z+o)%4], r3.at[3-o], peer((z+o)%4,y,x,c), 4+o, 8-o) for o in (2,1,3)]
        return [pltpu.make_async_remote_copy(src, dst, send.at[s,i], recv.at[s,k], device_id=to, device_id_type=MESH) for src, dst, to, i, k in moves]
    def add(s, p):
        r0, r1, r2, r3 = bufs(s)
        if p == 0:
            for h in range(2):
                for i in range(2):
                    r0[h,i] += g_ref[s,h,c,i]
        elif p == 1:
            r1[0] += r0[0,x]
            r1[1] += r0[1,:,y]
        elif p == 2:
            r2[0] += r1[0,y]
            r2[1] += r1[1,x]
        else:
            total = r2[:,z] + r3[0] + r3[1] + r3[2]
            for k in range(8):
                out_ref[:,:,STORED[8*s+k]] = total[:,:,k]
    def advance(s, p):
        if p:
            for d in live[s,p-1]: d.wait_recv()
            add(s, p-1)
        if p < 4:
            live[s,p] = copies(s,p)
            for d in live[s,p]: d.start()
    def finish():
        for ds in live.values():
            for d in ds: d.wait_send()
    return advance, finish

def tn(a, b): return lax.dot_general(a, b, (((0,),(0,)),((),())), preferred_element_type=F32)

def bwd_kernel(x_refs, o_refs, sc):
    X, S = x_refs, sc
    (G,) = o_refs
    sg, sn_total = S["sg"], X["total"]
    v_ref, wt, wup, st = X["v"], X["wt"], X["wup"], X["st"]
    gp18, gcols, big, ep, dp, s_hi, s_lo, gp, da, gres, gqkv, gmx = (S[k] for k in ("gp18","gcols","big","ep","dp","s_hi","s_lo","gp","da","gres","gqkv","gmx"))
    lane = iota((1,1,128),2)
    for k, C, per in (("same8",256,8), ("same4",128,4)):
        S[k][...] = one_hot(iota((C,C),0)//per == iota((C,C),1)//per)
    for k in ("gp18","dp","gp"):
        S[k][...] = jnp.zeros(S[k].shape, S[k].dtype)
    sg[...] = jnp.zeros((128,256),F32)
    def put_block(b, val):
        sg[b//2:b//2+1, 128*(b%2):128*(b%2)+128] = val
    def put_vec(name, val, C=C2):
        at, wide = BLOCK[name]
        for k in range(wide):
            put_block(at+k, val[:, 128*k:128*k+128])
    def rowsum(a): return jnp.sum(a, axis=0, keepdims=True)
    step, near = S["step"], S["near"]
    def put_g(val, col, row0=0):
        rows, width = val.shape
        col = 128*next(GROUP[o] + (col-o)//128 for o in sorted(GROUP, reverse=True) if col >= o)
        for c in range(width//128):
            at = col//128+c
            for r in range(row0, row0+rows, 8):
                if near: to = pl.ds(2048*(at//8) + 1024*(r//128) + 32*(r//32%4) + 8*(r//8%4) + at%8, 8, stride=128)
                else: to = pl.ds(64*r+at, 8, stride=64)
                G[to,:] = val[r-row0:r-row0+8, c*128:c*128+128]
    pm = S["pm"]
    pm[...] = one_hot(iota((256,256),1) == (row_of(iota((256,256),0)) if near else iota((256,256),0)))
    def turn(g): return nt(pm[...], g).astype(BF)
    pixels = 256.0*sn_total
    so = X["stat"][...]
    mt, mo = so[0:1]/pixels, so[2:3]/pixels
    vt_, vo = so[1:2]/pixels-mt*mt, so[3:4]/pixels-mo*mo
    cb = 4.0*(vo-vt_)/pixels
    ca = 2.0*(mo-mt)/pixels-cb*mo
    sn = X["snr"][...]*(2.0/(768.0*sn_total))
    acc=jnp.zeros((N,128),F32)
    def g0(y,acc):
        o=X["out"][pl.ds(y*16,16)]
        go = sn*(o-X["tgt"][pl.ds(y*16,16)]) + ca + cb*o
        gp18[y+1,1:17]=go.astype(BF)
        return acc+jnp.sum(go,axis=0)
    acc=lax.fori_loop(0,16,g0,acc)
    acc=rowsum(acc)
    lane2=iota((1,128),1)
    put_block(84, sum(jnp.where(lane2==c, jnp.sum(jnp.where(lane2==9*c,acc,0.0),axis=1,keepdims=True),0.0) for c in range(3)))
    def g1(y,_):
        for t in range(9):
            w = gp18[y+2-t//3, 2-t%3:18-t%3]
            cols = jnp.where((lane%9==t)&(lane<27), w, cols) if t else jnp.where((lane%9==0)&(lane<27), w, jnp.zeros_like(w))
        gcols[pl.ds(y*16,16)] = cols
        return 0
    lax.fori_loop(0,16,g1,0)
    big[...] = nn(gcols[...].reshape(4096,128), X["wfb"][...]).reshape(256,16,128)
    def gn_bwd(src, dref, si, gname, sname, C, per, same, rows, k, act_put, dx_put, silu=True):
        m, inv = st[2*si,:,0:C], st[2*si+1,:,0:C]
        g, s = vec(v_ref,gname,C), vec(v_ref,sname,C)
        w = 512//C
        zero = jnp.zeros((w,N,C),F32)
        def pick(v): return jnp.sum(v.reshape((-1,w)+v.shape[1:]),axis=0)
        def p1(y,c):
            A,B=c
            xh=(src[pl.ds(y*k,k)]-m)*inv
            d=dref[pl.ds(y*k,k)]
            if silu:
                h=xh*(0.5*g)+0.5*s
                th=jnp.tanh(h); sg=0.5+0.5*th; act=h+h*th
                act_put(y,act.astype(BF))
                d=d*(sg+act*(1.0-sg))
                dref[pl.ds(y*k,k)]=d
            else:
                act_put(y,(xh*g+s).astype(BF))
            return A+pick(d), B+pick(d*xh)
        A,B=lax.fori_loop(0,rows,p1,(zero,zero),unroll=4)
        A,B=jnp.sum(A,axis=0),jnp.sum(B,axis=0)
        put_vec(gname,rowsum(B),C); put_vec(sname,rowsum(A),C)
        cnt=1.0/(per*rows*k)
        ga=group_sum(g*A,same)*cnt; gb=group_sum(g*B,same)*cnt
        ig=inv*g; ib=inv*inv*gb; ic=m*ib-inv*ga
        def p2(y,acc):
            dx=ig*dref[pl.ds(y*k,k)]-ib*src[pl.ds(y*k,k)]+ic
            return acc+pick(dx_put(y,dx))
        return lambda: jnp.sum(lax.fori_loop(0,rows,p2,zero,unroll=4),axis=0)
    def act4(y,a): ep[pl.ds(y*16,16)]=a
    def dx4(y,dx):
        big[pl.ds(y*16,16)]=dx
        b=dx.astype(BF).reshape(8,2,16,128)
        p=y+1
        dp[p//2,p%2,0:8,1]=b[:,0]
        dp[p//2,p%2,1:9,0]=b[:,1]
        return dx
    fin=gn_bwd(X["up"].reshape(256,16,128),big,3,"g4","s4",128,4,S["same4"][...],16,16,act4,dx4)
    dwf = tn(gcols[...].reshape(4096,128), ep[...].reshape(4096,128))
    flat = jnp.zeros((9,384),F32)
    for c in range(3):
        p3 = one_hot(iota((128,384),1) == 3*iota((128,384),0) + c)
        piece = dwf[9*c:9*c+9]
        hi = piece.astype(BF); rest = piece-hi.astype(F32)
        mi = rest.astype(BF); lo = (rest-mi.astype(F32)).astype(BF)
        flat += nn(hi,p3)+nn(mi,p3)+nn(lo,p3)
    for t in range(9):
        for h in range(3):
            put_block(27+3*t+h, flat[t:t+1,128*h:128*h+128])
    put_vec("b_up",rowsum(fin()),128)
    PAIR={-1:((1,0),(1,1)),0:((0,1),(1,0)),1:((0,0),(0,1))}
    def su(i,_):
        for r in (-1,0,1):
            (ra,pa),(rb,pb)=PAIR[r]
            V={}
            for cp in range(2):
                V[cp]=dp[i+ra,pa,:,cp].astype(F32)+dp[i+rb,pb,:,cp].astype(F32)
            for c in (-1,0,1):
                (ca_,qa),(cb_,qb)=PAIR[c]
                s=V[qa][ca_:ca_+8]+V[qb][cb_:cb_+8]
                t=(r+1)*3+c+1
                hi=s.astype(BF)
                s_hi[t,pl.ds(i*8,8)]=hi
                s_lo[t,pl.ds(i*8,8)]=(s-hi.astype(F32)).astype(BF)
        return 0
    lax.fori_loop(0,8,su,0)
    cat=lambda ref: jnp.concatenate([ref[t].reshape(1024,128) for t in range(9)],axis=1)
    wu=wup[...].reshape(1152,256)
    gatt=nn(cat(s_hi),wu)+nn(cat(s_lo),wu)
    gres[...]=gatt.reshape(64,16,256)
    put_vec("b_proj",rowsum(gatt))
    gab=gatt.astype(BF)
    attb=X["attb"][...]
    kk, ci = iota((256,256),1), iota((256,256),0)
    peo=one_hot(ci == 2*(kk % 128) + kk // 128)
    aeo=nn(attb,peo).astype(BF)
    for t in range(9):
        hi,lo=[nt(pm[0:128,0:128],v[t].reshape(1024,128)).astype(BF) for v in (s_hi,s_lo)]
        r=nn(hi,aeo)+nn(lo,aeo)
        put_g(r[:,0:128],O_UP+t*128,0); put_g(r[:,128:256],O_UP+t*128,128)
    step((0,0))
    obb=X["ob"][...]
    put_g(nn(turn(gab),obb),O_PROJ)
    gm=nn(gab,wt[:,O_PROJ:O_PROJ+256]).astype(BF).astype(F32)
    gmx[0]=gm[:,0:128]; gmx[1]=gm[:,128:256]
    qkv=X["qkv"]
    sc_=C2**-0.5
    def pair(ref,j,n): return jnp.concatenate([ref[2*j,pl.ds(n,64,stride=16),:],ref[2*j+1,pl.ds(n,64,stride=16),:]],axis=1).astype(BF)
    s=jnp.concatenate([nt(pair(qkv,0,n),pair(qkv,1,n)) for n in range(N)],axis=0)*sc_
    e=jnp.exp(s-jnp.max(s,axis=1,keepdims=True))
    p=e/jnp.sum(e,axis=1,keepdims=True)
    ga=jnp.concatenate([nt(pair(gmx,0,n),pair(qkv,2,n)) for n in range(N)],axis=0)
    gs=(p*(ga-jnp.sum(ga*p,axis=1,keepdims=True))).astype(BF)
    pb=p.astype(BF)
    for n in range(N):
        gsn,pn=gs[64*n:64*n+64],pb[64*n:64*n+64]
        for j,o in enumerate((nn(gsn,pair(qkv,1,n))*sc_, tn(gsn,pair(qkv,0,n))*sc_, tn(pn,pair(gmx,0,n)))):
            o=o.astype(BF).astype(F32)
            gqkv[2*j,pl.ds(n,64,stride=16),:]=o[:,0:128]
            gqkv[2*j+1,pl.ds(n,64,stride=16),:]=o[:,128:256]
    step((0,1))
    gq=[jnp.concatenate([gqkv[2*j],gqkv[2*j+1]],axis=1) for j in range(3)]
    put_vec("b_query",rowsum(gq[0])); put_vec("b_value",rowsum(gq[2]))
    gqb=[g.astype(BF) for g in gq]
    da[...]=nn(jnp.concatenate(gqb,axis=1),jnp.concatenate([wt[:,O_QKV+256*j:O_QKV+256*j+256] for j in range(3)],axis=0)).reshape(64,16,256)
    nbs=S["nb"]
    def act3(y,a): nbs[pl.ds(y*8,8)]=a
    def dx3(y,dx):
        z=gres[pl.ds(y*8,8)]+dx
        gres[pl.ds(y*8,8)]=z
        gp[y+1,1:9]=z.astype(BF)
        return z
    fin=gn_bwd(X["res"],da,2,"g3","s3",256,8,S["same8"][...],8,8,act3,dx3,silu=False)
    nb=nbs[...].reshape(1024,256)
    for j in range(3): put_g(nn(turn(gqb[j]),nb),O_QKV+256*j)
    step((1,0))
    put_vec("b_res2",rowsum(fin()))
    step((0,2))
    def conv_dgrad(off):
        return nn(jnp.concatenate([gp[2-t//3:10-t//3,2-t%3:10-t%3].reshape(1024,256) for t in range(9)],axis=1),
                  jnp.concatenate([wt[:,off+256*t:off+256*t+256] for t in range(9)],axis=0))
    def conv_wgrad(g,ap,off,steps):
        gt=turn(g)
        for t in range(9):
            put_g(nn(gt,ap[t//3:t//3+8,t%3:t%3+8].reshape(1024,256)),off+256*t)
            step(*steps.get(t,()))
    def act_(y,a): pass
    conv_wgrad(gp[1:9,1:9].reshape(1024,256),X["ap2"],O_R2,{3:((2,0),(1,1)),7:((3,0),),8:((0,3),)})
    da[...]=conv_dgrad(O_R2).reshape(64,16,256)
    step((2,1),(1,2))
    def dxm(y,dx):
        gp[y+1,1:9]=dx.astype(BF)
        return dx
    fin=gn_bwd(X["mid"],da,1,"g2","s2",256,8,S["same8"][...],8,8,act_,dxm)
    step((3,1),(0,4))
    gemb=fin()
    step((2,2),(1,3))
    put_vec("b_time",rowsum(gemb)); put_vec("b_res1",rowsum(gemb))
    put_g(nn(turn(gemb.astype(BF)),X["feat"][...]),O_TIME)
    conv_wgrad(gp[1:9,1:9].reshape(1024,256),X["ap"],O_R1,{1:((4,0),),3:((3,2),),5:((5,0),),8:((2,3),(4,1))})
    da[...]=conv_dgrad(O_R1).reshape(64,16,256)
    step((5,1),(4,2),(3,3),(1,4))
    def dxl(y,dx):
        z=gres[pl.ds(y*8,8)]+dx
        gp[y+1,1:9]=z.astype(BF)
        return z
    fin=gn_bwd(X["low"],da,0,"g1","s1",256,8,S["same8"][...],8,8,act_,dxl)
    step((5,2),(2,4))
    put_vec("b_down",rowsum(fin()))
    step((4,3),(3,4))
    glb=gp[1:9,1:9].reshape(1024,256)
    glt=turn(glb)
    tp=X["tp"]
    for t in range(9):
        ty,tx=t//3,t%3
        put_g(nn(glt,tp[ty//2:ty//2+8,ty%2,tx//2:tx//2+8,tx%2].reshape(1024,128)),O_DOWN+128*t)
        step(*{1:((6,0),),8:((5,3),)}.get(t,()))
    big6=big.reshape(8,2,8,2,16,128)
    dt6=S["dt"].reshape(8,2,8,2,16,128)
    SRC={0:((1,0),),1:((0,1),(2,0))}
    total=jnp.zeros((N,128),F32)
    for a in range(2):
        for b in range(2):
            taps=[(3*ty+tx,1+oy,1+ox) for ty,oy in SRC[a] for tx,ox in SRC[b]]
            z=nn(jnp.concatenate([gp[oy:oy+8,ox:ox+8].reshape(1024,256) for _,oy,ox in taps],axis=1),
                 jnp.concatenate([wt[:,O_DOWN+128*t:O_DOWN+128*t+128] for t,_,_ in taps],axis=0)).reshape(8,8,16,128)
            z=z+big6[:,a,:,b]
            dt6[:,a,:,b]=z.astype(BF)
            total=total+jnp.sum(jnp.sum(z,axis=0),axis=0)
    put_vec("b_in",rowsum(total),128)
    step((6,1),(4,4))
    dwi=tn(X["cols"][...].reshape(4096,128),S["dt"][...].reshape(4096,128))
    for k in range(27):
        put_block(k, dwi[9*(k%3)+k//3:9*(k%3)+k//3+1])
    kept = nt(split3(sg[...]), pm[...])
    put_g((kept[0:128]+kept[128:256]+kept[256:384]).T, MID)

def bwd_scratch():
    V=pltpu.VMEM
    return dict(gp18=V((18,18,16,128),BF),gcols=V((256,16,128),BF),big=V((256,16,128),F32),ep=V((256,16,128),BF),dp=V((9,2,9,2,16,128),BF),
      s_hi=V((9,64,16,128),BF),s_lo=V((9,64,16,128),BF),gp=V((10,10,16,256),BF),da=V((64,16,256),F32),gres=V((64,16,256),F32),
      gqkv=V((6,1024,128),F32),gmx=V((2,1024,128),F32),nb=V((64,16,256),BF),dt=V((256,16,128),BF),sg=V((128,256),F32),pm=V((256,256),BF),same8=V((256,256),BF),same4=V((128,128),BF))
BIN=["out","tgt","snr","stat","cols","tp","low","mid","res","qkv","obb","attb","up","st","feat","wt","wup","wfb","sm","ap","ap2"]
GROUP = {O_UP:0, O_PROJ:9, O_QKV:11, O_R2:17, O_TIME:35, O_R1:36, O_DOWN:54, MID:63}
STORED = [next(at//128 + i - g for at, g in sorted(GROUP.items(), key=lambda e: -e[1]) if i >= g) for i in range(64)]
def bwd_call(ins, total, near):
    vm=pl.BlockSpec(memory_space=pltpu.VMEM)
    sc=bwd_scratch()
    if near:
        sc.update(box=pltpu.VMEM((10,8,128),F32), send=pltpu.SemaphoreType.DMA((5,)), recv=pltpu.SemaphoreType.DMA((5,)), g=pltpu.VMEM((256*64,128),F32), own=pltpu.VMEM((8,64,128),F32))
        sc.update(scatter_scratch())
    keys=list(sc)
    def k(*refs):
        a=dict(zip(BIN,refs[:len(BIN)])); a["v"]=a["sm"]; a["ob"]=a["obb"]; a["total"]=float(total)
        s=dict(zip(keys,refs[len(BIN)+2:]))
        grad_ref,sum_ref=refs[len(BIN):len(BIN)+2]
        if not near:
            sum_ref[...]=a["stat"][...]
            s["step"],s["near"]=(lambda *_: None),False
            a["stat"]=sum_ref
            bwd_kernel(a,(grad_ref,),s)
            return
        greet(partners())
        sum_kernel(a["stat"],sum_ref,s["box"],s["send"],s["recv"])
        a["stat"]=sum_ref
        own=s["own"]
        advance,finish=scatter_steps(s["g"].reshape(8,2,2,2,2,4,4,8,128),own.reshape(2,4,64,128),s)
        def step(*moves):
            for m in moves: advance(*m)
        s["step"],s["near"]=step,True
        bwd_kernel(a,(s["g"],),s)
        step((7,0),(6,2),(5,4),(7,1),(6,3),(7,2))
        kq,lq=iota((768,768),0),iota((768,768),1)
        at=O_QKV//128
        rows=nn(split3(jnp.concatenate([own[:,at+i] for i in range(6)],axis=1)),one_hot(lq==3*(kq%256)+kq//256))
        rows=rows[0:8]+rows[8:16]+rows[16:24]
        for i in range(6): own[:,at+i]=rows[:,128*i:128*i+128]
        step((6,4),(7,3),(7,4))
        finish()
        for hi in range(2):
            shift=14-hi
            src=own[4-4*hi:8-4*hi]
            mid=pltpu.roll(src.reshape(256,128),shift,1).reshape(4,64,128)
            rest=own[4*hi:4*hi+4,63:64]
            for k in range(64):
                before=rest[:,0] if k==0 else mid[:,k-1]
                after=rest[:,0] if k==63 else mid[:,k]
                grad_ref[4*hi:4*hi+4,128*k:128*k+128]=jnp.where(iota((1,128),1)<shift,before,after)
    extra=dict(collective_id=2, has_side_effects=True) if near else {}
    shape=(8,MID+128) if near else (256*64,128)
    return pl.pallas_call(k,out_shape=(jax.ShapeDtypeStruct(shape,F32),jax.ShapeDtypeStruct((8,128),F32)),
        in_specs=[vm]*len(BIN),out_specs=(vm,vm),scratch_shapes=list(sc.values()), name="student_backward",
        compiler_params=pltpu.CompilerParams(vmem_limit_bytes=63<<20, **extra))(*[ins[k] for k in BIN])

def segments():
    matrices = [("w_in", 27, C1), ("w_down", 9 * C1, C2), ("w_res1", 9 * C2, C2), ("w_res2", 9 * C2, C2), ("w_time", C1, C2),
                ("w_qkv", C2, 3 * C2), ("w_proj", C2, C2), ("w_up", 9 * C2, C1), ("w_final", 9 * C1, 3)]
    vectors = [("g1", C2), ("s1", C2), ("g2", C2), ("s2", C2), ("g3", C2), ("s3", C2), ("g4", C1), ("s4", C1), ("b_in", C1),
               ("b_down", C2), ("b_res1", C2), ("b_res2", C2), ("b_time", C2), ("b_query", C2), ("b_value", C2), ("b_proj", C2),
               ("b_up", C1), ("b_final", 3)]
    listing, cursor = [], 0
    for name, height, breadth in matrices:
        listing.append((name, cursor, (height, breadth), "matrix"))
        cursor += height * breadth
    for name, length in vectors:
        listing.append((name, cursor, (length,), "gain" if name[0] != "b" else "bias"))
        cursor += length
    return listing

def rates(position):
    learn = jnp.zeros(position.shape, F32)
    decay = jnp.zeros(position.shape, F32)
    for name, offset, shape, kind in segments():
        inside = (position >= offset) & (position < offset + math.prod(shape))
        if kind == "matrix":
            spread = shape[0] ** (-0.5) * ((SIDE * SIDE / 4.0) ** 0.5 if name == "w_proj" else 1.0)
            learn = jnp.where(inside, 0.5 * spread, learn)
            decay = jnp.where(inside, 0.01, decay)
        elif kind == "gain":
            learn = jnp.where(inside, 0.2, learn)
        else:
            learn = jnp.where(inside, 0.05, learn)
    return learn, decay

def angle_of(step):
    return 0.1 + 1.35 * step.astype(F32) / TGRID

def time_features(step):
    half = C1 // 2
    freqs = jnp.exp(-math.log(1000.0) * jnp.arange(half).astype(F32) / half)
    phases = step.astype(F32)[..., None] * freqs
    return jnp.concatenate([jnp.sin(phases), jnp.cos(phases)], axis=-1)

def to_columns(shard, R):
    cols = shard.reshape(-1, R).T
    return jnp.pad(cols, ((0,0),(0,MID+128-cols.shape[1])))

def from_columns(cols, start, D, L):
    R = 256 // D
    body = R * MID
    def piece(at, width): return cols[:, 128*GROUP[at]:128*GROUP[at]+width]
    q = piece(O_QKV,768).reshape(R,3,256).transpose(0,2,1).reshape(R,768)
    cols = jnp.concatenate([piece(O_DOWN,1152), piece(O_R1,2304), piece(O_R2,2304), piece(O_TIME,128), q, piece(O_PROJ,256), piece(O_UP,1152),
                            piece(MID,L//R-MID)], axis=1)
    flat = cols.T.reshape(-1)
    if HEAD % D == 0:
        return jnp.concatenate([flat[body:body+start], flat[:body], flat[body+start:]])
    rest = flat[body:]
    at = jnp.arange(L)
    mid = lax.dynamic_update_slice(jnp.zeros((L,), F32), flat[:body], (start,))
    low = jnp.pad(rest, (0, body)); high = jnp.pad(rest, (body, 0))
    return jnp.where(at < start, low, jnp.where(at < start + body, mid, high))

def lanes(images):
    v = jnp.repeat(images.transpose(1,2,0,3).reshape(256,N,3), 9, axis=2)
    return jnp.pad(v, ((0,0),(0,0),(0,101)))

def local(images, noise, timestep, stride, bucket, steps_table, master, first_moment, second_moment, teacher, step_count):
    axes = ("dp", "mp")
    D = lax.axis_size("dp") * lax.axis_size("mp")
    me = lax.axis_index(axes)
    R, L = 256 // D, master.shape[0]
    start = HEAD // D if HEAD % D == 0 else (HEAD - me + D - 1) // D
    near = lax.axis_size("dp") == 16 and lax.axis_size("mp") == 2
    teacher_cols = to_columns(teacher, R)
    angle = angle_of(timestep)
    if near:
        teacher_all, noisy = gather_call(teacher_cols, jnp.cos(angle), jnp.sin(angle), images, noise, 1)
    else:
        teacher_all = lax.all_gather(teacher_cols, axes, axis=0, tiled=True)
        noisy = lanes(jnp.cos(angle)[:,None,None,None] * images + jnp.sin(angle)[:,None,None,None] * noise)
    student_all = lax.all_gather(to_columns(master.astype(BF), R), axes, axis=0, tiled=True)
    wide = lambda v: jnp.where(jnp.arange(128) < 27, v[..., None], 0.0)
    picked = jnp.sum(jnp.where(jnp.arange(steps_table.shape[0]) == bucket[0], steps_table, 0))
    turn = jnp.arange(KMAX)[:, None]
    current = timestep[None] - turn * stride[None]
    later = current - stride[None]
    keep = jnp.sin(angle_of(later)) / jnp.sin(angle_of(current))
    take = jnp.cos(angle_of(later)) - keep * jnp.cos(angle_of(current))
    features = jax.nn.silu(time_features(current)).astype(BF)
    final_t = timestep - picked * stride
    below = jnp.sin(angle - angle_of(final_t))
    target = teacher_call(D, picked.reshape(1), noisy, features, wide(take), wide(keep), wide(jnp.sin(angle)/below),
                          wide(-jnp.sin(angle_of(final_t))/below), teacher_all)
    snr = wide(jnp.maximum(jnp.square(jnp.cos(angle)/jnp.sin(angle)), 1.0))
    out, sums, kept = student_call(D, noisy, target, snr, features[0], student_all)
    if not near:
        sums = lax.psum(sums, axes)
    total = images.shape[0] * D
    grads, sums = bwd_call(dict(kept, out=out, tgt=target, snr=snr, stat=sums, feat=features[0]), total, near)
    pick = sums[:5, 0:27:9]
    mean_t, mean_o = pick[0]/(256*total), pick[2]/(256*total)
    var_t, var_o = pick[1]/(256*total) - jnp.square(mean_t), pick[3]/(256*total) - jnp.square(mean_o)
    loss = jnp.sum(pick[4])/(768*total) + jnp.sum(jnp.square(mean_o-mean_t) + jnp.square(var_o-var_t))
    if near:
        part = grads
    else:
        order = grads.reshape(R, D, MID+128)
        if HEAD % D:
            order = jnp.concatenate([jnp.roll(order[:, :, :MID], HEAD % D, axis=1), order[:, :, MID:]], axis=2)
        part = lax.psum_scatter(order, axes, scatter_dimension=1, tiled=True).reshape(R, MID+128)
    grad = part[:, :L//R].T.reshape(-1) if near else from_columns(part, start, D, L)
    learn, decay = rates(jnp.arange(L, dtype=jnp.int32) * D + me)
    steps_done = step_count[0].astype(F32)
    new_first = 0.5 * first_moment + 0.5 * grad
    new_second = 0.5 * second_moment + 0.5 * jnp.square(grad)
    fix_rate = 1.0 - jnp.power(0.5, steps_done)
    new_master = master - learn * (new_first / fix_rate / (jnp.sqrt(new_second / fix_rate) + 1e-08) + decay * master)
    return loss, new_master, new_first, new_second

def solution(mesh):
    s = P(("dp", "mp"))
    i = P(("dp", "mp"), None, None, None)
    return jax.shard_map(local, mesh=mesh, in_specs=(i, i, s, s, s, P(), s, s, s, s, P()), out_specs=(P(), s, s, s), check_vma=False)
```

```python
import math
import jax
import jax.numpy as jnp
from jax import lax
from jax.experimental import pallas as pl
from jax.experimental.pallas import tpu as pltpu
from jax.sharding import PartitionSpec as P

C1, C2, N = 128, 256, 16
SIDE, TGRID, KMAX = 16, 64, 4
F32, BF = jnp.float32, jnp.bfloat16
O_DOWN, O_R1, O_R2, O_TIME, O_QKV, O_PROJ, O_UP, MID = 0, 1152, 3456, 5760, 5888, 6656, 6912, 8064
HEAD = 3456
BLOCK = {}
_at = 54
for _name, _wide in (("g1",2),("s1",2),("g2",2),("s2",2),("g3",2),("s3",2),("g4",1),("s4",1),("b_in",1),("b_down",2),("b_res1",2),
                     ("b_res2",2),("b_time",2),("b_query",2),("b_value",2),("b_proj",2),("b_up",1),("b_final",1)):
    BLOCK[_name] = (_at, _wide)
    _at += _wide

def iota(shape, d): return lax.broadcasted_iota(jnp.int32, shape, d)

def nt(a, b): return lax.dot_general(a, b, (((1,),(1,)),((),())), preferred_element_type=F32)
def nn(a, b): return lax.dot_general(a, b, (((1,),(0,)),((),())), preferred_element_type=F32)

def one_hot(cond): return jnp.where(cond, 1.0, 0.0).astype(BF)

def split3(v):
    hi = v.astype(BF); r = v - hi.astype(F32)
    mid = r.astype(BF); lo = (r - mid.astype(F32)).astype(BF)
    return jnp.concatenate([hi, mid, lo], axis=0)

def pile(v, k):
    return jnp.sum(jnp.sum(v.reshape((-1, k) + v.shape[1:]), axis=0), axis=0)

def group_sum(v, same):
    r = nn(split3(v), same)
    return r[0:N] + r[N:2*N] + r[2*N:3*N]

def prep(tg_ref, wt_ref, wup_ref, win_ref, wfin_ref, wfb_ref, sm_ref, D):
    R = 256 // D
    row, rho = iota((256,256),1), iota((256,256),0)
    perm = one_hot(rho == row // R + D * (row % R))
    CH = 1152
    for c in range(7):
        wt_ref[0:128, c*CH:(c+1)*CH] = nn(perm[128:256], tg_ref[:, 13+c*CH:13+(c+1)*CH]).astype(BF)
        wt_ref[128:256, c*CH:(c+1)*CH] = nn(perm[0:128], tg_ref[:, 14+c*CH:14+(c+1)*CH]).astype(BF)
    kk, ci = iota((256,256),0), iota((256,256),1)
    peo = one_hot(ci == 2*(kk % 128) + kk // 128)
    for t in range(9):
        cs = O_UP + t*128
        both = jnp.concatenate([wt_ref[0:128, cs:cs+128], wt_ref[128:256, cs:cs+128]], axis=1)
        wup_ref[t] = nn(both, peo).astype(BF)
    kq, lq = iota((768,768),0), iota((768,768),1)
    pq = one_hot(kq == 3*(lq % 256) + lq // 256)
    wt_ref[:, O_QKV:O_QKV+768] = nn(wt_ref[:, O_QKV:O_QKV+768], pq).astype(BF)
    scol, srho = iota((256,128),1), iota((256,128),0)
    sm_ref[...] = jnp.where((scol < 13) | ((scol == 13) & (srho < 128)), nn(perm, tg_ref[:, 0:128]), nn(perm, tg_ref[:, MID:MID+128])).T
    halves = jnp.concatenate([sm_ref[0:32, 0:128], sm_ref[0:32, 128:256]], axis=0).astype(BF)
    l, r = iota((128,64),0), iota((128,64),1)
    k = 3*(l % 9) + l // 9
    win_ref[...] = nn(one_hot((l < 27) & (r == 32*(k % 2) + k // 2)), halves).astype(BF)
    t16, r16 = iota((16,64),0), iota((16,64),1)
    pieces = []
    for h in range(3):
        blk = 27 + 3*t16 + h
        pieces.append(nn(one_hot((t16 < 9) & (r16 == 32*(blk % 2) + blk // 2)), halves))
    flat = jnp.concatenate(pieces, axis=1).astype(BF)
    acc = jnp.zeros((128,128), F32)
    for c in range(3):
        wc = nn(flat, one_hot(iota((384,128),0) == 3*iota((384,128),1) + c)).astype(BF)
        acc += nn(one_hot((iota((128,16),1) < 9) & (iota((128,16),0) == 9*c + iota((128,16),1))), wc)
    wfb = acc.astype(BF)
    wfb_ref[...] = wfb
    a, z = iota((128,128),0), iota((128,128),1)
    for r in range(3):
        wfin_ref[:, 128*r:128*r+128] = nn(one_hot((a < 81) & (z == 9*(a % 27 // 9) + 3*r + a // 27)), wfb).astype(BF)

def final_bias(sm_ref):
    b = sm_ref[42:43, 0:128].astype(BF)
    return nn(b, one_hot((iota((128,128),1) < 27) & (iota((128,128),0) == iota((128,128),1) // 9)))

def gn_stats(src, P, per, same):
    k = 4
    B = 16
    s = [pile(src[pl.ds(i,B)], k) for i in range(0,P,B)]
    m = sum(s[1:], s[0]) * (1.0/P)
    q = [pile(jnp.square(src[pl.ds(i,B)] - m), k) for i in range(0,P,B)]
    mean = group_sum(m, same) * (1.0/per)
    spread = sum(q[1:], q[0]) * (1.0/P) + jnp.square(m - mean)
    return mean, lax.rsqrt(group_sum(spread, same) * (1.0/per) + 1e-5)

def vec(v_ref, name, C=C2):
    at, wide = BLOCK[name]
    return jnp.concatenate([v_ref[b//2:b//2+1, 128*(b%2):128*(b%2)+128] for b in range(at, at+wide)], axis=1)

def net(x_ref, feat, wt, wup, win, wfin, v_ref, sc):
    xp, tp, top, low, ap, mid, res, qkv, ob, yp, up, ep = (sc[k] for k in ("xp","tp","top","low","ap","mid","res","qkv","ob","yp","up","ep"))
    ap2 = sc.get("ap2", ap)
    lane = iota((1,1,128),2)
    def save(si, m, inv):
        if "st" in sc:
            C = m.shape[1]
            sc["st"][2*si,:,0:C] = m
            sc["st"][2*si+1,:,0:C] = inv
    bfin = final_bias(v_ref)
    def a0(y, _):
        xp[y+1, 1:17] = x_ref[pl.ds(y*16,16)].astype(BF)
        return 0
    lax.fori_loop(0,16,a0,0)
    def a1(y2, _):
        pieces=[]
        for k in range(4):
            y = y2*4+k
            cols = jnp.zeros((16,16,128),BF)
            for t in range(9):
                w = xp[y+t//3, t%3:t%3+16]
                cols = jnp.where((lane%9==t)&(lane<27), w, cols) if t else jnp.where((lane%9==0)&(lane<27), w, jnp.zeros_like(w))
            if "cols" in sc: sc["cols"][pl.ds(y*16,16)] = cols
            pieces.append(cols.reshape(256,128))
        r = nn(jnp.concatenate(pieces,axis=0), win[...]) + vec(v_ref,"b_in",C1)
        top[pl.ds(y2*64,64)] = r.reshape(64,16,128)
        rb = r.astype(BF).reshape(4,8,2,16,128)
        for k in range(4):
            p = y2*4+k+1
            tp[p//2, p%2, 0:8, 1] = rb[k,:,0]
            tp[p//2, p%2, 1:9, 0] = rb[k,:,1]
        return 0
    lax.fori_loop(0,4,a1,0)
    taps=[]
    for t in range(9):
        ty,tx=t//3,t%3
        taps.append(tp[ty//2:ty//2+8, ty%2, tx//2:tx//2+8, tx%2].reshape(1024,128))
    low[...] = (nt(jnp.concatenate(taps,axis=1), wt[:,O_DOWN:O_DOWN+1152]) + vec(v_ref,"b_down")).reshape(64,16,256)
    def norm_act(src, ap, g, s, si):
        m, inv = gn_stats(src, 64, 8, sc["same8"][...])
        save(si, m, inv)
        half = 0.5*inv*vec(v_ref,g)
        shift = 0.5*vec(v_ref,s) - m*half
        for y in range(8):
            h = src[y*8:y*8+8]*half + shift
            ap[y+1,1:9] = (h + h*jnp.tanh(h)).astype(BF)
    def conv3(ap, off):
        return nt(jnp.concatenate([ap[t//3:t//3+8, t%3:t%3+8].reshape(1024,256) for t in range(9)],axis=1), wt[:,off:off+2304])
    norm_act(low,ap,"g1","s1",0)
    emb = nt(feat, wt[:,O_TIME:O_TIME+128]) + vec(v_ref,"b_time")
    mid[...] = (conv3(ap,O_R1) + vec(v_ref,"b_res1")).reshape(64,16,256) + emb
    norm_act(mid,ap2,"g2","s2",1)
    res[...] = low[...] + (conv3(ap2,O_R2) + vec(v_ref,"b_res2")).reshape(64,16,256)
    m, inv = gn_stats(res, 64, 8, sc["same8"][...])
    save(2, m, inv)
    gain = inv*vec(v_ref,"g3")
    nb = (res[...]*gain + (vec(v_ref,"s3") - m*gain)).astype(BF).reshape(1024,256)
    q = nt(nb, wt[:,O_QKV:O_QKV+256]) + vec(v_ref,"b_query")
    k_ = nt(nb, wt[:,O_QKV+256:O_QKV+512])
    v_ = nt(nb, wt[:,O_QKV+512:O_QKV+768])+vec(v_ref,"b_value")
    for i, z in enumerate((q, k_, v_)):
        z = z.astype(BF).astype(F32)
        qkv[2*i] = z[:,0:128]
        qkv[2*i+1] = z[:,128:256]
    def head(j, n):
        return jnp.concatenate([qkv[2*j,pl.ds(n,64,stride=16),:], qkv[2*j+1,pl.ds(n,64,stride=16),:]], axis=1).astype(BF)
    s = jnp.concatenate([nt(head(0,n), head(1,n)) for n in range(N)], axis=0)*(C2**-0.5)
    e = jnp.exp(s - jnp.max(s,axis=1,keepdims=True))
    p = (e/jnp.sum(e,axis=1,keepdims=True)).astype(BF)
    for n in range(N):
        o = nn(p[64*n:64*n+64], head(2,n)).astype(BF).astype(F32)
        ob[0,pl.ds(n,64,stride=16),:] = o[:,0:128]
        ob[1,pl.ds(n,64,stride=16),:] = o[:,128:256]
    obb = jnp.concatenate([ob[0],ob[1]],axis=1).astype(BF)
    if "obb" in sc: sc["obb"][...] = obb
    att_out = res[...].reshape(1024,256) + (nt(obb, wt[:,O_PROJ:O_PROJ+256]) + vec(v_ref,"b_proj"))
    attb = att_out.astype(BF)
    if "attb" in sc: sc["attb"][...] = attb
    for t in range(0,9,2):
        k = min(2, 9-t)
        r = nt(attb, wup[t:t+k].reshape(128*k,256))
        for i in range(k):
            yp[t+i,1:9,1:9] = r[:,128*i:128*i+128].reshape(8,8,16,128)
    def u(i,_):
        for a in range(2):
            for b in range(2):
                acc=None
                for t in range(9):
                    r,c=t//3-1,t%3-1
                    dr=(a+r)//2; dc=(b+c)//2
                    v=yp[t, i+dr+1, 1+dc:9+dc]
                    acc = v if acc is None else acc+v
                up[i,a,:,b] = acc + vec(v_ref,"b_up",C1) + sc["top6"][i,a,:,b]
        return 0
    lax.fori_loop(0,8,u,0)
    upf = sc["up3"]
    m, inv = gn_stats(upf, 256, 4, sc["same4"][...])
    save(3, m, inv)
    half = 0.5*inv*vec(v_ref,"g4",C1)
    shift = 0.5*vec(v_ref,"s4",C1) - m*half
    def b4(y,_):
        h = upf[pl.ds(y*16,16)]*half + shift
        ep[y+1,1:17] = (h + h*jnp.tanh(h)).astype(BF)
        return 0
    lax.fori_loop(0,16,b4,0,unroll=4)
    def fin(put):
        def f(y4,_):
            cols=jnp.concatenate([ep[pl.ds(y4*8+r,8)].reshape(2304,128) for r in range(3)],axis=1)
            d=nt(cols, wfin[...]).reshape(8,18,16,128)
            put(y4, (d[:,0:16] + pltpu.roll(d[:,1:17].reshape(2048,128),101,1).reshape(8,16,16,128)
                     + pltpu.roll(d[:,2:18].reshape(2048,128),74,1).reshape(8,16,16,128)).reshape(128,16,128) + bfin)
            return 0
        lax.fori_loop(0,2,f,0)
    return fin

def scratch():
    V=pltpu.VMEM
    return dict(wt=V((256,MID),BF), wup=V((9,128,256),BF), win=V((128,128),BF), wfin=V((128,384),BF), wfb=V((128,128),BF), sm=V((128,256),F32), xp=V((18,18,16,128),BF), tp=V((9,2,9,2,16,128),BF),
      top=V((256,16,128),F32), low=V((64,16,256),F32), ap=V((10,10,16,256),BF), mid=V((64,16,256),F32), res=V((64,16,256),F32),
      qkv=V((6,1024,128),F32), ob=V((2,1024,128),F32), yp=V((9,10,10,16,128),F32), up=V((8,2,8,2,16,128),F32), ep=V((18,18,16,128),BF), same8=V((256,256),BF), same4=V((128,128),BF))
KEYS=list(scratch().keys())

def zero_borders(sc):
    for k in ("xp","ep","tp","ap","ap2"):
        if k in sc: sc[k][...] = jnp.zeros(sc[k].shape, sc[k].dtype)
    yp = sc["yp"]
    edge = jnp.zeros((9,10,16,128), F32)
    for k in (0,9):
        yp[:,k] = edge
        yp[:,:,k] = edge
    for k, C, per in (("same8",256,8), ("same4",128,4)):
        sc[k][...] = one_hot(iota((C,C),0)//per == iota((C,C),1)//per)

def views(sc):
    sc=dict(sc)
    sc["top6"]=sc["top"].reshape(8,2,8,2,16,128)
    sc["up3"]=sc["up"].reshape(256,16,128)
    return sc

def teacher_call(D, cnt, x, feat, ce, cl, tc, nc, tg):
    def kern(cnt_ref, x_ref, feat_ref, ce_ref, cl_ref, tc_ref, nc_ref, tg_ref, out_ref, *scr):
        sc = views(dict(zip(KEYS, scr)))
        zero_borders(sc)
        prep(tg_ref, *(sc[k] for k in WKEYS), D)
        out_ref[...] = x_ref[...]
        def step(j, _):
            fin = net(out_ref, feat_ref[j], sc["wt"], sc["wup"], sc["win"], sc["wfin"], sc["sm"], sc)
            ce_, cl_ = ce_ref[j], cl_ref[j]
            def put(y4, e):
                out_ref[pl.ds(y4*128,128)] = ce_*e + cl_*out_ref[pl.ds(y4*128,128)]
            fin(put)
            return 0
        lax.fori_loop(0, cnt_ref[0], step, 0)
        def tgt(i, _):
            out_ref[pl.ds(i*16,16)] = tc_ref[...]*out_ref[pl.ds(i*16,16)] + nc_ref[...]*x_ref[pl.ds(i*16,16)]
            return 0
        lax.fori_loop(0, 16, tgt, 0)
    vm = pl.BlockSpec(memory_space=pltpu.VMEM)
    return pl.pallas_call(kern, out_shape=jax.ShapeDtypeStruct((256,16,128),F32),
        in_specs=[pl.BlockSpec(memory_space=pltpu.SMEM)]+[vm]*7, out_specs=vm, scratch_shapes=list(scratch().values()), name="teacher_steps",
        compiler_params=pltpu.CompilerParams(vmem_limit_bytes=60<<20))(cnt, x, feat, ce, cl, tc, nc, tg)

WKEYS = ["wt","wup","win","wfin","wfb","sm"]
RES = ["wt","wup","wfb","sm","tp","low","ap","mid","res","qkv","up"]
def loss_sums(t_ref, out_ref, snr_ref, sum_ref):
    def s(i,c):
        t,o=t_ref[pl.ds(i*16,16)],out_ref[pl.ds(i*16,16)]
        d=o-t
        return tuple(a+jnp.sum(b,axis=0) for a,b in zip(c,(t,t*t,o,o*o,d*d)))
    z=jnp.zeros((N,128),F32)
    r=lax.fori_loop(0,16,s,(z,)*5)
    r=r[:4]+(r[4]*snr_ref[...],)
    sum_ref[...]=jnp.concatenate([jnp.sum(a,axis=0,keepdims=True) for a in r]+[jnp.zeros((3,128),F32)],axis=0)

def student_call(D, x, tgt, snr, feat, tg):
    vm=pl.BlockSpec(memory_space=pltpu.VMEM)
    sh=scratch()
    extra=dict(st=pltpu.VMEM((8,16,256),F32),cols=pltpu.VMEM((256,16,128),BF),attb=pltpu.VMEM((1024,256),BF),obb=pltpu.VMEM((1024,256),BF),ap2=pltpu.VMEM((10,10,16,256),BF))
    outs={k:sh[k] for k in RES}; outs.update(extra)
    scr={k:v for k,v in sh.items() if k not in outs}
    ok,sk=list(outs),list(scr)
    def kern(x_ref,t_ref,snr_ref,feat_ref,tg_ref,out_ref,sum_ref,*refs):
        sc=views(dict(zip(ok+sk,refs)))
        zero_borders(sc)
        prep(tg_ref,*(sc[k] for k in WKEYS),D)
        fin=net(x_ref,feat_ref[...],sc["wt"],sc["wup"],sc["win"],sc["wfin"],sc["sm"],sc)
        def put(y4,e): out_ref[pl.ds(y4*128,128)]=e
        fin(put)
        loss_sums(t_ref,out_ref,snr_ref,sum_ref)
    res=pl.pallas_call(kern,
        out_shape=(jax.ShapeDtypeStruct((256,16,128),F32),jax.ShapeDtypeStruct((8,128),F32))+tuple(jax.ShapeDtypeStruct(outs[k].shape,outs[k].dtype) for k in ok),
        in_specs=[vm]*5,out_specs=(vm,)*(2+len(ok)),scratch_shapes=[scr[k] for k in sk], name="student_forward",
        compiler_params=pltpu.CompilerParams(vmem_limit_bytes=62<<20))(x,tgt,snr,feat,tg)
    return res[0],res[1],dict(zip(ok,res[2:]))

MESH = pl.DeviceIdType.MESH

def place():
    dp = lax.axis_index("dp")
    return dp // 4, dp // 2 % 2, dp % 2, lax.axis_index("mp")

def peer(z, y, x, c):
    return {"dp": z*4 + y*2 + x, "mp": c}

def greet(peers):
    barrier = pltpu.get_barrier_semaphore()
    for p in peers:
        pl.semaphore_signal(barrier, inc=1, device_id=p, device_id_type=MESH)
    pl.semaphore_wait(barrier, len(peers))

def partners():
    z, y, x, c = place()
    return [peer(z,y,x,1-c), peer(z,y,1-x,c), peer(z,1-y,x,c)] + [peer((z+o)%4,y,x,c) for o in (1,2,3)]

def gather_copies(s, p, streams, in_ref, out_ref, send, recv):
    z, y, x, c = place()
    wide = in_ref.shape[1] // streams
    all_, lo, hi = pl.ds(s*wide, wide), pl.ds(s*wide, wide//2), pl.ds(s*wide + wide//2, wide//2)
    to_x, to_y = peer(z,y,1-x,c), peer(z,1-y,x,c)
    if p == 0:
        return [pltpu.make_async_remote_copy(in_ref.at[:,all_], out_ref.at[z,y,x,c,:,all_], send.at[s,o-1], recv.at[s,3-o],
                device_id=peer((z+o)%4,y,x,c), device_id_type=MESH) for o in (2,1,3)]
    if p == 1:
        moves = [(out_ref.at[:,y,x,c,:,lo], to_x, 3), (out_ref.at[:,y,x,c,:,hi], to_y, 4)]
    elif p == 2:
        moves = [(out_ref.at[:,y,:,c,:,lo], to_y, 5), (out_ref.at[:,:,x,c,:,hi], to_x, 6)]
    else:
        moves = [(out_ref.at[:,:,:,c,:,all_], peer(z,y,x,1-c), 7)]
    return [pltpu.make_async_remote_copy(part, part, send.at[s,i], recv.at[s,i], device_id=to, device_id_type=MESH) for part, to, i in moves]

def mix_images(ca_ref, sa_ref, im_ref, ns_ref, x_ref, flat, planes):
    flat[...] = jnp.zeros(flat.shape, F32)
    for n in range(N):
        for c in range(3):
            flat[16*n:16*n+16, 16*c:16*c+16] = ca_ref[n]*im_ref[n,c] + sa_ref[n]*ns_ref[n,c]
    parts = split3(flat[...])
    k, l = iota((128,512),0), iota((128,512),1)
    for q in range(4):
        r = nn(parts, one_hot((l % 128 < 27) & (k == 16*(l % 128 // 9) + 4*q + l // 128)))
        r = r[0:256] + r[256:512] + r[512:768]
        for i in range(4): planes[4*q+i] = r[:,128*i:128*i+128]
    for y in range(SIDE):
        for x in range(SIDE):
            x_ref[SIDE*y+x] = planes[x,pl.ds(y,N,stride=SIDE),:]

def gather_kernel(streams, ca_ref, sa_ref, im_ref, ns_ref, in_ref, out_ref, x_ref, send, recv, keep, flat, planes):
    z, y, x, c = place()
    greet(partners())
    own = pltpu.make_async_copy(in_ref, out_ref.at[z,y,x,c], keep)
    own.start()
    live = {(s,p): gather_copies(s,p,streams,in_ref,out_ref,send,recv) for s in range(streams) for p in range(4)}
    for s in range(streams):
        for d in live[s,0]: d.start()
    mix_images(ca_ref, sa_ref, im_ref, ns_ref, x_ref, flat, planes)
    own.wait()
    for step in range(streams + 3):
        for s in range(streams):
            p = step - s
            if 0 <= p <= 3:
                for d in live[s,p]: d.wait_recv()
                if p < 3:
                    for d in live[s,p+1]: d.start()
    for ds in live.values():
        for d in ds: d.wait_send()

def gather_call(block, ca, sa, images, noise, cid, streams=4):
    rows, wide = block.shape
    any_, vm, sm = (pl.BlockSpec(memory_space=m) for m in (pl.ANY, pltpu.VMEM, pltpu.SMEM))
    out, noisy = pl.pallas_call(lambda *r: gather_kernel(streams, *r),
        out_shape=(jax.ShapeDtypeStruct((4,2,2,2,rows,wide), block.dtype), jax.ShapeDtypeStruct((256,N,128), F32)),
        in_specs=[sm,sm,vm,vm,any_], out_specs=(any_,vm), name="gather_columns",
        scratch_shapes=[pltpu.SemaphoreType.DMA((streams,8)), pltpu.SemaphoreType.DMA((streams,8)), pltpu.SemaphoreType.DMA,
                        pltpu.VMEM((256,128),F32), pltpu.VMEM((16,256,128),F32)],
        compiler_params=pltpu.CompilerParams(collective_id=cid, has_side_effects=True, vmem_limit_bytes=24<<20))(
            ca, sa, images.transpose(0,3,1,2), noise.transpose(0,3,1,2), block)
    return out.reshape(32*rows, wide), noisy

def sum_kernel(in_ref, out_ref, box, send, recv):
    z, y, x, c = place()
    hops = [peer(z,y,x,1-c), peer(z,y,1-x,c), peer(z,1-y,x,c), peer(z+1-2*(z%2),y,x,c), peer((z+2)%4,y,x,c)]
    out_ref[...] = in_ref[...]
    for k, to in enumerate(hops):
        box[k] = out_ref[...]
        d = pltpu.make_async_remote_copy(box.at[k], box.at[5+k], send.at[k], recv.at[k], device_id=to, device_id_type=MESH)
        d.start()
        d.wait()
        out_ref[...] += box[5+k]

STREAMS = ((0,2), (2,2), (4,2), (6,1), (7,1))

def row_of(r):
    return 128*(r//128) + 32*(r//8%4) + 8*(r//32%4) + 4*(r%2) + 2*(r//2%2) + r//4%2

def scatter_scratch():
    V = pltpu.VMEM
    sc = {}
    for s, (_, u) in enumerate(STREAMS):
        sc[f"c{s}"] = V((u,2,2,2,4,4,8,128),F32)
        sc[f"h{s}"] = V((u,2,2,4,4,8,128),F32)
        sc[f"q{s}"] = V((u,2,4,4,8,128),F32)
        sc[f"z{s}"] = V((3,u,2,4,8,128),F32)
    sc["ssem"] = pltpu.SemaphoreType.DMA((len(STREAMS),8))
    sc["rsem"] = pltpu.SemaphoreType.DMA((len(STREAMS),8))
    return sc

def scatter_steps(g_ref, out_ref, sc):
    z, y, x, c = place()
    send, recv = sc["ssem"], sc["rsem"]
    live = {}
    def bufs(s): return tuple(sc[f"{k}{s}"] for k in "chqz")
    def copies(s, p):
        r0, r1, r2, r3 = bufs(s)
        to_x, to_y = peer(z,y,1-x,c), peer(z,1-y,x,c)
        if p == 0:
            moves = [(g_ref.at[pl.ds(*STREAMS[s]),:,1-c], r0, peer(z,y,x,1-c), 0, 0)]
        elif p == 1:
            moves = [(r0.at[:,0,1-x], r1.at[:,0], to_x, 1, 1), (r0.at[:,1,:,1-y], r1.at[:,1], to_y, 2, 2)]
        elif p == 2:
            moves = [(r1.at[:,0,1-y], r2.at[:,0], to_y, 3, 3), (r1.at[:,1,1-x], r2.at[:,1], to_x, 4, 4)]
        else:
            moves = [(r2.at[:,:,(z+o)%4], r3.at[3-o], peer((z+o)%4,y,x,c), 4+o, 8-o) for o in (2,1,3)]
        return [pltpu.make_async_remote_copy(src, dst, send.at[s,i], recv.at[s,k], device_id=to, device_id_type=MESH) for src, dst, to, i, k in moves]
    def add(s, p):
        r0, r1, r2, r3 = bufs(s)
        first, number = STREAMS[s]
        for u in range(number):
            if p == 0:
                for h in range(2):
                    for i in range(2):
                        r0[u,h,i] += g_ref[first+u,h,c,i]
            elif p == 1:
                r1[u,0] += r0[u,0,x]
                r1[u,1] += r0[u,1,:,y]
            elif p == 2:
                r2[u,0] += r1[u,0,y]
                r2[u,1] += r1[u,1,x]
            else:
                total = r2[u,:,z] + r3[0,u] + r3[1,u] + r3[2,u]
                for k in range(8):
                    out_ref[:,:,STORED[8*(first+u)+k]] = total[:,:,k]
    def advance(s, p):
        if p:
            for d in live[s,p-1]: d.wait_recv()
            add(s, p-1)
        if p < 4:
            live[s,p] = copies(s,p)
            for d in live[s,p]: d.start()
    def finish():
        for ds in live.values():
            for d in ds: d.wait_send()
    return advance, finish

def tn(a, b): return lax.dot_general(a, b, (((0,),(0,)),((),())), preferred_element_type=F32)

def bwd_kernel(x_refs, o_refs, sc):
    X, S = x_refs, sc
    (G,) = o_refs
    sg, sn_total = S["sg"], X["total"]
    v_ref, wt, wup, st = X["v"], X["wt"], X["wup"], X["st"]
    gp18, gcols, big, dp, s_hi, s_lo, gp, da, gres, gqkv, gmx = (S[k] for k in ("gp18","gcols","big","dp","s_hi","s_lo","gp","da","gres","gqkv","gmx"))
    lane = iota((1,1,128),2)
    for k, C, per in (("same8",256,8), ("same4",128,4)):
        S[k][...] = one_hot(iota((C,C),0)//per == iota((C,C),1)//per)
    for k in ("gp18","dp","gp"):
        S[k][...] = jnp.zeros(S[k].shape, S[k].dtype)
    sg[...] = jnp.zeros((128,256),F32)
    def put_block(b, val):
        sg[b//2:b//2+1, 128*(b%2):128*(b%2)+128] = val
    def put_vec(name, val, C=C2):
        at, wide = BLOCK[name]
        for k in range(wide):
            put_block(at+k, val[:, 128*k:128*k+128])
    def rowsum(a): return jnp.sum(a, axis=0, keepdims=True)
    step, near = S["step"], S["near"]
    def put_g(val, col, row0=0):
        rows, width = val.shape
        col = 128*next(GROUP[o] + (col-o)//128 for o in sorted(GROUP, reverse=True) if col >= o)
        for c in range(width//128):
            at = col//128+c
            for r in range(row0, row0+rows, 8):
                if near: to = pl.ds(2048*(at//8) + 1024*(r//128) + 32*(r//32%4) + 8*(r//8%4) + at%8, 8, stride=128)
                else: to = pl.ds(64*r+at, 8, stride=64)
                G[to,:] = val[r-row0:r-row0+8, c*128:c*128+128]
    pm = S["pm"]
    pm[...] = one_hot(iota((256,256),1) == (row_of(iota((256,256),0)) if near else iota((256,256),0)))
    def turn(g): return nt(pm[...], g).astype(BF)
    pixels = 256.0*sn_total
    so = X["stat"][...]
    mt, mo = so[0:1]/pixels, so[2:3]/pixels
    vt_, vo = so[1:2]/pixels-mt*mt, so[3:4]/pixels-mo*mo
    cb = 4.0*(vo-vt_)/pixels
    ca = 2.0*(mo-mt)/pixels-cb*mo
    sn = X["snr"][...]*(2.0/(768.0*sn_total))
    acc=jnp.zeros((N,128),F32)
    def g0(y,acc):
        o=X["out"][pl.ds(y*16,16)]
        go = sn*(o-X["tgt"][pl.ds(y*16,16)]) + ca + cb*o
        gp18[y+1,1:17]=go.astype(BF)
        return acc+jnp.sum(go,axis=0)
    acc=lax.fori_loop(0,16,g0,acc)
    acc=rowsum(acc)
    lane2=iota((1,128),1)
    put_block(84, sum(jnp.where(lane2==c, jnp.sum(jnp.where(lane2==9*c,acc,0.0),axis=1,keepdims=True),0.0) for c in range(3)))
    def g1(y,_):
        for t in range(9):
            w = gp18[y+2-t//3, 2-t%3:18-t%3]
            cols = jnp.where((lane%9==t)&(lane<27), w, cols) if t else jnp.where((lane%9==0)&(lane<27), w, jnp.zeros_like(w))
        gcols[pl.ds(y*16,16)] = cols
        return 0
    lax.fori_loop(0,16,g1,0)
    big[...] = nn(gcols[...].reshape(4096,128), X["wfb"][...]).reshape(256,16,128)
    def gn_bwd(src, dref, si, gname, sname, C, per, same, rows, k, act_put, dx_put, silu=True):
        m, inv = st[2*si,:,0:C], st[2*si+1,:,0:C]
        g, s = vec(v_ref,gname,C), vec(v_ref,sname,C)
        w = 512//C
        zero = jnp.zeros((w,N,C),F32)
        def pick(v): return jnp.sum(v.reshape((-1,w)+v.shape[1:]),axis=0)
        def p1(y,c):
            A,B=c
            xh=(src[pl.ds(y*k,k)]-m)*inv
            d=dref[pl.ds(y*k,k)]
            if silu:
                h=xh*(0.5*g)+0.5*s
                th=jnp.tanh(h); sg=0.5+0.5*th; act=h+h*th
                act_put(y,act.astype(BF))
                d=d*(sg+act*(1.0-sg))
                dref[pl.ds(y*k,k)]=d
            else:
                act_put(y,(xh*g+s).astype(BF))
            return A+pick(d), B+pick(d*xh)
        A,B=lax.fori_loop(0,rows,p1,(zero,zero),unroll=4)
        A,B=jnp.sum(A,axis=0),jnp.sum(B,axis=0)
        put_vec(gname,rowsum(B),C); put_vec(sname,rowsum(A),C)
        cnt=1.0/(per*rows*k)
        ga=group_sum(g*A,same)*cnt; gb=group_sum(g*B,same)*cnt
        ig=inv*g; ib=inv*inv*gb; ic=m*ib-inv*ga
        def p2(y,acc):
            dx=ig*dref[pl.ds(y*k,k)]-ib*src[pl.ds(y*k,k)]+ic
            return acc+pick(dx_put(y,dx))
        return lambda: jnp.sum(lax.fori_loop(0,rows,p2,zero,unroll=4),axis=0)
    fused = "ep18" in S
    def act4(y,a):
        if not fused: S["ep"][pl.ds(y*16,16)]=a
    def dx4(y,dx):
        big[pl.ds(y*16,16)]=dx
        b=dx.astype(BF).reshape(8,2,16,128)
        p=y+1
        dp[p//2,p%2,0:8,1]=b[:,0]
        dp[p//2,p%2,1:9,0]=b[:,1]
        return dx
    fin=gn_bwd(X["up"].reshape(256,16,128),big,3,"g4","s4",128,4,S["same4"][...],16,16,act4,dx4)
    dwf = tn(gcols[...].reshape(4096,128), (S["ep18"][1:17,1:17] if fused else S["ep"][...]).reshape(4096,128))
    flat = jnp.zeros((9,384),F32)
    for c in range(3):
        p3 = one_hot(iota((128,384),1) == 3*iota((128,384),0) + c)
        piece = dwf[9*c:9*c+9]
        hi = piece.astype(BF); rest = piece-hi.astype(F32)
        mi = rest.astype(BF); lo = (rest-mi.astype(F32)).astype(BF)
        flat += nn(hi,p3)+nn(mi,p3)+nn(lo,p3)
    for t in range(9):
        for h in range(3):
            put_block(27+3*t+h, flat[t:t+1,128*h:128*h+128])
    put_vec("b_up",rowsum(fin()),128)
    PAIR={-1:((1,0),(1,1)),0:((0,1),(1,0)),1:((0,0),(0,1))}
    def su(i,_):
        for r in (-1,0,1):
            (ra,pa),(rb,pb)=PAIR[r]
            V={}
            for cp in range(2):
                V[cp]=dp[i+ra,pa,:,cp].astype(F32)+dp[i+rb,pb,:,cp].astype(F32)
            for c in (-1,0,1):
                (ca_,qa),(cb_,qb)=PAIR[c]
                s=V[qa][ca_:ca_+8]+V[qb][cb_:cb_+8]
                t=(r+1)*3+c+1
                hi=s.astype(BF)
                s_hi[t,pl.ds(i*8,8)]=hi
                s_lo[t,pl.ds(i*8,8)]=(s-hi.astype(F32)).astype(BF)
        return 0
    lax.fori_loop(0,8,su,0)
    cat=lambda ref: jnp.concatenate([ref[t].reshape(1024,128) for t in range(9)],axis=1)
    wu=wup[...].reshape(1152,256)
    gatt=nn(cat(s_hi),wu)+nn(cat(s_lo),wu)
    gres[...]=gatt.reshape(64,16,256)
    put_vec("b_proj",rowsum(gatt))
    gab=gatt.astype(BF)
    attb=X["attb"][...]
    kk, ci = iota((256,256),1), iota((256,256),0)
    peo=one_hot(ci == 2*(kk % 128) + kk // 128)
    aeo=nn(attb,peo).astype(BF)
    for t in range(9):
        hi,lo=[nt(pm[0:128,0:128],v[t].reshape(1024,128)).astype(BF) for v in (s_hi,s_lo)]
        r=nn(hi,aeo)+nn(lo,aeo)
        put_g(r[:,0:128],O_UP+t*128,0); put_g(r[:,128:256],O_UP+t*128,128)
    obb=X["ob"][...]
    put_g(nn(turn(gab),obb),O_PROJ)
    gm=nn(gab,wt[:,O_PROJ:O_PROJ+256]).astype(BF).astype(F32)
    gmx[0]=gm[:,0:128]; gmx[1]=gm[:,128:256]
    qkv=X["qkv"]
    sc_=C2**-0.5
    def pair(ref,j,n): return jnp.concatenate([ref[2*j,pl.ds(n,64,stride=16),:],ref[2*j+1,pl.ds(n,64,stride=16),:]],axis=1).astype(BF)
    s=jnp.concatenate([nt(pair(qkv,0,n),pair(qkv,1,n)) for n in range(N)],axis=0)*sc_
    e=jnp.exp(s-jnp.max(s,axis=1,keepdims=True))
    p=e/jnp.sum(e,axis=1,keepdims=True)
    ga=jnp.concatenate([nt(pair(gmx,0,n),pair(qkv,2,n)) for n in range(N)],axis=0)
    gs=(p*(ga-jnp.sum(ga*p,axis=1,keepdims=True))).astype(BF)
    pb=p.astype(BF)
    for n in range(N):
        gsn,pn=gs[64*n:64*n+64],pb[64*n:64*n+64]
        for j,o in enumerate((nn(gsn,pair(qkv,1,n))*sc_, tn(gsn,pair(qkv,0,n))*sc_, tn(pn,pair(gmx,0,n)))):
            o=o.astype(BF).astype(F32)
            gqkv[2*j,pl.ds(n,64,stride=16),:]=o[:,0:128]
            gqkv[2*j+1,pl.ds(n,64,stride=16),:]=o[:,128:256]
    gq=[jnp.concatenate([gqkv[2*j],gqkv[2*j+1]],axis=1) for j in range(3)]
    put_vec("b_query",rowsum(gq[0])); put_vec("b_value",rowsum(gq[2]))
    gqb=[g.astype(BF) for g in gq]
    da[...]=nn(jnp.concatenate(gqb,axis=1),jnp.concatenate([wt[:,O_QKV+256*j:O_QKV+256*j+256] for j in range(3)],axis=0)).reshape(64,16,256)
    nbs=S["nb"]
    def act3(y,a): nbs[pl.ds(y*8,8)]=a
    def dx3(y,dx):
        z=gres[pl.ds(y*8,8)]+dx
        gres[pl.ds(y*8,8)]=z
        gp[y+1,1:9]=z.astype(BF)
        return z
    fin=gn_bwd(X["res"],da,2,"g3","s3",256,8,S["same8"][...],8,8,act3,dx3,silu=False)
    nb=nbs[...].reshape(1024,256)
    for j in range(3): put_g(nn(turn(gqb[j]),nb),O_QKV+256*j)
    step((0,0))
    put_vec("b_res2",rowsum(fin()))
    def conv_dgrad(off):
        return nn(jnp.concatenate([gp[2-t//3:10-t//3,2-t%3:10-t%3].reshape(1024,256) for t in range(9)],axis=1),
                  jnp.concatenate([wt[:,off+256*t:off+256*t+256] for t in range(9)],axis=0))
    def conv_wgrad(g,ap,off,steps):
        gt=turn(g)
        for t in range(9):
            put_g(nn(gt,ap[t//3:t//3+8,t%3:t%3+8].reshape(1024,256)),off+256*t)
            step(*steps.get(t,()))
    def act_(y,a): pass
    conv_wgrad(gp[1:9,1:9].reshape(1024,256),X["ap2"],O_R2,{3:((0,1),),7:((1,0),)})
    da[...]=conv_dgrad(O_R2).reshape(64,16,256)
    step((1,1))
    def dxm(y,dx):
        gp[y+1,1:9]=dx.astype(BF)
        return dx
    fin=gn_bwd(X["mid"],da,1,"g2","s2",256,8,S["same8"][...],8,8,act_,dxm)
    step((0,2))
    gemb=fin()
    put_vec("b_time",rowsum(gemb)); put_vec("b_res1",rowsum(gemb))
    put_g(nn(turn(gemb.astype(BF)),X["feat"][...]),O_TIME)
    conv_wgrad(gp[1:9,1:9].reshape(1024,256),X["ap"],O_R1,{3:((0,3),),5:((2,0),),8:((1,2),)})
    da[...]=conv_dgrad(O_R1).reshape(64,16,256)
    step((2,1),(0,4))
    def dxl(y,dx):
        z=gres[pl.ds(y*8,8)]+dx
        gp[y+1,1:9]=z.astype(BF)
        return z
    fin=gn_bwd(X["low"],da,0,"g1","s1",256,8,S["same8"][...],8,8,act_,dxl)
    step((1,3))
    put_vec("b_down",rowsum(fin()))
    glb=gp[1:9,1:9].reshape(1024,256)
    glt=turn(glb)
    tp=X["tp"]
    for t in range(9):
        ty,tx=t//3,t%3
        put_g(nn(glt,tp[ty//2:ty//2+8,ty%2,tx//2:tx//2+8,tx%2].reshape(1024,128)),O_DOWN+128*t)
        if t==1: step((3,0))
    big6=big.reshape(8,2,8,2,16,128)
    dt6=S["dt"].reshape(8,2,8,2,16,128)
    SRC={0:((1,0),),1:((0,1),(2,0))}
    total=jnp.zeros((N,128),F32)
    for a in range(2):
        for b in range(2):
            taps=[(3*ty+tx,1+oy,1+ox) for ty,oy in SRC[a] for tx,ox in SRC[b]]
            z=nn(jnp.concatenate([gp[oy:oy+8,ox:ox+8].reshape(1024,256) for _,oy,ox in taps],axis=1),
                 jnp.concatenate([wt[:,O_DOWN+128*t:O_DOWN+128*t+128] for t,_,_ in taps],axis=0)).reshape(8,8,16,128)
            z=z+big6[:,a,:,b]
            dt6[:,a,:,b]=z.astype(BF)
            total=total+jnp.sum(jnp.sum(z,axis=0),axis=0)
    put_vec("b_in",rowsum(total),128)
    step((3,1),(2,2),(1,4))
    dwi=tn(X["cols"][...].reshape(4096,128),S["dt"][...].reshape(4096,128))
    for k in range(27):
        put_block(k, dwi[9*(k%3)+k//3:9*(k%3)+k//3+1])
    kept = nt(split3(sg[...]), pm[...])
    put_g((kept[0:128]+kept[128:256]+kept[256:384]).T, MID)

def bwd_scratch():
    V=pltpu.VMEM
    return dict(gp18=V((18,18,16,128),BF),gcols=V((256,16,128),BF),big=V((256,16,128),F32),ep=V((256,16,128),BF),dp=V((9,2,9,2,16,128),BF),
      s_hi=V((9,64,16,128),BF),s_lo=V((9,64,16,128),BF),gp=V((10,10,16,256),BF),da=V((64,16,256),F32),gres=V((64,16,256),F32),
      gqkv=V((6,1024,128),F32),gmx=V((2,1024,128),F32),nb=V((64,16,256),BF),dt=V((256,16,128),BF),sg=V((128,256),F32),pm=V((256,256),BF),same8=V((256,256),BF),same4=V((128,128),BF))
BIN=["out","tgt","snr","stat","cols","tp","low","mid","res","qkv","obb","attb","up","st","feat","wt","wup","wfb","sm","ap","ap2"]
GROUP = {O_UP:0, O_PROJ:9, O_QKV:11, O_R2:17, O_TIME:35, O_R1:36, O_DOWN:54, MID:63}
STORED = [next(at//128 + i - g for at, g in sorted(GROUP.items(), key=lambda e: -e[1]) if i >= g) for i in range(64)]
def bwd_call(ins, total):
    vm=pl.BlockSpec(memory_space=pltpu.VMEM)
    sc=bwd_scratch(); keys=list(sc)
    def k(*refs):
        a=dict(zip(BIN,refs[:len(BIN)])); a["v"]=a["sm"]; a["ob"]=a["obb"]; a["total"]=float(total)
        s=dict(zip(keys,refs[len(BIN)+1:]))
        s["step"],s["near"]=(lambda *_: None),False
        bwd_kernel(a,(refs[len(BIN)],),s)
    return pl.pallas_call(k,out_shape=jax.ShapeDtypeStruct((256*64,128),F32),
        in_specs=[vm]*len(BIN),out_specs=vm,scratch_shapes=list(sc.values()), name="student_backward",
        compiler_params=pltpu.CompilerParams(vmem_limit_bytes=63<<20))(*[ins[k] for k in BIN])

def student_step(D, x, tgt, snr, feat, tg, total, cid):
    V=pltpu.VMEM
    sc=scratch()
    del sc["yp"]
    sc.update(st=V((8,16,256),F32), cols=V((256,16,128),BF), attb=V((1024,256),BF), obb=V((1024,256),BF), ap2=V((10,10,16,256),BF),
              out=V((256,16,128),F32), part=V((8,128),F32))
    sc.update({k:v for k,v in bwd_scratch().items() if k not in ("gp18","big","ep","gmx","dt","same8","same4")})
    sc.update(box=V((10,8,128),F32), send=pltpu.SemaphoreType.DMA((5,)), recv=pltpu.SemaphoreType.DMA((5,)), load=pltpu.SemaphoreType.DMA((2,)),
              g=V((256*64,128),F32), own=V((8,64,128),F32))
    sc.update(scatter_scratch())
    keys=list(sc)
    def kern(x_ref,t_ref,snr_ref,feat_ref,tg_ref,grad_ref,sum_ref,*refs):
        s=dict(zip(keys,refs))
        s["yp"]=s["g"].at[0:14400].reshape(9,10,10,16,128)
        s=views(s)
        out,top=s["out"],s["top"]
        take=pltpu.make_async_copy(x_ref,out,s["load"].at[0])
        take.start()
        greet(partners())
        zero_borders(s)
        prep(tg_ref,*(s[k] for k in WKEYS),D)
        take.wait()
        fin=net(out,feat_ref[...],s["wt"],s["wup"],s["win"],s["wfin"],s["sm"],s)
        take=pltpu.make_async_copy(t_ref,top,s["load"].at[1])
        take.start()
        def put(y4,e): out[pl.ds(y4*128,128)]=e
        fin(put)
        take.wait()
        loss_sums(top,out,snr_ref,s["part"])
        sum_kernel(s["part"],sum_ref,s["box"],s["send"],s["recv"])
        a={k:s[k] for k in BIN if k in s}
        a.update(tgt=top,snr=snr_ref,stat=sum_ref,feat=feat_ref,v=s["sm"],ob=s["obb"],total=float(total))
        own=s["own"]
        advance,finish=scatter_steps(s["g"].reshape(8,2,2,2,2,4,4,8,128),own.reshape(2,4,64,128),s)
        def step(*moves):
            for m in moves: advance(*m)
        s.update(gp18=s["xp"],big=top,ep18=s["ep"],gmx=s["ob"],dt=s["gcols"],step=step,near=True)
        bwd_kernel(a,(s["g"],),s)
        step((4,0),(4,1),(3,2),(2,3),(3,3),(4,2))
        kq,lq=iota((768,768),0),iota((768,768),1)
        at=O_QKV//128
        rows=nn(split3(jnp.concatenate([own[:,at+i] for i in range(6)],axis=1)),one_hot(lq==3*(kq%256)+kq//256))
        rows=rows[0:8]+rows[8:16]+rows[16:24]
        for i in range(6): own[:,at+i]=rows[:,128*i:128*i+128]
        step((2,4),(4,3),(3,4),(4,4))
        finish()
        for hi in range(2):
            shift=14-hi
            src=own[4-4*hi:8-4*hi]
            mid=pltpu.roll(src.reshape(256,128),shift,1).reshape(4,64,128)
            rest=own[4*hi:4*hi+4,63:64]
            for k in range(64):
                before=rest[:,0] if k==0 else mid[:,k-1]
                after=rest[:,0] if k==63 else mid[:,k]
                grad_ref[4*hi:4*hi+4,128*k:128*k+128]=jnp.where(iota((1,128),1)<shift,before,after)
    vm,any_=pl.BlockSpec(memory_space=pltpu.VMEM),pl.BlockSpec(memory_space=pl.ANY)
    return pl.pallas_call(kern,out_shape=(jax.ShapeDtypeStruct((8,MID+128),F32),jax.ShapeDtypeStruct((8,128),F32)),
        in_specs=[any_,any_,vm,vm,vm],out_specs=(vm,vm),scratch_shapes=list(sc.values()), name="student_step",
        compiler_params=pltpu.CompilerParams(vmem_limit_bytes=63<<20, collective_id=cid, has_side_effects=True))(x,tgt,snr,feat,tg)

def segments():
    matrices = [("w_in", 27, C1), ("w_down", 9 * C1, C2), ("w_res1", 9 * C2, C2), ("w_res2", 9 * C2, C2), ("w_time", C1, C2),
                ("w_qkv", C2, 3 * C2), ("w_proj", C2, C2), ("w_up", 9 * C2, C1), ("w_final", 9 * C1, 3)]
    vectors = [("g1", C2), ("s1", C2), ("g2", C2), ("s2", C2), ("g3", C2), ("s3", C2), ("g4", C1), ("s4", C1), ("b_in", C1),
               ("b_down", C2), ("b_res1", C2), ("b_res2", C2), ("b_time", C2), ("b_query", C2), ("b_value", C2), ("b_proj", C2),
               ("b_up", C1), ("b_final", 3)]
    listing, cursor = [], 0
    for name, height, breadth in matrices:
        listing.append((name, cursor, (height, breadth), "matrix"))
        cursor += height * breadth
    for name, length in vectors:
        listing.append((name, cursor, (length,), "gain" if name[0] != "b" else "bias"))
        cursor += length
    return listing

def rates(position):
    learn = jnp.zeros(position.shape, F32)
    decay = jnp.zeros(position.shape, F32)
    for name, offset, shape, kind in segments():
        inside = (position >= offset) & (position < offset + math.prod(shape))
        if kind == "matrix":
            spread = shape[0] ** (-0.5) * ((SIDE * SIDE / 4.0) ** 0.5 if name == "w_proj" else 1.0)
            learn = jnp.where(inside, 0.5 * spread, learn)
            decay = jnp.where(inside, 0.01, decay)
        elif kind == "gain":
            learn = jnp.where(inside, 0.2, learn)
        else:
            learn = jnp.where(inside, 0.05, learn)
    return learn, decay

def angle_of(step):
    return 0.1 + 1.35 * step.astype(F32) / TGRID

def time_features(step):
    half = C1 // 2
    freqs = jnp.exp(-math.log(1000.0) * jnp.arange(half).astype(F32) / half)
    phases = step.astype(F32)[..., None] * freqs
    return jnp.concatenate([jnp.sin(phases), jnp.cos(phases)], axis=-1)

def to_columns(shard, R):
    cols = shard.reshape(-1, R).T
    return jnp.pad(cols, ((0,0),(0,MID+128-cols.shape[1])))

def from_columns(cols, start, D, L):
    R = 256 // D
    body = R * MID
    def piece(at, width): return cols[:, 128*GROUP[at]:128*GROUP[at]+width]
    q = piece(O_QKV,768).reshape(R,3,256).transpose(0,2,1).reshape(R,768)
    cols = jnp.concatenate([piece(O_DOWN,1152), piece(O_R1,2304), piece(O_R2,2304), piece(O_TIME,128), q, piece(O_PROJ,256), piece(O_UP,1152),
                            piece(MID,L//R-MID)], axis=1)
    flat = cols.T.reshape(-1)
    if HEAD % D == 0:
        return jnp.concatenate([flat[body:body+start], flat[:body], flat[body+start:]])
    rest = flat[body:]
    at = jnp.arange(L)
    mid = lax.dynamic_update_slice(jnp.zeros((L,), F32), flat[:body], (start,))
    low = jnp.pad(rest, (0, body)); high = jnp.pad(rest, (body, 0))
    return jnp.where(at < start, low, jnp.where(at < start + body, mid, high))

def lanes(images):
    v = jnp.repeat(images.transpose(1,2,0,3).reshape(256,N,3), 9, axis=2)
    return jnp.pad(v, ((0,0),(0,0),(0,101)))

def local(images, noise, timestep, stride, bucket, steps_table, master, first_moment, second_moment, teacher, step_count):
    axes = ("dp", "mp")
    D = lax.axis_size("dp") * lax.axis_size("mp")
    me = lax.axis_index(axes)
    R, L = 256 // D, master.shape[0]
    start = HEAD // D if HEAD % D == 0 else (HEAD - me + D - 1) // D
    near = lax.axis_size("dp") == 16 and lax.axis_size("mp") == 2
    teacher_cols = to_columns(teacher, R)
    angle = angle_of(timestep)
    if near:
        teacher_all, noisy = gather_call(teacher_cols, jnp.cos(angle), jnp.sin(angle), images, noise, 1)
    else:
        teacher_all = lax.all_gather(teacher_cols, axes, axis=0, tiled=True)
        noisy = lanes(jnp.cos(angle)[:,None,None,None] * images + jnp.sin(angle)[:,None,None,None] * noise)
    student_all = lax.all_gather(to_columns(master.astype(BF), R), axes, axis=0, tiled=True)
    wide = lambda v: jnp.where(jnp.arange(128) < 27, v[..., None], 0.0)
    picked = jnp.sum(jnp.where(jnp.arange(steps_table.shape[0]) == bucket[0], steps_table, 0))
    turn = jnp.arange(KMAX)[:, None]
    current = timestep[None] - turn * stride[None]
    later = current - stride[None]
    keep = jnp.sin(angle_of(later)) / jnp.sin(angle_of(current))
    take = jnp.cos(angle_of(later)) - keep * jnp.cos(angle_of(current))
    features = jax.nn.silu(time_features(current)).astype(BF)
    final_t = timestep - picked * stride
    below = jnp.sin(angle - angle_of(final_t))
    target = teacher_call(D, picked.reshape(1), noisy, features, wide(take), wide(keep), wide(jnp.sin(angle)/below),
                          wide(-jnp.sin(angle_of(final_t))/below), teacher_all)
    snr = wide(jnp.maximum(jnp.square(jnp.cos(angle)/jnp.sin(angle)), 1.0))
    total = images.shape[0] * D
    if near:
        grads, sums = student_step(D, noisy, target, snr, features[0], student_all, total, 2)
    else:
        out, sums, kept = student_call(D, noisy, target, snr, features[0], student_all)
        sums = lax.psum(sums, axes)
        grads = bwd_call(dict(kept, out=out, tgt=target, snr=snr, stat=sums, feat=features[0]), total)
    pick = sums[:5, 0:27:9]
    mean_t, mean_o = pick[0]/(256*total), pick[2]/(256*total)
    var_t, var_o = pick[1]/(256*total) - jnp.square(mean_t), pick[3]/(256*total) - jnp.square(mean_o)
    loss = jnp.sum(pick[4])/(768*total) + jnp.sum(jnp.square(mean_o-mean_t) + jnp.square(var_o-var_t))
    if near:
        part = grads
    else:
        order = grads.reshape(R, D, MID+128)
        if HEAD % D:
            order = jnp.concatenate([jnp.roll(order[:, :, :MID], HEAD % D, axis=1), order[:, :, MID:]], axis=2)
        part = lax.psum_scatter(order, axes, scatter_dimension=1, tiled=True).reshape(R, MID+128)
    grad = part[:, :L//R].T.reshape(-1) if near else from_columns(part, start, D, L)
    learn, decay = rates(jnp.arange(L, dtype=jnp.int32) * D + me)
    steps_done = step_count[0].astype(F32)
    new_first = 0.5 * first_moment + 0.5 * grad
    new_second = 0.5 * second_moment + 0.5 * jnp.square(grad)
    fix_rate = 1.0 - jnp.power(0.5, steps_done)
    new_master = master - learn * (new_first / fix_rate / (jnp.sqrt(new_second / fix_rate) + 1e-08) + decay * master)
    return loss, new_master, new_first, new_second

def solution(mesh):
    s = P(("dp", "mp"))
    i = P(("dp", "mp"), None, None, None)
    return jax.shard_map(local, mesh=mesh, in_specs=(i, i, s, s, s, P(), s, s, s, s, P()), out_specs=(P(), s, s, s), check_vma=False)
```

```python
import math
import jax
import jax.numpy as jnp
from jax import lax
from jax.experimental import pallas as pl
from jax.experimental.pallas import tpu as pltpu
from jax.sharding import PartitionSpec as P

C1, C2, N = 128, 256, 16
SIDE, TGRID, KMAX = 16, 64, 4
F32, BF = jnp.float32, jnp.bfloat16
O_DOWN, O_R1, O_R2, O_TIME, O_QKV, O_PROJ, O_UP, MID = 0, 1152, 3456, 5760, 5888, 6656, 6912, 8064
HEAD = 3456
BLOCK = {}
_at = 54
for _name, _wide in (("g1",2),("s1",2),("g2",2),("s2",2),("g3",2),("s3",2),("g4",1),("s4",1),("b_in",1),("b_down",2),("b_res1",2),
                     ("b_res2",2),("b_time",2),("b_query",2),("b_value",2),("b_proj",2),("b_up",1),("b_final",1)):
    BLOCK[_name] = (_at, _wide)
    _at += _wide

def iota(shape, d): return lax.broadcasted_iota(jnp.int32, shape, d)

def nt(a, b): return lax.dot_general(a, b, (((1,),(1,)),((),())), preferred_element_type=F32)
def nn(a, b): return lax.dot_general(a, b, (((1,),(0,)),((),())), preferred_element_type=F32)

def one_hot(cond): return jnp.where(cond, 1.0, 0.0).astype(BF)

def split3(v):
    hi = v.astype(BF); r = v - hi.astype(F32)
    mid = r.astype(BF); lo = (r - mid.astype(F32)).astype(BF)
    return jnp.concatenate([hi, mid, lo], axis=0)

def pile(v, k):
    return jnp.sum(jnp.sum(v.reshape((-1, k) + v.shape[1:]), axis=0), axis=0)

def group_sum(v, same):
    r = nn(split3(v), same)
    return r[0:N] + r[N:2*N] + r[2*N:3*N]

def prep(tg_ref, wt_ref, wup_ref, win_ref, wfin_ref, wfb_ref, sm_ref, D):
    R = 256 // D
    row, rho = iota((256,256),1), iota((256,256),0)
    perm = one_hot(rho == row // R + D * (row % R))
    CH = 1152
    for c in range(7):
        wt_ref[0:128, c*CH:(c+1)*CH] = nn(perm[128:256], tg_ref[:, 13+c*CH:13+(c+1)*CH]).astype(BF)
        wt_ref[128:256, c*CH:(c+1)*CH] = nn(perm[0:128], tg_ref[:, 14+c*CH:14+(c+1)*CH]).astype(BF)
    kk, ci = iota((256,256),0), iota((256,256),1)
    peo = one_hot(ci == 2*(kk % 128) + kk // 128)
    for t in range(9):
        cs = O_UP + t*128
        both = jnp.concatenate([wt_ref[0:128, cs:cs+128], wt_ref[128:256, cs:cs+128]], axis=1)
        wup_ref[t] = nn(both, peo).astype(BF)
    kq, lq = iota((768,768),0), iota((768,768),1)
    pq = one_hot(kq == 3*(lq % 256) + lq // 256)
    wt_ref[:, O_QKV:O_QKV+768] = nn(wt_ref[:, O_QKV:O_QKV+768], pq).astype(BF)
    scol, srho = iota((256,128),1), iota((256,128),0)
    sm_ref[...] = jnp.where((scol < 13) | ((scol == 13) & (srho < 128)), nn(perm, tg_ref[:, 0:128]), nn(perm, tg_ref[:, MID:MID+128])).T
    halves = jnp.concatenate([sm_ref[0:32, 0:128], sm_ref[0:32, 128:256]], axis=0).astype(BF)
    l, r = iota((128,64),0), iota((128,64),1)
    k = 3*(l % 9) + l // 9
    win_ref[...] = nn(one_hot((l < 27) & (r == 32*(k % 2) + k // 2)), halves).astype(BF)
    t16, r16 = iota((16,64),0), iota((16,64),1)
    pieces = []
    for h in range(3):
        blk = 27 + 3*t16 + h
        pieces.append(nn(one_hot((t16 < 9) & (r16 == 32*(blk % 2) + blk // 2)), halves))
    flat = jnp.concatenate(pieces, axis=1).astype(BF)
    acc = jnp.zeros((128,128), F32)
    for c in range(3):
        wc = nn(flat, one_hot(iota((384,128),0) == 3*iota((384,128),1) + c)).astype(BF)
        acc += nn(one_hot((iota((128,16),1) < 9) & (iota((128,16),0) == 9*c + iota((128,16),1))), wc)
    wfb = acc.astype(BF)
    wfb_ref[...] = wfb
    a, z = iota((128,128),0), iota((128,128),1)
    for r in range(3):
        wfin_ref[:, 128*r:128*r+128] = nn(one_hot((a < 81) & (z == 9*(a % 27 // 9) + 3*r + a // 27)), wfb).astype(BF)

def final_bias(sm_ref):
    b = sm_ref[42:43, 0:128].astype(BF)
    return nn(b, one_hot((iota((128,128),1) < 27) & (iota((128,128),0) == iota((128,128),1) // 9)))

def gn_stats(src, P, per, same):
    k = 4
    B = 16
    s = [pile(src[pl.ds(i,B)], k) for i in range(0,P,B)]
    m = sum(s[1:], s[0]) * (1.0/P)
    q = [pile(jnp.square(src[pl.ds(i,B)] - m), k) for i in range(0,P,B)]
    mean = group_sum(m, same) * (1.0/per)
    spread = sum(q[1:], q[0]) * (1.0/P) + jnp.square(m - mean)
    return mean, lax.rsqrt(group_sum(spread, same) * (1.0/per) + 1e-5)

def vec(v_ref, name, C=C2):
    at, wide = BLOCK[name]
    return jnp.concatenate([v_ref[b//2:b//2+1, 128*(b%2):128*(b%2)+128] for b in range(at, at+wide)], axis=1)

def net(x_ref, feat, wt, wup, win, wfin, v_ref, sc):
    xp, tp, top, low, ap, mid, res, qkv, ob, yp, up, ep = (sc[k] for k in ("xp","tp","top","low","ap","mid","res","qkv","ob","yp","up","ep"))
    ap2 = sc.get("ap2", ap)
    lane = iota((1,1,128),2)
    def save(si, m, inv):
        if "st" in sc:
            C = m.shape[1]
            sc["st"][2*si,:,0:C] = m
            sc["st"][2*si+1,:,0:C] = inv
    bfin = final_bias(v_ref)
    def a0(y, _):
        xp[y+1, 1:17] = x_ref[pl.ds(y*16,16)].astype(BF)
        return 0
    lax.fori_loop(0,16,a0,0,unroll=4)
    def a1(y2, _):
        pieces=[]
        for k in range(4):
            y = y2*4+k
            cols = jnp.zeros((16,16,128),BF)
            for t in range(9):
                w = xp[y+t//3, t%3:t%3+16]
                cols = jnp.where((lane%9==t)&(lane<27), w, cols) if t else jnp.where((lane%9==0)&(lane<27), w, jnp.zeros_like(w))
            if "cols" in sc: sc["cols"][pl.ds(y*16,16)] = cols
            pieces.append(cols.reshape(256,128))
        r = nn(jnp.concatenate(pieces,axis=0), win[...]) + vec(v_ref,"b_in",C1)
        top[pl.ds(y2*64,64)] = r.reshape(64,16,128)
        rb = r.astype(BF).reshape(4,8,2,16,128)
        for k in range(4):
            p = y2*4+k+1
            tp[p//2, p%2, 0:8, 1] = rb[k,:,0]
            tp[p//2, p%2, 1:9, 0] = rb[k,:,1]
        return 0
    lax.fori_loop(0,4,a1,0,unroll=2)
    taps=[]
    for t in range(9):
        ty,tx=t//3,t%3
        taps.append(tp[ty//2:ty//2+8, ty%2, tx//2:tx//2+8, tx%2].reshape(1024,128))
    low[...] = (nt(jnp.concatenate(taps,axis=1), wt[:,O_DOWN:O_DOWN+1152]) + vec(v_ref,"b_down")).reshape(64,16,256)
    def norm_act(src, ap, g, s, si):
        m, inv = gn_stats(src, 64, 8, sc["same8"][...])
        save(si, m, inv)
        half = 0.5*inv*vec(v_ref,g)
        shift = 0.5*vec(v_ref,s) - m*half
        for y in range(8):
            h = src[y*8:y*8+8]*half + shift
            ap[y+1,1:9] = (h + h*jnp.tanh(h)).astype(BF)
    def conv3(ap, off):
        return nt(jnp.concatenate([ap[t//3:t//3+8, t%3:t%3+8].reshape(1024,256) for t in range(9)],axis=1), wt[:,off:off+2304])
    norm_act(low,ap,"g1","s1",0)
    emb = nt(feat, wt[:,O_TIME:O_TIME+128]) + vec(v_ref,"b_time")
    mid[...] = (conv3(ap,O_R1) + vec(v_ref,"b_res1")).reshape(64,16,256) + emb
    norm_act(mid,ap2,"g2","s2",1)
    res[...] = low[...] + (conv3(ap2,O_R2) + vec(v_ref,"b_res2")).reshape(64,16,256)
    m, inv = gn_stats(res, 64, 8, sc["same8"][...])
    save(2, m, inv)
    gain = inv*vec(v_ref,"g3")
    nb = (res[...]*gain + (vec(v_ref,"s3") - m*gain)).astype(BF).reshape(1024,256)
    q = nt(nb, wt[:,O_QKV:O_QKV+256]) + vec(v_ref,"b_query")
    k_ = nt(nb, wt[:,O_QKV+256:O_QKV+512])
    v_ = nt(nb, wt[:,O_QKV+512:O_QKV+768])+vec(v_ref,"b_value")
    for i, z in enumerate((q, k_, v_)):
        z = z.astype(BF).astype(F32)
        qkv[2*i] = z[:,0:128]
        qkv[2*i+1] = z[:,128:256]
    def head(j, n):
        return jnp.concatenate([qkv[2*j,pl.ds(n,64,stride=16),:], qkv[2*j+1,pl.ds(n,64,stride=16),:]], axis=1).astype(BF)
    s = jnp.concatenate([nt(head(0,n), head(1,n)) for n in range(N)], axis=0)*(C2**-0.5)
    e = jnp.exp(s - jnp.max(s,axis=1,keepdims=True))
    p = (e/jnp.sum(e,axis=1,keepdims=True)).astype(BF)
    for n in range(N):
        o = nn(p[64*n:64*n+64], head(2,n)).astype(BF).astype(F32)
        ob[0,pl.ds(n,64,stride=16),:] = o[:,0:128]
        ob[1,pl.ds(n,64,stride=16),:] = o[:,128:256]
    obb = jnp.concatenate([ob[0],ob[1]],axis=1).astype(BF)
    if "obb" in sc: sc["obb"][...] = obb
    att_out = res[...].reshape(1024,256) + (nt(obb, wt[:,O_PROJ:O_PROJ+256]) + vec(v_ref,"b_proj"))
    attb = att_out.astype(BF)
    if "attb" in sc: sc["attb"][...] = attb
    for t in range(0,9,2):
        k = min(2, 9-t)
        r = nt(attb, wup[t:t+k].reshape(128*k,256))
        for i in range(k):
            yp[t+i,1:9,1:9] = r[:,128*i:128*i+128].reshape(8,8,16,128)
    def u(i,_):
        for a in range(2):
            for b in range(2):
                acc=None
                for t in range(9):
                    r,c=t//3-1,t%3-1
                    dr=(a+r)//2; dc=(b+c)//2
                    v=yp[t, i+dr+1, 1+dc:9+dc]
                    acc = v if acc is None else acc+v
                up[i,a,:,b] = acc + vec(v_ref,"b_up",C1) + sc["top6"][i,a,:,b]
        return 0
    lax.fori_loop(0,8,u,0,unroll=2)
    upf = sc["up3"]
    m, inv = gn_stats(upf, 256, 4, sc["same4"][...])
    save(3, m, inv)
    half = 0.5*inv*vec(v_ref,"g4",C1)
    shift = 0.5*vec(v_ref,"s4",C1) - m*half
    def b4(y,_):
        h = upf[pl.ds(y*16,16)]*half + shift
        ep[y+1,1:17] = (h + h*jnp.tanh(h)).astype(BF)
        return 0
    lax.fori_loop(0,16,b4,0,unroll=4)
    def fin(put):
        def f(y4,_):
            cols=jnp.concatenate([ep[pl.ds(y4*8+r,8)].reshape(2304,128) for r in range(3)],axis=1)
            d=nt(cols, wfin[...]).reshape(8,18,16,128)
            put(y4, (d[:,0:16] + pltpu.roll(d[:,1:17].reshape(2048,128),101,1).reshape(8,16,16,128)
                     + pltpu.roll(d[:,2:18].reshape(2048,128),74,1).reshape(8,16,16,128)).reshape(128,16,128) + bfin)
            return 0
        lax.fori_loop(0,2,f,0,unroll=2)
    return fin

def scratch():
    V=pltpu.VMEM
    return dict(wt=V((256,MID),BF), wup=V((9,128,256),BF), win=V((128,128),BF), wfin=V((128,384),BF), wfb=V((128,128),BF), sm=V((128,256),F32), xp=V((18,18,16,128),BF), tp=V((9,2,9,2,16,128),BF),
      top=V((256,16,128),F32), low=V((64,16,256),F32), ap=V((10,10,16,256),BF), mid=V((64,16,256),F32), res=V((64,16,256),F32),
      qkv=V((6,1024,128),F32), ob=V((2,1024,128),F32), yp=V((9,10,10,16,128),F32), up=V((8,2,8,2,16,128),F32), ep=V((18,18,16,128),BF), same8=V((256,256),BF), same4=V((128,128),BF))
KEYS=list(scratch().keys())

def zero_borders(sc):
    for k in ("xp","ep","tp","ap","ap2"):
        if k in sc: sc[k][...] = jnp.zeros(sc[k].shape, sc[k].dtype)
    yp = sc["yp"]
    edge = jnp.zeros((9,10,16,128), F32)
    for k in (0,9):
        yp[:,k] = edge
        yp[:,:,k] = edge
    for k, C, per in (("same8",256,8), ("same4",128,4)):
        sc[k][...] = one_hot(iota((C,C),0)//per == iota((C,C),1)//per)

def views(sc):
    sc=dict(sc)
    sc["top6"]=sc["top"].reshape(8,2,8,2,16,128)
    sc["up3"]=sc["up"].reshape(256,16,128)
    return sc

def teacher_call(D, cnt, x, feat, ce, cl, tc, nc, tg):
    def kern(cnt_ref, x_ref, feat_ref, ce_ref, cl_ref, tc_ref, nc_ref, tg_ref, out_ref, *scr):
        sc = views(dict(zip(KEYS, scr)))
        zero_borders(sc)
        prep(tg_ref, *(sc[k] for k in WKEYS), D)
        out_ref[...] = x_ref[...]
        def step(j, _):
            fin = net(out_ref, feat_ref[j], sc["wt"], sc["wup"], sc["win"], sc["wfin"], sc["sm"], sc)
            ce_, cl_ = ce_ref[j], cl_ref[j]
            def put(y4, e):
                out_ref[pl.ds(y4*128,128)] = ce_*e + cl_*out_ref[pl.ds(y4*128,128)]
            fin(put)
            return 0
        lax.fori_loop(0, cnt_ref[0], step, 0)
        def tgt(i, _):
            out_ref[pl.ds(i*16,16)] = tc_ref[...]*out_ref[pl.ds(i*16,16)] + nc_ref[...]*x_ref[pl.ds(i*16,16)]
            return 0
        lax.fori_loop(0, 16, tgt, 0)
    vm = pl.BlockSpec(memory_space=pltpu.VMEM)
    return pl.pallas_call(kern, out_shape=jax.ShapeDtypeStruct((256,16,128),F32),
        in_specs=[pl.BlockSpec(memory_space=pltpu.SMEM)]+[vm]*7, out_specs=vm, scratch_shapes=list(scratch().values()), name="teacher_steps",
        compiler_params=pltpu.CompilerParams(vmem_limit_bytes=60<<20))(cnt, x, feat, ce, cl, tc, nc, tg)

WKEYS = ["wt","wup","win","wfin","wfb","sm"]
RES = ["wt","wup","wfb","sm","tp","low","ap","mid","res","qkv","up"]
def loss_sums(t_ref, out_ref, snr_ref, sum_ref):
    def s(i,c):
        t,o=t_ref[pl.ds(i*16,16)],out_ref[pl.ds(i*16,16)]
        d=o-t
        return tuple(a+jnp.sum(b,axis=0) for a,b in zip(c,(t,t*t,o,o*o,d*d)))
    z=jnp.zeros((N,128),F32)
    r=lax.fori_loop(0,16,s,(z,)*5)
    r=r[:4]+(r[4]*snr_ref[...],)
    sum_ref[...]=jnp.concatenate([jnp.sum(a,axis=0,keepdims=True) for a in r]+[jnp.zeros((3,128),F32)],axis=0)

def student_call(D, x, tgt, snr, feat, tg):
    vm=pl.BlockSpec(memory_space=pltpu.VMEM)
    sh=scratch()
    extra=dict(st=pltpu.VMEM((8,16,256),F32),cols=pltpu.VMEM((256,16,128),BF),attb=pltpu.VMEM((1024,256),BF),obb=pltpu.VMEM((1024,256),BF),ap2=pltpu.VMEM((10,10,16,256),BF))
    outs={k:sh[k] for k in RES}; outs.update(extra)
    scr={k:v for k,v in sh.items() if k not in outs}
    ok,sk=list(outs),list(scr)
    def kern(x_ref,t_ref,snr_ref,feat_ref,tg_ref,out_ref,sum_ref,*refs):
        sc=views(dict(zip(ok+sk,refs)))
        zero_borders(sc)
        prep(tg_ref,*(sc[k] for k in WKEYS),D)
        fin=net(x_ref,feat_ref[...],sc["wt"],sc["wup"],sc["win"],sc["wfin"],sc["sm"],sc)
        def put(y4,e): out_ref[pl.ds(y4*128,128)]=e
        fin(put)
        loss_sums(t_ref,out_ref,snr_ref,sum_ref)
    res=pl.pallas_call(kern,
        out_shape=(jax.ShapeDtypeStruct((256,16,128),F32),jax.ShapeDtypeStruct((8,128),F32))+tuple(jax.ShapeDtypeStruct(outs[k].shape,outs[k].dtype) for k in ok),
        in_specs=[vm]*5,out_specs=(vm,)*(2+len(ok)),scratch_shapes=[scr[k] for k in sk], name="student_forward",
        compiler_params=pltpu.CompilerParams(vmem_limit_bytes=62<<20))(x,tgt,snr,feat,tg)
    return res[0],res[1],dict(zip(ok,res[2:]))

MESH = pl.DeviceIdType.MESH

def place():
    dp = lax.axis_index("dp")
    return dp // 4, dp // 2 % 2, dp % 2, lax.axis_index("mp")

def peer(z, y, x, c):
    return {"dp": z*4 + y*2 + x, "mp": c}

def greet(peers):
    barrier = pltpu.get_barrier_semaphore()
    for p in peers:
        pl.semaphore_signal(barrier, inc=1, device_id=p, device_id_type=MESH)
    pl.semaphore_wait(barrier, len(peers))

def partners():
    z, y, x, c = place()
    return [peer(z,y,x,1-c), peer(z,y,1-x,c), peer(z,1-y,x,c)] + [peer((z+o)%4,y,x,c) for o in (1,2,3)]

def gather_copies(s, p, streams, in_ref, out_ref, send, recv):
    z, y, x, c = place()
    wide = in_ref.shape[1] // streams
    all_, lo, hi = pl.ds(s*wide, wide), pl.ds(s*wide, wide//2), pl.ds(s*wide + wide//2, wide//2)
    to_x, to_y = peer(z,y,1-x,c), peer(z,1-y,x,c)
    if p == 0:
        return [pltpu.make_async_remote_copy(in_ref.at[:,all_], out_ref.at[z,y,x,c,:,all_], send.at[s,o-1], recv.at[s,3-o],
                device_id=peer((z+o)%4,y,x,c), device_id_type=MESH) for o in (2,1,3)]
    if p == 1:
        moves = [(out_ref.at[:,y,x,c,:,lo], to_x, 3), (out_ref.at[:,y,x,c,:,hi], to_y, 4)]
    elif p == 2:
        moves = [(out_ref.at[:,y,:,c,:,lo], to_y, 5), (out_ref.at[:,:,x,c,:,hi], to_x, 6)]
    else:
        moves = [(out_ref.at[:,:,:,c,:,all_], peer(z,y,x,1-c), 7)]
    return [pltpu.make_async_remote_copy(part, part, send.at[s,i], recv.at[s,i], device_id=to, device_id_type=MESH) for part, to, i in moves]

def mix_images(ca_ref, sa_ref, im_ref, ns_ref, x_ref, flat, planes):
    flat[...] = jnp.zeros(flat.shape, F32)
    for n in range(N):
        for c in range(3):
            flat[16*n:16*n+16, 16*c:16*c+16] = ca_ref[n]*im_ref[n,c] + sa_ref[n]*ns_ref[n,c]
    parts = split3(flat[...])
    k, l = iota((128,512),0), iota((128,512),1)
    for q in range(4):
        r = nn(parts, one_hot((l % 128 < 27) & (k == 16*(l % 128 // 9) + 4*q + l // 128)))
        r = r[0:256] + r[256:512] + r[512:768]
        for i in range(4): planes[4*q+i] = r[:,128*i:128*i+128]
    for y in range(SIDE):
        for x in range(SIDE):
            x_ref[SIDE*y+x] = planes[x,pl.ds(y,N,stride=SIDE),:]

def gather_kernel(streams, ca_ref, sa_ref, im_ref, ns_ref, in_ref, out_ref, x_ref, send, recv, keep, flat, planes):
    z, y, x, c = place()
    greet(partners())
    own = pltpu.make_async_copy(in_ref, out_ref.at[z,y,x,c], keep)
    own.start()
    live = {(s,p): gather_copies(s,p,streams,in_ref,out_ref,send,recv) for s in range(streams) for p in range(4)}
    for s in range(streams):
        for d in live[s,0]: d.start()
    mix_images(ca_ref, sa_ref, im_ref, ns_ref, x_ref, flat, planes)
    own.wait()
    for step in range(streams + 3):
        for s in range(streams):
            p = step - s
            if 0 <= p <= 3:
                for d in live[s,p]: d.wait_recv()
                if p < 3:
                    for d in live[s,p+1]: d.start()
    for ds in live.values():
        for d in ds: d.wait_send()

def gather_call(block, ca, sa, images, noise, cid, streams=4):
    rows, wide = block.shape
    any_, vm, sm = (pl.BlockSpec(memory_space=m) for m in (pl.ANY, pltpu.VMEM, pltpu.SMEM))
    out, noisy = pl.pallas_call(lambda *r: gather_kernel(streams, *r),
        out_shape=(jax.ShapeDtypeStruct((4,2,2,2,rows,wide), block.dtype), jax.ShapeDtypeStruct((256,N,128), F32)),
        in_specs=[sm,sm,vm,vm,any_], out_specs=(any_,vm), name="gather_columns",
        scratch_shapes=[pltpu.SemaphoreType.DMA((streams,8)), pltpu.SemaphoreType.DMA((streams,8)), pltpu.SemaphoreType.DMA,
                        pltpu.VMEM((256,128),F32), pltpu.VMEM((16,256,128),F32)],
        compiler_params=pltpu.CompilerParams(collective_id=cid, has_side_effects=True, vmem_limit_bytes=24<<20))(
            ca, sa, images.transpose(0,3,1,2), noise.transpose(0,3,1,2), block)
    return out.reshape(32*rows, wide), noisy

def sum_kernel(in_ref, out_ref, box, send, recv):
    z, y, x, c = place()
    hops = [peer(z,y,x,1-c), peer(z,y,1-x,c), peer(z,1-y,x,c), peer(z+1-2*(z%2),y,x,c), peer((z+2)%4,y,x,c)]
    out_ref[...] = in_ref[...]
    for k, to in enumerate(hops):
        box[k] = out_ref[...]
        d = pltpu.make_async_remote_copy(box.at[k], box.at[5+k], send.at[k], recv.at[k], device_id=to, device_id_type=MESH)
        d.start()
        d.wait()
        out_ref[...] += box[5+k]

STREAMS = ((0,2), (2,2), (4,2), (6,1), (7,1))

def row_of(r):
    return 128*(r//128) + 32*(r//8%4) + 8*(r//32%4) + 4*(r%2) + 2*(r//2%2) + r//4%2

def scatter_scratch():
    V = pltpu.VMEM
    sc = {}
    for s, (_, u) in enumerate(STREAMS):
        sc[f"c{s}"] = V((u,2,2,2,4,4,8,128),F32)
        sc[f"h{s}"] = V((u,2,2,4,4,8,128),F32)
        sc[f"q{s}"] = V((u,2,4,4,8,128),F32)
        sc[f"z{s}"] = V((3,u,2,4,8,128),F32)
    sc["ssem"] = pltpu.SemaphoreType.DMA((len(STREAMS),8))
    sc["rsem"] = pltpu.SemaphoreType.DMA((len(STREAMS),8))
    return sc

def scatter_steps(g_ref, out_ref, sc):
    z, y, x, c = place()
    send, recv = sc["ssem"], sc["rsem"]
    live = {}
    def bufs(s): return tuple(sc[f"{k}{s}"] for k in "chqz")
    def copies(s, p):
        r0, r1, r2, r3 = bufs(s)
        to_x, to_y = peer(z,y,1-x,c), peer(z,1-y,x,c)
        if p == 0:
            moves = [(g_ref.at[pl.ds(*STREAMS[s]),:,1-c], r0, peer(z,y,x,1-c), 0, 0)]
        elif p == 1:
            moves = [(r0.at[:,0,1-x], r1.at[:,0], to_x, 1, 1), (r0.at[:,1,:,1-y], r1.at[:,1], to_y, 2, 2)]
        elif p == 2:
            moves = [(r1.at[:,0,1-y], r2.at[:,0], to_y, 3, 3), (r1.at[:,1,1-x], r2.at[:,1], to_x, 4, 4)]
        else:
            moves = [(r2.at[:,:,(z+o)%4], r3.at[3-o], peer((z+o)%4,y,x,c), 4+o, 8-o) for o in (2,1,3)]
        return [pltpu.make_async_remote_copy(src, dst, send.at[s,i], recv.at[s,k], device_id=to, device_id_type=MESH) for src, dst, to, i, k in moves]
    def add(s, p):
        r0, r1, r2, r3 = bufs(s)
        first, number = STREAMS[s]
        for u in range(number):
            if p == 0:
                for h in range(2):
                    for i in range(2):
                        r0[u,h,i] += g_ref[first+u,h,c,i]
            elif p == 1:
                r1[u,0] += r0[u,0,x]
                r1[u,1] += r0[u,1,:,y]
            elif p == 2:
                r2[u,0] += r1[u,0,y]
                r2[u,1] += r1[u,1,x]
            else:
                total = r2[u,:,z] + r3[0,u] + r3[1,u] + r3[2,u]
                for k in range(8):
                    out_ref[:,:,STORED[8*(first+u)+k]] = total[:,:,k]
    def advance(s, p):
        if p:
            for d in live[s,p-1]: d.wait_recv()
            add(s, p-1)
        if p < 4:
            live[s,p] = copies(s,p)
            for d in live[s,p]: d.start()
    def finish():
        for ds in live.values():
            for d in ds: d.wait_send()
    return advance, finish

def tn(a, b): return lax.dot_general(a, b, (((0,),(0,)),((),())), preferred_element_type=F32)

def bwd_kernel(x_refs, o_refs, sc):
    X, S = x_refs, sc
    (G,) = o_refs
    sg, sn_total = S["sg"], X["total"]
    v_ref, wt, wup, st = X["v"], X["wt"], X["wup"], X["st"]
    gp18, gcols, big, dp, s_hi, s_lo, gp, da, gres, gqkv, gmx = (S[k] for k in ("gp18","gcols","big","dp","s_hi","s_lo","gp","da","gres","gqkv","gmx"))
    lane = iota((1,1,128),2)
    for k, C, per in (("same8",256,8), ("same4",128,4)):
        S[k][...] = one_hot(iota((C,C),0)//per == iota((C,C),1)//per)
    for k in ("gp18","dp","gp"):
        S[k][...] = jnp.zeros(S[k].shape, S[k].dtype)
    sg[...] = jnp.zeros((128,256),F32)
    def put_block(b, val):
        sg[b//2:b//2+1, 128*(b%2):128*(b%2)+128] = val
    def put_vec(name, val, C=C2):
        at, wide = BLOCK[name]
        for k in range(wide):
            put_block(at+k, val[:, 128*k:128*k+128])
    def rowsum(a): return jnp.sum(a, axis=0, keepdims=True)
    step, near = S["step"], S["near"]
    def put_g(val, col, row0=0):
        rows, width = val.shape
        col = 128*next(GROUP[o] + (col-o)//128 for o in sorted(GROUP, reverse=True) if col >= o)
        for c in range(width//128):
            at = col//128+c
            for r in range(row0, row0+rows, 8):
                if near: to = pl.ds(2048*(at//8) + 1024*(r//128) + 32*(r//32%4) + 8*(r//8%4) + at%8, 8, stride=128)
                else: to = pl.ds(64*r+at, 8, stride=64)
                G[to,:] = val[r-row0:r-row0+8, c*128:c*128+128]
    pm = S["pm"]
    pm[...] = one_hot(iota((256,256),1) == (row_of(iota((256,256),0)) if near else iota((256,256),0)))
    def turn(g): return nt(pm[...], g).astype(BF)
    pixels = 256.0*sn_total
    so = X["stat"][...]
    mt, mo = so[0:1]/pixels, so[2:3]/pixels
    vt_, vo = so[1:2]/pixels-mt*mt, so[3:4]/pixels-mo*mo
    cb = 4.0*(vo-vt_)/pixels
    ca = 2.0*(mo-mt)/pixels-cb*mo
    sn = X["snr"][...]*(2.0/(768.0*sn_total))
    acc=jnp.zeros((N,128),F32)
    def g0(y,acc):
        o=X["out"][pl.ds(y*16,16)]
        go = sn*(o-X["tgt"][pl.ds(y*16,16)]) + ca + cb*o
        gp18[y+1,1:17]=go.astype(BF)
        return acc+jnp.sum(go,axis=0)
    acc=lax.fori_loop(0,16,g0,acc)
    acc=rowsum(acc)
    lane2=iota((1,128),1)
    put_block(84, sum(jnp.where(lane2==c, jnp.sum(jnp.where(lane2==9*c,acc,0.0),axis=1,keepdims=True),0.0) for c in range(3)))
    def g1(y,_):
        for t in range(9):
            w = gp18[y+2-t//3, 2-t%3:18-t%3]
            cols = jnp.where((lane%9==t)&(lane<27), w, cols) if t else jnp.where((lane%9==0)&(lane<27), w, jnp.zeros_like(w))
        gcols[pl.ds(y*16,16)] = cols
        return 0
    lax.fori_loop(0,16,g1,0)
    big[...] = nn(gcols[...].reshape(4096,128), X["wfb"][...]).reshape(256,16,128)
    def gn_bwd(src, dref, si, gname, sname, C, per, same, rows, k, act_put, dx_put, silu=True):
        m, inv = st[2*si,:,0:C], st[2*si+1,:,0:C]
        g, s = vec(v_ref,gname,C), vec(v_ref,sname,C)
        w = 512//C
        zero = jnp.zeros((w,N,C),F32)
        def pick(v): return jnp.sum(v.reshape((-1,w)+v.shape[1:]),axis=0)
        def p1(y,c):
            A,B=c
            xh=(src[pl.ds(y*k,k)]-m)*inv
            d=dref[pl.ds(y*k,k)]
            if silu:
                h=xh*(0.5*g)+0.5*s
                th=jnp.tanh(h); sg=0.5+0.5*th; act=h+h*th
                act_put(y,act.astype(BF))
                d=d*(sg+act*(1.0-sg))
                dref[pl.ds(y*k,k)]=d
            else:
                act_put(y,(xh*g+s).astype(BF))
            return A+pick(d), B+pick(d*xh)
        A,B=lax.fori_loop(0,rows,p1,(zero,zero),unroll=4)
        A,B=jnp.sum(A,axis=0),jnp.sum(B,axis=0)
        put_vec(gname,rowsum(B),C); put_vec(sname,rowsum(A),C)
        cnt=1.0/(per*rows*k)
        ga=group_sum(g*A,same)*cnt; gb=group_sum(g*B,same)*cnt
        ig=inv*g; ib=inv*inv*gb; ic=m*ib-inv*ga
        def p2(y,acc):
            dx=ig*dref[pl.ds(y*k,k)]-ib*src[pl.ds(y*k,k)]+ic
            return acc+pick(dx_put(y,dx))
        return lambda: jnp.sum(lax.fori_loop(0,rows,p2,zero,unroll=4),axis=0)
    fused = "ep18" in S
    def act4(y,a):
        if not fused: S["ep"][pl.ds(y*16,16)]=a
    def dx4(y,dx):
        big[pl.ds(y*16,16)]=dx
        b=dx.astype(BF).reshape(8,2,16,128)
        p=y+1
        dp[p//2,p%2,0:8,1]=b[:,0]
        dp[p//2,p%2,1:9,0]=b[:,1]
        return dx
    fin=gn_bwd(X["up"].reshape(256,16,128),big,3,"g4","s4",128,4,S["same4"][...],16,16,act4,dx4)
    dwf = tn(gcols[...].reshape(4096,128), (S["ep18"][1:17,1:17] if fused else S["ep"][...]).reshape(4096,128))
    flat = jnp.zeros((9,384),F32)
    for c in range(3):
        p3 = one_hot(iota((128,384),1) == 3*iota((128,384),0) + c)
        piece = dwf[9*c:9*c+9]
        hi = piece.astype(BF); rest = piece-hi.astype(F32)
        mi = rest.astype(BF); lo = (rest-mi.astype(F32)).astype(BF)
        flat += nn(hi,p3)+nn(mi,p3)+nn(lo,p3)
    for t in range(9):
        for h in range(3):
            put_block(27+3*t+h, flat[t:t+1,128*h:128*h+128])
    put_vec("b_up",rowsum(fin()),128)
    PAIR={-1:((1,0),(1,1)),0:((0,1),(1,0)),1:((0,0),(0,1))}
    def su(i,_):
        for r in (-1,0,1):
            (ra,pa),(rb,pb)=PAIR[r]
            V={}
            for cp in range(2):
                V[cp]=dp[i+ra,pa,:,cp].astype(F32)+dp[i+rb,pb,:,cp].astype(F32)
            for c in (-1,0,1):
                (ca_,qa),(cb_,qb)=PAIR[c]
                s=V[qa][ca_:ca_+8]+V[qb][cb_:cb_+8]
                t=(r+1)*3+c+1
                hi=s.astype(BF)
                s_hi[t,pl.ds(i*8,8)]=hi
                s_lo[t,pl.ds(i*8,8)]=(s-hi.astype(F32)).astype(BF)
        return 0
    lax.fori_loop(0,8,su,0)
    cat=lambda ref: jnp.concatenate([ref[t].reshape(1024,128) for t in range(9)],axis=1)
    wu=wup[...].reshape(1152,256)
    gatt=nn(cat(s_hi),wu)+nn(cat(s_lo),wu)
    gres[...]=gatt.reshape(64,16,256)
    put_vec("b_proj",rowsum(gatt))
    gab=gatt.astype(BF)
    attb=X["attb"][...]
    kk, ci = iota((256,256),1), iota((256,256),0)
    peo=one_hot(ci == 2*(kk % 128) + kk // 128)
    aeo=nn(attb,peo).astype(BF)
    for t in range(9):
        hi,lo=[nt(pm[0:128,0:128],v[t].reshape(1024,128)).astype(BF) for v in (s_hi,s_lo)]
        r=nn(hi,aeo)+nn(lo,aeo)
        put_g(r[:,0:128],O_UP+t*128,0); put_g(r[:,128:256],O_UP+t*128,128)
    obb=X["ob"][...]
    put_g(nn(turn(gab),obb),O_PROJ)
    gm=nn(gab,wt[:,O_PROJ:O_PROJ+256]).astype(BF).astype(F32)
    gmx[0]=gm[:,0:128]; gmx[1]=gm[:,128:256]
    qkv=X["qkv"]
    sc_=C2**-0.5
    def pair(ref,j,n): return jnp.concatenate([ref[2*j,pl.ds(n,64,stride=16),:],ref[2*j+1,pl.ds(n,64,stride=16),:]],axis=1).astype(BF)
    s=jnp.concatenate([nt(pair(qkv,0,n),pair(qkv,1,n)) for n in range(N)],axis=0)*sc_
    e=jnp.exp(s-jnp.max(s,axis=1,keepdims=True))
    p=e/jnp.sum(e,axis=1,keepdims=True)
    ga=jnp.concatenate([nt(pair(gmx,0,n),pair(qkv,2,n)) for n in range(N)],axis=0)
    gs=(p*(ga-jnp.sum(ga*p,axis=1,keepdims=True))).astype(BF)
    pb=p.astype(BF)
    for n in range(N):
        gsn,pn=gs[64*n:64*n+64],pb[64*n:64*n+64]
        for j,o in enumerate((nn(gsn,pair(qkv,1,n))*sc_, tn(gsn,pair(qkv,0,n))*sc_, tn(pn,pair(gmx,0,n)))):
            o=o.astype(BF).astype(F32)
            gqkv[2*j,pl.ds(n,64,stride=16),:]=o[:,0:128]
            gqkv[2*j+1,pl.ds(n,64,stride=16),:]=o[:,128:256]
    gq=[jnp.concatenate([gqkv[2*j],gqkv[2*j+1]],axis=1) for j in range(3)]
    put_vec("b_query",rowsum(gq[0])); put_vec("b_value",rowsum(gq[2]))
    gqb=[g.astype(BF) for g in gq]
    da[...]=nn(jnp.concatenate(gqb,axis=1),jnp.concatenate([wt[:,O_QKV+256*j:O_QKV+256*j+256] for j in range(3)],axis=0)).reshape(64,16,256)
    nbs=S["nb"]
    def act3(y,a): nbs[pl.ds(y*8,8)]=a
    def dx3(y,dx):
        z=gres[pl.ds(y*8,8)]+dx
        gres[pl.ds(y*8,8)]=z
        gp[y+1,1:9]=z.astype(BF)
        return z
    fin=gn_bwd(X["res"],da,2,"g3","s3",256,8,S["same8"][...],8,8,act3,dx3,silu=False)
    nb=nbs[...].reshape(1024,256)
    for j in range(3): put_g(nn(turn(gqb[j]),nb),O_QKV+256*j)
    step((0,0))
    put_vec("b_res2",rowsum(fin()))
    def conv_dgrad(off):
        return nn(jnp.concatenate([gp[2-t//3:10-t//3,2-t%3:10-t%3].reshape(1024,256) for t in range(9)],axis=1),
                  jnp.concatenate([wt[:,off+256*t:off+256*t+256] for t in range(9)],axis=0))
    def conv_wgrad(g,ap,off,steps):
        gt=turn(g)
        for t in range(9):
            put_g(nn(gt,ap[t//3:t//3+8,t%3:t%3+8].reshape(1024,256)),off+256*t)
            step(*steps.get(t,()))
    def act_(y,a): pass
    conv_wgrad(gp[1:9,1:9].reshape(1024,256),X["ap2"],O_R2,{3:((0,1),),7:((1,0),)})
    da[...]=conv_dgrad(O_R2).reshape(64,16,256)
    step((1,1))
    def dxm(y,dx):
        gp[y+1,1:9]=dx.astype(BF)
        return dx
    fin=gn_bwd(X["mid"],da,1,"g2","s2",256,8,S["same8"][...],8,8,act_,dxm)
    step((0,2))
    gemb=fin()
    put_vec("b_time",rowsum(gemb)); put_vec("b_res1",rowsum(gemb))
    put_g(nn(turn(gemb.astype(BF)),X["feat"][...]),O_TIME)
    conv_wgrad(gp[1:9,1:9].reshape(1024,256),X["ap"],O_R1,{3:((0,3),),5:((2,0),),8:((1,2),)})
    da[...]=conv_dgrad(O_R1).reshape(64,16,256)
    step((2,1),(0,4))
    def dxl(y,dx):
        z=gres[pl.ds(y*8,8)]+dx
        gp[y+1,1:9]=z.astype(BF)
        return z
    fin=gn_bwd(X["low"],da,0,"g1","s1",256,8,S["same8"][...],8,8,act_,dxl)
    step((1,3))
    put_vec("b_down",rowsum(fin()))
    glb=gp[1:9,1:9].reshape(1024,256)
    glt=turn(glb)
    tp=X["tp"]
    for t in range(9):
        ty,tx=t//3,t%3
        put_g(nn(glt,tp[ty//2:ty//2+8,ty%2,tx//2:tx//2+8,tx%2].reshape(1024,128)),O_DOWN+128*t)
        if t==1: step((3,0))
    big6=big.reshape(8,2,8,2,16,128)
    dt6=S["dt"].reshape(8,2,8,2,16,128)
    SRC={0:((1,0),),1:((0,1),(2,0))}
    total=jnp.zeros((N,128),F32)
    for a in range(2):
        for b in range(2):
            taps=[(3*ty+tx,1+oy,1+ox) for ty,oy in SRC[a] for tx,ox in SRC[b]]
            z=nn(jnp.concatenate([gp[oy:oy+8,ox:ox+8].reshape(1024,256) for _,oy,ox in taps],axis=1),
                 jnp.concatenate([wt[:,O_DOWN+128*t:O_DOWN+128*t+128] for t,_,_ in taps],axis=0)).reshape(8,8,16,128)
            z=z+big6[:,a,:,b]
            dt6[:,a,:,b]=z.astype(BF)
            total=total+jnp.sum(jnp.sum(z,axis=0),axis=0)
    put_vec("b_in",rowsum(total),128)
    step((3,1),(2,2),(1,4))
    dwi=tn(X["cols"][...].reshape(4096,128),S["dt"][...].reshape(4096,128))
    for k in range(27):
        put_block(k, dwi[9*(k%3)+k//3:9*(k%3)+k//3+1])
    kept = nt(split3(sg[...]), pm[...])
    put_g((kept[0:128]+kept[128:256]+kept[256:384]).T, MID)

def bwd_scratch():
    V=pltpu.VMEM
    return dict(gp18=V((18,18,16,128),BF),gcols=V((256,16,128),BF),big=V((256,16,128),F32),ep=V((256,16,128),BF),dp=V((9,2,9,2,16,128),BF),
      s_hi=V((9,64,16,128),BF),s_lo=V((9,64,16,128),BF),gp=V((10,10,16,256),BF),da=V((64,16,256),F32),gres=V((64,16,256),F32),
      gqkv=V((6,1024,128),F32),gmx=V((2,1024,128),F32),nb=V((64,16,256),BF),dt=V((256,16,128),BF),sg=V((128,256),F32),pm=V((256,256),BF),same8=V((256,256),BF),same4=V((128,128),BF))
BIN=["out","tgt","snr","stat","cols","tp","low","mid","res","qkv","obb","attb","up","st","feat","wt","wup","wfb","sm","ap","ap2"]
GROUP = {O_UP:0, O_PROJ:9, O_QKV:11, O_R2:17, O_TIME:35, O_R1:36, O_DOWN:54, MID:63}
STORED = [next(at//128 + i - g for at, g in sorted(GROUP.items(), key=lambda e: -e[1]) if i >= g) for i in range(64)]
def bwd_call(ins, total):
    vm=pl.BlockSpec(memory_space=pltpu.VMEM)
    sc=bwd_scratch(); keys=list(sc)
    def k(*refs):
        a=dict(zip(BIN,refs[:len(BIN)])); a["v"]=a["sm"]; a["ob"]=a["obb"]; a["total"]=float(total)
        s=dict(zip(keys,refs[len(BIN)+1:]))
        s["step"],s["near"]=(lambda *_: None),False
        bwd_kernel(a,(refs[len(BIN)],),s)
    return pl.pallas_call(k,out_shape=jax.ShapeDtypeStruct((256*64,128),F32),
        in_specs=[vm]*len(BIN),out_specs=vm,scratch_shapes=list(sc.values()), name="student_backward",
        compiler_params=pltpu.CompilerParams(vmem_limit_bytes=63<<20))(*[ins[k] for k in BIN])

def student_step(D, x, tgt, snr, feat, tg, total, cid):
    V=pltpu.VMEM
    sc=scratch()
    del sc["yp"]
    sc.update(st=V((8,16,256),F32), cols=V((256,16,128),BF), attb=V((1024,256),BF), obb=V((1024,256),BF), ap2=V((10,10,16,256),BF),
              out=V((256,16,128),F32), part=V((8,128),F32))
    sc.update({k:v for k,v in bwd_scratch().items() if k not in ("gp18","big","ep","gmx","dt","same8","same4")})
    sc.update(box=V((10,8,128),F32), send=pltpu.SemaphoreType.DMA((5,)), recv=pltpu.SemaphoreType.DMA((5,)), load=pltpu.SemaphoreType.DMA((2,)),
              g=V((256*64,128),F32), own=V((8,64,128),F32))
    sc.update(scatter_scratch())
    keys=list(sc)
    def kern(x_ref,t_ref,snr_ref,feat_ref,tg_ref,grad_ref,sum_ref,*refs):
        s=dict(zip(keys,refs))
        s["yp"]=s["g"].at[0:14400].reshape(9,10,10,16,128)
        s=views(s)
        out,top=s["out"],s["top"]
        take=pltpu.make_async_copy(x_ref,out,s["load"].at[0])
        take.start()
        greet(partners())
        zero_borders(s)
        prep(tg_ref,*(s[k] for k in WKEYS),D)
        take.wait()
        fin=net(out,feat_ref[...],s["wt"],s["wup"],s["win"],s["wfin"],s["sm"],s)
        take=pltpu.make_async_copy(t_ref,top,s["load"].at[1])
        take.start()
        def put(y4,e): out[pl.ds(y4*128,128)]=e
        fin(put)
        take.wait()
        loss_sums(top,out,snr_ref,s["part"])
        sum_kernel(s["part"],sum_ref,s["box"],s["send"],s["recv"])
        a={k:s[k] for k in BIN if k in s}
        a.update(tgt=top,snr=snr_ref,stat=sum_ref,feat=feat_ref,v=s["sm"],ob=s["obb"],total=float(total))
        own=s["own"]
        advance,finish=scatter_steps(s["g"].reshape(8,2,2,2,2,4,4,8,128),own.reshape(2,4,64,128),s)
        def step(*moves):
            for m in moves: advance(*m)
        s.update(gp18=s["xp"],big=top,ep18=s["ep"],gmx=s["ob"],dt=s["gcols"],step=step,near=True)
        bwd_kernel(a,(s["g"],),s)
        step((4,0),(4,1),(3,2),(2,3),(3,3),(4,2))
        kq,lq=iota((768,768),0),iota((768,768),1)
        at=O_QKV//128
        rows=nn(split3(jnp.concatenate([own[:,at+i] for i in range(6)],axis=1)),one_hot(lq==3*(kq%256)+kq//256))
        rows=rows[0:8]+rows[8:16]+rows[16:24]
        for i in range(6): own[:,at+i]=rows[:,128*i:128*i+128]
        step((2,4),(4,3),(3,4),(4,4))
        finish()
        for hi in range(2):
            shift=14-hi
            src=own[4-4*hi:8-4*hi]
            mid=pltpu.roll(src.reshape(256,128),shift,1).reshape(4,64,128)
            rest=own[4*hi:4*hi+4,63:64]
            for k in range(64):
                before=rest[:,0] if k==0 else mid[:,k-1]
                after=rest[:,0] if k==63 else mid[:,k]
                grad_ref[4*hi:4*hi+4,128*k:128*k+128]=jnp.where(iota((1,128),1)<shift,before,after)
    vm,any_=pl.BlockSpec(memory_space=pltpu.VMEM),pl.BlockSpec(memory_space=pl.ANY)
    return pl.pallas_call(kern,out_shape=(jax.ShapeDtypeStruct((8,MID+128),F32),jax.ShapeDtypeStruct((8,128),F32)),
        in_specs=[any_,any_,vm,vm,vm],out_specs=(vm,vm),scratch_shapes=list(sc.values()), name="student_step",
        compiler_params=pltpu.CompilerParams(vmem_limit_bytes=63<<20, collective_id=cid, has_side_effects=True))(x,tgt,snr,feat,tg)

def segments():
    matrices = [("w_in", 27, C1), ("w_down", 9 * C1, C2), ("w_res1", 9 * C2, C2), ("w_res2", 9 * C2, C2), ("w_time", C1, C2),
                ("w_qkv", C2, 3 * C2), ("w_proj", C2, C2), ("w_up", 9 * C2, C1), ("w_final", 9 * C1, 3)]
    vectors = [("g1", C2), ("s1", C2), ("g2", C2), ("s2", C2), ("g3", C2), ("s3", C2), ("g4", C1), ("s4", C1), ("b_in", C1),
               ("b_down", C2), ("b_res1", C2), ("b_res2", C2), ("b_time", C2), ("b_query", C2), ("b_value", C2), ("b_proj", C2),
               ("b_up", C1), ("b_final", 3)]
    listing, cursor = [], 0
    for name, height, breadth in matrices:
        listing.append((name, cursor, (height, breadth), "matrix"))
        cursor += height * breadth
    for name, length in vectors:
        listing.append((name, cursor, (length,), "gain" if name[0] != "b" else "bias"))
        cursor += length
    return listing

def rates(position):
    learn = jnp.zeros(position.shape, F32)
    decay = jnp.zeros(position.shape, F32)
    for name, offset, shape, kind in segments():
        inside = (position >= offset) & (position < offset + math.prod(shape))
        if kind == "matrix":
            spread = shape[0] ** (-0.5) * ((SIDE * SIDE / 4.0) ** 0.5 if name == "w_proj" else 1.0)
            learn = jnp.where(inside, 0.5 * spread, learn)
            decay = jnp.where(inside, 0.01, decay)
        elif kind == "gain":
            learn = jnp.where(inside, 0.2, learn)
        else:
            learn = jnp.where(inside, 0.05, learn)
    return learn, decay

def angle_of(step):
    return 0.1 + 1.35 * step.astype(F32) / TGRID

def time_features(step):
    half = C1 // 2
    freqs = jnp.exp(-math.log(1000.0) * jnp.arange(half).astype(F32) / half)
    phases = step.astype(F32)[..., None] * freqs
    return jnp.concatenate([jnp.sin(phases), jnp.cos(phases)], axis=-1)

def to_columns(shard, R):
    cols = jnp.swapaxes(shard.reshape(shard.shape[:-1] + (-1, R)), -1, -2)
    return jnp.pad(cols, ((0,0),)*(cols.ndim-1) + ((0,MID+128-cols.shape[-1]),))

def from_columns(cols, start, D, L):
    R = 256 // D
    body = R * MID
    def piece(at, width): return cols[:, 128*GROUP[at]:128*GROUP[at]+width]
    q = piece(O_QKV,768).reshape(R,3,256).transpose(0,2,1).reshape(R,768)
    cols = jnp.concatenate([piece(O_DOWN,1152), piece(O_R1,2304), piece(O_R2,2304), piece(O_TIME,128), q, piece(O_PROJ,256), piece(O_UP,1152),
                            piece(MID,L//R-MID)], axis=1)
    flat = cols.T.reshape(-1)
    if HEAD % D == 0:
        return jnp.concatenate([flat[body:body+start], flat[:body], flat[body+start:]])
    rest = flat[body:]
    at = jnp.arange(L)
    mid = lax.dynamic_update_slice(jnp.zeros((L,), F32), flat[:body], (start,))
    low = jnp.pad(rest, (0, body)); high = jnp.pad(rest, (body, 0))
    return jnp.where(at < start, low, jnp.where(at < start + body, mid, high))

def lanes(images):
    v = jnp.repeat(images.transpose(1,2,0,3).reshape(256,N,3), 9, axis=2)
    return jnp.pad(v, ((0,0),(0,0),(0,101)))

def local(images, noise, timestep, stride, bucket, steps_table, master, first_moment, second_moment, teacher, step_count):
    axes = ("dp", "mp")
    D = lax.axis_size("dp") * lax.axis_size("mp")
    me = lax.axis_index(axes)
    R, L = 256 // D, master.shape[0]
    start = HEAD // D if HEAD % D == 0 else (HEAD - me + D - 1) // D
    near = lax.axis_size("dp") == 16 and lax.axis_size("mp") == 2
    teacher_cols, student_cols = to_columns(jnp.stack([teacher, master.astype(BF)]), R)
    angle = angle_of(timestep)
    if near:
        teacher_all, noisy = gather_call(teacher_cols, jnp.cos(angle), jnp.sin(angle), images, noise, 1)
    else:
        teacher_all = lax.all_gather(teacher_cols, axes, axis=0, tiled=True)
        noisy = lanes(jnp.cos(angle)[:,None,None,None] * images + jnp.sin(angle)[:,None,None,None] * noise)
    student_all = lax.all_gather(student_cols, axes, axis=0, tiled=True)
    wide = lambda v: jnp.where(jnp.arange(128) < 27, v[..., None], 0.0)
    picked = jnp.sum(jnp.where(jnp.arange(steps_table.shape[0]) == bucket[0], steps_table, 0))
    turn = jnp.arange(KMAX)[:, None]
    current = timestep[None] - turn * stride[None]
    later = current - stride[None]
    keep = jnp.sin(angle_of(later)) / jnp.sin(angle_of(current))
    take = jnp.cos(angle_of(later)) - keep * jnp.cos(angle_of(current))
    features = jax.nn.silu(time_features(current)).astype(BF)
    final_t = timestep - picked * stride
    below = jnp.sin(angle - angle_of(final_t))
    target = teacher_call(D, picked.reshape(1), noisy, features, wide(take), wide(keep), wide(jnp.sin(angle)/below),
                          wide(-jnp.sin(angle_of(final_t))/below), teacher_all)
    snr = wide(jnp.maximum(jnp.square(jnp.cos(angle)/jnp.sin(angle)), 1.0))
    total = images.shape[0] * D
    if near:
        grads, sums = student_step(D, noisy, target, snr, features[0], student_all, total, 2)
    else:
        out, sums, kept = student_call(D, noisy, target, snr, features[0], student_all)
        sums = lax.psum(sums, axes)
        grads = bwd_call(dict(kept, out=out, tgt=target, snr=snr, stat=sums, feat=features[0]), total)
    pick = sums[:5, 0:27:9]
    mean_t, mean_o = pick[0]/(256*total), pick[2]/(256*total)
    var_t, var_o = pick[1]/(256*total) - jnp.square(mean_t), pick[3]/(256*total) - jnp.square(mean_o)
    loss = jnp.sum(pick[4])/(768*total) + jnp.sum(jnp.square(mean_o-mean_t) + jnp.square(var_o-var_t))
    if near:
        part = grads
    else:
        order = grads.reshape(R, D, MID+128)
        if HEAD % D:
            order = jnp.concatenate([jnp.roll(order[:, :, :MID], HEAD % D, axis=1), order[:, :, MID:]], axis=2)
        part = lax.psum_scatter(order, axes, scatter_dimension=1, tiled=True).reshape(R, MID+128)
    grad = part[:, :L//R].T.reshape(-1) if near else from_columns(part, start, D, L)
    learn, decay = rates(jnp.arange(L, dtype=jnp.int32) * D + me)
    steps_done = step_count[0].astype(F32)
    new_first = 0.5 * first_moment + 0.5 * grad
    new_second = 0.5 * second_moment + 0.5 * jnp.square(grad)
    fix_rate = 1.0 - jnp.power(0.5, steps_done)
    new_master = master - learn * (new_first / fix_rate / (jnp.sqrt(new_second / fix_rate) + 1e-08) + decay * master)
    return loss, new_master, new_first, new_second

def solution(mesh):
    s = P(("dp", "mp"))
    i = P(("dp", "mp"), None, None, None)
    return jax.shard_map(local, mesh=mesh, in_specs=(i, i, s, s, s, P(), s, s, s, s, P()), out_specs=(P(), s, s, s), check_vma=False)
```
